32 devices in a mesh: dp: 8 (over z, x), mp: 4 (over y, core).
Axes of the slice: x: 2, y: 2, z: 4, core: 2. Of those that a mesh axis runs over, the one named last changes fastest.
Arguments:
- hidden_in: bfloat16 [8, 2048, 960], P('dp', 'mp'), may hold values from -6 to 6
- cotangent: bfloat16 [8, 2048, 960], P('dp', 'mp'), may hold values from -6 to 6
- segments: int32 [8, 2048], P('dp'), may hold values from 0 to 3, never falling along the last dimension, each value on 1 to 1024 neighbouring positions
- positions: int32 [8, 2048], P('dp', 'mp'), may hold values from 0 to 4095
- attn_in: bfloat16 [960, 1600], P('dp', 'mp'), may hold values from -0.1875 to 0.1875
- attn_out: bfloat16 [960, 960], P('mp', 'dp'), may hold values from -0.75 to 0.75
- w_gate: bfloat16 [960, 2560], P('dp', 'mp'), may hold values from -0.1875 to 0.1875
- w_up: bfloat16 [960, 2560], P('dp', 'mp'), may hold values from -0.1875 to 0.1875
- w_down: bfloat16 [2560, 960], P('mp', 'dp'), may hold values from -0.125 to 0.125
- norm1_gain: bfloat16 [960], P('dp'), may hold values from 0.099609375 to 1.8984375
- norm2_gain: bfloat16 [960], P('dp'), may hold values from 0.099609375 to 1.8984375
Outputs:
- hidden_out: bfloat16 [8, 2048, 960], P('dp', 'mp')
- grad_hidden: float32 [8, 2048, 960], P('dp', 'mp')
- grad_attn_in: float32 [960, 1600], P('dp', 'mp')
- grad_attn_out: float32 [960, 960], P('mp', 'dp')
- grad_gate: float32 [960, 2560], P('dp', 'mp')
- grad_up: float32 [960, 2560], P('dp', 'mp')
- grad_down: float32 [2560, 960], P('mp', 'dp')
- grad_gain1: float32 [960], P('dp')
- grad_gain2: float32 [960], P('dp')
The draws below stay inside these ranges and needn't reach their ends.
Inputs may be any that keep to these rules, and one draw needn't show every extreme that they name: `segments`: segment numbers never fall along a sequence; every segment is a run of 1 to 1024 tokens.
All inputs are finite; a program needn't handle non-finite values.
Results may differ from the reference program's by a relative error of at most 0.015.
Values may be sent and summed in bfloat16 or wider, within the bound.
A program may use at most 192 MiB of HBM per device.

```python
import math
import jax
import jax.numpy as jnp
import numpy as np
from jax import lax

D = 960
HEADS = 15
KV_HEADS = 5
HEAD_DIM = 64
FF = 2560
SEQ_LEN = 2048
SEQS = 8
QKV = 1600
QW = 960


def set_ends(entries, rng, least, top_value):
    spot = [jax.random.randint(jax.random.fold_in(rng, axis), (), 0, length) for axis, length in enumerate(entries.shape)]
    main_axis = entries.shape.index(max(entries.shape))
    beside = spot[:main_axis] + [(spot[main_axis] + 1) % entries.shape[main_axis]] + spot[main_axis + 1:]
    return entries.at[tuple(spot)].set(least).at[tuple(beside)].set(top_value)


def block_scale(stream_key, dims, shards, smallest, high):
    level = 1.0
    for dim, parts in shards:
        heights = jax.random.uniform(jax.random.fold_in(jax.random.fold_in(stream_key, 6), dim), (parts,), jnp.float32, smallest / len(shards), high / len(shards))
        level = level * jnp.repeat(jnp.exp(heights), dims[dim] // parts).reshape((-1,) + (1,) * (len(dims) - 1 - dim))
    return level


def length_profile(amount, total, bound, skew):
    loads = [(1 << 20) // math.isqrt(standing ** skew) + 1 for standing in range(2, amount + 1)]
    rest, counts = total - bound - (amount - 1), [1] * (amount - 1)
    while rest > 0:
        candidates = [i for i in range(amount - 1) if counts[i] < bound]
        pool, left = sum([loads[i] for i in candidates]), rest
        for i in candidates:
            addition = min(bound - counts[i], max(1, left * loads[i] // pool), rest)
            counts[i] = counts[i] + addition
            rest = rest - addition
    return np.array([bound] + counts)


def ragged_sizes(key, count, total, most, slope):
    if count == 2:
        one = jax.random.randint(key, (), max(1, total - most), min(most, total - 1) + 1)
        return jnp.stack([one, total - one])
    lengths = jnp.asarray(length_profile(count, total, most, slope), jnp.int32)
    pairs = (count - 1) // 2
    donor, taker = lengths[1:1 + 2 * pairs:2], lengths[2:2 + 2 * pairs:2]
    room = jnp.minimum(donor - 1, most - taker)
    passed = jax.random.randint(jax.random.fold_in(key, 1), (pairs,), 0, 1 << 20) % (room + 1)
    lengths = lengths.at[1:1 + 2 * pairs:2].set(donor - passed).at[2:2 + 2 * pairs:2].set(taker + passed)
    return lengths[jax.random.permutation(jax.random.fold_in(key, 2), count)]


def centred(key, shape, deviation, most, shards=(), kind=jnp.bfloat16):
    level = block_scale(key, shape, shards, -0.22, 0.18) if shards else 1.0
    result = jax.random.normal(key, shape, jnp.float32) * deviation * level
    return jnp.minimum(jnp.maximum(result, -most), most).astype(kind)


def setup_inputs(seed: int = 0) -> dict:
    arg_keys = jax.random.split(jax.random.key(seed), 12)
    return {
        "hidden_in": centred(arg_keys[0], (SEQS, SEQ_LEN, D), 1.0, 6.0, ((0, 8), (1, 4))),
        "cotangent": centred(arg_keys[1], (SEQS, SEQ_LEN, D), 1.0, 6.0, ((0, 8), (1, 4))),
        "segments": jax.vmap(lambda own: jnp.searchsorted(jnp.cumsum(ragged_sizes(own, 4, SEQ_LEN, SEQ_LEN // 2, 2)), jnp.arange(SEQ_LEN), side="right"))(jax.random.split(arg_keys[2], SEQS)).reshape((SEQS, SEQ_LEN)).astype(jnp.int32),
        "positions": set_ends(jax.random.randint(arg_keys[3], (SEQS, SEQ_LEN), 0, 2 * SEQ_LEN), jax.random.fold_in(arg_keys[3], 1), 0, (2 * SEQ_LEN) - 1).astype(jnp.int32),
        "attn_in": centred(arg_keys[4], (D, QKV), D ** -0.5, 0.1875, ((0, 8), (1, 4))),
        "attn_out": centred(arg_keys[5], (QW, D), (QW // 16) ** -0.5, 0.75, ((0, 4), (1, 8))),
        "w_gate": centred(arg_keys[6], (D, FF), D ** -0.5, 0.1875, ((0, 8), (1, 4))),
        "w_up": centred(arg_keys[7], (D, FF), D ** -0.5, 0.1875, ((0, 8), (1, 4))),
        "w_down": centred(arg_keys[8], (FF, D), FF ** -0.5, 0.125, ((0, 4), (1, 8))),
        "norm1_gain": jnp.clip(1.0 + 0.18 * jax.random.normal(arg_keys[9], (D,), jnp.float32), 0.099609375, 1.8984375).astype(jnp.bfloat16),
        "norm2_gain": jnp.clip(1.0 + 0.18 * jax.random.normal(arg_keys[10], (D,), jnp.float32), 0.099609375, 1.8984375).astype(jnp.bfloat16),
    }


EPSILON = 1e-05
SCORE_SCALE = 0.125
MASK_FILL = -1e+30

def rms_forward(values_in, gain):
    inverse = lax.rsqrt(lax.optimization_barrier(jnp.mean(values_in * values_in, axis=-1, keepdims=True)) + EPSILON)
    return (values_in * inverse * gain, inverse)

def rms_backward(values_in, inverse, gain, upstream):
    scaled = upstream * gain
    grad_in = inverse * (scaled - values_in * inverse * inverse * lax.optimization_barrier(jnp.mean(scaled * values_in, axis=-1, keepdims=True)))
    return (grad_in, lax.optimization_barrier(jnp.sum(upstream * values_in * inverse, axis=0)))

def rotary_tables(position_ids):
    half_dim = HEAD_DIM // 2
    frequency = jnp.exp(jnp.arange(half_dim, dtype=jnp.float32) * (-2.0 * math.log(10000.0) / HEAD_DIM))
    angles = position_ids.astype(jnp.float32)[:, None] * frequency[None, :]
    return (jnp.cos(angles)[:, None, :], jnp.sin(angles)[:, None, :])

def rotate(tensor, cosine, sine):
    half_dim = HEAD_DIM // 2
    first, second = (tensor[..., :half_dim], tensor[..., half_dim:])
    return jnp.concatenate([first * cosine - second * sine, second * cosine + first * sine], axis=-1)

def rotate_back(tensor, cosine, sine):
    half_dim = HEAD_DIM // 2
    first, second = (tensor[..., :half_dim], tensor[..., half_dim:])
    return jnp.concatenate([first * cosine + second * sine, second * cosine - first * sine], axis=-1)

def score_block(queries, keys, allowed):
    scores = jnp.einsum('grd,sd->grs', queries.astype(jnp.float32), keys.astype(jnp.float32)) * SCORE_SCALE
    return jnp.where(allowed[None], scores, MASK_FILL)

def attend(queries, keys, values, allowed):
    scores = score_block(queries, keys, allowed)
    peak = lax.optimization_barrier(jnp.max(scores, axis=-1, keepdims=True))
    total = lax.optimization_barrier(jnp.sum(jnp.exp(scores - peak), axis=-1, keepdims=True))
    log_total = peak + jnp.log(total)
    probs = jnp.exp(scores - log_total).astype(jnp.bfloat16)
    output = jnp.einsum('grs,sd->grd', probs.astype(jnp.float32), values.astype(jnp.float32))
    return (output, log_total[..., 0])

def attend_back(queries, keys, values, allowed, log_total, output_b, grad_out_b):
    scores = score_block(queries, keys, allowed)
    probs = jnp.exp(scores - log_total[..., None])
    probs_b = probs.astype(jnp.bfloat16)
    grad_out = grad_out_b.astype(jnp.float32)
    grad_probs = jnp.einsum('grd,sd->grs', grad_out, values.astype(jnp.float32))
    delta = lax.optimization_barrier(jnp.sum(grad_out * output_b.astype(jnp.float32), axis=-1, keepdims=True))
    grad_scores = (probs * (grad_probs - delta)).astype(jnp.bfloat16).astype(jnp.float32)
    grad_q = jnp.einsum('grs,sd->grd', grad_scores, keys.astype(jnp.float32)) * SCORE_SCALE
    grad_k = jnp.einsum('grs,grd->sd', grad_scores, queries.astype(jnp.float32)) * SCORE_SCALE
    grad_v = jnp.einsum('grs,grd->sd', probs_b.astype(jnp.float32), grad_out)
    return (grad_q, grad_k, grad_v)

def reference(hidden_in, cotangent, segments, positions, attn_in, attn_out, w_gate, w_up, w_down, norm1_gain, norm2_gain):
    group_size = HEADS // KV_HEADS
    query_cols = HEADS * HEAD_DIM
    kv_cols = KV_HEADS * HEAD_DIM
    gain_one = norm1_gain.astype(jnp.float32)
    gain_two = norm2_gain.astype(jnp.float32)

    def one_sequence(carry, inputs):
        seq_in, seq_cot, seq_seg, seq_pos = inputs
        seq_rows = seq_in.shape[0]
        resid_in = seq_in.astype(jnp.float32)
        normed1, inv_one = rms_forward(resid_in, gain_one)
        normed1_b = normed1.astype(jnp.bfloat16)
        projected = jnp.dot(normed1_b, attn_in, preferred_element_type=jnp.float32)
        cosine, sine = rotary_tables(seq_pos)
        queries = rotate(projected[:, :query_cols].reshape(seq_rows, HEADS, HEAD_DIM), cosine, sine).astype(jnp.bfloat16)
        keys = rotate(projected[:, query_cols:query_cols + kv_cols].reshape(seq_rows, KV_HEADS, HEAD_DIM), cosine, sine).astype(jnp.bfloat16)
        values = projected[:, query_cols + kv_cols:].reshape(seq_rows, KV_HEADS, HEAD_DIM).astype(jnp.bfloat16)
        index = jnp.arange(seq_rows, dtype=jnp.int32)
        allowed = (seq_seg[:, None] == seq_seg[None, :]) & (index[None, :] <= index[:, None])
        query_groups = queries.reshape(seq_rows, KV_HEADS, group_size, HEAD_DIM).transpose(1, 2, 0, 3)
        key_groups = keys.transpose(1, 0, 2)
        value_groups = values.transpose(1, 0, 2)
        outputs, log_totals = lax.map(lambda pack: attend(pack[0], pack[1], pack[2], allowed), (query_groups, key_groups, value_groups))
        out_groups = outputs.astype(jnp.bfloat16)
        attn_b = out_groups.transpose(2, 0, 1, 3).reshape(seq_rows, query_cols)
        middle = resid_in + jnp.dot(attn_b, attn_out, preferred_element_type=jnp.float32)
        normed2, inv_two = rms_forward(middle, gain_two)
        normed2_b = normed2.astype(jnp.bfloat16)
        gate = jnp.dot(normed2_b, w_gate, preferred_element_type=jnp.float32)
        upper = jnp.dot(normed2_b, w_up, preferred_element_type=jnp.float32)
        sigma = jax.nn.sigmoid(gate)
        silu_gate = gate * sigma
        hidden_b = (silu_gate * upper).astype(jnp.bfloat16)
        seq_out = (middle + jnp.dot(hidden_b, w_down, preferred_element_type=jnp.float32)).astype(jnp.bfloat16)
        cot_f = seq_cot.astype(jnp.float32)
        g_down = jnp.dot(hidden_b.T, seq_cot, preferred_element_type=jnp.float32)
        grad_hid = jnp.dot(seq_cot, w_down.T, preferred_element_type=jnp.float32)
        grad_gate_act = (grad_hid * upper * sigma * (1.0 + gate * (1.0 - sigma))).astype(jnp.bfloat16)
        grad_up_act = (grad_hid * silu_gate).astype(jnp.bfloat16)
        g_gate = jnp.dot(normed2_b.T, grad_gate_act, preferred_element_type=jnp.float32)
        g_up = jnp.dot(normed2_b.T, grad_up_act, preferred_element_type=jnp.float32)
        grad_norm2 = jnp.dot(grad_gate_act, w_gate.T, preferred_element_type=jnp.float32) + jnp.dot(grad_up_act, w_up.T, preferred_element_type=jnp.float32)
        grad_mid_norm, g_gain2 = rms_backward(middle, inv_two, gain_two, grad_norm2)
        grad_middle = cot_f + grad_mid_norm
        middle_b = grad_middle.astype(jnp.bfloat16)
        g_out = jnp.dot(attn_b.T, middle_b, preferred_element_type=jnp.float32)
        grad_attn_b = jnp.dot(middle_b, attn_out.T, preferred_element_type=jnp.float32).astype(jnp.bfloat16)
        grad_groups = grad_attn_b.reshape(seq_rows, KV_HEADS, group_size, HEAD_DIM).transpose(1, 2, 0, 3)
        grad_q, grad_k, grad_v = lax.map(lambda pack: attend_back(pack[0], pack[1], pack[2], allowed, pack[3], pack[4], pack[5]), (query_groups, key_groups, value_groups, log_totals, out_groups, grad_groups))
        grad_q = rotate_back(grad_q.transpose(2, 0, 1, 3).reshape(seq_rows, HEADS, HEAD_DIM), cosine, sine)
        grad_k = rotate_back(grad_k.transpose(1, 0, 2), cosine, sine)
        grad_v = grad_v.transpose(1, 0, 2)
        grad_proj = jnp.concatenate([grad_q.reshape(seq_rows, query_cols), grad_k.reshape(seq_rows, kv_cols), grad_v.reshape(seq_rows, kv_cols)], axis=1).astype(jnp.bfloat16)
        g_in = jnp.dot(normed1_b.T, grad_proj, preferred_element_type=jnp.float32)
        grad_norm1 = jnp.dot(grad_proj, attn_in.T, preferred_element_type=jnp.float32)
        grad_in_norm, g_gain1 = rms_backward(resid_in, inv_one, gain_one, grad_norm1)
        grad_input = grad_middle + grad_in_norm
        acc_in, acc_out, acc_gate, acc_up, acc_down, acc_g1, acc_g2 = carry
        new_carry = (acc_in + g_in, acc_out + g_out, acc_gate + g_gate, acc_up + g_up, acc_down + g_down, acc_g1 + g_gain1, acc_g2 + g_gain2)
        return (new_carry, (seq_out, grad_input))
    start = (jnp.zeros(attn_in.shape, jnp.float32), jnp.zeros(attn_out.shape, jnp.float32), jnp.zeros(w_gate.shape, jnp.float32), jnp.zeros(w_up.shape, jnp.float32), jnp.zeros(w_down.shape, jnp.float32), jnp.zeros(norm1_gain.shape, jnp.float32), jnp.zeros(norm2_gain.shape, jnp.float32))
    totals, (hidden_out, grad_hidden) = lax.scan(one_sequence, start, (hidden_in, cotangent, segments, positions))
    return (hidden_out, grad_hidden, totals[0], totals[1], totals[2], totals[3], totals[4], totals[5], totals[6])
```

```python
import functools
import math

import jax
import jax.numpy as jnp
from jax import lax
from jax.experimental import pallas as pl
from jax.experimental.pallas import tpu as pltpu
from jax.sharding import PartitionSpec as P

HEADS = 15
KV_HEADS = 5
GROUP = HEADS // KV_HEADS
HEAD_DIM = 64
DPAD = 1024
TILE = 256
EPSILON = 1e-05
SCORE_SCALE = 0.125
MASK_FILL = -1e30
LOG2E = 1.4426950408889634
EXP_SCALE = SCORE_SCALE * LOG2E
BF16 = jnp.bfloat16
F32 = jnp.float32


def dot(a, b):
    return jnp.dot(a, b, preferred_element_type=F32)


def dot_nt(a, b):
    return lax.dot_general(a, b, (((1,), (1,)), ((), ())), preferred_element_type=F32)


def vmem_specs(count):
    return [pl.BlockSpec(memory_space=pltpu.VMEM)] * count


def params():
    return pltpu.CompilerParams(vmem_limit_bytes=56 << 20)


class Links:
    def __init__(self, dp_size):
        self.dp_size = dp_size
        self.depth = dp_size // 2

    def pairs(self, move):
        found = []
        for d in range(self.dp_size):
            for m in range(4):
                target = move(d, m)
                if target is not None:
                    found.append((d * 4 + m, target[0] * 4 + target[1]))
        return found

    def send(self, value, move):
        return lax.ppermute(value, ("dp", "mp"), self.pairs(move))

    def over_z(self, value, k):
        return self.send(value, lambda d, m: (d ^ (2 * k), m))

    def over_x(self, value):
        return self.send(value, lambda d, m: (d ^ 1, m))

    def over_y(self, value):
        return self.send(value, lambda d, m: (d, m ^ 2))

    def over_core(self, value):
        return self.send(value, lambda d, m: (d, m ^ 1))

    def some(self, value, table):
        return self.send(value, lambda d, m: (d, table[m]) if m in table else None)

    def gather(self, value):
        half = self.depth // 2
        own = jnp.stack([value] + [self.over_z(value, k) for k in range(1, self.depth)])
        by_x = self.over_x(own)
        by_y = self.over_y(own)
        low = self.over_y(by_x[:half])
        high = self.over_x(by_y[half:])
        return own, by_x, by_y, low, high

    def scatter(self, parts):
        p00, p01a, p01b, p10a, p10b, p11a, p11b = parts
        half = self.depth // 2
        r11a = self.over_y(p11a)
        r11b = self.over_x(p11b)
        r01b = self.over_x(p01b)
        r10a = self.over_y(p10a)
        s01a = (p01a.astype(F32) + r11a.astype(F32)).astype(BF16)
        s10b = (p10b.astype(F32) + r11b.astype(F32)).astype(BF16)
        r01a = self.over_x(s01a)
        r10b = self.over_y(s10b)
        sums = p00.astype(F32) + jnp.concatenate(
            [r10a.astype(F32) + r01a.astype(F32), r01b.astype(F32) + r10b.astype(F32)], axis=0
        )
        total = sums[0]
        for k in range(1, self.depth):
            total = total + self.over_z(sums[k].astype(BF16), k).astype(F32)
        return total

    def all_sum(self, value):
        value = value + self.over_core(value)
        value = value + self.over_y(value)
        value = value + self.over_x(value)
        k = 1
        while k < self.depth:
            value = value + self.over_z(value, k)
            k *= 2
        return value


def assemble_kernel(depth, rows, pad, ids, own, by_x, by_y, low, high, out):
    dp_index, y = ids[0], ids[1]
    half = depth // 2
    out[...] = jnp.zeros_like(out)
    for jz in range(depth):
        for jx in range(2):
            for jy in range(2):
                if jx and jy:
                    block = low[jz] if jz < half else high[jz - half]
                else:
                    block = (by_x if jx else by_y if jy else own)[jz]
                start = pl.multiple_of((dp_index ^ (2 * jz + jx)) * pad, pad)
                out[y ^ jy, pl.ds(start, rows), :] = block


def assemble(blocks, ids):
    depth, rows, cols = blocks[0].shape
    pad = DPAD // (2 * depth)
    return pl.pallas_call(
        functools.partial(assemble_kernel, depth, rows, pad),
        out_shape=jax.ShapeDtypeStruct((2, DPAD, cols), BF16),
        in_specs=[pl.BlockSpec(memory_space=pltpu.SMEM)] + vmem_specs(5),
        out_specs=pl.BlockSpec(memory_space=pltpu.VMEM),
        compiler_params=params(),
        cost_estimate=pl.CostEstimate(
            flops=0, bytes_accessed=DPAD * cols * 8, transcendentals=0
        ),
        name="assemble",
    )(ids, *blocks)


def wgrad_plane_kernel(depth, rows, pad, ids, lhs, rhs, *refs):
    outs, acc = refs[:-1], refs[-1]
    dp_index, y = ids[0], ids[1]
    z, x = dp_index // 2, dp_index % 2
    half = depth // 2
    for part in range(2):

        def body(i, carry):
            jz = part * half + i
            start = pl.multiple_of((z ^ jz) * (2 * pad), 2 * pad)
            left = lhs[pl.ds(start, 2 * pad), :]
            for jy in range(2):
                acc[...] = dot(left, rhs[y ^ jy])
                for jx in range(2):
                    block = acc[pl.ds(pl.multiple_of((x ^ jx) * pad, pad), rows), :]
                    if jy == 0 and jx == 0:
                        outs[0][jz] = block.astype(BF16)
                    else:
                        outs[1 + 2 * (2 * jy + jx - 1) + part][i] = block.astype(BF16)
            return carry

        lax.fori_loop(0, half, body, 0)


def wgrad_plane(lhs, rhs, ids, depth, rows):
    pad = DPAD // (2 * depth)
    tokens, cols = rhs.shape[1:]
    full = jax.ShapeDtypeStruct((depth, rows, cols), BF16)
    part = jax.ShapeDtypeStruct((depth // 2, rows, cols), BF16)
    order = [full, part, part, part, part, part, part]
    return pl.pallas_call(
        functools.partial(wgrad_plane_kernel, depth, rows, pad),
        out_shape=order,
        in_specs=[pl.BlockSpec(memory_space=pltpu.SMEM)] + vmem_specs(2),
        out_specs=vmem_specs(7),
        scratch_shapes=[pltpu.VMEM((2 * pad, cols), F32)],
        compiler_params=params(),
        cost_estimate=pl.CostEstimate(
            flops=4 * DPAD * tokens * cols, bytes_accessed=DPAD * (tokens + 4 * cols) * 2,
            transcendentals=0,
        ),
        name="wgrad_plane",
    )(ids, lhs, rhs)


def wgrad_all_kernel(depth, rows, pad, ids, lhs, rhs, own, oth, acc):
    dp_index, m = ids[0], ids[2]
    z, x = dp_index // 2, dp_index % 2

    def body(jz, carry):
        start = pl.multiple_of((z ^ jz) * (2 * pad), 2 * pad)
        left = lhs[pl.ds(start, 2 * pad), :]
        for jy in range(2):
            for jc in range(2):
                acc[...] = dot(left, rhs[m ^ (2 * jy + jc)])
                for jx in range(2):
                    block = acc[pl.ds(pl.multiple_of((x ^ jx) * pad, pad), rows), :]
                    (oth if jc else own)[jy, jx, jz] = block.astype(BF16)
        return carry

    lax.fori_loop(0, depth, body, 0)


def wgrad_all(lhs, rhs, ids, depth, rows):
    pad = DPAD // (2 * depth)
    tokens, cols = rhs.shape[1:]
    shape = jax.ShapeDtypeStruct((2, 2, depth, rows, cols), BF16)
    return pl.pallas_call(
        functools.partial(wgrad_all_kernel, depth, rows, pad),
        out_shape=[shape, shape],
        in_specs=[pl.BlockSpec(memory_space=pltpu.SMEM)] + vmem_specs(2),
        out_specs=vmem_specs(2),
        scratch_shapes=[pltpu.VMEM((2 * pad, cols), F32)],
        compiler_params=params(),
        cost_estimate=pl.CostEstimate(
            flops=8 * DPAD * tokens * cols, bytes_accessed=DPAD * (tokens + 8 * cols) * 2,
            transcendentals=0,
        ),
        name="wgrad_all",
    )(ids, lhs, rhs)


def scatter_all(links, own, oth):
    half = links.depth // 2
    got = links.over_core(oth)
    total = (own.astype(F32) + got.astype(F32)).astype(BF16)
    return links.scatter(
        (
            total[0, 0],
            total[0, 1, :half],
            total[0, 1, half:],
            total[1, 0, :half],
            total[1, 0, half:],
            total[1, 1, :half],
            total[1, 1, half:],
        )
    )


def transposed(value):
    return value.astype(F32).T.astype(BF16)


def mask_tile(segment_start, q_tile, k_tile, tokens):
    key = k_tile * TILE + lax.broadcasted_iota(jnp.int32, (TILE, TILE), 0)
    query = 2 * tokens + q_tile * TILE + lax.broadcasted_iota(jnp.int32, (TILE, TILE), 1)
    allowed = (key >= segment_start) & (key <= query)
    return jnp.where(allowed, 0.0, MASK_FILL)


def attend_kernel(tokens, first, seg, q, kv2, kv1, kv0, out, lse, q_t, k3, v_t, acc, peak, total, bias):
    q_t[...] = transposed(q[...])
    for s, kv in enumerate((kv2, kv1, kv0)):
        span = pl.ds(s * tokens, tokens)
        v_t[:, span] = transposed(kv[...])[KV_HEADS * HEAD_DIM :]
        for g in range(KV_HEADS):
            k3[g, span, :] = kv[:, g * HEAD_DIM : (g + 1) * HEAD_DIM]
    acc[...] = jnp.zeros_like(acc)
    peak[...] = jnp.full_like(peak, MASK_FILL)
    total[...] = jnp.zeros_like(total)
    for i in range(tokens // TILE):
        cols = pl.ds(i * TILE, TILE)

        def step(t, carry):
            bias[...] = mask_tile(seg[0:1, cols], i, t, tokens)
            keys = pl.ds(pl.multiple_of(t * TILE, TILE), TILE)

            def group(g, carry):
                k_g = k3[g, keys, :]
                v_g = v_t[pl.ds(pl.multiple_of(g * HEAD_DIM, HEAD_DIM), HEAD_DIM), keys]
                for j in range(GROUP):
                    h = g * GROUP + j
                    rows = pl.ds(pl.multiple_of(h * HEAD_DIM, HEAD_DIM), HEAD_DIM)
                    scores = dot(k_g, q_t[rows, cols]) + bias[...]
                    old = peak[pl.ds(h, 1), cols]
                    new = jnp.maximum(old, jnp.max(scores, axis=0, keepdims=True))
                    probs = jnp.exp2(scores * EXP_SCALE - new * EXP_SCALE)
                    scale = jnp.exp2((old - new) * EXP_SCALE)
                    peak[pl.ds(h, 1), cols] = new
                    total[pl.ds(h, 1), cols] = total[pl.ds(h, 1), cols] * scale + jnp.sum(
                        probs, axis=0, keepdims=True
                    )
                    acc[rows, cols] = acc[rows, cols] * scale + dot(v_g, probs.astype(BF16))
                return carry

            return lax.fori_loop(0, KV_HEADS, group, carry)

        lax.fori_loop(first[i], i + 2 * tokens // TILE + 1, step, 0)
    for h in range(HEADS):
        rows = pl.ds(h * HEAD_DIM, HEAD_DIM)
        acc[rows, :] = acc[rows, :] / total[h : h + 1, :]
    out[...] = acc[...].T.astype(BF16)
    lse[...] = peak[...] * EXP_SCALE + jnp.log2(jnp.maximum(total[...], 1e-37))


def attend(first, seg, q, kv2, kv1, kv0):
    tokens, width = q.shape
    window = 3 * tokens
    return pl.pallas_call(
        functools.partial(attend_kernel, tokens),
        out_shape=[
            jax.ShapeDtypeStruct((tokens, width), BF16),
            jax.ShapeDtypeStruct((HEADS + 1, tokens), F32),
        ],
        in_specs=[pl.BlockSpec(memory_space=pltpu.SMEM)] + vmem_specs(5),
        out_specs=vmem_specs(2),
        scratch_shapes=[
            pltpu.VMEM((width, tokens), BF16),
            pltpu.VMEM((KV_HEADS, window, HEAD_DIM), BF16),
            pltpu.VMEM((KV_HEADS * HEAD_DIM, window), BF16),
            pltpu.VMEM((width, tokens), F32),
            pltpu.VMEM((HEADS + 1, tokens), F32),
            pltpu.VMEM((HEADS + 1, tokens), F32),
            pltpu.VMEM((TILE, TILE), F32),
        ],
        compiler_params=params(),
        cost_estimate=pl.CostEstimate(
            flops=16 << 30, bytes_accessed=6 << 20, transcendentals=8 << 20
        ),
        name="attend",
    )(first, seg, q, kv2, kv1, kv0)


def attend_back_kernel(
    tokens, first, seg, q, kv2, kv1, kv0, grad, lse, delta,
    dq, d2, d1, d0,
    q_t, g_t, q3, g3, k3, v3, k_t, dq_t, dk, dv, bias,
):
    q_t[...] = transposed(q[...])
    g_t[...] = transposed(grad[...])
    for h in range(HEADS):
        q3[h] = q[:, h * HEAD_DIM : (h + 1) * HEAD_DIM]
        g3[h] = grad[:, h * HEAD_DIM : (h + 1) * HEAD_DIM]
    for s, kv in enumerate((kv2, kv1, kv0)):
        span = pl.ds(s * tokens, tokens)
        k_t[:, span] = transposed(kv[...])[: KV_HEADS * HEAD_DIM]
        for g in range(KV_HEADS):
            k3[g, span, :] = kv[:, g * HEAD_DIM : (g + 1) * HEAD_DIM]
            v3[g, span, :] = kv[:, (KV_HEADS + g) * HEAD_DIM : (KV_HEADS + g + 1) * HEAD_DIM]
    dq_t[...] = jnp.zeros_like(dq_t)
    dk[...] = jnp.zeros_like(dk)
    dv[...] = jnp.zeros_like(dv)
    for i in range(tokens // TILE):
        cols = pl.ds(i * TILE, TILE)

        def step(t, carry):
            bias[...] = mask_tile(seg[0:1, cols], i, t, tokens)
            keys = pl.ds(pl.multiple_of(t * TILE, TILE), TILE)

            def group(g, carry):
                k_g = k3[g, keys, :]
                v_g = v3[g, keys, :]
                kt_g = k_t[pl.ds(pl.multiple_of(g * HEAD_DIM, HEAD_DIM), HEAD_DIM), keys]
                for j in range(GROUP):
                    h = g * GROUP + j
                    rows = pl.ds(pl.multiple_of(h * HEAD_DIM, HEAD_DIM), HEAD_DIM)
                    scores = dot(k_g, q_t[rows, cols]) * EXP_SCALE + bias[...]
                    probs = jnp.exp2(scores - lse[pl.ds(h, 1), cols])
                    dprobs = dot(v_g, g_t[rows, cols])
                    dscores = (probs * (dprobs - delta[pl.ds(h, 1), cols])).astype(BF16)
                    dv[g, keys, :] += dot(probs.astype(BF16), g3[h, cols, :])
                    dk[g, keys, :] += dot(dscores, q3[h, cols, :])
                    dq_t[rows, cols] += dot(kt_g, dscores)
                return carry

            return lax.fori_loop(0, KV_HEADS, group, carry)

        lax.fori_loop(first[i], i + 2 * tokens // TILE + 1, step, 0)
    dq[...] = dq_t[...].T * SCORE_SCALE
    for s, out in enumerate((d2, d1, d0)):
        span = pl.ds(s * tokens, tokens)
        for g in range(KV_HEADS):
            out[:, g * HEAD_DIM : (g + 1) * HEAD_DIM] = (dk[g, span, :] * SCORE_SCALE).astype(
                out.dtype
            )
            out[:, (KV_HEADS + g) * HEAD_DIM : (KV_HEADS + g + 1) * HEAD_DIM] = dv[
                g, span, :
            ].astype(out.dtype)


def attend_back(first, seg, q, kv2, kv1, kv0, grad, lse, delta):
    tokens, width = q.shape
    window = 3 * tokens
    kv_width = kv0.shape[1]
    return pl.pallas_call(
        functools.partial(attend_back_kernel, tokens),
        out_shape=[
            jax.ShapeDtypeStruct((tokens, width), F32),
            jax.ShapeDtypeStruct((tokens, kv_width), BF16),
            jax.ShapeDtypeStruct((tokens, kv_width), BF16),
            jax.ShapeDtypeStruct((tokens, kv_width), F32),
        ],
        in_specs=[pl.BlockSpec(memory_space=pltpu.SMEM)] + vmem_specs(8),
        out_specs=vmem_specs(4),
        scratch_shapes=[
            pltpu.VMEM((width, tokens), BF16),
            pltpu.VMEM((width, tokens), BF16),
            pltpu.VMEM((HEADS, tokens, HEAD_DIM), BF16),
            pltpu.VMEM((HEADS, tokens, HEAD_DIM), BF16),
            pltpu.VMEM((KV_HEADS, window, HEAD_DIM), BF16),
            pltpu.VMEM((KV_HEADS, window, HEAD_DIM), BF16),
            pltpu.VMEM((KV_HEADS * HEAD_DIM, window), BF16),
            pltpu.VMEM((width, tokens), F32),
            pltpu.VMEM((KV_HEADS, window, HEAD_DIM), F32),
            pltpu.VMEM((KV_HEADS, window, HEAD_DIM), F32),
            pltpu.VMEM((TILE, TILE), F32),
        ],
        compiler_params=params(),
        cost_estimate=pl.CostEstimate(
            flops=32 << 30, bytes_accessed=10 << 20, transcendentals=8 << 20
        ),
        name="attend_back",
    )(first, seg, q, kv2, kv1, kv0, grad, lse, delta)


def mean_square(value, width):
    return jnp.sum(value * value, axis=-1, keepdims=True) / width


def norm_back(values_in, inverse, gain, upstream, width):
    scaled = upstream * gain
    mean = jnp.sum(scaled * values_in, axis=-1, keepdims=True) / width
    grad_in = inverse * (scaled - values_in * inverse * inverse * mean)
    return grad_in, jnp.sum(upstream * values_in * inverse, axis=0)


def rotary_tables(position_ids):
    half_dim = HEAD_DIM // 2
    frequency = jnp.exp(
        jnp.arange(half_dim, dtype=F32) * (-2.0 * math.log(10000.0) / HEAD_DIM)
    )
    angles = position_ids.astype(F32)[:, None] * frequency[None, :]
    return jnp.cos(angles)[:, None, :], jnp.sin(angles)[:, None, :]


def rotate(tensor, cosine, sine):
    first, second = jnp.split(tensor, 2, axis=-1)
    return jnp.concatenate(
        [first * cosine - second * sine, second * cosine + first * sine], axis=-1
    )


def per_device(
    hidden_in, cotangent, segments, positions, attn_in, attn_out, w_gate, w_up, w_down,
    norm1_gain, norm2_gain,
):
    tokens, width = hidden_in.shape[1:]
    dp_size = lax.axis_size("dp")
    links = Links(dp_size)
    depth = links.depth
    rows = width // dp_size
    pad = DPAD // dp_size
    dp_index, m = lax.axis_index("dp"), lax.axis_index("mp")
    core = m % 2
    ids = jnp.stack([dp_index, m // 2, m]).astype(jnp.int32)
    query_cols, kv_cols = HEADS * HEAD_DIM, KV_HEADS * HEAD_DIM

    def padded(value):
        value = value.reshape(value.shape[0], dp_size, rows)
        return jnp.pad(value, ((0, 0), (0, 0), (0, pad - rows))).reshape(-1, DPAD)

    def unpadded(value):
        return value.reshape(-1, dp_size, pad)[:, :, :rows].reshape(-1, width)

    in_blocks = links.gather(attn_in)
    gains_z = [jnp.stack([norm1_gain, norm2_gain])]
    gains_z += [links.over_z(gains_z[0], k) for k in range(1, depth)]
    gains_own = jnp.stack(gains_z)
    gains = jnp.stack([gains_own, links.over_x(gains_own)], axis=1).reshape(dp_size, 2, rows)
    gains = jnp.take(gains, dp_index ^ jnp.arange(dp_size), axis=0).transpose(1, 0, 2)
    gains = padded(gains.reshape(2, width)).astype(F32)
    gain_one, gain_two = gains[0], gains[1]
    out_blocks = links.gather(attn_out.T)
    gate_blocks = links.gather(w_gate)
    up_blocks = links.gather(w_up)
    down_blocks = links.gather(w_down.T)

    def all_columns(blocks):
        own = assemble(blocks, ids)
        other = links.over_core(own)
        first = jnp.where(core == 0, own, other)
        second = jnp.where(core == 0, other, own)
        return jnp.concatenate([first[0], second[0], first[1], second[1]], axis=1)

    resid_in = padded(hidden_in[0]).astype(F32)
    cot = padded(cotangent[0])
    cot_other = links.over_core(cot)
    inv_one = lax.rsqrt(mean_square(resid_in, width) + EPSILON)
    normed1_b = (resid_in * inv_one * gain_one).astype(BF16)
    qkv_weight = all_columns(in_blocks)
    projected = dot(normed1_b, qkv_weight)
    cosine, sine = rotary_tables(positions[0])
    turned = rotate(
        projected[:, : query_cols + kv_cols].reshape(tokens, HEADS + KV_HEADS, HEAD_DIM),
        cosine,
        sine,
    ).astype(BF16).reshape(tokens, query_cols + kv_cols)
    queries = turned[:, :query_cols]
    kv0 = jnp.concatenate(
        [turned[:, query_cols:], projected[:, query_cols + kv_cols :].astype(BF16)], axis=1
    )
    kv2 = links.some(kv0, {0: 2, 1: 3})
    kv1 = links.some(kv0, {0: 1, 2: 3})
    kv1 = jnp.where(m == 2, links.some(kv2, {3: 2}), kv1)

    seq_seg = segments[0]
    own_seg = lax.dynamic_slice_in_dim(seq_seg, m * tokens, tokens, 0)
    start = jnp.sum(seq_seg[None, :] < own_seg[:, None], axis=1, dtype=jnp.int32)
    start = start - (m - 2) * tokens
    first = start.reshape(-1, TILE)[:, 0] // TILE
    seg = start[None, :]
    attn_b, lse = attend(first, seg, queries, kv2, kv1, kv0)
    out_weight_t = all_columns(out_blocks)
    middle = resid_in + dot_nt(attn_b, out_weight_t)
    inv_two = lax.rsqrt(mean_square(middle, width) + EPSILON)
    normed2_b = (middle * inv_two * gain_two).astype(BF16)

    def columns(blocks):
        pair = assemble(blocks, ids)
        return jnp.concatenate([pair[0], pair[1]], axis=1)

    gate_w, up_w, down_t = columns(gate_blocks), columns(up_blocks), columns(down_blocks)
    both_normed = jnp.concatenate([normed2_b, links.over_core(normed2_b)], axis=0)
    both_cot = jnp.concatenate([cot, cot_other], axis=0)
    gate = dot(both_normed, gate_w)
    upper = dot(both_normed, up_w)
    sigma = jax.nn.sigmoid(gate)
    silu_gate = gate * sigma
    hidden_b = (silu_gate * upper).astype(BF16)
    ffn = dot_nt(hidden_b, down_t)
    ffn_own = ffn[:tokens] + links.over_core(ffn[tokens:].astype(BF16)).astype(F32)
    hidden_out = unpadded((middle + ffn_own).astype(BF16))

    def halves(value):
        return value.reshape(value.shape[0], 2, -1).transpose(1, 0, 2)

    down_parts = wgrad_plane(both_cot.T, halves(hidden_b), ids, depth, rows)
    grad_hid = dot(both_cot, down_t)
    grad_gate_act = (grad_hid * upper * sigma * (1.0 + gate * (1.0 - sigma))).astype(BF16)
    grad_up_act = (grad_hid * silu_gate).astype(BF16)
    grad_n2 = dot_nt(grad_gate_act, gate_w) + dot_nt(grad_up_act, up_w)
    grad_n2 = grad_n2[:tokens] + links.over_core(grad_n2[tokens:].astype(BF16)).astype(F32)
    normed2_t = both_normed.T
    gate_parts = wgrad_plane(normed2_t, halves(grad_gate_act), ids, depth, rows)
    up_parts = wgrad_plane(normed2_t, halves(grad_up_act), ids, depth, rows)
    g_down = links.scatter(down_parts)
    g_gate = links.scatter(gate_parts)
    g_up = links.scatter(up_parts)

    grad_mid_norm, g_gain2 = norm_back(middle, inv_two, gain_two, grad_n2, width)
    grad_middle = cot.astype(F32) + grad_mid_norm
    middle_b = grad_middle.astype(BF16)
    quarters = lambda value: value.reshape(value.shape[0], 4, -1).transpose(1, 0, 2)
    g_out_parts = wgrad_all(middle_b.T, quarters(attn_b), ids, depth, rows)
    g_out = scatter_all(links, *g_out_parts)
    grad_attn = dot(middle_b, out_weight_t).astype(BF16)
    delta = jnp.sum(
        (grad_attn.astype(F32) * attn_b.astype(F32)).reshape(tokens, HEADS, HEAD_DIM), axis=-1
    ).T
    delta = jnp.pad(delta, ((0, 1), (0, 0)))

    grad_q, part2, part1, part0 = attend_back(
        first, seg, queries, kv2, kv1, kv0, grad_attn, lse, delta
    )
    passed = links.some(part1, {2: 3})
    part2 = (part2.astype(F32) + passed.astype(F32)).astype(BF16)
    grad_kv = (
        part0
        + links.some(part1, {1: 0, 3: 2}).astype(F32)
        + links.some(part2, {2: 0, 3: 1}).astype(F32)
    )
    turned_back = rotate(
        jnp.concatenate([grad_q, grad_kv[:, :kv_cols]], axis=1).reshape(
            tokens, HEADS + KV_HEADS, HEAD_DIM
        ),
        cosine,
        -sine,
    ).reshape(tokens, query_cols + kv_cols)
    grad_proj = jnp.concatenate([turned_back, grad_kv[:, kv_cols:]], axis=1).astype(BF16)
    g_in_parts = wgrad_all(normed1_b.T, quarters(grad_proj), ids, depth, rows)
    g_in = scatter_all(links, *g_in_parts)
    grad_n1 = dot_nt(grad_proj, qkv_weight)
    grad_in_norm, g_gain1 = norm_back(resid_in, inv_one, gain_one, grad_n1, width)
    grad_input = unpadded(grad_middle + grad_in_norm)
    g_gains = links.all_sum(jnp.stack([g_gain1, g_gain2]))
    g_gains = lax.dynamic_slice_in_dim(g_gains, dp_index * pad, rows, 1)
    return (
        hidden_out[None],
        grad_input[None],
        g_in,
        g_out.T,
        g_gate,
        g_up,
        g_down.T,
        g_gains[0],
        g_gains[1],
    )


def solution(mesh):
    return jax.shard_map(
        per_device,
        mesh=mesh,
        in_specs=(
            P("dp", "mp", None),
            P("dp", "mp", None),
            P("dp", None),
            P("dp", "mp"),
            P("dp", "mp"),
            P("mp", "dp"),
            P("dp", "mp"),
            P("dp", "mp"),
            P("mp", "dp"),
            P("dp"),
            P("dp"),
        ),
        out_specs=(
            P("dp", "mp", None),
            P("dp", "mp", None),
            P("dp", "mp"),
            P("mp", "dp"),
            P("dp", "mp"),
            P("dp", "mp"),
            P("mp", "dp"),
            P("dp"),
            P("dp"),
        ),
        check_vma=False,
    )
```

```python
import functools
import math

import jax
import jax.numpy as jnp
from jax import lax
from jax.experimental import pallas as pl
from jax.experimental.pallas import tpu as pltpu
from jax.sharding import PartitionSpec as P

HEADS = 15
KV_HEADS = 5
GROUP = HEADS // KV_HEADS
HEAD_DIM = 64
DPAD = 1024
TILE = 256
EPSILON = 1e-05
SCORE_SCALE = 0.125
MASK_FILL = -1e30
LOG2E = 1.4426950408889634
EXP_SCALE = SCORE_SCALE * LOG2E
BF16 = jnp.bfloat16
F32 = jnp.float32


def dot(a, b):
    return jnp.dot(a, b, preferred_element_type=F32)


def dot_nt(a, b):
    return lax.dot_general(a, b, (((1,), (1,)), ((), ())), preferred_element_type=F32)


def vmem_specs(count):
    return [pl.BlockSpec(memory_space=pltpu.VMEM)] * count


def params():
    return pltpu.CompilerParams(vmem_limit_bytes=56 << 20)


class Links:
    def __init__(self, dp_size):
        self.dp_size = dp_size
        self.depth = dp_size // 2

    def pairs(self, move):
        found = []
        for d in range(self.dp_size):
            for m in range(4):
                target = move(d, m)
                if target is not None:
                    found.append((d * 4 + m, target[0] * 4 + target[1]))
        return found

    def send(self, value, move):
        return lax.ppermute(value, ("dp", "mp"), self.pairs(move))

    def over_z(self, value, k):
        return self.send(value, lambda d, m: (d ^ (2 * k), m))

    def over_x(self, value):
        return self.send(value, lambda d, m: (d ^ 1, m))

    def over_y(self, value):
        return self.send(value, lambda d, m: (d, m ^ 2))

    def over_core(self, value):
        return self.send(value, lambda d, m: (d, m ^ 1))

    def some(self, value, table):
        return self.send(value, lambda d, m: (d, table[m]) if m in table else None)

    def scatter(self, parts):
        p00, p01a, p01b, p10a, p10b, p11a, p11b = parts
        half = self.depth // 2
        r11a = self.over_y(p11a)
        r11b = self.over_x(p11b)
        r01b = self.over_x(p01b)
        r10a = self.over_y(p10a)
        s01a = (p01a.astype(F32) + r11a.astype(F32)).astype(BF16)
        s10b = (p10b.astype(F32) + r11b.astype(F32)).astype(BF16)
        r01a = self.over_x(s01a)
        r10b = self.over_y(s10b)
        sums = p00.astype(F32) + jnp.concatenate(
            [r10a.astype(F32) + r01a.astype(F32), r01b.astype(F32) + r10b.astype(F32)], axis=0
        )
        total = sums[0]
        for k in range(1, self.depth):
            total = total + self.over_z(sums[k].astype(BF16), k).astype(F32)
        return total

    def all_sum(self, value):
        value = value + self.over_core(value)
        value = value + self.over_y(value)
        value = value + self.over_x(value)
        k = 1
        while k < self.depth:
            value = value + self.over_z(value, k)
            k *= 2
        return value


def wgrad_plane_kernel(depth, rows, pad, ids, lhs, rhs, *refs):
    outs, acc = refs[:-1], refs[-1]
    dp_index, y = ids[0], ids[1]
    z, x = dp_index // 2, dp_index % 2
    half = depth // 2
    for part in range(2):

        def body(i, carry):
            jz = part * half + i
            for jx in range(2):
                start = pl.multiple_of(((x ^ jx) * depth + (z ^ jz)) * pad, pad)
                left = lhs[pl.ds(start, pad), :]
                for jy in range(2):
                    acc[...] = dot(left, rhs[y ^ jy])
                    block = acc[pl.ds(0, rows), :]
                    if jy == 0 and jx == 0:
                        outs[0][jz] = block.astype(BF16)
                    else:
                        outs[1 + 2 * (2 * jy + jx - 1) + part][i] = block.astype(BF16)
            return carry

        lax.fori_loop(0, half, body, 0)


def wgrad_plane(lhs, rhs, ids, depth, rows):
    pad = DPAD // (2 * depth)
    tokens, cols = rhs.shape[1:]
    full = jax.ShapeDtypeStruct((depth, rows, cols), BF16)
    part = jax.ShapeDtypeStruct((depth // 2, rows, cols), BF16)
    order = [full, part, part, part, part, part, part]
    return pl.pallas_call(
        functools.partial(wgrad_plane_kernel, depth, rows, pad),
        out_shape=order,
        in_specs=[pl.BlockSpec(memory_space=pltpu.SMEM)] + vmem_specs(2),
        out_specs=vmem_specs(7),
        scratch_shapes=[pltpu.VMEM((pad, cols), F32)],
        compiler_params=params(),
        cost_estimate=pl.CostEstimate(
            flops=4 * DPAD * tokens * cols, bytes_accessed=DPAD * (tokens + 4 * cols) * 2,
            transcendentals=0,
        ),
        name="wgrad_plane",
    )(ids, lhs, rhs)


def wgrad_all_kernel(depth, rows, pad, ids, lhs, rhs, own, oth, acc):
    dp_index, m = ids[0], ids[2]
    z, x = dp_index // 2, dp_index % 2

    def body(jz, carry):
        for jx in range(2):
            start = pl.multiple_of(((x ^ jx) * depth + (z ^ jz)) * pad, pad)
            left = lhs[pl.ds(start, pad), :]
            for jy in range(2):
                for jc in range(2):
                    acc[...] = dot(left, rhs[m ^ (2 * jy + jc)])
                    block = acc[pl.ds(0, rows), :]
                    (oth if jc else own)[jy, jx, jz] = block.astype(BF16)
        return carry

    lax.fori_loop(0, depth, body, 0)


def wgrad_all(lhs, rhs, ids, depth, rows):
    pad = DPAD // (2 * depth)
    tokens, cols = rhs.shape[1:]
    shape = jax.ShapeDtypeStruct((2, 2, depth, rows, cols), BF16)
    return pl.pallas_call(
        functools.partial(wgrad_all_kernel, depth, rows, pad),
        out_shape=[shape, shape],
        in_specs=[pl.BlockSpec(memory_space=pltpu.SMEM)] + vmem_specs(2),
        out_specs=vmem_specs(2),
        scratch_shapes=[pltpu.VMEM((pad, cols), F32)],
        compiler_params=params(),
        cost_estimate=pl.CostEstimate(
            flops=8 * DPAD * tokens * cols, bytes_accessed=DPAD * (tokens + 8 * cols) * 2,
            transcendentals=0,
        ),
        name="wgrad_all",
    )(ids, lhs, rhs)


def scatter_all(links, own, oth):
    half = links.depth // 2
    got = links.over_core(oth)
    total = (own.astype(F32) + got.astype(F32)).astype(BF16)
    return links.scatter(
        (
            total[0, 0],
            total[0, 1, :half],
            total[0, 1, half:],
            total[1, 0, :half],
            total[1, 0, half:],
            total[1, 1, :half],
            total[1, 1, half:],
        )
    )


def transposed(value):
    return value.astype(F32).T.astype(BF16)


class Place:
    def __init__(self, depth, send_sems, recv_sems):
        dp_index, m = lax.axis_index("dp"), lax.axis_index("mp")
        self.depth = depth
        self.z, self.x = dp_index // 2, dp_index % 2
        self.m, self.y, self.c = m, m // 2, m % 2
        self.send_sems, self.recv_sems = send_sems, recv_sems
        self.count = 0

    def peer(self, kind):
        z, x, y, c = self.z, self.x, self.y, self.c
        if kind == "x":
            x = 1 - x
        elif kind == "y":
            y = 1 - y
        elif kind == "c":
            c = 1 - c
        else:
            z = (z + kind) % self.depth
        return 2 * z + x, 2 * y + c

    def kinds(self):
        return ["x", "y", "c"] + list(range(1, self.depth))

    def barrier(self):
        semaphore = pltpu.get_barrier_semaphore()
        for kind in self.kinds():
            pl.semaphore_signal(
                semaphore, inc=1, device_id=self.peer(kind), device_id_type=pl.DeviceIdType.MESH
            )
        pl.semaphore_wait(semaphore, len(self.kinds()))

    def copy(self, kind, source, target=None):
        index = self.count
        self.count += 1
        made = pltpu.make_async_remote_copy(
            src_ref=source,
            dst_ref=source if target is None else target,
            send_sem=self.send_sems.at[index],
            recv_sem=self.recv_sems.at[index],
            device_id=self.peer(kind),
            device_id_type=pl.DeviceIdType.MESH,
        )
        made.start()
        return made


class PlaneGather:
    def __init__(self, place, source, buffer, diagonal_by_x=False):
        self.place, self.source, self.buffer = place, source, buffer
        self.diagonal_by_x = diagonal_by_x
        self.sent = []

    def over_z(self):
        p = self.place
        slot = self.buffer.at[p.y, p.x, p.z]
        self.arriving = [p.copy(k, self.source, slot) for k in range(1, p.depth)]
        self.sent += self.arriving

    def over_xy(self):
        p = self.place
        for made in self.arriving:
            made.wait_recv()
        own = self.buffer.at[p.y, p.x]
        self.by_x, self.by_y = p.copy("x", own), p.copy("y", own)
        self.sent += [self.by_x, self.by_y]

    def diagonal(self):
        p = self.place
        half = p.depth // 2
        self.by_x.wait_recv()
        if self.diagonal_by_x:
            self.by_y.wait_recv()
            self.last = [p.copy("x", self.buffer.at[1 - p.y, p.x])]
        else:
            low = p.copy("y", self.buffer.at[p.y, 1 - p.x, pl.ds(0, half)])
            self.by_y.wait_recv()
            self.last = [low, p.copy("x", self.buffer.at[1 - p.y, p.x, pl.ds(half, half)])]
        self.sent += self.last

    def arrived(self):
        for made in self.last:
            made.wait_recv()

    def finish(self):
        for made in self.sent:
            made.wait_send()


def rope(value, cosine, sine):
    lane = lax.broadcasted_iota(jnp.int32, value.shape, 1)
    half = HEAD_DIM // 2
    partner = jnp.where(
        lane % HEAD_DIM < half, pltpu.roll(value, 128 - half, 1), pltpu.roll(value, half, 1)
    )
    return value * cosine + partner * sine


def mean_rows(value, width):
    return jnp.sum(value, axis=-1, keepdims=True) * (1.0 / width)


def mask_tile(start, query_tile, key_tile):
    key = key_tile * TILE + lax.broadcasted_iota(jnp.int32, (TILE, TILE), 0)
    query = query_tile * TILE + lax.broadcasted_iota(jnp.int32, (TILE, TILE), 1)
    return jnp.where((key >= start) & (key <= query), 0.0, MASK_FILL)


def front_kernel(
    depth, rows, width, in_cols,
    pack_a, pack_g, x_in, cosine, sine, seg,
    q, kv, attn, lse, middle, normed1, normed2, gains, attn_w, ffn_w,
    a_buf, proj, q_t, k3, v_t, acc, peak, total, bias, send_sems, recv_sems, local_sems,
):
    tokens = x_in.shape[0]
    tiles = tokens // TILE
    back = 1024 // TILE
    pad = DPAD // (2 * depth)
    p = Place(depth, send_sems, recv_sems)
    a_buf[p.c, p.y, p.x, p.z] = pack_a[...]
    own = [
        pltpu.make_async_copy(pack_g.at[w], ffn_w.at[w, p.y, p.x, p.z], local_sems.at[w])
        for w in range(3)
    ]
    for made in own:
        made.start()
    p.barrier()
    plane = PlaneGather(p, pack_a, a_buf.at[p.c])
    gate, up, down = [
        PlaneGather(p, pack_g.at[w], ffn_w.at[w], w == 2) for w in range(3)
    ]
    plane.over_z()
    plane.over_xy()
    gate.over_z()
    plane.diagonal()
    plane.arrived()
    cross = p.copy("c", a_buf.at[p.c])
    for made in own:
        made.wait()
    up.over_z()
    gate.over_xy()
    x_f = x_in[...].astype(F32)
    inv_one = lax.rsqrt(mean_rows(x_f * x_f, width) + EPSILON)
    cross.wait()
    for b in range(2 * depth):
        gains[:, b * pad : (b + 1) * pad] = a_buf[
            0, 0, b // depth, b % depth, pl.ds(rows, 2), 0:pad
        ].astype(F32)
    normed1[...] = (x_f * inv_one * gains[0:1, :]).astype(BF16)

    def project(r, carry):
        span = pl.ds(pl.multiple_of(r * TILE, TILE), TILE)
        for b in range(4):
            weight = a_buf[b % 2, b // 2].reshape(DPAD, -1)[:, :in_cols]
            proj[span, b * in_cols : (b + 1) * in_cols] = dot(normed1[span, :], weight)
        for j in range((HEADS + KV_HEADS) * HEAD_DIM // 128):
            lanes = slice(128 * j, 128 * (j + 1))
            proj[span, lanes] = rope(proj[span, lanes], cosine[span, :], sine[span, :])
        return carry

    lax.fori_loop(0, tiles, project, 0)
    query_cols = HEADS * HEAD_DIM
    q[...] = proj[:, :query_cols].astype(BF16)
    kv[p.m] = proj[:, query_cols : query_cols + 2 * KV_HEADS * HEAD_DIM].astype(BF16)
    mine = kv.at[p.m]
    kv_y, kv_c = p.copy("y", mine), p.copy("c", mine)
    down.over_z()
    q_t[...] = proj[:, :query_cols].T.astype(BF16)
    acc[...] = jnp.zeros_like(acc)
    peak[...] = jnp.full_like(peak, MASK_FILL)
    total[...] = jnp.zeros_like(total)

    def spread(block):
        span = pl.ds(pl.multiple_of(block * tokens, tokens), tokens)
        k3_parts = kv[block]
        v_t[:, span] = transposed(k3_parts)[KV_HEADS * HEAD_DIM :]
        for g in range(KV_HEADS):
            k3[g, span, :] = k3_parts[:, g * HEAD_DIM : (g + 1) * HEAD_DIM]

    def attend_tile(i, t):
        cols = pl.ds(i * TILE, TILE)
        bias[...] = mask_tile(seg[0:1, cols], p.m * tiles + i, t)
        keys = pl.ds(pl.multiple_of(t * TILE, TILE), TILE)

        def group(g, carry):
            k_g = k3[g, keys, :]
            v_g = v_t[pl.ds(pl.multiple_of(g * HEAD_DIM, HEAD_DIM), HEAD_DIM), keys]
            heads = [g * GROUP + j for j in range(GROUP)]
            places = [pl.ds(pl.multiple_of(h * HEAD_DIM, HEAD_DIM), HEAD_DIM) for h in heads]
            old = [peak[pl.ds(h, 1), cols] for h in heads]
            sums = [total[pl.ds(h, 1), cols] for h in heads]
            accs = [acc[s, cols] for s in places]
            scores = [dot(k_g, q_t[s, cols]) + bias[...] for s in places]
            new = [jnp.maximum(o, jnp.max(s, axis=0, keepdims=True)) for o, s in zip(old, scores)]
            probs = [jnp.exp2(s * EXP_SCALE - n * EXP_SCALE) for s, n in zip(scores, new)]
            scale = [jnp.exp2((o - n) * EXP_SCALE) for o, n in zip(old, new)]
            outs = [dot(v_g, b.astype(BF16)) for b in probs]
            for j, h in enumerate(heads):
                peak[pl.ds(h, 1), cols] = new[j]
                total[pl.ds(h, 1), cols] = sums[j] * scale[j] + jnp.sum(
                    probs[j], axis=0, keepdims=True
                )
                acc[places[j], cols] = accs[j] * scale[j] + outs[j]
            return carry

        lax.fori_loop(0, KV_HEADS, group, 0)

    def attend_span(i, low, high):
        def step(t, carry):
            attend_tile(i, t)
            return carry

        lax.fori_loop(low, high, step, 0)

    spread(p.m)
    first_tile = p.m * tiles
    for i in range(tiles):
        attend_span(i, first_tile, first_tile + i + 1)
    kv_y.wait_recv()
    kv_cy = p.copy("c", kv.at[(p.m + 2) % 4])
    up.over_xy()
    gate.diagonal()
    kv_c.wait_recv()
    kv_cy.wait_recv()
    for k in range(1, 4):
        spread((p.m + k) % 4)
    for i in range(tiles):
        attend_span(i, jnp.maximum(first_tile + i - back, 0), first_tile)
        if i == 0:
            down.over_xy()
            up.diagonal()
    for h in range(HEADS):
        span = pl.ds(h * HEAD_DIM, HEAD_DIM)
        acc[span, :] = acc[span, :] / total[h : h + 1, :]
    attn[...] = acc[...].T.astype(BF16)
    lse[...] = peak[...] * EXP_SCALE + jnp.log2(jnp.maximum(total[...], 1e-37))
    saved = pltpu.make_async_copy(a_buf, attn_w, local_sems.at[0])
    saved.start()
    down.diagonal()
    out_cols = query_cols // 4

    def project_out(r, carry):
        span = pl.ds(pl.multiple_of(r * TILE, TILE), TILE)
        mid = x_in[span, :].astype(F32)
        for b in range(4):
            weight = a_buf[b % 2, b // 2].reshape(DPAD, -1)[:, in_cols : in_cols + out_cols]
            mid += dot_nt(attn[span, b * out_cols : (b + 1) * out_cols], weight)
        middle[span, :] = mid
        inv = lax.rsqrt(mean_rows(mid * mid, width) + EPSILON)
        normed2[span, :] = (mid * inv * gains[1:2, :]).astype(BF16)
        return carry

    lax.fori_loop(0, tiles, project_out, 0)
    gate.arrived()
    up.arrived()
    down.arrived()
    for part in (plane, gate, up, down):
        part.finish()
    for made in (kv_y, kv_c, kv_cy):
        made.wait_send()
    saved.wait()


def front(pack_a, pack_g, x_in, cosine, sine, seg, depth, rows, width, in_cols):
    tokens = x_in.shape[0]
    pad = DPAD // (2 * depth)
    cols = pack_a.shape[1]
    query_cols, kv_cols = HEADS * HEAD_DIM, 2 * KV_HEADS * HEAD_DIM
    whole = 4 * tokens
    copies = 4 * (depth - 1) + 4 * 4 + 4
    anywhere = pl.BlockSpec(memory_space=pl.ANY)
    return pl.pallas_call(
        functools.partial(front_kernel, depth, rows, width, in_cols),
        out_shape=[
            jax.ShapeDtypeStruct((tokens, query_cols), BF16),
            jax.ShapeDtypeStruct((4, tokens, kv_cols), BF16),
            jax.ShapeDtypeStruct((tokens, query_cols), BF16),
            jax.ShapeDtypeStruct((HEADS + 1, tokens), F32),
            jax.ShapeDtypeStruct((tokens, DPAD), F32),
            jax.ShapeDtypeStruct((tokens, DPAD), BF16),
            jax.ShapeDtypeStruct((tokens, DPAD), BF16),
            jax.ShapeDtypeStruct((2, DPAD), F32),
            jax.ShapeDtypeStruct((2, 2, 2, depth, pad, cols), BF16),
            jax.ShapeDtypeStruct((3, 2, 2, depth, pad, cols), BF16),
        ],
        in_specs=vmem_specs(1) + [anywhere] + vmem_specs(4),
        out_specs=vmem_specs(8) + [anywhere] * 2,
        scratch_shapes=[
            pltpu.VMEM((2, 2, 2, depth, pad, cols), BF16),
            pltpu.VMEM((tokens, query_cols + kv_cols), F32),
            pltpu.VMEM((query_cols, tokens), BF16),
            pltpu.VMEM((KV_HEADS, whole, HEAD_DIM), BF16),
            pltpu.VMEM((KV_HEADS * HEAD_DIM, whole), BF16),
            pltpu.VMEM((query_cols, tokens), F32),
            pltpu.VMEM((HEADS + 1, tokens), F32),
            pltpu.VMEM((HEADS + 1, tokens), F32),
            pltpu.VMEM((TILE, TILE), F32),
            pltpu.SemaphoreType.DMA((copies,)),
            pltpu.SemaphoreType.DMA((copies,)),
            pltpu.SemaphoreType.DMA((3,)),
        ],
        compiler_params=pltpu.CompilerParams(
            vmem_limit_bytes=58 << 20, collective_id=0, has_side_effects=True
        ),
        cost_estimate=pl.CostEstimate(
            flops=20 << 30, bytes_accessed=40 << 20, transcendentals=8 << 20
        ),
        name="front",
    )(pack_a, pack_g, x_in, cosine, sine, seg)


def attend_back_kernel(
    tokens, first, seg, q, kv2, kv1, kv0, grad, lse, delta,
    dq, d2, d1, d0,
    q_t, g_t, q3, g3, k3, v3, k_t, dq_t, dk, dv, bias,
):
    q_t[...] = transposed(q[...])
    g_t[...] = transposed(grad[...])
    for h in range(HEADS):
        q3[h] = q[:, h * HEAD_DIM : (h + 1) * HEAD_DIM]
        g3[h] = grad[:, h * HEAD_DIM : (h + 1) * HEAD_DIM]
    for s, kv in enumerate((kv2, kv1, kv0)):
        span = pl.ds(s * tokens, tokens)
        k_t[:, span] = transposed(kv[...])[: KV_HEADS * HEAD_DIM]
        for g in range(KV_HEADS):
            k3[g, span, :] = kv[:, g * HEAD_DIM : (g + 1) * HEAD_DIM]
            v3[g, span, :] = kv[:, (KV_HEADS + g) * HEAD_DIM : (KV_HEADS + g + 1) * HEAD_DIM]
    dq_t[...] = jnp.zeros_like(dq_t)
    dk[...] = jnp.zeros_like(dk)
    dv[...] = jnp.zeros_like(dv)
    for i in range(tokens // TILE):
        cols = pl.ds(i * TILE, TILE)

        def step(t, carry):
            bias[...] = mask_tile(seg[0:1, cols], i + 2 * tokens // TILE, t)
            keys = pl.ds(pl.multiple_of(t * TILE, TILE), TILE)

            def group(g, carry):
                k_g = k3[g, keys, :]
                v_g = v3[g, keys, :]
                kt_g = k_t[pl.ds(pl.multiple_of(g * HEAD_DIM, HEAD_DIM), HEAD_DIM), keys]
                for j in range(GROUP):
                    h = g * GROUP + j
                    rows = pl.ds(pl.multiple_of(h * HEAD_DIM, HEAD_DIM), HEAD_DIM)
                    scores = dot(k_g, q_t[rows, cols]) * EXP_SCALE + bias[...]
                    probs = jnp.exp2(scores - lse[pl.ds(h, 1), cols])
                    dprobs = dot(v_g, g_t[rows, cols])
                    dscores = (probs * (dprobs - delta[pl.ds(h, 1), cols])).astype(BF16)
                    dv[g, keys, :] += dot(probs.astype(BF16), g3[h, cols, :])
                    dk[g, keys, :] += dot(dscores, q3[h, cols, :])
                    dq_t[rows, cols] += dot(kt_g, dscores)
                return carry

            return lax.fori_loop(0, KV_HEADS, group, carry)

        lax.fori_loop(first[i], i + 2 * tokens // TILE + 1, step, 0)
    dq[...] = dq_t[...].T * SCORE_SCALE
    for s, out in enumerate((d2, d1, d0)):
        span = pl.ds(s * tokens, tokens)
        for g in range(KV_HEADS):
            out[:, g * HEAD_DIM : (g + 1) * HEAD_DIM] = (dk[g, span, :] * SCORE_SCALE).astype(
                out.dtype
            )
            out[:, (KV_HEADS + g) * HEAD_DIM : (KV_HEADS + g + 1) * HEAD_DIM] = dv[
                g, span, :
            ].astype(out.dtype)


def attend_back(first, seg, q, kv2, kv1, kv0, grad, lse, delta):
    tokens, width = q.shape
    window = 3 * tokens
    kv_width = kv0.shape[1]
    return pl.pallas_call(
        functools.partial(attend_back_kernel, tokens),
        out_shape=[
            jax.ShapeDtypeStruct((tokens, width), F32),
            jax.ShapeDtypeStruct((tokens, kv_width), BF16),
            jax.ShapeDtypeStruct((tokens, kv_width), BF16),
            jax.ShapeDtypeStruct((tokens, kv_width), F32),
        ],
        in_specs=[pl.BlockSpec(memory_space=pltpu.SMEM)] + vmem_specs(8),
        out_specs=vmem_specs(4),
        scratch_shapes=[
            pltpu.VMEM((width, tokens), BF16),
            pltpu.VMEM((width, tokens), BF16),
            pltpu.VMEM((HEADS, tokens, HEAD_DIM), BF16),
            pltpu.VMEM((HEADS, tokens, HEAD_DIM), BF16),
            pltpu.VMEM((KV_HEADS, window, HEAD_DIM), BF16),
            pltpu.VMEM((KV_HEADS, window, HEAD_DIM), BF16),
            pltpu.VMEM((KV_HEADS * HEAD_DIM, window), BF16),
            pltpu.VMEM((width, tokens), F32),
            pltpu.VMEM((KV_HEADS, window, HEAD_DIM), F32),
            pltpu.VMEM((KV_HEADS, window, HEAD_DIM), F32),
            pltpu.VMEM((TILE, TILE), F32),
        ],
        compiler_params=params(),
        cost_estimate=pl.CostEstimate(
            flops=32 << 30, bytes_accessed=10 << 20, transcendentals=8 << 20
        ),
        name="attend_back",
    )(first, seg, q, kv2, kv1, kv0, grad, lse, delta)


def mean_square(value, width):
    return jnp.sum(value * value, axis=-1, keepdims=True) / width


def norm_back(values_in, inverse, gain, upstream, width):
    scaled = upstream * gain
    mean = jnp.sum(scaled * values_in, axis=-1, keepdims=True) / width
    grad_in = inverse * (scaled - values_in * inverse * inverse * mean)
    return grad_in, jnp.sum(upstream * values_in * inverse, axis=0)


def rotary_tables(position_ids):
    half_dim = HEAD_DIM // 2
    frequency = jnp.exp(
        jnp.arange(half_dim, dtype=F32) * (-2.0 * math.log(10000.0) / HEAD_DIM)
    )
    angles = position_ids.astype(F32)[:, None] * frequency[None, :]
    return jnp.cos(angles)[:, None, :], jnp.sin(angles)[:, None, :]


def rotate(tensor, cosine, sine):
    first, second = jnp.split(tensor, 2, axis=-1)
    return jnp.concatenate(
        [first * cosine - second * sine, second * cosine + first * sine], axis=-1
    )


def per_device(
    hidden_in, cotangent, segments, positions, attn_in, attn_out, w_gate, w_up, w_down,
    norm1_gain, norm2_gain,
):
    tokens, width = hidden_in.shape[1:]
    dp_size = lax.axis_size("dp")
    links = Links(dp_size)
    depth = links.depth
    rows = width // dp_size
    pad = DPAD // dp_size
    dp_index, m = lax.axis_index("dp"), lax.axis_index("mp")
    core = m % 2
    ids = jnp.stack([dp_index, m // 2, m]).astype(jnp.int32)
    query_cols, kv_cols = HEADS * HEAD_DIM, KV_HEADS * HEAD_DIM

    def padded(value):
        value = value.reshape(value.shape[0], depth, 2, rows).transpose(0, 2, 1, 3)
        return jnp.pad(value, ((0, 0), (0, 0), (0, 0), (0, pad - rows))).reshape(-1, DPAD)

    def unpadded(value):
        value = value.reshape(-1, 2, depth, pad)[..., :rows]
        return value.transpose(0, 2, 1, 3).reshape(-1, width)

    in_cols = attn_in.shape[1]
    out_cols = attn_out.shape[0]
    gains_in = jnp.pad(
        jnp.stack([norm1_gain, norm2_gain]), ((0, pad - rows - 2), (0, in_cols + out_cols - rows))
    )
    pack_a = jnp.concatenate(
        [jnp.concatenate([attn_in, attn_out.T], axis=1), gains_in], axis=0
    )
    pack_g = jnp.pad(jnp.stack([w_gate, w_up, w_down.T]), ((0, 0), (0, pad - rows), (0, 0)))
    x_in = padded(hidden_in[0])
    cot = padded(cotangent[0])
    cosine, sine = rotary_tables(positions[0])
    cos_lanes = jnp.tile(cosine[:, 0], (1, 4))
    sin_lanes = jnp.tile(jnp.concatenate([-sine[:, 0], sine[:, 0]], axis=1), (1, 2))
    seq_seg = segments[0]
    own_seg = lax.dynamic_slice_in_dim(seq_seg, m * tokens, tokens, 0)
    start = jnp.sum(seq_seg[None, :] < own_seg[:, None], axis=1, dtype=jnp.int32)
    queries, kv_all, attn_b, lse, middle, normed1_b, normed2_b, gains, attn_w, ffn_w = front(
        pack_a, pack_g, x_in, cos_lanes, sin_lanes, start[None, :], depth, rows, width, in_cols
    )
    gain_one, gain_two = gains[0], gains[1]
    attn_w = attn_w.reshape(2, 2, DPAD, -1)
    attn_w = jnp.concatenate(
        [attn_w[0, 0], attn_w[1, 0], attn_w[0, 1], attn_w[1, 1]], axis=1
    ).reshape(DPAD, 4, -1)
    qkv_weight = attn_w[:, :, :in_cols].reshape(DPAD, -1)
    out_weight_t = attn_w[:, :, in_cols:].reshape(DPAD, -1)
    resid_in = x_in.astype(F32)
    inv_one = lax.rsqrt(mean_square(resid_in, width) + EPSILON)
    inv_two = lax.rsqrt(mean_square(middle, width) + EPSILON)
    cot_other = links.over_core(cot)
    kv0 = lax.dynamic_index_in_dim(kv_all, m, 0, keepdims=False)
    kv1 = lax.dynamic_index_in_dim(kv_all, jnp.maximum(m - 1, 0), 0, keepdims=False)
    kv2 = lax.dynamic_index_in_dim(kv_all, jnp.maximum(m - 2, 0), 0, keepdims=False)
    start = start - (m - 2) * tokens
    first = start.reshape(-1, TILE)[:, 0] // TILE
    seg = start[None, :]

    ffn_w = ffn_w.reshape(3, 2, DPAD, -1)
    gate_w, up_w, down_t = [jnp.concatenate([w[0], w[1]], axis=1) for w in ffn_w]
    both_normed = jnp.concatenate([normed2_b, links.over_core(normed2_b)], axis=0)
    both_cot = jnp.concatenate([cot, cot_other], axis=0)
    gate = dot(both_normed, gate_w)
    upper = dot(both_normed, up_w)
    sigma = jax.nn.sigmoid(gate)
    silu_gate = gate * sigma
    hidden_b = (silu_gate * upper).astype(BF16)
    ffn = dot_nt(hidden_b, down_t)
    ffn_own = ffn[:tokens] + links.over_core(ffn[tokens:].astype(BF16)).astype(F32)
    hidden_out = unpadded((middle + ffn_own).astype(BF16))

    def halves(value):
        return value.reshape(value.shape[0], 2, -1).transpose(1, 0, 2)

    down_parts = wgrad_plane(both_cot.T, halves(hidden_b), ids, depth, rows)
    grad_hid = dot(both_cot, down_t)
    grad_gate_act = (grad_hid * upper * sigma * (1.0 + gate * (1.0 - sigma))).astype(BF16)
    grad_up_act = (grad_hid * silu_gate).astype(BF16)
    grad_n2 = dot_nt(grad_gate_act, gate_w) + dot_nt(grad_up_act, up_w)
    grad_n2 = grad_n2[:tokens] + links.over_core(grad_n2[tokens:].astype(BF16)).astype(F32)
    normed2_t = both_normed.T
    gate_parts = wgrad_plane(normed2_t, halves(grad_gate_act), ids, depth, rows)
    up_parts = wgrad_plane(normed2_t, halves(grad_up_act), ids, depth, rows)
    g_down = links.scatter(down_parts)
    g_gate = links.scatter(gate_parts)
    g_up = links.scatter(up_parts)

    grad_mid_norm, g_gain2 = norm_back(middle, inv_two, gain_two, grad_n2, width)
    grad_middle = cot.astype(F32) + grad_mid_norm
    middle_b = grad_middle.astype(BF16)
    quarters = lambda value: value.reshape(value.shape[0], 4, -1).transpose(1, 0, 2)
    g_out_parts = wgrad_all(middle_b.T, quarters(attn_b), ids, depth, rows)
    g_out = scatter_all(links, *g_out_parts)
    grad_attn = dot(middle_b, out_weight_t).astype(BF16)
    delta = jnp.sum(
        (grad_attn.astype(F32) * attn_b.astype(F32)).reshape(tokens, HEADS, HEAD_DIM), axis=-1
    ).T
    delta = jnp.pad(delta, ((0, 1), (0, 0)))

    grad_q, part2, part1, part0 = attend_back(
        first, seg, queries, kv2, kv1, kv0, grad_attn, lse, delta
    )
    passed = links.some(part1, {2: 3})
    part2 = (part2.astype(F32) + passed.astype(F32)).astype(BF16)
    grad_kv = (
        part0
        + links.some(part1, {1: 0, 3: 2}).astype(F32)
        + links.some(part2, {2: 0, 3: 1}).astype(F32)
    )
    turned_back = rotate(
        jnp.concatenate([grad_q, grad_kv[:, :kv_cols]], axis=1).reshape(
            tokens, HEADS + KV_HEADS, HEAD_DIM
        ),
        cosine,
        -sine,
    ).reshape(tokens, query_cols + kv_cols)
    grad_proj = jnp.concatenate([turned_back, grad_kv[:, kv_cols:]], axis=1).astype(BF16)
    g_in_parts = wgrad_all(normed1_b.T, quarters(grad_proj), ids, depth, rows)
    g_in = scatter_all(links, *g_in_parts)
    grad_n1 = dot_nt(grad_proj, qkv_weight)
    grad_in_norm, g_gain1 = norm_back(resid_in, inv_one, gain_one, grad_n1, width)
    grad_input = unpadded(grad_middle + grad_in_norm)
    g_gains = links.all_sum(jnp.stack([g_gain1, g_gain2]))
    position = (dp_index % 2) * depth + dp_index // 2
    g_gains = lax.dynamic_slice_in_dim(g_gains, position * pad, rows, 1)
    return (
        hidden_out[None],
        grad_input[None],
        g_in,
        g_out.T,
        g_gate,
        g_up,
        g_down.T,
        g_gains[0],
        g_gains[1],
    )


def solution(mesh):
    return jax.shard_map(
        per_device,
        mesh=mesh,
        in_specs=(
            P("dp", "mp", None),
            P("dp", "mp", None),
            P("dp", None),
            P("dp", "mp"),
            P("dp", "mp"),
            P("mp", "dp"),
            P("dp", "mp"),
            P("dp", "mp"),
            P("mp", "dp"),
            P("dp"),
            P("dp"),
        ),
        out_specs=(
            P("dp", "mp", None),
            P("dp", "mp", None),
            P("dp", "mp"),
            P("mp", "dp"),
            P("dp", "mp"),
            P("dp", "mp"),
            P("mp", "dp"),
            P("dp"),
            P("dp"),
        ),
        check_vma=False,
    )
```

```python
import functools
import math

import jax
import jax.numpy as jnp
from jax import lax
from jax.experimental import pallas as pl
from jax.experimental.pallas import tpu as pltpu
from jax.sharding import PartitionSpec as P

HEADS = 15
KV_HEADS = 5
GROUP = HEADS // KV_HEADS
HEAD_DIM = 64
DPAD = 1024
TILE = 256
EPSILON = 1e-05
SCORE_SCALE = 0.125
MASK_FILL = -1e30
LOG2E = 1.4426950408889634
EXP_SCALE = SCORE_SCALE * LOG2E
BF16 = jnp.bfloat16
F32 = jnp.float32


def dot(a, b):
    return jnp.dot(a, b, preferred_element_type=F32)


def dot_nt(a, b):
    return lax.dot_general(a, b, (((1,), (1,)), ((), ())), preferred_element_type=F32)


def vmem_specs(count):
    return [pl.BlockSpec(memory_space=pltpu.VMEM)] * count


def transposed(value):
    return value.astype(F32).T.astype(BF16)


class Place:
    def __init__(self, depth, send_sems, recv_sems):
        dp_index, m = lax.axis_index("dp"), lax.axis_index("mp")
        self.depth = depth
        self.z, self.x = dp_index // 2, dp_index % 2
        self.m, self.y, self.c = m, m // 2, m % 2
        self.send_sems, self.recv_sems = send_sems, recv_sems
        self.count = 0

    def peer(self, kind):
        z, x, y, c = self.z, self.x, self.y, self.c
        if kind == "x":
            x = 1 - x
        elif kind == "y":
            y = 1 - y
        elif kind == "c":
            c = 1 - c
        else:
            z = (z + kind) % self.depth
        return 2 * z + x, 2 * y + c

    def kinds(self):
        return ["x", "y", "c"] + list(range(1, self.depth))

    def barrier(self, kinds=None):
        semaphore = pltpu.get_barrier_semaphore()
        kinds = kinds or self.kinds()
        for kind in kinds:
            pl.semaphore_signal(
                semaphore, inc=1, device_id=self.peer(kind), device_id_type=pl.DeviceIdType.MESH
            )
        pl.semaphore_wait(semaphore, len(kinds))

    def copy(self, kind, source, target=None):
        index = self.count
        self.count += 1
        made = pltpu.make_async_remote_copy(
            src_ref=source,
            dst_ref=source if target is None else target,
            send_sem=self.send_sems.at[index],
            recv_sem=self.recv_sems.at[index],
            device_id=self.peer(kind),
            device_id_type=pl.DeviceIdType.MESH,
        )
        made.start()
        return made


class PlaneGather:
    def __init__(self, place, source, buffer, diagonal_by_x=False):
        self.place, self.source, self.buffer = place, source, buffer
        self.diagonal_by_x = diagonal_by_x
        self.sent = []

    def over_z(self):
        p = self.place
        slot = self.buffer.at[p.y, p.x, p.z]
        self.arriving = [p.copy(k, self.source, slot) for k in range(1, p.depth)]
        self.sent += self.arriving

    def over_xy(self):
        p = self.place
        for made in self.arriving:
            made.wait_recv()
        own = self.buffer.at[p.y, p.x]
        self.by_x, self.by_y = p.copy("x", own), p.copy("y", own)
        self.sent += [self.by_x, self.by_y]

    def diagonal(self):
        p = self.place
        half = p.depth // 2
        self.by_x.wait_recv()
        if self.diagonal_by_x:
            self.by_y.wait_recv()
            self.last = [p.copy("x", self.buffer.at[1 - p.y, p.x])]
        else:
            low = p.copy("y", self.buffer.at[p.y, 1 - p.x, pl.ds(0, half)])
            self.by_y.wait_recv()
            self.last = [low, p.copy("x", self.buffer.at[1 - p.y, p.x, pl.ds(half, half)])]
        self.sent += self.last

    def arrived(self):
        for made in self.last:
            made.wait_recv()

    def finish(self):
        for made in self.sent:
            made.wait_send()


def rope(value, cosine, sine):
    lane = lax.broadcasted_iota(jnp.int32, value.shape, 1)
    half = HEAD_DIM // 2
    partner = jnp.where(
        lane % HEAD_DIM < half, pltpu.roll(value, 128 - half, 1), pltpu.roll(value, half, 1)
    )
    return value * cosine + partner * sine


def mean_rows(value, width):
    return jnp.sum(value, axis=-1, keepdims=True) * (1.0 / width)


def mask_tile(start, query_tile, key_tile):
    key = key_tile * TILE + lax.broadcasted_iota(jnp.int32, (TILE, TILE), 0)
    query = query_tile * TILE + lax.broadcasted_iota(jnp.int32, (TILE, TILE), 1)
    return jnp.where((key >= start) & (key <= query), 0.0, MASK_FILL)


def front_kernel(
    depth, rows, width, in_cols,
    pack_a, pack_g, x_in, cosine, sine, seg,
    q, kv, attn, lse, middle, normed1, normed2, gains, out_w, attn_w, ffn_w,
    a_buf, proj, q_t, k3, v_t, acc, peak, total, bias, send_sems, recv_sems, local_sems,
):
    tokens = x_in.shape[0]
    tiles = tokens // TILE
    back = 1024 // TILE
    pad = DPAD // (2 * depth)
    p = Place(depth, send_sems, recv_sems)
    a_buf[p.c, p.y, p.x, p.z] = pack_a[...]
    own = [
        pltpu.make_async_copy(pack_g.at[w], ffn_w.at[w, p.y, p.x, p.z], local_sems.at[w])
        for w in range(3)
    ]
    for made in own:
        made.start()
    p.barrier()
    plane = PlaneGather(p, pack_a, a_buf.at[p.c])
    gate, up, down = [
        PlaneGather(p, pack_g.at[w], ffn_w.at[w], w == 2) for w in range(3)
    ]
    plane.over_z()
    plane.over_xy()
    gate.over_z()
    plane.diagonal()
    plane.arrived()
    cross = p.copy("c", a_buf.at[p.c])
    for made in own:
        made.wait()
    up.over_z()
    gate.over_xy()
    x_f = x_in[...].astype(F32)
    inv_one = lax.rsqrt(mean_rows(x_f * x_f, width) + EPSILON)
    cross.wait()
    for b in range(2 * depth):
        gains[:, b * pad : (b + 1) * pad] = a_buf[
            0, 0, b // depth, b % depth, pl.ds(rows, 2), 0:pad
        ].astype(F32)
    normed1[...] = (x_f * inv_one * gains[0:1, :]).astype(BF16)

    def project(r, carry):
        span = pl.ds(pl.multiple_of(r * TILE, TILE), TILE)
        for b in range(4):
            weight = a_buf[b % 2, b // 2].reshape(DPAD, -1)[:, :in_cols]
            proj[span, b * in_cols : (b + 1) * in_cols] = dot(normed1[span, :], weight)
        for j in range((HEADS + KV_HEADS) * HEAD_DIM // 128):
            lanes = slice(128 * j, 128 * (j + 1))
            proj[span, lanes] = rope(proj[span, lanes], cosine[span, :], sine[span, :])
        return carry

    lax.fori_loop(0, tiles, project, 0)
    query_cols = HEADS * HEAD_DIM
    q[...] = proj[:, :query_cols].astype(BF16)
    kv[p.m] = proj[:, query_cols : query_cols + 2 * KV_HEADS * HEAD_DIM].astype(BF16)
    mine = kv.at[p.m]
    kv_y, kv_c = p.copy("y", mine), p.copy("c", mine)
    down.over_z()
    q_t[...] = proj[:, :query_cols].T.astype(BF16)
    acc[...] = jnp.zeros_like(acc)
    peak[...] = jnp.full_like(peak, MASK_FILL)
    total[...] = jnp.zeros_like(total)

    def spread(block):
        span = pl.ds(pl.multiple_of(block * tokens, tokens), tokens)
        k3_parts = kv[block]
        v_t[:, span] = transposed(k3_parts)[KV_HEADS * HEAD_DIM :]
        for g in range(KV_HEADS):
            k3[g, span, :] = k3_parts[:, g * HEAD_DIM : (g + 1) * HEAD_DIM]

    def attend_tile(i, t):
        cols = pl.ds(i * TILE, TILE)
        bias[...] = mask_tile(seg[0:1, cols], p.m * tiles + i, t)
        keys = pl.ds(pl.multiple_of(t * TILE, TILE), TILE)

        def group(g, carry):
            k_g = k3[g, keys, :]
            v_g = v_t[pl.ds(pl.multiple_of(g * HEAD_DIM, HEAD_DIM), HEAD_DIM), keys]
            heads = [g * GROUP + j for j in range(GROUP)]
            places = [pl.ds(pl.multiple_of(h * HEAD_DIM, HEAD_DIM), HEAD_DIM) for h in heads]
            old = [peak[pl.ds(h, 1), cols] for h in heads]
            sums = [total[pl.ds(h, 1), cols] for h in heads]
            accs = [acc[s, cols] for s in places]
            scores = [dot(k_g, q_t[s, cols]) + bias[...] for s in places]
            new = [jnp.maximum(o, jnp.max(s, axis=0, keepdims=True)) for o, s in zip(old, scores)]
            probs = [jnp.exp2(s * EXP_SCALE - n * EXP_SCALE) for s, n in zip(scores, new)]
            scale = [jnp.exp2((o - n) * EXP_SCALE) for o, n in zip(old, new)]
            outs = [dot(v_g, b.astype(BF16)) for b in probs]
            for j, h in enumerate(heads):
                peak[pl.ds(h, 1), cols] = new[j]
                total[pl.ds(h, 1), cols] = sums[j] * scale[j] + jnp.sum(
                    probs[j], axis=0, keepdims=True
                )
                acc[places[j], cols] = accs[j] * scale[j] + outs[j]
            return carry

        lax.fori_loop(0, KV_HEADS, group, 0)

    def attend_span(i, low, high):
        def step(t, carry):
            attend_tile(i, t)
            return carry

        lax.fori_loop(low, high, step, 0)

    spread(p.m)
    first_tile = p.m * tiles
    for i in range(tiles):
        attend_span(i, first_tile, first_tile + i + 1)
    kv_y.wait_recv()
    kv_cy = p.copy("c", kv.at[(p.m + 2) % 4])
    up.over_xy()
    gate.diagonal()
    kv_c.wait_recv()
    kv_cy.wait_recv()
    for k in range(1, 4):
        spread((p.m + k) % 4)
    for i in range(tiles):
        attend_span(i, jnp.maximum(first_tile + i - back, 0), first_tile)
        if i == 0:
            down.over_xy()
            up.diagonal()
    for h in range(HEADS):
        span = pl.ds(h * HEAD_DIM, HEAD_DIM)
        acc[span, :] = acc[span, :] / total[h : h + 1, :]
    attn[...] = acc[...].T.astype(BF16)
    lse[...] = peak[...] * EXP_SCALE + jnp.log2(jnp.maximum(total[...], 1e-37))
    saved = pltpu.make_async_copy(a_buf, attn_w, local_sems.at[0])
    saved.start()
    down.diagonal()
    out_cols = query_cols // 4
    for b in range(4):
        weight = a_buf[b % 2, b // 2].reshape(DPAD, -1)
        out_w[b % 2, b // 2] = weight[:, in_cols : in_cols + out_cols]

    def project_out(r, carry):
        span = pl.ds(pl.multiple_of(r * TILE, TILE), TILE)
        mid = x_in[span, :].astype(F32)
        for b in range(4):
            mid += dot_nt(attn[span, b * out_cols : (b + 1) * out_cols], out_w[b % 2, b // 2])
        middle[span, :] = mid
        inv = lax.rsqrt(mean_rows(mid * mid, width) + EPSILON)
        normed2[span, :] = (mid * inv * gains[1:2, :]).astype(BF16)
        return carry

    lax.fori_loop(0, tiles, project_out, 0)
    gate.arrived()
    up.arrived()
    down.arrived()
    for part in (plane, gate, up, down):
        part.finish()
    for made in (kv_y, kv_c, kv_cy):
        made.wait_send()
    saved.wait()


def front(pack_a, pack_g, x_in, cosine, sine, seg, depth, rows, width, in_cols):
    tokens = x_in.shape[0]
    pad = DPAD // (2 * depth)
    cols = pack_a.shape[1]
    query_cols, kv_cols = HEADS * HEAD_DIM, 2 * KV_HEADS * HEAD_DIM
    whole = 4 * tokens
    copies = 4 * (depth - 1) + 4 * 4 + 4
    anywhere = pl.BlockSpec(memory_space=pl.ANY)
    return pl.pallas_call(
        functools.partial(front_kernel, depth, rows, width, in_cols),
        out_shape=[
            jax.ShapeDtypeStruct((tokens, query_cols), BF16),
            jax.ShapeDtypeStruct((4, tokens, kv_cols), BF16),
            jax.ShapeDtypeStruct((tokens, query_cols), BF16),
            jax.ShapeDtypeStruct((HEADS + 1, tokens), F32),
            jax.ShapeDtypeStruct((tokens, DPAD), F32),
            jax.ShapeDtypeStruct((tokens, DPAD), BF16),
            jax.ShapeDtypeStruct((tokens, DPAD), BF16),
            jax.ShapeDtypeStruct((2, DPAD), F32),
            jax.ShapeDtypeStruct((2, 2, DPAD, query_cols // 4), BF16),
            jax.ShapeDtypeStruct((2, 2, 2, depth, pad, cols), BF16),
            jax.ShapeDtypeStruct((3, 2, 2, depth, pad, cols), BF16),
        ],
        in_specs=vmem_specs(1) + [anywhere] + vmem_specs(4),
        out_specs=vmem_specs(9) + [anywhere] * 2,
        scratch_shapes=[
            pltpu.VMEM((2, 2, 2, depth, pad, cols), BF16),
            pltpu.VMEM((tokens, query_cols + kv_cols), F32),
            pltpu.VMEM((query_cols, tokens), BF16),
            pltpu.VMEM((KV_HEADS, whole, HEAD_DIM), BF16),
            pltpu.VMEM((KV_HEADS * HEAD_DIM, whole), BF16),
            pltpu.VMEM((query_cols, tokens), F32),
            pltpu.VMEM((HEADS + 1, tokens), F32),
            pltpu.VMEM((HEADS + 1, tokens), F32),
            pltpu.VMEM((TILE, TILE), F32),
            pltpu.SemaphoreType.DMA((copies,)),
            pltpu.SemaphoreType.DMA((copies,)),
            pltpu.SemaphoreType.DMA((3,)),
        ],
        compiler_params=pltpu.CompilerParams(
            vmem_limit_bytes=58 << 20, collective_id=0, has_side_effects=True
        ),
        cost_estimate=pl.CostEstimate(
            flops=20 << 30, bytes_accessed=40 << 20, transcendentals=8 << 20
        ),
        name="front",
    )(pack_a, pack_g, x_in, cosine, sine, seg)


class PlaneScatter:
    def __init__(self, place, source, recv, stage=None, local_sems=None):
        self.place, self.source, self.recv = place, source, recv
        p, half = place, place.depth // 2
        self.half = half
        places = [(p.y, 1 - p.x, 0, half), (1 - p.y, p.x, half, half), (p.y, p.x, 0, p.depth)]
        views = [
            source.at[y, pl.ds(x * p.depth + first, size)] for y, x, first, size in places
        ]
        self.loads = []
        if stage is None:
            self.by_x, self.by_y, self.total = views
        else:
            self.by_x, self.by_y = stage.at[pl.ds(0, half)], stage.at[pl.ds(half, half)]
            self.total = stage.at[pl.ds(p.depth, p.depth)]
            for n, (view, kept) in enumerate(zip(views, (self.by_x, self.by_y, self.total))):
                self.loads.append(pltpu.make_async_copy(view, kept, local_sems.at[n]))

    def slot(self, n):
        return self.recv.at[pl.ds(n * self.half, self.half)]

    def start(self):
        p, half = self.place, self.half
        for load in self.loads:
            load.start()
        far, here, there = (1 - p.x) * p.depth, p.x * p.depth, 1 - p.y
        self.far_y = p.copy("y", self.source.at[there, pl.ds(far, half)], self.slot(0))
        self.far_x = p.copy("x", self.source.at[there, pl.ds(far + half, half)], self.slot(1))
        self.near_y = p.copy("y", self.source.at[there, pl.ds(here, half)], self.slot(2))
        self.near_x = p.copy("x", self.source.at[p.y, pl.ds(far + half, half)], self.slot(3))
        self.sent = [self.far_y, self.far_x, self.near_y, self.near_x]

    def forward(self):
        p = self.place
        for load in self.loads:
            load.wait()
        self.far_y.wait_recv()
        self.by_x[...] = (self.by_x[...].astype(F32) + self.slot(0)[...].astype(F32)).astype(BF16)
        self.last_x = p.copy("x", self.by_x, self.slot(4))
        self.far_x.wait_recv()
        self.by_y[...] = (self.by_y[...].astype(F32) + self.slot(1)[...].astype(F32)).astype(BF16)
        self.last_y = p.copy("y", self.by_y, self.slot(5))
        self.sent += [self.last_x, self.last_y]

    def over_z(self):
        p, half = self.place, self.half
        for made in (self.near_y, self.near_x, self.last_x, self.last_y):
            made.wait_recv()
        for first, slots in ((0, (2, 4)), (half, (3, 5))):
            span = self.total.at[pl.ds(first, half)]
            terms = [self.slot(n)[...].astype(F32) for n in slots]
            span[...] = (span[...].astype(F32) + terms[0] + terms[1]).astype(BF16)
        self.arriving = [
            p.copy(
                k, self.total.at[(p.z + k) % p.depth], self.recv.at[6 * half + k - 1]
            )
            for k in range(1, p.depth)
        ]
        self.sent += self.arriving

    def result(self):
        value = self.total[self.place.z].astype(F32)
        for k, made in enumerate(self.arriving):
            made.wait_recv()
            value += self.recv[6 * self.half + k].astype(F32)
        return value

    def finish(self):
        for made in self.sent:
            made.wait_send()


def scatter_slots(depth):
    return 3 * depth + depth - 1


def scatter_copies(depth):
    return 6 + depth - 1


def store_blocks(ref, start, value):
    pad = ref.shape[1]
    for k in range(TILE // pad):
        ref[start // pad + k] = value[k * pad : (k + 1) * pad]


def row_tiles(count, body):
    def step(r, carry):
        body(pl.multiple_of(r * TILE, TILE))
        return carry

    lax.fori_loop(0, count // TILE, step, 0)


def ffn_kernel(
    depth, normed2, cot, middle, ffn_w, grads, hidden_out, grad_n2,
    n_other, c_other, hid, d_gate, d_up, n_t, c_t, ffn_own, parts, received, packed,
    send_sems, recv_sems, local_sems,
):
    tokens = normed2.shape[0]
    cols = ffn_w.shape[-1]
    p = Place(depth, send_sems, recv_sems)
    p.barrier(["c"])
    n_copy = p.copy("c", normed2, n_other)
    c_copy = p.copy("c", cot, c_other)
    for s in range(2):
        if s:
            n_copy.wait_recv()
            c_copy.wait_recv()
        n_from, c_from = (n_other, c_other) if s else (normed2, cot)

        def tile(start):
            span = pl.ds(start, TILE)
            both = pl.ds(s * tokens + start, TILE)
            n_rows, c_rows = n_from[span, :], c_from[span, :]
            n_t[:, both] = transposed(n_rows)
            c_t[:, both] = transposed(c_rows)
            part, back = None, None
            for y in range(2):
                lanes = slice(y * cols, (y + 1) * cols)
                w_gate, w_up, w_down = [ffn_w[w, y].reshape(DPAD, cols) for w in range(3)]
                gate, upper = dot(n_rows, w_gate), dot(n_rows, w_up)
                sigma = jax.nn.sigmoid(gate)
                silu = gate * sigma
                hidden = (silu * upper).astype(BF16)
                hid[both, lanes] = hidden
                grad_hid = dot(c_rows, w_down)
                gate_act = (grad_hid * upper * sigma * (1.0 + gate * (1.0 - sigma))).astype(BF16)
                up_act = (grad_hid * silu).astype(BF16)
                d_gate[both, lanes] = gate_act
                d_up[both, lanes] = up_act
                out = dot_nt(hidden, w_down)
                grad = dot_nt(gate_act, w_gate) + dot_nt(up_act, w_up)
                part = out if part is None else part + out
                back = grad if back is None else back + grad
            if s:
                parts[0, span, :] = part.astype(BF16)
                parts[1, span, :] = back.astype(BF16)
            else:
                ffn_own[span, :] = part + middle[span, :]
                grad_n2[span, :] = back

        row_tiles(tokens, tile)
    shared = [p.copy("c", parts.at[n], received.at[n]) for n in range(2)]
    saved = []
    for w, left, right in ((2, c_t, hid), (0, n_t, d_gate), (1, n_t, d_up)):
        for y in range(2):
            lanes = slice(y * cols, (y + 1) * cols)

            def tile(start):
                span = pl.ds(start, TILE)
                packed[w, y, span, :] = dot(left[span, :], right[:, lanes]).astype(BF16)

            row_tiles(DPAD, tile)
        made = pltpu.make_async_copy(packed.at[w], grads.at[w], local_sems.at[w])
        made.start()
        saved.append(made)
    for made in shared:
        made.wait_recv()

    def finish(start):
        span = pl.ds(start, TILE)
        hidden_out[span, :] = (ffn_own[span, :] + received[0, span, :].astype(F32)).astype(BF16)
        grad_n2[span, :] += received[1, span, :].astype(F32)

    row_tiles(tokens, finish)
    for made in shared + [n_copy, c_copy]:
        made.wait_send()
    for made in saved:
        made.wait()


def ffn(normed2, cot, middle, ffn_w):
    tokens = cot.shape[0]
    depth, pad, cols = ffn_w.shape[3:]
    token_rows = pltpu.VMEM((tokens, DPAD), BF16)
    wide = pltpu.VMEM((2 * tokens, 2 * cols), BF16)
    flipped = pltpu.VMEM((DPAD, 2 * tokens), BF16)
    pair = pltpu.VMEM((2, tokens, DPAD), BF16)
    return pl.pallas_call(
        functools.partial(ffn_kernel, depth),
        out_shape=[
            jax.ShapeDtypeStruct((3, 2, DPAD, cols), BF16),
            jax.ShapeDtypeStruct((tokens, DPAD), BF16),
            jax.ShapeDtypeStruct((tokens, DPAD), F32),
        ],
        in_specs=vmem_specs(4),
        out_specs=[pl.BlockSpec(memory_space=pl.ANY)] + vmem_specs(2),
        scratch_shapes=[
            token_rows, token_rows, wide, wide, wide, flipped, flipped,
            pltpu.VMEM((tokens, DPAD), F32), pair, pair,
            pltpu.VMEM((3, 2, DPAD, cols), BF16),
            pltpu.SemaphoreType.DMA((4,)),
            pltpu.SemaphoreType.DMA((4,)),
            pltpu.SemaphoreType.DMA((3,)),
        ],
        compiler_params=pltpu.CompilerParams(
            vmem_limit_bytes=60 << 20, collective_id=1, has_side_effects=True
        ),
        cost_estimate=pl.CostEstimate(
            flops=24 << 30, bytes_accessed=30 << 20, transcendentals=2 << 20
        ),
        name="ffn",
    )(normed2, cot, middle, ffn_w)


def mid_kernel(
    depth, width,
    ffn_g, grad_n2, middle, cot, gains, out_w, q, kv, attn, lse, seg,
    dq, dkv_sum, grad_middle, gain_grad, out_grad, ffn_grad,
    mid_t, out_g, out_c, out_r, ffn_r, stage, grad_attn, q_t, g_t, q3, g3, k3, v3, k_t, dq_t,
    delta, dkv, acc_kv, bias, kv_c, kv_y, send_sems, recv_sems, local_sems,
):
    tokens = q.shape[0]
    tiles = tokens // TILE
    back = 1024 // TILE
    rows = ffn_grad.shape[1]
    out_cols = HEADS * HEAD_DIM // 4
    p = Place(depth, send_sems, recv_sems)
    p.barrier()
    ffn_sums = [
        PlaneScatter(p, ffn_g.at[w], ffn_r.at[w], stage.at[w], local_sems.at[pl.ds(3 * w, 3)])
        for w in range(3)
    ]
    for w in (2, 0, 1):
        ffn_sums[w].start()

    gain = gains[1:2, :]
    gain_grad[...] = jnp.zeros_like(gain_grad)

    def norm_tile(start):
        span = pl.ds(start, TILE)
        mid, up = middle[span, :], grad_n2[span, :]
        inv = lax.rsqrt(mean_rows(mid * mid, width) + EPSILON)
        scaled = up * gain
        mean = mean_rows(scaled * mid, width)
        grad = cot[span, :].astype(F32) + inv * (scaled - mid * (inv * inv * mean))
        grad_middle[span, :] = grad
        gain_grad[...] += jnp.sum(up * mid * inv, axis=0, keepdims=True)
        mid_b = grad.astype(BF16)
        mid_t[:, span] = transposed(mid_b)
        for b in range(4):
            side = dot(mid_b, out_w[b % 2, b // 2])
            grad_attn[span, b * out_cols : (b + 1) * out_cols] = side.astype(BF16)

    row_tiles(tokens, norm_tile)
    for b in range(4):
        side = attn[:, b * out_cols : (b + 1) * out_cols]

        def out_tile(start):
            span = pl.ds(start, TILE)
            store_blocks(out_g.at[b % 2, b // 2], start, dot(mid_t[span, :], side).astype(BF16))

        row_tiles(DPAD, out_tile)
    out_cross = p.copy("c", out_g.at[1 - p.c], out_c)

    g_t[...] = transposed(grad_attn[...])
    attn_t = attn[...].astype(F32).T
    for h in range(HEADS):
        span = slice(h * HEAD_DIM, (h + 1) * HEAD_DIM)
        delta[h : h + 1, :] = jnp.sum(
            g_t[span, :].astype(F32) * attn_t[span, :], axis=0, keepdims=True
        )
        q3[h] = q[:, span]
        g3[h] = grad_attn[:, span]
    q_t[...] = transposed(q[...])
    for s in range(4):
        span = slice(s * tokens, (s + 1) * tokens)
        part = kv[s]
        k_t[:, span] = transposed(part)[: KV_HEADS * HEAD_DIM]
        for g in range(KV_HEADS):
            k3[g, span, :] = part[:, g * HEAD_DIM : (g + 1) * HEAD_DIM]
            v3[g, span, :] = part[:, (KV_HEADS + g) * HEAD_DIM : (KV_HEADS + g + 1) * HEAD_DIM]
    dq_t[...] = jnp.zeros_like(dq_t)
    dkv[...] = jnp.zeros_like(dkv)
    ffn_sums[2].forward()

    def key_tile(t, queries):
        keys = pl.ds(pl.multiple_of(t * TILE, TILE), TILE)
        for i in queries:
            bias[i] = mask_tile(seg[0:1, i * TILE : (i + 1) * TILE], p.m * tiles + i, t)

        def group(g, carry):
            k_g, v_g = k3[g, keys, :], v3[g, keys, :]
            kt_g = k_t[pl.ds(pl.multiple_of(g * HEAD_DIM, HEAD_DIM), HEAD_DIM), keys]
            units = [(i, g * GROUP + j) for i in queries for j in range(GROUP)]
            places = [
                (pl.ds(pl.multiple_of(h * HEAD_DIM, HEAD_DIM), HEAD_DIM), pl.ds(i * TILE, TILE))
                for i, h in units
            ]
            dk, dv = None, None
            for (i, h), (span, cols) in zip(units, places):
                scores = dot(k_g, q_t[span, cols]) * EXP_SCALE + bias[i]
                probs = jnp.exp2(scores - lse[pl.ds(h, 1), cols])
                dprobs = dot(v_g, g_t[span, cols])
                dscores = (probs * (dprobs - delta[pl.ds(h, 1), cols])).astype(BF16)
                add_v = dot(probs.astype(BF16), g3[h, cols, :])
                add_k = dot(dscores, q3[h, cols, :])
                dq_t[span, cols] += dot(kt_g, dscores)
                dk = add_k if dk is None else dk + add_k
                dv = add_v if dv is None else dv + add_v
            acc_kv[g] = dk * SCORE_SCALE
            acc_kv[KV_HEADS + g] = dv
            return carry

        lax.fori_loop(0, KV_HEADS, group, 0)
        for n in range(2 * KV_HEADS):
            dkv[keys, n * HEAD_DIM : (n + 1) * HEAD_DIM] = acc_kv[n].astype(BF16)

    def key_span(low, high, queries):
        def step(t, carry):
            key_tile(t, queries)
            return carry

        lax.fori_loop(low, high, step, 0)

    first = p.m * tiles
    key_tile(first + 1, (1,))
    ffn_sums[0].forward()
    key_span(first, first + 1, (0, 1))
    ffn_sums[1].forward()
    out_cross.wait_recv()
    own = out_g.at[p.c]
    own[...] = (own[...].astype(F32) + out_c[...].astype(F32)).astype(BF16)
    out_sum = PlaneScatter(p, own, out_r)
    out_sum.start()
    ffn_sums[2].over_z()
    key_span(jnp.maximum(first - 2, 0), first, (0, 1))
    ffn_sums[0].over_z()
    key_span(jnp.maximum(first + 1 - back, 0), jnp.maximum(first - 2, 0), (0, 1))
    key_span(jnp.maximum(first - back, 0), jnp.maximum(first + 1 - back, 0), (0,))

    def part_of(index):
        return dkv.at[pl.ds(pl.multiple_of(index * tokens, tokens), tokens)]

    beside = p.m + 1 - 2 * p.c
    cross = [
        p.copy("c", part_of(index), kv_c.at[n])
        for n, index in enumerate((beside, (beside + 2) % 4))
    ]
    dq[...] = dq_t[...].T * SCORE_SCALE
    cross[1].wait_recv()
    away = part_of((p.m + 2) % 4)
    away[...] = (away[...].astype(F32) + kv_c[1].astype(F32)).astype(BF16)
    across = p.copy("y", away, kv_y)
    out_sum.forward()
    ffn_sums[1].over_z()
    for w in range(3):
        ffn_grad[w] = ffn_sums[w].result()[:rows]
    cross[0].wait_recv()
    out_sum.over_z()
    across.wait_recv()
    dkv_sum[...] = part_of(p.m)[...].astype(F32) + kv_c[0].astype(F32) + kv_y[...].astype(F32)
    out_grad[...] = out_sum.result()[:rows]
    for part in ffn_sums + [out_sum]:
        part.finish()
    for made in cross + [across, out_cross]:
        made.wait_send()


def middle_back(ffn_g, grad_n2, middle, cot, gains, out_w, q, kv, attn, lse, seg,
                depth, rows, width):
    tokens, query_cols = q.shape
    pad = DPAD // (2 * depth)
    cols = ffn_g.shape[-1]
    kv_cols = kv.shape[-1]
    out_cols = query_cols // 4
    whole = 4 * tokens
    slots = scatter_slots(depth)
    copies = 4 * scatter_copies(depth) + 4
    heads_q = pltpu.VMEM((HEADS, tokens, HEAD_DIM), BF16)
    heads_kv = pltpu.VMEM((KV_HEADS, whole, HEAD_DIM), BF16)
    flipped = pltpu.VMEM((query_cols, tokens), BF16)
    return pl.pallas_call(
        functools.partial(mid_kernel, depth, width),
        out_shape=[
            jax.ShapeDtypeStruct((tokens, query_cols), F32),
            jax.ShapeDtypeStruct((tokens, kv_cols), F32),
            jax.ShapeDtypeStruct((tokens, DPAD), F32),
            jax.ShapeDtypeStruct((1, DPAD), F32),
            jax.ShapeDtypeStruct((rows, out_cols), F32),
            jax.ShapeDtypeStruct((3, rows, cols), F32),
        ],
        in_specs=[pl.BlockSpec(memory_space=pl.ANY)] + vmem_specs(10),
        out_specs=vmem_specs(6),
        scratch_shapes=[
            pltpu.VMEM((DPAD, tokens), BF16),
            pltpu.VMEM((2, 2, 2 * depth, pad, out_cols), BF16),
            pltpu.VMEM((2, 2 * depth, pad, out_cols), BF16),
            pltpu.VMEM((slots, pad, out_cols), BF16),
            pltpu.VMEM((3, slots, pad, cols), BF16),
            pltpu.VMEM((3, 2 * depth, pad, cols), BF16),
            pltpu.VMEM((tokens, query_cols), BF16),
            flipped, flipped, heads_q, heads_q, heads_kv, heads_kv,
            pltpu.VMEM((KV_HEADS * HEAD_DIM, whole), BF16),
            pltpu.VMEM((query_cols, tokens), F32),
            pltpu.VMEM((HEADS + 1, tokens), F32),
            pltpu.VMEM((whole, kv_cols), BF16),
            pltpu.VMEM((2 * KV_HEADS, TILE, HEAD_DIM), F32),
            pltpu.VMEM((tokens // TILE, TILE, TILE), F32),
            pltpu.VMEM((2, tokens, kv_cols), BF16),
            pltpu.VMEM((tokens, kv_cols), BF16),
            pltpu.SemaphoreType.DMA((copies,)),
            pltpu.SemaphoreType.DMA((copies,)),
            pltpu.SemaphoreType.DMA((9,)),
        ],
        compiler_params=pltpu.CompilerParams(
            vmem_limit_bytes=61 << 20, collective_id=2, has_side_effects=True
        ),
        cost_estimate=pl.CostEstimate(
            flops=40 << 30, bytes_accessed=50 << 20, transcendentals=8 << 20
        ),
        name="middle_back",
    )(ffn_g, grad_n2, middle, cot, gains, out_w, q, kv, attn, lse, seg)


def tail_kernel(
    depth, width, in_cols,
    dq, dkv, cosine, sine, normed1, x_in, grad_middle, gains, attn_w, gain2,
    grad_hidden, in_grad, gain_sum,
    proj, proj_b, n_t, in_g, in_c, in_r, gain_own, gain_r, send_sems, recv_sems,
):
    tokens = dq.shape[0]
    rows = in_grad.shape[0]
    query_cols = dq.shape[1]
    turned = (HEADS + KV_HEADS) * HEAD_DIM
    p = Place(depth, send_sems, recv_sems)
    p.barrier()
    proj[:, :query_cols] = dq[...]
    proj[:, query_cols:] = dkv[...]

    def proj_tile(start):
        span = pl.ds(start, TILE)
        for j in range(turned // 128):
            lanes = slice(128 * j, 128 * (j + 1))
            proj[span, lanes] = rope(proj[span, lanes], cosine[span, :], -sine[span, :])
        for b in range(4):
            proj_b[b, span, :] = proj[span, b * in_cols : (b + 1) * in_cols].astype(BF16)
        n_t[:, span] = transposed(normed1[span, :])

    row_tiles(tokens, proj_tile)
    for other in (1, 0):
        for y in range(2):
            def in_tile(start):
                span = pl.ds(start, TILE)
                for c in range(2):
                    @pl.when((p.c == c) if not other else (p.c != c))
                    def _():
                        side = dot(n_t[span, :], proj_b[2 * y + c]).astype(BF16)
                        store_blocks(in_g.at[c, y], start, side)

            row_tiles(DPAD, in_tile)
        if other:
            in_cross = p.copy("c", in_g.at[1 - p.c], in_c)
    in_cross.wait_recv()
    own = in_g.at[p.c]
    own[...] = (own[...].astype(F32) + in_c[...].astype(F32)).astype(BF16)
    in_sum = PlaneScatter(p, own, in_r)
    in_sum.start()
    gain = gains[0:1, :]
    gain_own[...] = jnp.zeros_like(gain_own)
    gain_own[1:2, :] = gain2[...]

    def norm_tile(start):
        span = pl.ds(start, TILE)
        x_f = x_in[span, :].astype(F32)
        up = None
        for b in range(4):
            weight = attn_w[b % 2, b // 2].reshape(DPAD, -1)[:, :in_cols]
            term = dot_nt(proj_b[b, span, :], weight)
            up = term if up is None else up + term
        inv = lax.rsqrt(mean_rows(x_f * x_f, width) + EPSILON)
        scaled = up * gain
        mean = mean_rows(scaled * x_f, width)
        grad_hidden[span, :] = grad_middle[span, :] + inv * (scaled - x_f * (inv * inv * mean))
        gain_own[0:1, :] += jnp.sum(up * x_f * inv, axis=0, keepdims=True)

    row_tiles(tokens, norm_tile)
    in_sum.forward()
    sent = []
    for n, kind in enumerate(("c", "y", "x")):
        made = p.copy(kind, gain_own.at[pl.ds(8 * n, 8)], gain_r.at[pl.ds(8 * n, 8)])
        sent.append(made)
        made.wait_recv()
        if n == 1:
            in_sum.over_z()
        gain_own[8 * (n + 1) : 8 * (n + 2), :] = (
            gain_own[8 * n : 8 * (n + 1), :] + gain_r[8 * n : 8 * (n + 1), :]
        )
    last = gain_own.at[pl.ds(24, 8)]
    arriving = [p.copy(k, last, gain_r.at[pl.ds(24 + 8 * k, 8)]) for k in range(1, depth)]
    total = last[...]
    for k, made in enumerate(arriving):
        made.wait_recv()
        total += gain_r[32 + 8 * k : 40 + 8 * k, :]
    gain_sum[...] = total
    in_grad[...] = in_sum.result()[:rows]
    in_sum.finish()
    for made in sent + arriving + [in_cross]:
        made.wait_send()


def tail(dq, dkv, cosine, sine, normed1, x_in, grad_middle, gains, attn_w, gain2,
         depth, rows, width, in_cols):
    tokens = dq.shape[0]
    pad = DPAD // (2 * depth)
    total = dq.shape[1] + dkv.shape[1]
    slots = scatter_slots(depth)
    copies = scatter_copies(depth) + 1 + 3 + depth - 1
    return pl.pallas_call(
        functools.partial(tail_kernel, depth, width, in_cols),
        out_shape=[
            jax.ShapeDtypeStruct((tokens, DPAD), F32),
            jax.ShapeDtypeStruct((rows, in_cols), F32),
            jax.ShapeDtypeStruct((8, DPAD), F32),
        ],
        in_specs=vmem_specs(10),
        out_specs=vmem_specs(3),
        scratch_shapes=[
            pltpu.VMEM((tokens, total), F32),
            pltpu.VMEM((4, tokens, in_cols), BF16),
            pltpu.VMEM((DPAD, tokens), BF16),
            pltpu.VMEM((2, 2, 2 * depth, pad, in_cols), BF16),
            pltpu.VMEM((2, 2 * depth, pad, in_cols), BF16),
            pltpu.VMEM((slots, pad, in_cols), BF16),
            pltpu.VMEM((32, DPAD), F32),
            pltpu.VMEM((24 + 8 * depth, DPAD), F32),
            pltpu.SemaphoreType.DMA((copies,)),
            pltpu.SemaphoreType.DMA((copies,)),
        ],
        compiler_params=pltpu.CompilerParams(
            vmem_limit_bytes=60 << 20, collective_id=3, has_side_effects=True
        ),
        cost_estimate=pl.CostEstimate(
            flops=8 << 30, bytes_accessed=30 << 20, transcendentals=0
        ),
        name="tail",
    )(dq, dkv, cosine, sine, normed1, x_in, grad_middle, gains, attn_w, gain2)


def rotary_tables(position_ids):
    half_dim = HEAD_DIM // 2
    frequency = jnp.exp(
        jnp.arange(half_dim, dtype=F32) * (-2.0 * math.log(10000.0) / HEAD_DIM)
    )
    angles = position_ids.astype(F32)[:, None] * frequency[None, :]
    return jnp.cos(angles), jnp.sin(angles)


def per_device(
    hidden_in, cotangent, segments, positions, attn_in, attn_out, w_gate, w_up, w_down,
    norm1_gain, norm2_gain,
):
    tokens, width = hidden_in.shape[1:]
    dp_size = lax.axis_size("dp")
    depth = dp_size // 2
    rows = width // dp_size
    pad = DPAD // dp_size
    dp_index, m = lax.axis_index("dp"), lax.axis_index("mp")

    def padded(value):
        value = value.reshape(value.shape[0], depth, 2, rows).transpose(0, 2, 1, 3)
        return jnp.pad(value, ((0, 0), (0, 0), (0, 0), (0, pad - rows))).reshape(-1, DPAD)

    def unpadded(value):
        value = value.reshape(-1, 2, depth, pad)[..., :rows]
        return value.transpose(0, 2, 1, 3).reshape(-1, width)

    in_cols = attn_in.shape[1]
    out_cols = attn_out.shape[0]
    gains_in = jnp.pad(
        jnp.stack([norm1_gain, norm2_gain]), ((0, pad - rows - 2), (0, in_cols + out_cols - rows))
    )
    pack_a = jnp.concatenate(
        [jnp.concatenate([attn_in, attn_out.T], axis=1), gains_in], axis=0
    )
    pack_g = jnp.pad(jnp.stack([w_gate, w_up, w_down.T]), ((0, 0), (0, pad - rows), (0, 0)))
    x_in = padded(hidden_in[0])
    cot = padded(cotangent[0])
    cosine, sine = rotary_tables(positions[0])
    cos_lanes = jnp.tile(cosine, (1, 4))
    sin_lanes = jnp.tile(jnp.concatenate([-sine, sine], axis=1), (1, 2))
    seq_seg = segments[0]
    own_seg = lax.dynamic_slice_in_dim(seq_seg, m * tokens, tokens, 0)
    start = jnp.sum(seq_seg[None, :] < own_seg[:, None], axis=1, dtype=jnp.int32)[None, :]
    queries, kv_all, attn_b, lse, middle, normed1, normed2, gains, out_w, attn_w, ffn_w = front(
        pack_a, pack_g, x_in, cos_lanes, sin_lanes, start, depth, rows, width, in_cols
    )
    ffn_g, hidden_out, grad_n2 = ffn(normed2, cot, middle, ffn_w)
    ffn_g = ffn_g.reshape(3, 2, dp_size, pad, -1)
    dq, dkv, grad_middle, gain2, g_out, g_ffn = middle_back(
        ffn_g, grad_n2, middle, cot, gains, out_w, queries, kv_all, attn_b, lse, start,
        depth, rows, width,
    )
    grad_hidden, g_in, g_gains = tail(
        dq, dkv, cos_lanes, sin_lanes, normed1, x_in, grad_middle, gains, attn_w, gain2,
        depth, rows, width, in_cols,
    )
    position = (dp_index % 2) * depth + dp_index // 2
    g_gains = lax.dynamic_slice_in_dim(g_gains, position * pad, rows, 1)
    return (
        unpadded(hidden_out)[None],
        unpadded(grad_hidden)[None],
        g_in,
        g_out.T,
        g_ffn[0],
        g_ffn[1],
        g_ffn[2].T,
        g_gains[0],
        g_gains[1],
    )


def solution(mesh):
    return jax.shard_map(
        per_device,
        mesh=mesh,
        in_specs=(
            P("dp", "mp", None),
            P("dp", "mp", None),
            P("dp", None),
            P("dp", "mp"),
            P("dp", "mp"),
            P("mp", "dp"),
            P("dp", "mp"),
            P("dp", "mp"),
            P("mp", "dp"),
            P("dp"),
            P("dp"),
        ),
        out_specs=(
            P("dp", "mp", None),
            P("dp", "mp", None),
            P("dp", "mp"),
            P("mp", "dp"),
            P("dp", "mp"),
            P("dp", "mp"),
            P("mp", "dp"),
            P("dp"),
            P("dp"),
        ),
        check_vma=False,
    )
```

```python
import functools
import math

import jax
import jax.numpy as jnp
from jax import lax
from jax.experimental import pallas as pl
from jax.experimental.pallas import tpu as pltpu
from jax.sharding import PartitionSpec as P

HEADS = 15
KV_HEADS = 5
GROUP = HEADS // KV_HEADS
HEAD_DIM = 64
DPAD = 1024
TILE = 256
EPSILON = 1e-05
SCORE_SCALE = 0.125
MASK_FILL = -1e30
LOG2E = 1.4426950408889634
EXP_SCALE = SCORE_SCALE * LOG2E
BF16 = jnp.bfloat16
F32 = jnp.float32


def dot(a, b):
    return jnp.dot(a, b, preferred_element_type=F32)


def dot_nt(a, b):
    return lax.dot_general(a, b, (((1,), (1,)), ((), ())), preferred_element_type=F32)


def vmem_specs(count):
    return [pl.BlockSpec(memory_space=pltpu.VMEM)] * count


def transposed(value):
    return value.astype(F32).T.astype(BF16)


class Place:
    def __init__(self, depth, send_sems, recv_sems):
        dp_index, m = lax.axis_index("dp"), lax.axis_index("mp")
        self.depth = depth
        self.z, self.x = dp_index // 2, dp_index % 2
        self.m, self.y, self.c = m, m // 2, m % 2
        self.send_sems, self.recv_sems = send_sems, recv_sems
        self.count = 0

    def peer(self, kind):
        z, x, y, c = self.z, self.x, self.y, self.c
        if kind == "x":
            x = 1 - x
        elif kind == "y":
            y = 1 - y
        elif kind == "c":
            c = 1 - c
        else:
            z = (z + kind) % self.depth
        return 2 * z + x, 2 * y + c

    def kinds(self):
        return ["x", "y", "c"] + list(range(1, self.depth))

    def barrier(self, kinds=None):
        semaphore = pltpu.get_barrier_semaphore()
        kinds = kinds or self.kinds()
        for kind in kinds:
            pl.semaphore_signal(
                semaphore, inc=1, device_id=self.peer(kind), device_id_type=pl.DeviceIdType.MESH
            )
        pl.semaphore_wait(semaphore, len(kinds))

    def copy(self, kind, source, target=None):
        index = self.count
        self.count += 1
        made = pltpu.make_async_remote_copy(
            src_ref=source,
            dst_ref=source if target is None else target,
            send_sem=self.send_sems.at[index],
            recv_sem=self.recv_sems.at[index],
            device_id=self.peer(kind),
            device_id_type=pl.DeviceIdType.MESH,
        )
        made.start()
        return made


class PlaneGather:
    def __init__(self, place, source, buffer, by_x):
        self.place, self.source, self.buffer = place, source, buffer
        self.split = place.depth - by_x
        self.sent, self.last = [], []

    def over_z(self, slot=None):
        p = self.place
        slot = self.buffer.at[p.y, p.x, p.z] if slot is None else slot
        self.arriving = [p.copy(k, self.source, slot) for k in range(1, p.depth)]
        self.sent += self.arriving

    def stacked(self):
        for made in self.arriving:
            made.wait_recv()

    def over_x(self):
        p = self.place
        self.by_x = p.copy("x", self.buffer.at[p.y, p.x])
        self.sent.append(self.by_x)

    def over_y(self):
        p = self.place
        self.by_y = p.copy("y", self.buffer.at[p.y, p.x])
        self.sent.append(self.by_y)

    def diagonal_x(self):
        p = self.place
        self.by_y.wait_recv()
        span = pl.ds(self.split, p.depth - self.split)
        self.last.append(p.copy("x", self.buffer.at[1 - p.y, p.x, span]))

    def diagonal_y(self):
        p = self.place
        self.by_x.wait_recv()
        if self.split:
            self.last.append(p.copy("y", self.buffer.at[p.y, 1 - p.x, pl.ds(0, self.split)]))

    def arrived(self):
        for made in self.last:
            made.wait_recv()

    def finish(self):
        for made in self.sent + self.last:
            made.wait_send()


def rope(value, cosine, sine):
    lane = lax.broadcasted_iota(jnp.int32, value.shape, 1)
    half = HEAD_DIM // 2
    partner = jnp.where(
        lane % HEAD_DIM < half, pltpu.roll(value, 128 - half, 1), pltpu.roll(value, half, 1)
    )
    return value * cosine + partner * sine


def mean_rows(value, width):
    return jnp.sum(value, axis=-1, keepdims=True) * (1.0 / width)


def mask_tile(start, query_tile, key_tile):
    key = key_tile * TILE + lax.broadcasted_iota(jnp.int32, (TILE, TILE), 0)
    query = query_tile * TILE + lax.broadcasted_iota(jnp.int32, (TILE, TILE), 1)
    return jnp.where((key >= start) & (key <= query), 0.0, MASK_FILL)


def front_kernel(
    depth, rows, width, in_cols,
    pack_a, pack_g, x_in, cosine, sine, seg,
    q, kv, attn, lse, middle, normed1, normed2, gains, out_w, attn_w, ffn_w, down_w,
    a_buf, proj, q_t, k3, v_t, acc, peak, total, bias, send_sems, recv_sems, local_sems,
):
    tokens = x_in.shape[0]
    tiles = tokens // TILE
    back = 1024 // TILE
    pad = DPAD // (2 * depth)
    p = Place(depth, send_sems, recv_sems)
    a_buf[p.c, p.y, p.x, p.z] = pack_a[...]
    own = [
        pltpu.make_async_copy(pack_g.at[w], ffn_w.at[w, p.y, p.x, p.z], local_sems.at[w])
        for w in range(2)
    ]
    own.append(pltpu.make_async_copy(pack_g.at[2], down_w.at[p.z], local_sems.at[2]))
    for made in own:
        made.start()
    p.barrier()
    plane = PlaneGather(p, pack_a, a_buf.at[p.c], depth // 2)
    gate, up = [
        PlaneGather(p, pack_g.at[w], ffn_w.at[w], n) for w, n in ((0, depth), (1, depth // 2))
    ]
    down = PlaneGather(p, pack_g.at[2], None, 0)
    plane.over_z()
    plane.stacked()
    plane.over_x()
    plane.over_y()
    gate.over_z()
    plane.diagonal_y()
    plane.diagonal_x()
    for made in own:
        made.wait()
    up.over_z()
    plane.arrived()
    cross = p.copy("c", a_buf.at[p.c])
    gate.stacked()
    gate.over_x()
    gate.over_y()
    x_f = x_in[...].astype(F32)
    inv_one = lax.rsqrt(mean_rows(x_f * x_f, width) + EPSILON)
    cross.wait()
    for b in range(2 * depth):
        gains[:, b * pad : (b + 1) * pad] = a_buf[
            0, 0, b // depth, b % depth, pl.ds(rows, 2), 0:pad
        ].astype(F32)
    normed1[...] = (x_f * inv_one * gains[0:1, :]).astype(BF16)

    def project(r, carry):
        span = pl.ds(pl.multiple_of(r * TILE, TILE), TILE)
        for b in range(4):
            weight = a_buf[b % 2, b // 2].reshape(DPAD, -1)[:, :in_cols]
            proj[span, b * in_cols : (b + 1) * in_cols] = dot(normed1[span, :], weight)
        for j in range((HEADS + KV_HEADS) * HEAD_DIM // 128):
            lanes = slice(128 * j, 128 * (j + 1))
            proj[span, lanes] = rope(proj[span, lanes], cosine[span, :], sine[span, :])
        return carry

    lax.fori_loop(0, tiles, project, 0)
    query_cols = HEADS * HEAD_DIM
    q[...] = proj[:, :query_cols].astype(BF16)
    kv[p.m] = proj[:, query_cols : query_cols + 2 * KV_HEADS * HEAD_DIM].astype(BF16)
    mine = kv.at[p.m]
    kv_y, kv_c = p.copy("y", mine), p.copy("c", mine)
    down.over_z(down_w.at[p.z])
    up.stacked()
    up.over_x()
    q_t[...] = proj[:, :query_cols].T.astype(BF16)
    acc[...] = jnp.zeros_like(acc)
    peak[...] = jnp.full_like(peak, MASK_FILL)
    total[...] = jnp.zeros_like(total)

    def spread(block):
        span = pl.ds(pl.multiple_of(block * tokens, tokens), tokens)
        k3_parts = kv[block]
        v_t[:, span] = transposed(k3_parts)[KV_HEADS * HEAD_DIM :]
        for g in range(KV_HEADS):
            k3[g, span, :] = k3_parts[:, g * HEAD_DIM : (g + 1) * HEAD_DIM]

    def attend_tile(i, t):
        cols = pl.ds(i * TILE, TILE)
        bias[...] = mask_tile(seg[0:1, cols], p.m * tiles + i, t)
        keys = pl.ds(pl.multiple_of(t * TILE, TILE), TILE)

        def group(g, carry):
            k_g = k3[g, keys, :]
            v_g = v_t[pl.ds(pl.multiple_of(g * HEAD_DIM, HEAD_DIM), HEAD_DIM), keys]
            heads = [g * GROUP + j for j in range(GROUP)]
            places = [pl.ds(pl.multiple_of(h * HEAD_DIM, HEAD_DIM), HEAD_DIM) for h in heads]
            old = [peak[pl.ds(h, 1), cols] for h in heads]
            sums = [total[pl.ds(h, 1), cols] for h in heads]
            accs = [acc[s, cols] for s in places]
            scores = [dot(k_g, q_t[s, cols]) + bias[...] for s in places]
            new = [jnp.maximum(o, jnp.max(s, axis=0, keepdims=True)) for o, s in zip(old, scores)]
            probs = [jnp.exp2(s * EXP_SCALE - n * EXP_SCALE) for s, n in zip(scores, new)]
            scale = [jnp.exp2((o - n) * EXP_SCALE) for o, n in zip(old, new)]
            outs = [dot(v_g, b.astype(BF16)) for b in probs]
            for j, h in enumerate(heads):
                peak[pl.ds(h, 1), cols] = new[j]
                total[pl.ds(h, 1), cols] = sums[j] * scale[j] + jnp.sum(
                    probs[j], axis=0, keepdims=True
                )
                acc[places[j], cols] = accs[j] * scale[j] + outs[j]
            return carry

        lax.fori_loop(0, KV_HEADS, group, 0)

    def attend_span(i, low, high):
        def step(t, carry):
            attend_tile(i, t)
            return carry

        lax.fori_loop(low, high, step, 0)

    spread(p.m)
    first_tile = p.m * tiles
    for i in range(tiles):
        attend_span(i, first_tile, first_tile + i + 1)
        if i == 0:
            gate.diagonal_x()
            gate.diagonal_y()
    kv_y.wait_recv()
    kv_cy = p.copy("c", kv.at[(p.m + 2) % 4])
    up.over_y()
    kv_c.wait_recv()
    spread((p.m + 1 - 2 * p.c) % 4)
    kv_cy.wait_recv()
    for k in (2, 3):
        spread((p.m + (k if k == 2 else 3 - 2 * p.c)) % 4)
    for i in range(tiles):
        attend_span(i, jnp.maximum(first_tile + i - back, 0), first_tile)
        if i == 0:
            up.diagonal_y()
    up.diagonal_x()
    for h in range(HEADS):
        span = pl.ds(h * HEAD_DIM, HEAD_DIM)
        acc[span, :] = acc[span, :] / total[h : h + 1, :]
    attn[...] = acc[...].T.astype(BF16)
    lse[...] = peak[...] * EXP_SCALE + jnp.log2(jnp.maximum(total[...], 1e-37))
    saved = pltpu.make_async_copy(a_buf, attn_w, local_sems.at[0])
    saved.start()
    out_cols = query_cols // 4
    for b in range(4):
        weight = a_buf[b % 2, b // 2].reshape(DPAD, -1)
        out_w[b % 2, b // 2] = weight[:, in_cols : in_cols + out_cols]

    def project_out(r, carry):
        span = pl.ds(pl.multiple_of(r * TILE, TILE), TILE)
        mid = x_in[span, :].astype(F32)
        for b in range(4):
            mid += dot_nt(attn[span, b * out_cols : (b + 1) * out_cols], out_w[b % 2, b // 2])
        middle[span, :] = mid
        inv = lax.rsqrt(mean_rows(mid * mid, width) + EPSILON)
        normed2[span, :] = (mid * inv * gains[1:2, :]).astype(BF16)
        return carry

    lax.fori_loop(0, tiles, project_out, 0)
    gate.arrived()
    up.arrived()
    down.stacked()
    for part in (plane, gate, up, down):
        part.finish()
    for made in (kv_y, kv_c, kv_cy):
        made.wait_send()
    saved.wait()


def front(pack_a, pack_g, x_in, cosine, sine, seg, depth, rows, width, in_cols):
    tokens = x_in.shape[0]
    pad = DPAD // (2 * depth)
    cols = pack_a.shape[1]
    query_cols, kv_cols = HEADS * HEAD_DIM, 2 * KV_HEADS * HEAD_DIM
    whole = 4 * tokens
    copies = 4 * (depth - 1) + 4 * 4 + 4
    anywhere = pl.BlockSpec(memory_space=pl.ANY)
    return pl.pallas_call(
        functools.partial(front_kernel, depth, rows, width, in_cols),
        out_shape=[
            jax.ShapeDtypeStruct((tokens, query_cols), BF16),
            jax.ShapeDtypeStruct((4, tokens, kv_cols), BF16),
            jax.ShapeDtypeStruct((tokens, query_cols), BF16),
            jax.ShapeDtypeStruct((HEADS + 1, tokens), F32),
            jax.ShapeDtypeStruct((tokens, DPAD), F32),
            jax.ShapeDtypeStruct((tokens, DPAD), BF16),
            jax.ShapeDtypeStruct((tokens, DPAD), BF16),
            jax.ShapeDtypeStruct((2, DPAD), F32),
            jax.ShapeDtypeStruct((2, 2, DPAD, query_cols // 4), BF16),
            jax.ShapeDtypeStruct((2, 2, 2, depth, pad, cols), BF16),
            jax.ShapeDtypeStruct((2, 2, 2, depth, pad, cols), BF16),
            jax.ShapeDtypeStruct((depth, pad, cols), BF16),
        ],
        in_specs=vmem_specs(1) + [anywhere] + vmem_specs(4),
        out_specs=vmem_specs(9) + [anywhere] * 3,
        scratch_shapes=[
            pltpu.VMEM((2, 2, 2, depth, pad, cols), BF16),
            pltpu.VMEM((tokens, query_cols + kv_cols), F32),
            pltpu.VMEM((query_cols, tokens), BF16),
            pltpu.VMEM((KV_HEADS, whole, HEAD_DIM), BF16),
            pltpu.VMEM((KV_HEADS * HEAD_DIM, whole), BF16),
            pltpu.VMEM((query_cols, tokens), F32),
            pltpu.VMEM((HEADS + 1, tokens), F32),
            pltpu.VMEM((HEADS + 1, tokens), F32),
            pltpu.VMEM((TILE, TILE), F32),
            pltpu.SemaphoreType.DMA((copies,)),
            pltpu.SemaphoreType.DMA((copies,)),
            pltpu.SemaphoreType.DMA((3,)),
        ],
        compiler_params=pltpu.CompilerParams(
            vmem_limit_bytes=58 << 20, collective_id=0, has_side_effects=True
        ),
        cost_estimate=pl.CostEstimate(
            flops=20 << 30, bytes_accessed=40 << 20, transcendentals=8 << 20
        ),
        name="front",
    )(pack_a, pack_g, x_in, cosine, sine, seg)


class PlaneScatter:
    def __init__(self, place, source, recv, stage=None, local_sems=None):
        self.place, self.source, self.recv = place, source, recv
        p, half = place, place.depth // 2
        self.half = half
        places = [(p.y, 1 - p.x, 0, half), (1 - p.y, p.x, half, half), (p.y, p.x, 0, p.depth)]
        views = [
            source.at[y, pl.ds(x * p.depth + first, size)] for y, x, first, size in places
        ]
        self.loads = []
        if stage is None:
            self.by_x, self.by_y, self.total = views
        else:
            self.by_x, self.by_y = stage.at[pl.ds(0, half)], stage.at[pl.ds(half, half)]
            self.total = stage.at[pl.ds(p.depth, p.depth)]
            for n, (view, kept) in enumerate(zip(views, (self.by_x, self.by_y, self.total))):
                self.loads.append(pltpu.make_async_copy(view, kept, local_sems.at[n]))

    def slot(self, n):
        return self.recv.at[pl.ds(n * self.half, self.half)]

    def start(self):
        p, half = self.place, self.half
        for load in self.loads:
            load.start()
        far, here, there = (1 - p.x) * p.depth, p.x * p.depth, 1 - p.y
        self.far_y = p.copy("y", self.source.at[there, pl.ds(far, half)], self.slot(0))
        self.far_x = p.copy("x", self.source.at[there, pl.ds(far + half, half)], self.slot(1))
        self.near_y = p.copy("y", self.source.at[there, pl.ds(here, half)], self.slot(2))
        self.near_x = p.copy("x", self.source.at[p.y, pl.ds(far + half, half)], self.slot(3))
        self.sent = [self.far_y, self.far_x, self.near_y, self.near_x]

    def forward(self):
        p = self.place
        for load in self.loads:
            load.wait()
        self.far_y.wait_recv()
        self.by_x[...] = (self.by_x[...].astype(F32) + self.slot(0)[...].astype(F32)).astype(BF16)
        self.last_x = p.copy("x", self.by_x, self.slot(4))
        self.far_x.wait_recv()
        self.by_y[...] = (self.by_y[...].astype(F32) + self.slot(1)[...].astype(F32)).astype(BF16)
        self.last_y = p.copy("y", self.by_y, self.slot(5))
        self.sent += [self.last_x, self.last_y]

    def add(self):
        half = self.half
        for made in (self.near_y, self.near_x, self.last_x, self.last_y):
            made.wait_recv()
        for first, slots in ((0, (2, 4)), (half, (3, 5))):
            span = self.total.at[pl.ds(first, half)]
            terms = [self.slot(n)[...].astype(F32) for n in slots]
            span[...] = (span[...].astype(F32) + terms[0] + terms[1]).astype(BF16)

    def over_z(self):
        p, half = self.place, self.half
        self.add()
        self.arriving = [
            p.copy(
                k, self.total.at[(p.z + k) % p.depth], self.recv.at[6 * half + k - 1]
            )
            for k in range(1, p.depth)
        ]
        self.sent += self.arriving

    def result(self):
        value = self.total[self.place.z].astype(F32)
        for k, made in enumerate(self.arriving):
            made.wait_recv()
            value += self.recv[6 * self.half + k].astype(F32)
        return value

    def finish(self):
        for made in self.sent:
            made.wait_send()


def scatter_slots(depth):
    return 3 * depth + depth - 1


def scatter_copies(depth):
    return 6 + depth - 1


def store_blocks(ref, start, value):
    pad = ref.shape[1]
    for k in range(TILE // pad):
        ref[start // pad + k] = value[k * pad : (k + 1) * pad]


def row_tiles(count, body):
    def step(r, carry):
        body(pl.multiple_of(r * TILE, TILE))
        return carry

    lax.fori_loop(0, count // TILE, step, 0)


def ffn_kernel(
    depth, normed2, cot, middle, ffn_w, down_w, grads, down_sum, hidden_out, grad_n2,
    down_buf, down_g, down_r, n_other, c_other, hid, d_gate, d_up, n_t, c_t, ffn_own, parts,
    received, packed, send_sems, recv_sems, local_sems,
):
    tokens = normed2.shape[0]
    cols = ffn_w.shape[-1]
    p = Place(depth, send_sems, recv_sems)
    down_buf[p.y, p.x] = down_w[...]
    p.barrier(["c", "x", "y"])
    n_copy = p.copy("c", normed2, n_other)
    c_copy = p.copy("c", cot, c_other)
    down = PlaneGather(p, None, down_buf, depth // 2)
    down.over_x()
    down.over_y()

    def sides(s):
        return (n_other, c_other) if s else (normed2, cot)

    for s in range(2):
        if s:
            n_copy.wait_recv()
            c_copy.wait_recv()
        n_from, c_from = sides(s)
        both = slice(s * tokens, (s + 1) * tokens)
        n_t[:, both] = transposed(n_from[...])
        c_t[:, both] = transposed(c_from[...])
        for y in range(2):
            lanes = slice(y * cols, (y + 1) * cols)
            w_gate, w_up = [ffn_w[w, y].reshape(DPAD, cols) for w in range(2)]

            def tile(start):
                span = pl.ds(s * tokens + start, TILE)
                n_rows = n_from[pl.ds(start, TILE), :]
                gate, upper = dot(n_rows, w_gate), dot(n_rows, w_up)
                sigma = jax.nn.sigmoid(gate)
                silu = gate * sigma
                hid[span, lanes] = (silu * upper).astype(BF16)
                d_gate[span, lanes] = (upper * sigma * (1.0 + gate * (1.0 - sigma))).astype(BF16)
                d_up[span, lanes] = silu.astype(BF16)

            row_tiles(tokens, tile)
    down.diagonal_y()
    down.diagonal_x()

    def weight_grad(left, right, y, target):
        lanes = slice(y * cols, (y + 1) * cols)

        def tile(start):
            side = dot(left[pl.ds(start, TILE), :], right[:, lanes])
            store_blocks(target, start, side.astype(BF16))

        row_tiles(DPAD, tile)

    for y in range(2):
        weight_grad(c_t, hid, y, down_g.at[y])
    down.arrived()
    total = PlaneScatter(p, down_g, down_r)
    total.start()

    for s in (1, 0):
        n_from, c_from = sides(s)
        both = slice(s * tokens, (s + 1) * tokens)
        part, back = None, None
        for y in range(2):
            lanes = slice(y * cols, (y + 1) * cols)
            w_gate, w_up = [ffn_w[w, y].reshape(DPAD, cols) for w in range(2)]
            w_down = down_buf[y].reshape(DPAD, cols)
            grad_hid = dot(c_from[...], w_down)
            gate_act = (grad_hid * d_gate[both, lanes].astype(F32)).astype(BF16)
            up_act = (grad_hid * d_up[both, lanes].astype(F32)).astype(BF16)
            d_gate[both, lanes] = gate_act
            d_up[both, lanes] = up_act
            out = dot_nt(hid[both, lanes], w_down)
            grad = dot_nt(gate_act, w_gate) + dot_nt(up_act, w_up)
            part = out if part is None else part + out
            back = grad if back is None else back + grad
        if s:
            parts[0] = part.astype(BF16)
            parts[1] = back.astype(BF16)
            shared = [p.copy("c", parts.at[n], received.at[n]) for n in range(2)]
        else:
            ffn_own[...] = part + middle[...]
            grad_n2[...] = back
    total.forward()
    saved = []
    for w, right in ((0, d_gate), (1, d_up)):
        for y in range(2):
            weight_grad(n_t, right, y, packed.at[w, y])
        made = pltpu.make_async_copy(packed.at[w], grads.at[w], local_sems.at[w])
        made.start()
        saved.append(made)
    for made in shared:
        made.wait_recv()

    def finish(start):
        span = pl.ds(start, TILE)
        hidden_out[span, :] = (ffn_own[span, :] + received[0, span, :].astype(F32)).astype(BF16)
        grad_n2[span, :] += received[1, span, :].astype(F32)

    row_tiles(tokens, finish)
    total.add()
    down_sum[...] = total.total[...]
    total.finish()
    down.finish()
    for made in shared + [n_copy, c_copy]:
        made.wait_send()
    for made in saved:
        made.wait()


def ffn(normed2, cot, middle, ffn_w, down_w):
    tokens = cot.shape[0]
    depth, pad, cols = down_w.shape
    token_rows = pltpu.VMEM((tokens, DPAD), BF16)
    wide = pltpu.VMEM((2 * tokens, 2 * cols), BF16)
    flipped = pltpu.VMEM((DPAD, 2 * tokens), BF16)
    pair = pltpu.VMEM((2, tokens, DPAD), BF16)
    copies = 4 + 4 + 6
    return pl.pallas_call(
        functools.partial(ffn_kernel, depth),
        out_shape=[
            jax.ShapeDtypeStruct((2, 2, 2 * depth, pad, cols), BF16),
            jax.ShapeDtypeStruct((depth, pad, cols), BF16),
            jax.ShapeDtypeStruct((tokens, DPAD), BF16),
            jax.ShapeDtypeStruct((tokens, DPAD), F32),
        ],
        in_specs=vmem_specs(5),
        out_specs=[pl.BlockSpec(memory_space=pl.ANY)] + vmem_specs(3),
        scratch_shapes=[
            pltpu.VMEM((2, 2, depth, pad, cols), BF16),
            pltpu.VMEM((2, 2 * depth, pad, cols), BF16),
            pltpu.VMEM((3 * depth, pad, cols), BF16),
            token_rows, token_rows, wide, wide, wide, flipped, flipped,
            pltpu.VMEM((tokens, DPAD), F32), pair, pair,
            pltpu.VMEM((2, 2, 2 * depth, pad, cols), BF16),
            pltpu.SemaphoreType.DMA((copies,)),
            pltpu.SemaphoreType.DMA((copies,)),
            pltpu.SemaphoreType.DMA((2,)),
        ],
        compiler_params=pltpu.CompilerParams(
            vmem_limit_bytes=61 << 20, collective_id=1, has_side_effects=True
        ),
        cost_estimate=pl.CostEstimate(
            flops=24 << 30, bytes_accessed=30 << 20, transcendentals=2 << 20
        ),
        name="ffn",
    )(normed2, cot, middle, ffn_w, down_w)


def mid_kernel(
    depth, width,
    ffn_g, down_sum, grad_n2, middle, cot, gains, out_w, q, kv, attn, lse, seg,
    dq, dkv_sum, grad_middle, gain_grad, out_grad, ffn_grad,
    mid_t, out_g, out_c, out_r, ffn_r, down_r, stage, grad_attn, q_t, g_t, q3, g3, k3, v3, k_t, dq_t,
    delta, dkv, acc_kv, bias, kv_c, kv_y, send_sems, recv_sems, local_sems,
):
    tokens = q.shape[0]
    tiles = tokens // TILE
    back = 1024 // TILE
    rows = ffn_grad.shape[1]
    out_cols = HEADS * HEAD_DIM // 4
    p = Place(depth, send_sems, recv_sems)
    p.barrier()
    ffn_sums = [
        PlaneScatter(p, ffn_g.at[w], ffn_r.at[w], stage.at[w], local_sems.at[pl.ds(3 * w, 3)])
        for w in range(2)
    ]
    for w in range(2):
        ffn_sums[w].start()
    down_in = [
        p.copy(k, down_sum.at[(p.z + k) % depth], down_r.at[k - 1]) for k in range(1, depth)
    ]

    gain = gains[1:2, :]
    gain_grad[...] = jnp.zeros_like(gain_grad)

    def norm_tile(start):
        span = pl.ds(start, TILE)
        mid, up = middle[span, :], grad_n2[span, :]
        inv = lax.rsqrt(mean_rows(mid * mid, width) + EPSILON)
        scaled = up * gain
        mean = mean_rows(scaled * mid, width)
        grad = cot[span, :].astype(F32) + inv * (scaled - mid * (inv * inv * mean))
        grad_middle[span, :] = grad
        gain_grad[...] += jnp.sum(up * mid * inv, axis=0, keepdims=True)
        mid_b = grad.astype(BF16)
        mid_t[:, span] = transposed(mid_b)
        for b in range(4):
            side = dot(mid_b, out_w[b % 2, b // 2])
            grad_attn[span, b * out_cols : (b + 1) * out_cols] = side.astype(BF16)

    row_tiles(tokens, norm_tile)
    for b in range(4):
        side = attn[:, b * out_cols : (b + 1) * out_cols]

        def out_tile(start):
            span = pl.ds(start, TILE)
            store_blocks(out_g.at[b % 2, b // 2], start, dot(mid_t[span, :], side).astype(BF16))

        row_tiles(DPAD, out_tile)
    out_cross = p.copy("c", out_g.at[1 - p.c], out_c)

    g_t[...] = transposed(grad_attn[...])
    attn_t = attn[...].astype(F32).T
    for h in range(HEADS):
        span = slice(h * HEAD_DIM, (h + 1) * HEAD_DIM)
        delta[h : h + 1, :] = jnp.sum(
            g_t[span, :].astype(F32) * attn_t[span, :], axis=0, keepdims=True
        )
        q3[h] = q[:, span]
        g3[h] = grad_attn[:, span]
    q_t[...] = transposed(q[...])
    for s in range(4):
        span = slice(s * tokens, (s + 1) * tokens)
        part = kv[s]
        k_t[:, span] = transposed(part)[: KV_HEADS * HEAD_DIM]
        for g in range(KV_HEADS):
            k3[g, span, :] = part[:, g * HEAD_DIM : (g + 1) * HEAD_DIM]
            v3[g, span, :] = part[:, (KV_HEADS + g) * HEAD_DIM : (KV_HEADS + g + 1) * HEAD_DIM]
    dq_t[...] = jnp.zeros_like(dq_t)
    dkv[...] = jnp.zeros_like(dkv)

    def key_tile(t, queries):
        keys = pl.ds(pl.multiple_of(t * TILE, TILE), TILE)
        for i in queries:
            bias[i] = mask_tile(seg[0:1, i * TILE : (i + 1) * TILE], p.m * tiles + i, t)

        def group(g, carry):
            k_g, v_g = k3[g, keys, :], v3[g, keys, :]
            kt_g = k_t[pl.ds(pl.multiple_of(g * HEAD_DIM, HEAD_DIM), HEAD_DIM), keys]
            units = [(i, g * GROUP + j) for i in queries for j in range(GROUP)]
            places = [
                (pl.ds(pl.multiple_of(h * HEAD_DIM, HEAD_DIM), HEAD_DIM), pl.ds(i * TILE, TILE))
                for i, h in units
            ]
            dk, dv = None, None
            for (i, h), (span, cols) in zip(units, places):
                scores = dot(k_g, q_t[span, cols]) * EXP_SCALE + bias[i]
                probs = jnp.exp2(scores - lse[pl.ds(h, 1), cols])
                dprobs = dot(v_g, g_t[span, cols])
                dscores = (probs * (dprobs - delta[pl.ds(h, 1), cols])).astype(BF16)
                add_v = dot(probs.astype(BF16), g3[h, cols, :])
                add_k = dot(dscores, q3[h, cols, :])
                dq_t[span, cols] += dot(kt_g, dscores)
                dk = add_k if dk is None else dk + add_k
                dv = add_v if dv is None else dv + add_v
            acc_kv[g] = dk * SCORE_SCALE
            acc_kv[KV_HEADS + g] = dv
            return carry

        lax.fori_loop(0, KV_HEADS, group, 0)
        for n in range(2 * KV_HEADS):
            dkv[keys, n * HEAD_DIM : (n + 1) * HEAD_DIM] = acc_kv[n].astype(BF16)

    def key_span(low, high, queries):
        def step(t, carry):
            key_tile(t, queries)
            return carry

        lax.fori_loop(low, high, step, 0)

    first = p.m * tiles
    key_tile(first + 1, (1,))
    ffn_sums[0].forward()
    key_span(first, first + 1, (0, 1))
    ffn_sums[1].forward()
    out_cross.wait_recv()
    own = out_g.at[p.c]
    own[...] = (own[...].astype(F32) + out_c[...].astype(F32)).astype(BF16)
    out_sum = PlaneScatter(p, own, out_r)
    out_sum.start()
    key_span(jnp.maximum(first - 2, 0), first, (0, 1))
    ffn_sums[0].over_z()
    key_span(jnp.maximum(first + 1 - back, 0), jnp.maximum(first - 2, 0), (0, 1))
    key_span(jnp.maximum(first - back, 0), jnp.maximum(first + 1 - back, 0), (0,))

    def part_of(index):
        return dkv.at[pl.ds(pl.multiple_of(index * tokens, tokens), tokens)]

    beside = p.m + 1 - 2 * p.c
    cross = [
        p.copy("c", part_of(index), kv_c.at[n])
        for n, index in enumerate((beside, (beside + 2) % 4))
    ]
    dq[...] = dq_t[...].T * SCORE_SCALE
    cross[1].wait_recv()
    away = part_of((p.m + 2) % 4)
    away[...] = (away[...].astype(F32) + kv_c[1].astype(F32)).astype(BF16)
    across = p.copy("y", away, kv_y)
    out_sum.forward()
    ffn_sums[1].over_z()
    for w in range(2):
        ffn_grad[w] = ffn_sums[w].result()[:rows]
    value = down_sum[p.z].astype(F32)
    for k, made in enumerate(down_in):
        made.wait_recv()
        value += down_r[k].astype(F32)
    ffn_grad[2] = value[:rows]
    cross[0].wait_recv()
    out_sum.over_z()
    across.wait_recv()
    dkv_sum[...] = part_of(p.m)[...].astype(F32) + kv_c[0].astype(F32) + kv_y[...].astype(F32)
    out_grad[...] = out_sum.result()[:rows]
    for part in ffn_sums + [out_sum]:
        part.finish()
    for made in cross + [across, out_cross] + down_in:
        made.wait_send()


def middle_back(ffn_g, down_sum, grad_n2, middle, cot, gains, out_w, q, kv, attn, lse, seg,
                depth, rows, width):
    tokens, query_cols = q.shape
    pad = DPAD // (2 * depth)
    cols = ffn_g.shape[-1]
    kv_cols = kv.shape[-1]
    out_cols = query_cols // 4
    whole = 4 * tokens
    slots = scatter_slots(depth)
    copies = 3 * scatter_copies(depth) + 4 + depth - 1
    heads_q = pltpu.VMEM((HEADS, tokens, HEAD_DIM), BF16)
    heads_kv = pltpu.VMEM((KV_HEADS, whole, HEAD_DIM), BF16)
    flipped = pltpu.VMEM((query_cols, tokens), BF16)
    return pl.pallas_call(
        functools.partial(mid_kernel, depth, width),
        out_shape=[
            jax.ShapeDtypeStruct((tokens, query_cols), F32),
            jax.ShapeDtypeStruct((tokens, kv_cols), F32),
            jax.ShapeDtypeStruct((tokens, DPAD), F32),
            jax.ShapeDtypeStruct((1, DPAD), F32),
            jax.ShapeDtypeStruct((rows, out_cols), F32),
            jax.ShapeDtypeStruct((3, rows, cols), F32),
        ],
        in_specs=[pl.BlockSpec(memory_space=pl.ANY)] + vmem_specs(11),
        out_specs=vmem_specs(6),
        scratch_shapes=[
            pltpu.VMEM((DPAD, tokens), BF16),
            pltpu.VMEM((2, 2, 2 * depth, pad, out_cols), BF16),
            pltpu.VMEM((2, 2 * depth, pad, out_cols), BF16),
            pltpu.VMEM((slots, pad, out_cols), BF16),
            pltpu.VMEM((2, slots, pad, cols), BF16),
            pltpu.VMEM((depth - 1, pad, cols), BF16),
            pltpu.VMEM((2, 2 * depth, pad, cols), BF16),
            pltpu.VMEM((tokens, query_cols), BF16),
            flipped, flipped, heads_q, heads_q, heads_kv, heads_kv,
            pltpu.VMEM((KV_HEADS * HEAD_DIM, whole), BF16),
            pltpu.VMEM((query_cols, tokens), F32),
            pltpu.VMEM((HEADS + 1, tokens), F32),
            pltpu.VMEM((whole, kv_cols), BF16),
            pltpu.VMEM((2 * KV_HEADS, TILE, HEAD_DIM), F32),
            pltpu.VMEM((tokens // TILE, TILE, TILE), F32),
            pltpu.VMEM((2, tokens, kv_cols), BF16),
            pltpu.VMEM((tokens, kv_cols), BF16),
            pltpu.SemaphoreType.DMA((copies,)),
            pltpu.SemaphoreType.DMA((copies,)),
            pltpu.SemaphoreType.DMA((6,)),
        ],
        compiler_params=pltpu.CompilerParams(
            vmem_limit_bytes=61 << 20, collective_id=2, has_side_effects=True
        ),
        cost_estimate=pl.CostEstimate(
            flops=40 << 30, bytes_accessed=50 << 20, transcendentals=8 << 20
        ),
        name="middle_back",
    )(ffn_g, down_sum, grad_n2, middle, cot, gains, out_w, q, kv, attn, lse, seg)


def tail_kernel(
    depth, width, in_cols,
    dq, dkv, cosine, sine, normed1, x_in, grad_middle, gains, attn_w, gain2,
    grad_hidden, in_grad, gain_sum,
    proj, proj_b, n_t, in_g, in_c, in_r, gain_own, gain_r, send_sems, recv_sems,
):
    tokens = dq.shape[0]
    rows = in_grad.shape[0]
    query_cols = dq.shape[1]
    turned = (HEADS + KV_HEADS) * HEAD_DIM
    p = Place(depth, send_sems, recv_sems)
    p.barrier()
    proj[:, :query_cols] = dq[...]
    proj[:, query_cols:] = dkv[...]

    def proj_tile(start):
        span = pl.ds(start, TILE)
        for j in range(turned // 128):
            lanes = slice(128 * j, 128 * (j + 1))
            proj[span, lanes] = rope(proj[span, lanes], cosine[span, :], -sine[span, :])
        for b in range(4):
            proj_b[b, span, :] = proj[span, b * in_cols : (b + 1) * in_cols].astype(BF16)
        n_t[:, span] = transposed(normed1[span, :])

    row_tiles(tokens, proj_tile)
    for other in (1, 0):
        for y in range(2):
            def in_tile(start):
                span = pl.ds(start, TILE)
                for c in range(2):
                    @pl.when((p.c == c) if not other else (p.c != c))
                    def _():
                        side = dot(n_t[span, :], proj_b[2 * y + c]).astype(BF16)
                        store_blocks(in_g.at[c, y], start, side)

            row_tiles(DPAD, in_tile)
        if other:
            in_cross = p.copy("c", in_g.at[1 - p.c], in_c)
    in_cross.wait_recv()
    own = in_g.at[p.c]
    own[...] = (own[...].astype(F32) + in_c[...].astype(F32)).astype(BF16)
    in_sum = PlaneScatter(p, own, in_r)
    in_sum.start()
    gain = gains[0:1, :]
    gain_own[...] = jnp.zeros_like(gain_own)
    gain_own[1:2, :] = gain2[...]

    def norm_tile(start):
        span = pl.ds(start, TILE)
        x_f = x_in[span, :].astype(F32)
        up = None
        for b in range(4):
            weight = attn_w[b % 2, b // 2].reshape(DPAD, -1)[:, :in_cols]
            term = dot_nt(proj_b[b, span, :], weight)
            up = term if up is None else up + term
        inv = lax.rsqrt(mean_rows(x_f * x_f, width) + EPSILON)
        scaled = up * gain
        mean = mean_rows(scaled * x_f, width)
        grad_hidden[span, :] = grad_middle[span, :] + inv * (scaled - x_f * (inv * inv * mean))
        gain_own[0:1, :] += jnp.sum(up * x_f * inv, axis=0, keepdims=True)

    row_tiles(tokens, norm_tile)
    in_sum.forward()
    sent = []
    for n, kind in enumerate(("c", "y", "x")):
        made = p.copy(kind, gain_own.at[pl.ds(8 * n, 8)], gain_r.at[pl.ds(8 * n, 8)])
        sent.append(made)
        made.wait_recv()
        if n == 1:
            in_sum.over_z()
        gain_own[8 * (n + 1) : 8 * (n + 2), :] = (
            gain_own[8 * n : 8 * (n + 1), :] + gain_r[8 * n : 8 * (n + 1), :]
        )
    last = gain_own.at[pl.ds(24, 8)]
    arriving = [p.copy(k, last, gain_r.at[pl.ds(24 + 8 * k, 8)]) for k in range(1, depth)]
    total = last[...]
    for k, made in enumerate(arriving):
        made.wait_recv()
        total += gain_r[32 + 8 * k : 40 + 8 * k, :]
    gain_sum[...] = total
    in_grad[...] = in_sum.result()[:rows]
    in_sum.finish()
    for made in sent + arriving + [in_cross]:
        made.wait_send()


def tail(dq, dkv, cosine, sine, normed1, x_in, grad_middle, gains, attn_w, gain2,
         depth, rows, width, in_cols):
    tokens = dq.shape[0]
    pad = DPAD // (2 * depth)
    total = dq.shape[1] + dkv.shape[1]
    slots = scatter_slots(depth)
    copies = scatter_copies(depth) + 1 + 3 + depth - 1
    return pl.pallas_call(
        functools.partial(tail_kernel, depth, width, in_cols),
        out_shape=[
            jax.ShapeDtypeStruct((tokens, DPAD), F32),
            jax.ShapeDtypeStruct((rows, in_cols), F32),
            jax.ShapeDtypeStruct((8, DPAD), F32),
        ],
        in_specs=vmem_specs(10),
        out_specs=vmem_specs(3),
        scratch_shapes=[
            pltpu.VMEM((tokens, total), F32),
            pltpu.VMEM((4, tokens, in_cols), BF16),
            pltpu.VMEM((DPAD, tokens), BF16),
            pltpu.VMEM((2, 2, 2 * depth, pad, in_cols), BF16),
            pltpu.VMEM((2, 2 * depth, pad, in_cols), BF16),
            pltpu.VMEM((slots, pad, in_cols), BF16),
            pltpu.VMEM((32, DPAD), F32),
            pltpu.VMEM((24 + 8 * depth, DPAD), F32),
            pltpu.SemaphoreType.DMA((copies,)),
            pltpu.SemaphoreType.DMA((copies,)),
        ],
        compiler_params=pltpu.CompilerParams(
            vmem_limit_bytes=60 << 20, collective_id=3, has_side_effects=True
        ),
        cost_estimate=pl.CostEstimate(
            flops=8 << 30, bytes_accessed=30 << 20, transcendentals=0
        ),
        name="tail",
    )(dq, dkv, cosine, sine, normed1, x_in, grad_middle, gains, attn_w, gain2)


def rotary_tables(position_ids):
    half_dim = HEAD_DIM // 2
    frequency = jnp.exp(
        jnp.arange(half_dim, dtype=F32) * (-2.0 * math.log(10000.0) / HEAD_DIM)
    )
    angles = position_ids.astype(F32)[:, None] * frequency[None, :]
    return jnp.cos(angles), jnp.sin(angles)


def per_device(
    hidden_in, cotangent, segments, positions, attn_in, attn_out, w_gate, w_up, w_down,
    norm1_gain, norm2_gain,
):
    tokens, width = hidden_in.shape[1:]
    dp_size = lax.axis_size("dp")
    depth = dp_size // 2
    rows = width // dp_size
    pad = DPAD // dp_size
    dp_index, m = lax.axis_index("dp"), lax.axis_index("mp")

    def padded(value):
        value = value.reshape(value.shape[0], depth, 2, rows).transpose(0, 2, 1, 3)
        return jnp.pad(value, ((0, 0), (0, 0), (0, 0), (0, pad - rows))).reshape(-1, DPAD)

    def unpadded(value):
        value = value.reshape(-1, 2, depth, pad)[..., :rows]
        return value.transpose(0, 2, 1, 3).reshape(-1, width)

    in_cols = attn_in.shape[1]
    out_cols = attn_out.shape[0]
    gains_in = jnp.pad(
        jnp.stack([norm1_gain, norm2_gain]), ((0, pad - rows - 2), (0, in_cols + out_cols - rows))
    )
    pack_a = jnp.concatenate(
        [jnp.concatenate([attn_in, attn_out.T], axis=1), gains_in], axis=0
    )
    pack_g = jnp.pad(jnp.stack([w_gate, w_up, w_down.T]), ((0, 0), (0, pad - rows), (0, 0)))
    x_in = padded(hidden_in[0])
    cot = padded(cotangent[0])
    cosine, sine = rotary_tables(positions[0])
    cos_lanes = jnp.tile(cosine, (1, 4))
    sin_lanes = jnp.tile(jnp.concatenate([-sine, sine], axis=1), (1, 2))
    seq_seg = segments[0]
    own_seg = lax.dynamic_slice_in_dim(seq_seg, m * tokens, tokens, 0)
    start = jnp.sum(seq_seg[None, :] < own_seg[:, None], axis=1, dtype=jnp.int32)[None, :]
    queries, kv_all, attn_b, lse, middle, normed1, normed2, gains, out_w, attn_w, ffn_w, down_w = front(
        pack_a, pack_g, x_in, cos_lanes, sin_lanes, start, depth, rows, width, in_cols
    )
    ffn_g, down_sum, hidden_out, grad_n2 = ffn(normed2, cot, middle, ffn_w, down_w)
    dq, dkv, grad_middle, gain2, g_out, g_ffn = middle_back(
        ffn_g, down_sum, grad_n2, middle, cot, gains, out_w, queries, kv_all, attn_b, lse, start,
        depth, rows, width,
    )
    grad_hidden, g_in, g_gains = tail(
        dq, dkv, cos_lanes, sin_lanes, normed1, x_in, grad_middle, gains, attn_w, gain2,
        depth, rows, width, in_cols,
    )
    position = (dp_index % 2) * depth + dp_index // 2
    g_gains = lax.dynamic_slice_in_dim(g_gains, position * pad, rows, 1)
    return (
        unpadded(hidden_out)[None],
        unpadded(grad_hidden)[None],
        g_in,
        g_out.T,
        g_ffn[0],
        g_ffn[1],
        g_ffn[2].T,
        g_gains[0],
        g_gains[1],
    )


def solution(mesh):
    return jax.shard_map(
        per_device,
        mesh=mesh,
        in_specs=(
            P("dp", "mp", None),
            P("dp", "mp", None),
            P("dp", None),
            P("dp", "mp"),
            P("dp", "mp"),
            P("mp", "dp"),
            P("dp", "mp"),
            P("dp", "mp"),
            P("mp", "dp"),
            P("dp"),
            P("dp"),
        ),
        out_specs=(
            P("dp", "mp", None),
            P("dp", "mp", None),
            P("dp", "mp"),
            P("mp", "dp"),
            P("dp", "mp"),
            P("dp", "mp"),
            P("mp", "dp"),
            P("dp"),
            P("dp"),
        ),
        check_vma=False,
    )
```

```python
import functools
import math

import jax
import jax.numpy as jnp
from jax import lax
from jax.experimental import pallas as pl
from jax.experimental.pallas import tpu as pltpu
from jax.sharding import PartitionSpec as P

HEADS = 15
KV_HEADS = 5
GROUP = HEADS // KV_HEADS
HEAD_DIM = 64
DPAD = 1024
TILE = 256
EPSILON = 1e-05
SCORE_SCALE = 0.125
MASK_FILL = -1e30
LOG2E = 1.4426950408889634
EXP_SCALE = SCORE_SCALE * LOG2E
GAIN_ROWS = 16
BF16 = jnp.bfloat16
F32 = jnp.float32


def dot(a, b):
    return jnp.dot(a, b, preferred_element_type=F32)


def dot_nt(a, b):
    return lax.dot_general(a, b, (((1,), (1,)), ((), ())), preferred_element_type=F32)


def vmem_specs(count):
    return [pl.BlockSpec(memory_space=pltpu.VMEM)] * count


def transposed(value):
    return value.astype(F32).T.astype(BF16)


class Place:
    def __init__(self, depth, send_sems, recv_sems):
        dp_index, m = lax.axis_index("dp"), lax.axis_index("mp")
        self.depth = depth
        self.z, self.x = dp_index // 2, dp_index % 2
        self.m, self.y, self.c = m, m // 2, m % 2
        self.send_sems, self.recv_sems = send_sems, recv_sems
        self.count = 0

    def peer(self, kind):
        z, x, y, c = self.z, self.x, self.y, self.c
        if kind == "x":
            x = 1 - x
        elif kind == "y":
            y = 1 - y
        elif kind == "c":
            c = 1 - c
        else:
            z = (z + kind) % self.depth
        return 2 * z + x, 2 * y + c

    def kinds(self):
        return ["x", "y", "c"] + list(range(1, self.depth))

    def barrier(self, kinds=None):
        semaphore = pltpu.get_barrier_semaphore()
        kinds = kinds or self.kinds()
        for kind in kinds:
            pl.semaphore_signal(
                semaphore, inc=1, device_id=self.peer(kind), device_id_type=pl.DeviceIdType.MESH
            )
        pl.semaphore_wait(semaphore, len(kinds))

    def copy(self, kind, source, target=None):
        index = self.count
        self.count += 1
        made = pltpu.make_async_remote_copy(
            src_ref=source,
            dst_ref=source if target is None else target,
            send_sem=self.send_sems.at[index],
            recv_sem=self.recv_sems.at[index],
            device_id=self.peer(kind),
            device_id_type=pl.DeviceIdType.MESH,
        )
        made.start()
        return made


class PlaneGather:
    def __init__(self, place, source, buffer, by_x, part=lambda ref: ref):
        self.place, self.source, self.buffer, self.part = place, source, buffer, part
        self.split = place.depth - by_x
        self.sent, self.last = [], []

    def over_z(self, slot=None):
        p = self.place
        slot = self.part(self.buffer.at[p.y, p.x, p.z]) if slot is None else slot
        source = self.part(self.source)
        self.arriving = [p.copy(k, source, slot) for k in range(1, p.depth)]
        self.sent += self.arriving

    def stacked(self):
        for made in self.arriving:
            made.wait_recv()

    def over_x(self):
        p = self.place
        self.by_x = p.copy("x", self.part(self.buffer.at[p.y, p.x]))
        self.sent.append(self.by_x)

    def over_y(self):
        p = self.place
        self.by_y = p.copy("y", self.part(self.buffer.at[p.y, p.x]))
        self.sent.append(self.by_y)

    def diagonal_x(self):
        p = self.place
        self.by_y.wait_recv()
        span = pl.ds(self.split, p.depth - self.split)
        self.last.append(p.copy("x", self.part(self.buffer.at[1 - p.y, p.x, span])))

    def diagonal_y(self):
        p = self.place
        self.by_x.wait_recv()
        if self.split:
            span = pl.ds(0, self.split)
            self.last.append(p.copy("y", self.part(self.buffer.at[p.y, 1 - p.x, span])))

    def arrived(self):
        for made in self.last:
            made.wait_recv()

    def finish(self):
        for made in self.sent + self.last:
            made.wait_send()


def rope(value, cosine, sine):
    lane = lax.broadcasted_iota(jnp.int32, value.shape, 1)
    half = HEAD_DIM // 2
    partner = jnp.where(
        lane % HEAD_DIM < half, pltpu.roll(value, 128 - half, 1), pltpu.roll(value, half, 1)
    )
    return value * cosine + partner * sine


def natural(block, depth):
    return 2 * (block % depth) + block // depth


def widen(source, depth, rows, pad):
    filler = jnp.zeros((pad - rows, source.shape[1]), F32)
    parts = []
    for b in range(2 * depth):
        first = natural(b, depth) * rows
        parts += [source[first : first + rows, :].astype(F32), filler]
    return jnp.concatenate(parts, axis=0).T


def narrow(target, value, depth, rows, pad):
    flipped = value.T
    for b in range(2 * depth):
        first = natural(b, depth) * rows
        target[first : first + rows, :] = flipped[b * pad : b * pad + rows, :].astype(target.dtype)


def side_by_side(ref, first, size):
    _, depth, _, pad = ref.shape
    span = pl.ds(first, size)
    return jnp.concatenate(
        [ref[b // depth, b % depth, span, :] for b in range(2 * depth)], axis=1
    )


def lane_tables(table):
    return jnp.concatenate([table] * (256 // HEAD_DIM), axis=0).T


def signed(table, back):
    lane = lax.broadcasted_iota(jnp.int32, table.shape, 1) % HEAD_DIM
    first = lane < HEAD_DIM // 2
    return jnp.where(first, table, -table) if back else jnp.where(first, -table, table)


def mean_rows(value, width):
    return jnp.sum(value, axis=-1, keepdims=True) * (1.0 / width)


def mask_tile(start, query_tile, key_tile):
    key = key_tile * TILE + lax.broadcasted_iota(jnp.int32, (TILE, TILE), 0)
    query = query_tile * TILE + lax.broadcasted_iota(jnp.int32, (TILE, TILE), 1)
    return jnp.where((key >= start) & (key <= query), 0.0, MASK_FILL)


def front_kernel(
    depth, rows, width, in_cols,
    pack_a, pack_g, x_t, cosine_t, sine_t, segments,
    q, kv, attn, lse, middle, normed2, gains, seg, out_w, in_w, ffn_w, down_w,
    a_buf, x_in, cosine, sine, normed1, proj, q_t, k3, v_t, acc, peak, total, bias,
    send_sems, recv_sems, local_sems,
):
    tokens = x_in.shape[0]
    tiles = tokens // TILE
    back = 1024 // TILE
    pad = DPAD // (2 * depth)
    lead = in_cols + GAIN_ROWS
    query_cols = HEADS * HEAD_DIM
    out_cols = query_cols // 4
    p = Place(depth, send_sems, recv_sems)
    a_buf[p.c, p.y, p.x, p.z] = pack_a[...]
    own = [
        pltpu.make_async_copy(pack_g.at[w], ffn_w.at[w, p.y, p.x, p.z], local_sems.at[w])
        for w in range(2)
    ]
    own.append(pltpu.make_async_copy(pack_g.at[2], down_w.at[p.z], local_sems.at[2]))
    for made in own:
        made.start()
    p.barrier()
    first_part = lambda ref: ref.at[..., pl.ds(0, lead), :]
    last_part = lambda ref: ref.at[..., pl.ds(lead, out_cols), :]
    plane = PlaneGather(p, pack_a, a_buf.at[p.c], depth // 2, first_part)
    output = PlaneGather(p, pack_a, a_buf.at[p.c], depth // 2, last_part)
    gate, up = [
        PlaneGather(p, pack_g.at[w], ffn_w.at[w], n) for w, n in ((0, depth), (1, depth // 2))
    ]
    down = PlaneGather(p, pack_g.at[2], None, 0)
    plane.over_z()
    x_f = widen(x_t, depth, rows, pad)
    x_in[...] = x_f.astype(BF16)
    cosine[...] = lane_tables(cosine_t[...])
    sine[...] = signed(lane_tables(sine_t[...]), False)
    inv_one = lax.rsqrt(mean_rows(x_f * x_f, width) + EPSILON)
    own_seg = segments[:, pl.ds(pl.multiple_of(p.m * tokens, tokens), tokens)]
    start = jnp.zeros_like(own_seg)
    for n in range(3):
        count = jnp.sum((segments[...] == n).astype(jnp.int32), axis=1, keepdims=True)
        start += jnp.where(own_seg > n, count, 0)
    seg[...] = start
    plane.stacked()
    plane.over_x()
    plane.over_y()
    output.over_z()
    gate.over_z()
    plane.diagonal_y()
    plane.diagonal_x()
    for made in own:
        made.wait()
    up.over_z()
    plane.arrived()
    cross = p.copy("c", first_part(a_buf.at[p.c]))
    output.stacked()
    output.over_x()
    output.over_y()
    gate.stacked()
    gate.over_x()
    cross.wait()
    for b in range(2 * depth):
        gains[:, b * pad : (b + 1) * pad] = a_buf[
            0, 0, b // depth, b % depth, pl.ds(in_cols, 2), :
        ].astype(F32)
    normed1[...] = (x_f * inv_one * gains[0:1, :]).astype(BF16)
    for b in range(4):
        in_w[b % 2, b // 2] = side_by_side(a_buf.at[b % 2, b // 2], 0, in_cols)

    def project(r, carry):
        span = pl.ds(pl.multiple_of(r * TILE, TILE), TILE)
        for b in range(4):
            proj[span, b * in_cols : (b + 1) * in_cols] = dot_nt(
                normed1[span, :], in_w[b % 2, b // 2]
            )
        for j in range((HEADS + KV_HEADS) * HEAD_DIM // 128):
            lanes = slice(128 * j, 128 * (j + 1))
            proj[span, lanes] = rope(proj[span, lanes], cosine[span, :], sine[span, :])
        return carry

    lax.fori_loop(0, tiles, project, 0)
    q[...] = proj[:, :query_cols].astype(BF16)
    kv[p.m] = proj[:, query_cols : query_cols + 2 * KV_HEADS * HEAD_DIM].astype(BF16)
    mine = kv.at[p.m]
    kv_y, kv_c = p.copy("y", mine), p.copy("c", mine)
    down.over_z(down_w.at[p.z])
    up.stacked()
    up.over_x()
    q_t[...] = proj[:, :query_cols].T.astype(BF16)
    acc[...] = jnp.zeros_like(acc)
    peak[...] = jnp.full_like(peak, MASK_FILL)
    total[...] = jnp.zeros_like(total)

    def spread(block):
        span = pl.ds(pl.multiple_of(block * tokens, tokens), tokens)
        k3_parts = kv[block]
        v_t[:, span] = transposed(k3_parts)[KV_HEADS * HEAD_DIM :]
        for g in range(KV_HEADS):
            k3[g, span, :] = k3_parts[:, g * HEAD_DIM : (g + 1) * HEAD_DIM]

    def attend_tile(i, t):
        cols = pl.ds(i * TILE, TILE)
        bias[...] = mask_tile(seg[0:1, cols], p.m * tiles + i, t)
        keys = pl.ds(pl.multiple_of(t * TILE, TILE), TILE)

        def group(g, carry):
            k_g = k3[g, keys, :]
            v_g = v_t[pl.ds(pl.multiple_of(g * HEAD_DIM, HEAD_DIM), HEAD_DIM), keys]
            heads = [g * GROUP + j for j in range(GROUP)]
            places = [pl.ds(pl.multiple_of(h * HEAD_DIM, HEAD_DIM), HEAD_DIM) for h in heads]
            old = [peak[pl.ds(h, 1), cols] for h in heads]
            sums = [total[pl.ds(h, 1), cols] for h in heads]
            accs = [acc[s, cols] for s in places]
            scores = [dot(k_g, q_t[s, cols]) + bias[...] for s in places]
            new = [jnp.maximum(o, jnp.max(s, axis=0, keepdims=True)) for o, s in zip(old, scores)]
            probs = [jnp.exp2(s * EXP_SCALE - n * EXP_SCALE) for s, n in zip(scores, new)]
            scale = [jnp.exp2((o - n) * EXP_SCALE) for o, n in zip(old, new)]
            outs = [dot(v_g, b.astype(BF16)) for b in probs]
            for j, h in enumerate(heads):
                peak[pl.ds(h, 1), cols] = new[j]
                total[pl.ds(h, 1), cols] = sums[j] * scale[j] + jnp.sum(
                    probs[j], axis=0, keepdims=True
                )
                acc[places[j], cols] = accs[j] * scale[j] + outs[j]
            return carry

        lax.fori_loop(0, KV_HEADS, group, 0)

    def attend_span(i, low, high):
        def step(t, carry):
            attend_tile(i, t)
            return carry

        lax.fori_loop(low, high, step, 0)

    spread(p.m)
    first_tile = p.m * tiles
    for i in range(tiles):
        attend_span(i, first_tile, first_tile + i + 1)
        if i == 0:
            output.diagonal_x()
            output.diagonal_y()
    kv_y.wait_recv()
    kv_cy = p.copy("c", kv.at[(p.m + 2) % 4])
    gate.over_y()
    up.over_y()
    kv_c.wait_recv()
    spread((p.m + 1 - 2 * p.c) % 4)
    kv_cy.wait_recv()
    for k in (2, 3):
        spread((p.m + (k if k == 2 else 3 - 2 * p.c)) % 4)
    for i in range(tiles):
        attend_span(i, jnp.maximum(first_tile + i - back, 0), first_tile)
        if i == 0:
            output.arrived()
            out_cross = p.copy("c", last_part(a_buf.at[p.c]))
            gate.diagonal_x()
            gate.diagonal_y()
    up.diagonal_y()
    for h in range(HEADS):
        span = pl.ds(h * HEAD_DIM, HEAD_DIM)
        acc[span, :] = acc[span, :] / total[h : h + 1, :]
    attn[...] = acc[...].T.astype(BF16)
    lse[...] = peak[...] * EXP_SCALE + jnp.log2(jnp.maximum(total[...], 1e-37))
    out_cross.wait()
    for b in range(4):
        out_w[b % 2, b // 2] = side_by_side(a_buf.at[b % 2, b // 2], lead, out_cols)

    def project_out(r, carry):
        span = pl.ds(pl.multiple_of(r * TILE, TILE), TILE)
        mid = x_in[span, :].astype(F32)
        for b in range(4):
            mid += dot(attn[span, b * out_cols : (b + 1) * out_cols], out_w[b % 2, b // 2])
        middle[span, :] = mid
        inv = lax.rsqrt(mean_rows(mid * mid, width) + EPSILON)
        normed2[span, :] = (mid * inv * gains[1:2, :]).astype(BF16)
        return carry

    lax.fori_loop(0, tiles, project_out, 0)
    up.diagonal_x()
    gate.arrived()
    up.arrived()
    down.stacked()
    for part in (plane, output, gate, up, down):
        part.finish()
    for made in (kv_y, kv_c, kv_cy):
        made.wait_send()


def front(pack_a, pack_g, x_t, cosine_t, sine_t, segments, depth, rows, width, in_cols):
    tokens = x_t.shape[1]
    pad = DPAD // (2 * depth)
    a_rows, cols = pack_a.shape[0], pack_g.shape[2]
    query_cols, kv_cols = HEADS * HEAD_DIM, 2 * KV_HEADS * HEAD_DIM
    whole = 4 * tokens
    copies = 5 * (depth - 1) + 4 * 4 + 5
    anywhere = pl.BlockSpec(memory_space=pl.ANY)
    return pl.pallas_call(
        functools.partial(front_kernel, depth, rows, width, in_cols),
        out_shape=[
            jax.ShapeDtypeStruct((tokens, query_cols), BF16),
            jax.ShapeDtypeStruct((4, tokens, kv_cols), BF16),
            jax.ShapeDtypeStruct((tokens, query_cols), BF16),
            jax.ShapeDtypeStruct((HEADS + 1, tokens), F32),
            jax.ShapeDtypeStruct((tokens, DPAD), F32),
            jax.ShapeDtypeStruct((tokens, DPAD), BF16),
            jax.ShapeDtypeStruct((2, DPAD), F32),
            jax.ShapeDtypeStruct((1, tokens), jnp.int32),
            jax.ShapeDtypeStruct((2, 2, query_cols // 4, DPAD), BF16),
            jax.ShapeDtypeStruct((2, 2, in_cols, DPAD), BF16),
            jax.ShapeDtypeStruct((2, 2, 2, depth, pad, cols), BF16),
            jax.ShapeDtypeStruct((depth, pad, cols), BF16),
        ],
        in_specs=vmem_specs(1) + [anywhere] + vmem_specs(4),
        out_specs=vmem_specs(10) + [anywhere] * 2,
        scratch_shapes=[
            pltpu.VMEM((2, 2, 2, depth, a_rows, pad), BF16),
            pltpu.VMEM((tokens, DPAD), BF16),
            pltpu.VMEM((tokens, 128), F32),
            pltpu.VMEM((tokens, 128), F32),
            pltpu.VMEM((tokens, DPAD), BF16),
            pltpu.VMEM((tokens, query_cols + kv_cols), F32),
            pltpu.VMEM((query_cols, tokens), BF16),
            pltpu.VMEM((KV_HEADS, whole, HEAD_DIM), BF16),
            pltpu.VMEM((KV_HEADS * HEAD_DIM, whole), BF16),
            pltpu.VMEM((query_cols, tokens), F32),
            pltpu.VMEM((HEADS + 1, tokens), F32),
            pltpu.VMEM((HEADS + 1, tokens), F32),
            pltpu.VMEM((TILE, TILE), F32),
            pltpu.SemaphoreType.DMA((copies,)),
            pltpu.SemaphoreType.DMA((copies,)),
            pltpu.SemaphoreType.DMA((3,)),
        ],
        compiler_params=pltpu.CompilerParams(
            vmem_limit_bytes=58 << 20, collective_id=0, has_side_effects=True
        ),
        cost_estimate=pl.CostEstimate(
            flops=20 << 30, bytes_accessed=40 << 20, transcendentals=8 << 20
        ),
        name="front",
    )(pack_a, pack_g, x_t, cosine_t, sine_t, segments)


class PlaneScatter:
    def __init__(self, place, source, recv, stage=None, local_sems=None):
        self.place, self.source, self.recv = place, source, recv
        p, half = place, place.depth // 2
        self.half = half
        places = [(p.y, 1 - p.x, 0, half), (1 - p.y, p.x, half, half), (p.y, p.x, 0, p.depth)]
        views = [
            source.at[y, pl.ds(x * p.depth + first, size)] for y, x, first, size in places
        ]
        self.loads = []
        if stage is None:
            self.by_x, self.by_y, self.total = views
        else:
            self.by_x, self.by_y = stage.at[pl.ds(0, half)], stage.at[pl.ds(half, half)]
            self.total = stage.at[pl.ds(p.depth, p.depth)]
            for n, (view, kept) in enumerate(zip(views, (self.by_x, self.by_y, self.total))):
                self.loads.append(pltpu.make_async_copy(view, kept, local_sems.at[n]))

    def slot(self, n):
        return self.recv.at[pl.ds(n * self.half, self.half)]

    def start(self):
        p, half = self.place, self.half
        for load in self.loads:
            load.start()
        far, here, there = (1 - p.x) * p.depth, p.x * p.depth, 1 - p.y
        self.far_y = p.copy("y", self.source.at[there, pl.ds(far, half)], self.slot(0))
        self.far_x = p.copy("x", self.source.at[there, pl.ds(far + half, half)], self.slot(1))
        self.near_y = p.copy("y", self.source.at[there, pl.ds(here, half)], self.slot(2))
        self.near_x = p.copy("x", self.source.at[p.y, pl.ds(far + half, half)], self.slot(3))
        self.sent = [self.far_y, self.far_x, self.near_y, self.near_x]

    def forward(self):
        p = self.place
        for load in self.loads:
            load.wait()
        self.far_y.wait_recv()
        self.by_x[...] = (self.by_x[...].astype(F32) + self.slot(0)[...].astype(F32)).astype(BF16)
        self.last_x = p.copy("x", self.by_x, self.slot(4))
        self.far_x.wait_recv()
        self.by_y[...] = (self.by_y[...].astype(F32) + self.slot(1)[...].astype(F32)).astype(BF16)
        self.last_y = p.copy("y", self.by_y, self.slot(5))
        self.sent += [self.last_x, self.last_y]

    def add(self):
        half = self.half
        for made in (self.near_y, self.near_x, self.last_x, self.last_y):
            made.wait_recv()
        for first, slots in ((0, (2, 4)), (half, (3, 5))):
            span = self.total.at[pl.ds(first, half)]
            terms = [self.slot(n)[...].astype(F32) for n in slots]
            span[...] = (span[...].astype(F32) + terms[0] + terms[1]).astype(BF16)

    def over_z(self):
        p, half = self.place, self.half
        self.add()
        self.arriving = [
            p.copy(
                k, self.total.at[(p.z + k) % p.depth], self.recv.at[6 * half + k - 1]
            )
            for k in range(1, p.depth)
        ]
        self.sent += self.arriving

    def result(self):
        value = self.total[self.place.z].astype(F32)
        for k, made in enumerate(self.arriving):
            made.wait_recv()
            value += self.recv[6 * self.half + k].astype(F32)
        return value

    def finish(self):
        for made in self.sent:
            made.wait_send()


def block_shape(size, pad):
    return (size, pad) if pad % 128 == 0 else (pad, size)


def spread_blocks(target, value, pad):
    if pad % 128 == 0:
        for n in range(DPAD // pad):
            target[n] = value[:, n * pad : (n + 1) * pad].astype(BF16)
    else:
        flipped = value.T.astype(BF16)
        for n in range(DPAD // pad):
            target[n] = flipped[n * pad : (n + 1) * pad]


def one_block(value, rows, pad):
    return (value if pad % 128 == 0 else value.T)[:, :rows]


def scatter_slots(depth):
    return 3 * depth + depth - 1


def scatter_copies(depth):
    return 6 + depth - 1


def store_blocks(ref, start, value):
    pad = ref.shape[1]
    for k in range(TILE // pad):
        ref[start // pad + k] = value[k * pad : (k + 1) * pad]


def row_tiles(count, body):
    def step(r, carry):
        body(pl.multiple_of(r * TILE, TILE))
        return carry

    lax.fori_loop(0, count // TILE, step, 0)


def ffn_kernel(
    depth, rows, normed2, cot_t, middle, ffn_w, down_w, grads, down_sum, hidden_out, grad_n2, cot,
    down_buf, down_g, down_r, n_other, c_other, hid, d_gate, d_up, n_t, c_t, ffn_own, parts,
    received, packed, send_sems, recv_sems, local_sems,
):
    tokens = normed2.shape[0]
    cols = ffn_w.shape[-1]
    p = Place(depth, send_sems, recv_sems)
    pad = DPAD // (2 * depth)
    down_buf[p.y, p.x] = down_w[...]
    p.barrier(["c", "x", "y"])
    n_copy = p.copy("c", normed2, n_other)
    down = PlaneGather(p, None, down_buf, depth // 2)
    down.over_x()
    down.over_y()
    cot[...] = widen(cot_t, depth, rows, pad).astype(BF16)
    c_copy = p.copy("c", cot, c_other)

    def sides(s):
        return (n_other, c_other) if s else (normed2, cot)

    for s in range(2):
        if s:
            n_copy.wait_recv()
            c_copy.wait_recv()
        n_from, c_from = sides(s)
        both = slice(s * tokens, (s + 1) * tokens)
        n_t[:, both] = transposed(n_from[...])
        c_t[:, both] = transposed(c_from[...])
        for y in range(2):
            lanes = slice(y * cols, (y + 1) * cols)
            w_gate, w_up = [ffn_w[w, y].reshape(DPAD, cols) for w in range(2)]

            def tile(start):
                span = pl.ds(s * tokens + start, TILE)
                n_rows = n_from[pl.ds(start, TILE), :]
                gate, upper = dot(n_rows, w_gate), dot(n_rows, w_up)
                sigma = jax.nn.sigmoid(gate)
                silu = gate * sigma
                hid[span, lanes] = (silu * upper).astype(BF16)
                d_gate[span, lanes] = (upper * sigma * (1.0 + gate * (1.0 - sigma))).astype(BF16)
                d_up[span, lanes] = silu.astype(BF16)

            row_tiles(tokens, tile)
    down.diagonal_y()
    down.diagonal_x()

    def weight_grad(left, right, y, target):
        lanes = slice(y * cols, (y + 1) * cols)

        def tile(start):
            side = dot(left[pl.ds(start, TILE), :], right[:, lanes])
            store_blocks(target, start, side.astype(BF16))

        row_tiles(DPAD, tile)

    for y in range(2):
        weight_grad(c_t, hid, y, down_g.at[y])
    down.arrived()
    total = PlaneScatter(p, down_g, down_r)
    total.start()

    for s in (1, 0):
        n_from, c_from = sides(s)
        both = slice(s * tokens, (s + 1) * tokens)
        part, back = None, None
        for y in range(2):
            lanes = slice(y * cols, (y + 1) * cols)
            w_gate, w_up = [ffn_w[w, y].reshape(DPAD, cols) for w in range(2)]
            w_down = down_buf[y].reshape(DPAD, cols)
            grad_hid = dot(c_from[...], w_down)
            gate_act = (grad_hid * d_gate[both, lanes].astype(F32)).astype(BF16)
            up_act = (grad_hid * d_up[both, lanes].astype(F32)).astype(BF16)
            d_gate[both, lanes] = gate_act
            d_up[both, lanes] = up_act
            out = dot_nt(hid[both, lanes], w_down)
            grad = dot_nt(gate_act, w_gate) + dot_nt(up_act, w_up)
            part = out if part is None else part + out
            back = grad if back is None else back + grad
        if s:
            parts[0] = part.astype(BF16)
            parts[1] = back.astype(BF16)
            shared = [p.copy("c", parts.at[n], received.at[n]) for n in range(2)]
        else:
            ffn_own[...] = part + middle[...]
            grad_n2[...] = back
    total.forward()
    saved = []
    for w, right in ((0, d_gate), (1, d_up)):
        for y in range(2):
            weight_grad(n_t, right, y, packed.at[w, y])
        made = pltpu.make_async_copy(packed.at[w], grads.at[w], local_sems.at[w])
        made.start()
        saved.append(made)
    for made in shared:
        made.wait_recv()

    narrow(hidden_out, ffn_own[...] + received[0].astype(F32), depth, rows, pad)
    grad_n2[...] += received[1].astype(F32)
    total.add()
    down_sum[...] = total.total[...]
    total.finish()
    down.finish()
    for made in shared + [n_copy, c_copy]:
        made.wait_send()
    for made in saved:
        made.wait()


def ffn(normed2, cot_t, middle, ffn_w, down_w, rows):
    width, tokens = cot_t.shape
    depth, pad, cols = down_w.shape
    token_rows = pltpu.VMEM((tokens, DPAD), BF16)
    wide = pltpu.VMEM((2 * tokens, 2 * cols), BF16)
    flipped = pltpu.VMEM((DPAD, 2 * tokens), BF16)
    pair = pltpu.VMEM((2, tokens, DPAD), BF16)
    copies = 4 + 4 + 6
    return pl.pallas_call(
        functools.partial(ffn_kernel, depth, rows),
        out_shape=[
            jax.ShapeDtypeStruct((2, 2, 2 * depth, pad, cols), BF16),
            jax.ShapeDtypeStruct((depth, pad, cols), BF16),
            jax.ShapeDtypeStruct((width, tokens), BF16),
            jax.ShapeDtypeStruct((tokens, DPAD), F32),
            jax.ShapeDtypeStruct((tokens, DPAD), BF16),
        ],
        in_specs=vmem_specs(5),
        out_specs=[pl.BlockSpec(memory_space=pl.ANY)] + vmem_specs(4),
        scratch_shapes=[
            pltpu.VMEM((2, 2, depth, pad, cols), BF16),
            pltpu.VMEM((2, 2 * depth, pad, cols), BF16),
            pltpu.VMEM((3 * depth, pad, cols), BF16),
            token_rows, token_rows, wide, wide, wide, flipped, flipped,
            pltpu.VMEM((tokens, DPAD), F32), pair, pair,
            pltpu.VMEM((2, 2, 2 * depth, pad, cols), BF16),
            pltpu.SemaphoreType.DMA((copies,)),
            pltpu.SemaphoreType.DMA((copies,)),
            pltpu.SemaphoreType.DMA((2,)),
        ],
        compiler_params=pltpu.CompilerParams(
            vmem_limit_bytes=61 << 20, collective_id=1, has_side_effects=True
        ),
        cost_estimate=pl.CostEstimate(
            flops=24 << 30, bytes_accessed=30 << 20, transcendentals=2 << 20
        ),
        name="ffn",
    )(normed2, cot_t, middle, ffn_w, down_w)


def mid_kernel(
    depth, width,
    ffn_g, down_sum, grad_n2, middle, cot, gains, out_w, q, kv, attn, lse, seg,
    dq_t, dkv_sum, grad_middle, gain_grad, out_grad, ffn_grad,
    mid_b, out_g, out_c, out_r, ffn_r, down_r, stage, grad_attn, q_t, g_t, q3, g3, k3, v3, k_t,
    delta, dkv, acc_kv, bias, kv_c, kv_y, send_sems, recv_sems, local_sems,
):
    tokens = q.shape[0]
    tiles = tokens // TILE
    back = 1024 // TILE
    rows = ffn_grad.shape[1]
    pad = DPAD // (2 * depth)
    out_cols = HEADS * HEAD_DIM // 4
    p = Place(depth, send_sems, recv_sems)
    p.barrier()
    ffn_sums = [
        PlaneScatter(p, ffn_g.at[w], ffn_r.at[w], stage.at[w], local_sems.at[pl.ds(3 * w, 3)])
        for w in range(2)
    ]
    for w in range(2):
        ffn_sums[w].start()
    down_in = [
        p.copy(k, down_sum.at[(p.z + k) % depth], down_r.at[k - 1]) for k in range(1, depth)
    ]

    gain = gains[1:2, :]
    gain_grad[...] = jnp.zeros_like(gain_grad)

    def norm_tile(start):
        span = pl.ds(start, TILE)
        mid, up = middle[span, :], grad_n2[span, :]
        inv = lax.rsqrt(mean_rows(mid * mid, width) + EPSILON)
        scaled = up * gain
        mean = mean_rows(scaled * mid, width)
        grad = cot[span, :].astype(F32) + inv * (scaled - mid * (inv * inv * mean))
        grad_middle[span, :] = grad
        gain_grad[...] += jnp.sum(up * mid * inv, axis=0, keepdims=True)
        mid_b[span, :] = grad.astype(BF16)
        for b in range(4):
            side = dot_nt(mid_b[span, :], out_w[b % 2, b // 2])
            grad_attn[span, b * out_cols : (b + 1) * out_cols] = side.astype(BF16)

    row_tiles(tokens, norm_tile)
    attn_t = attn[...].astype(F32).T
    for b in range(4):
        left = attn_t[b * out_cols : (b + 1) * out_cols, :].astype(BF16)
        spread_blocks(out_g.at[b % 2, b // 2], dot(left, mid_b[...]), pad)
    out_cross = p.copy("c", out_g.at[1 - p.c], out_c)

    g_t[...] = transposed(grad_attn[...])
    for h in range(HEADS):
        span = slice(h * HEAD_DIM, (h + 1) * HEAD_DIM)
        delta[h : h + 1, :] = jnp.sum(
            g_t[span, :].astype(F32) * attn_t[span, :], axis=0, keepdims=True
        )
        q3[h] = q[:, span]
        g3[h] = grad_attn[:, span]
    q_t[...] = transposed(q[...])
    for s in range(4):
        span = slice(s * tokens, (s + 1) * tokens)
        part = kv[s]
        k_t[:, span] = transposed(part)[: KV_HEADS * HEAD_DIM]
        for g in range(KV_HEADS):
            k3[g, span, :] = part[:, g * HEAD_DIM : (g + 1) * HEAD_DIM]
            v3[g, span, :] = part[:, (KV_HEADS + g) * HEAD_DIM : (KV_HEADS + g + 1) * HEAD_DIM]
    dq_t[...] = jnp.zeros_like(dq_t)
    dkv[...] = jnp.zeros_like(dkv)

    def key_tile(t, queries):
        keys = pl.ds(pl.multiple_of(t * TILE, TILE), TILE)
        for i in queries:
            bias[i] = mask_tile(seg[0:1, i * TILE : (i + 1) * TILE], p.m * tiles + i, t)

        def group(g, carry):
            k_g, v_g = k3[g, keys, :], v3[g, keys, :]
            kt_g = k_t[pl.ds(pl.multiple_of(g * HEAD_DIM, HEAD_DIM), HEAD_DIM), keys]
            units = [(i, g * GROUP + j) for i in queries for j in range(GROUP)]
            places = [
                (pl.ds(pl.multiple_of(h * HEAD_DIM, HEAD_DIM), HEAD_DIM), pl.ds(i * TILE, TILE))
                for i, h in units
            ]
            dk, dv = None, None
            for (i, h), (span, cols) in zip(units, places):
                scores = dot(k_g, q_t[span, cols]) * EXP_SCALE + bias[i]
                probs = jnp.exp2(scores - lse[pl.ds(h, 1), cols])
                dprobs = dot(v_g, g_t[span, cols])
                dscores = (probs * (dprobs - delta[pl.ds(h, 1), cols])).astype(BF16)
                add_v = dot(probs.astype(BF16), g3[h, cols, :])
                add_k = dot(dscores, q3[h, cols, :])
                dq_t[span, cols] += dot(kt_g, dscores)
                dk = add_k if dk is None else dk + add_k
                dv = add_v if dv is None else dv + add_v
            acc_kv[g] = dk * SCORE_SCALE
            acc_kv[KV_HEADS + g] = dv
            return carry

        lax.fori_loop(0, KV_HEADS, group, 0)
        for n in range(2 * KV_HEADS):
            dkv[keys, n * HEAD_DIM : (n + 1) * HEAD_DIM] = acc_kv[n].astype(BF16)

    def key_span(low, high, queries):
        def step(t, carry):
            key_tile(t, queries)
            return carry

        lax.fori_loop(low, high, step, 0)

    first = p.m * tiles
    key_tile(first + 1, (1,))
    ffn_sums[0].forward()
    key_span(first, first + 1, (0, 1))
    ffn_sums[1].forward()
    out_cross.wait_recv()
    own = out_g.at[p.c]
    own[...] = (own[...].astype(F32) + out_c[...].astype(F32)).astype(BF16)
    out_sum = PlaneScatter(p, own, out_r)
    out_sum.start()
    key_span(jnp.maximum(first - 2, 0), first, (0, 1))
    ffn_sums[0].over_z()
    key_span(jnp.maximum(first + 1 - back, 0), jnp.maximum(first - 2, 0), (0, 1))
    key_span(jnp.maximum(first - back, 0), jnp.maximum(first + 1 - back, 0), (0,))

    def part_of(index):
        return dkv.at[pl.ds(pl.multiple_of(index * tokens, tokens), tokens)]

    beside = p.m + 1 - 2 * p.c
    cross = [
        p.copy("c", part_of(index), kv_c.at[n])
        for n, index in enumerate((beside, (beside + 2) % 4))
    ]
    cross[1].wait_recv()
    away = part_of((p.m + 2) % 4)
    away[...] = (away[...].astype(F32) + kv_c[1].astype(F32)).astype(BF16)
    across = p.copy("y", away, kv_y)
    out_sum.forward()
    ffn_sums[1].over_z()
    for w in range(2):
        ffn_grad[w] = ffn_sums[w].result()[:rows]
    value = down_sum[p.z].astype(F32)
    for k, made in enumerate(down_in):
        made.wait_recv()
        value += down_r[k].astype(F32)
    ffn_grad[2] = value[:rows]
    cross[0].wait_recv()
    out_sum.over_z()
    across.wait_recv()
    dkv_sum[...] = part_of(p.m)[...].astype(F32) + kv_c[0].astype(F32) + kv_y[...].astype(F32)
    out_grad[...] = one_block(out_sum.result(), rows, pad)
    for part in ffn_sums + [out_sum]:
        part.finish()
    for made in cross + [across, out_cross] + down_in:
        made.wait_send()


def middle_back(ffn_g, down_sum, grad_n2, middle, cot, gains, out_w, q, kv, attn, lse, seg,
                depth, rows, width):
    tokens, query_cols = q.shape
    pad = DPAD // (2 * depth)
    cols = ffn_g.shape[-1]
    kv_cols = kv.shape[-1]
    out_cols = query_cols // 4
    whole = 4 * tokens
    slots = scatter_slots(depth)
    copies = 3 * scatter_copies(depth) + 4 + depth - 1
    heads_q = pltpu.VMEM((HEADS, tokens, HEAD_DIM), BF16)
    heads_kv = pltpu.VMEM((KV_HEADS, whole, HEAD_DIM), BF16)
    flipped = pltpu.VMEM((query_cols, tokens), BF16)
    return pl.pallas_call(
        functools.partial(mid_kernel, depth, width),
        out_shape=[
            jax.ShapeDtypeStruct((query_cols, tokens), F32),
            jax.ShapeDtypeStruct((tokens, kv_cols), F32),
            jax.ShapeDtypeStruct((tokens, DPAD), F32),
            jax.ShapeDtypeStruct((1, DPAD), F32),
            jax.ShapeDtypeStruct((out_cols, rows), F32),
            jax.ShapeDtypeStruct((3, rows, cols), F32),
        ],
        in_specs=[pl.BlockSpec(memory_space=pl.ANY)] + vmem_specs(11),
        out_specs=vmem_specs(6),
        scratch_shapes=[
            pltpu.VMEM((tokens, DPAD), BF16),
            pltpu.VMEM((2, 2, 2 * depth, *block_shape(out_cols, pad)), BF16),
            pltpu.VMEM((2, 2 * depth, *block_shape(out_cols, pad)), BF16),
            pltpu.VMEM((slots, *block_shape(out_cols, pad)), BF16),
            pltpu.VMEM((2, slots, pad, cols), BF16),
            pltpu.VMEM((depth - 1, pad, cols), BF16),
            pltpu.VMEM((2, 2 * depth, pad, cols), BF16),
            pltpu.VMEM((tokens, query_cols), BF16),
            flipped, flipped, heads_q, heads_q, heads_kv, heads_kv,
            pltpu.VMEM((KV_HEADS * HEAD_DIM, whole), BF16),
            pltpu.VMEM((HEADS + 1, tokens), F32),
            pltpu.VMEM((whole, kv_cols), BF16),
            pltpu.VMEM((2 * KV_HEADS, TILE, HEAD_DIM), F32),
            pltpu.VMEM((tokens // TILE, TILE, TILE), F32),
            pltpu.VMEM((2, tokens, kv_cols), BF16),
            pltpu.VMEM((tokens, kv_cols), BF16),
            pltpu.SemaphoreType.DMA((copies,)),
            pltpu.SemaphoreType.DMA((copies,)),
            pltpu.SemaphoreType.DMA((6,)),
        ],
        compiler_params=pltpu.CompilerParams(
            vmem_limit_bytes=61 << 20, collective_id=2, has_side_effects=True
        ),
        cost_estimate=pl.CostEstimate(
            flops=40 << 30, bytes_accessed=50 << 20, transcendentals=8 << 20
        ),
        name="middle_back",
    )(ffn_g, down_sum, grad_n2, middle, cot, gains, out_w, q, kv, attn, lse, seg)


def tail_kernel(
    depth, rows, width,
    dq_t, dkv, cosine_t, sine_t, x_t, grad_middle, gains, in_w, gain2,
    grad_hidden, in_grad, gain_sum,
    proj, proj_b, in_g, in_c, in_r, grad_x, gain_own, gain_r, send_sems, recv_sems,
):
    query_cols, tokens = dq_t.shape
    in_cols = in_w.shape[2]
    pad = DPAD // (2 * depth)
    turned = (HEADS + KV_HEADS) * HEAD_DIM
    p = Place(depth, send_sems, recv_sems)
    p.barrier()
    x_f = widen(x_t, depth, rows, pad)
    gain = gains[0:1, :]
    inv = lax.rsqrt(mean_rows(x_f * x_f, width) + EPSILON)
    normed1 = (x_f * inv * gain).astype(BF16)
    cosine = lane_tables(cosine_t[...])
    sine = signed(lane_tables(sine_t[...]), True)
    proj[:, :query_cols] = dq_t[...].T * SCORE_SCALE
    proj[:, query_cols:] = dkv[...]
    for j in range(turned // 128):
        lanes = slice(128 * j, 128 * (j + 1))
        proj[:, lanes] = rope(proj[:, lanes], cosine, sine)
    for b in range(4):
        proj_b[b] = proj[:, b * in_cols : (b + 1) * in_cols].astype(BF16)
    for other in (1, 0):
        c = (1 - p.c) if other else p.c
        for y in range(2):
            left = transposed(proj_b[2 * y + c])
            spread_blocks(in_g.at[c, y], dot(left, normed1), pad)
        if other:
            in_cross = p.copy("c", in_g.at[c], in_c)
    in_cross.wait_recv()
    own = in_g.at[p.c]
    own[...] = (own[...].astype(F32) + in_c[...].astype(F32)).astype(BF16)
    in_sum = PlaneScatter(p, own, in_r)
    in_sum.start()
    up = None
    for b in range(4):
        term = dot(proj_b[b], in_w[b % 2, b // 2])
        up = term if up is None else up + term
    scaled = up * gain
    mean = mean_rows(scaled * x_f, width)
    grad_x[...] = grad_middle[...] + inv * (scaled - x_f * (inv * inv * mean))
    gain_own[...] = jnp.zeros_like(gain_own)
    gain_own[0:1, :] = jnp.sum(up * x_f * inv, axis=0, keepdims=True)
    gain_own[1:2, :] = gain2[...]
    in_sum.forward()
    sent = []
    for n, kind in enumerate(("c", "y", "x")):
        made = p.copy(kind, gain_own.at[pl.ds(8 * n, 8)], gain_r.at[pl.ds(8 * n, 8)])
        sent.append(made)
        if n == 0:
            narrow(grad_hidden, grad_x[...], depth, rows, pad)
        made.wait_recv()
        if n == 1:
            in_sum.over_z()
        gain_own[8 * (n + 1) : 8 * (n + 2), :] = (
            gain_own[8 * n : 8 * (n + 1), :] + gain_r[8 * n : 8 * (n + 1), :]
        )
    last = gain_own.at[pl.ds(24, 8)]
    arriving = [p.copy(k, last, gain_r.at[pl.ds(24 + 8 * k, 8)]) for k in range(1, depth)]
    total = last[...]
    for k, made in enumerate(arriving):
        made.wait_recv()
        total += gain_r[32 + 8 * k : 40 + 8 * k, :]
    mine = jnp.zeros((8, pad), F32)
    for n in range(2 * depth):
        mine = jnp.where(n == p.x * depth + p.z, total[:, n * pad : (n + 1) * pad], mine)
    gain_sum[...] = mine[:, :rows]
    in_grad[...] = one_block(in_sum.result(), rows, pad)
    in_sum.finish()
    for made in sent + arriving + [in_cross]:
        made.wait_send()


def tail(dq_t, dkv, cosine_t, sine_t, x_t, grad_middle, gains, in_w, gain2, depth, rows, width):
    tokens = dq_t.shape[1]
    pad = DPAD // (2 * depth)
    in_cols = in_w.shape[2]
    total = dq_t.shape[0] + dkv.shape[1]
    slots = scatter_slots(depth)
    copies = scatter_copies(depth) + 1 + 3 + depth - 1
    return pl.pallas_call(
        functools.partial(tail_kernel, depth, rows, width),
        out_shape=[
            jax.ShapeDtypeStruct((width, tokens), F32),
            jax.ShapeDtypeStruct((in_cols, rows), F32),
            jax.ShapeDtypeStruct((8, rows), F32),
        ],
        in_specs=vmem_specs(9),
        out_specs=vmem_specs(3),
        scratch_shapes=[
            pltpu.VMEM((tokens, total), F32),
            pltpu.VMEM((4, tokens, in_cols), BF16),
            pltpu.VMEM((2, 2, 2 * depth, *block_shape(in_cols, pad)), BF16),
            pltpu.VMEM((2, 2 * depth, *block_shape(in_cols, pad)), BF16),
            pltpu.VMEM((slots, *block_shape(in_cols, pad)), BF16),
            pltpu.VMEM((tokens, DPAD), F32),
            pltpu.VMEM((32, DPAD), F32),
            pltpu.VMEM((24 + 8 * depth, DPAD), F32),
            pltpu.SemaphoreType.DMA((copies,)),
            pltpu.SemaphoreType.DMA((copies,)),
        ],
        compiler_params=pltpu.CompilerParams(
            vmem_limit_bytes=61 << 20, collective_id=3, has_side_effects=True
        ),
        cost_estimate=pl.CostEstimate(
            flops=8 << 30, bytes_accessed=30 << 20, transcendentals=0
        ),
        name="tail",
    )(dq_t, dkv, cosine_t, sine_t, x_t, grad_middle, gains, in_w, gain2)


def rotary_tables(position_ids):
    half_dim = HEAD_DIM // 2
    frequency = jnp.exp(
        jnp.arange(half_dim, dtype=F32) * (-2.0 * math.log(10000.0) / HEAD_DIM)
    )
    angles = frequency[:, None] * position_ids.astype(F32)[None, :]
    return jnp.cos(angles), jnp.sin(angles)


def per_device(
    hidden_in, cotangent, segments, positions, attn_in, attn_out, w_gate, w_up, w_down,
    norm1_gain, norm2_gain,
):
    tokens, width = hidden_in.shape[1:]
    dp_size = lax.axis_size("dp")
    depth = dp_size // 2
    rows = width // dp_size
    pad = DPAD // dp_size

    in_cols = attn_in.shape[1]
    beside = ((0, 0), (0, pad - rows))
    gain_rows = jnp.concatenate(
        [norm1_gain[None], norm2_gain[None], jnp.zeros((GAIN_ROWS - 2, rows), BF16)], axis=0
    )
    pack_a = jnp.pad(jnp.concatenate([attn_in.T, gain_rows, attn_out], axis=0), beside)
    pack_g = jnp.pad(jnp.stack([w_gate, w_up, w_down.T]), ((0, 0), (0, pad - rows), (0, 0)))
    x_t, cot_t = hidden_in[0].T, cotangent[0].T
    cosine_t, sine_t = rotary_tables(positions[0])
    q, kv, attn, lse, middle, normed2, gains, seg, out_w, in_w, ffn_w, down_w = front(
        pack_a, pack_g, x_t, cosine_t, sine_t, segments, depth, rows, width, in_cols
    )
    ffn_g, down_sum, hidden_out, grad_n2, cot = ffn(normed2, cot_t, middle, ffn_w, down_w, rows)
    dq_t, dkv, grad_middle, gain2, g_out, g_ffn = middle_back(
        ffn_g, down_sum, grad_n2, middle, cot, gains, out_w, q, kv, attn, lse, seg,
        depth, rows, width,
    )
    grad_hidden, g_in, g_gains = tail(
        dq_t, dkv, cosine_t, sine_t, x_t, grad_middle, gains, in_w, gain2, depth, rows, width
    )
    return (
        hidden_out.T[None],
        grad_hidden.T[None],
        g_in.T,
        g_out,
        g_ffn[0],
        g_ffn[1],
        g_ffn[2].T,
        g_gains[0],
        g_gains[1],
    )


def solution(mesh):
    return jax.shard_map(
        per_device,
        mesh=mesh,
        in_specs=(
            P("dp", "mp", None),
            P("dp", "mp", None),
            P("dp", None),
            P("dp", "mp"),
            P("dp", "mp"),
            P("mp", "dp"),
            P("dp", "mp"),
            P("dp", "mp"),
            P("mp", "dp"),
            P("dp"),
            P("dp"),
        ),
        out_specs=(
            P("dp", "mp", None),
            P("dp", "mp", None),
            P("dp", "mp"),
            P("mp", "dp"),
            P("dp", "mp"),
            P("dp", "mp"),
            P("mp", "dp"),
            P("dp"),
            P("dp"),
        ),
        check_vma=False,
    )
```

```python
import functools
import math

import jax
import jax.numpy as jnp
from jax import lax
from jax.experimental import pallas as pl
from jax.experimental.pallas import tpu as pltpu
from jax.sharding import PartitionSpec as P

HEADS = 15
KV_HEADS = 5
GROUP = HEADS // KV_HEADS
HEAD_DIM = 64
DPAD = 1024
TILE = 256
EPSILON = 1e-05
SCORE_SCALE = 0.125
MASK_FILL = -1e30
LOG2E = 1.4426950408889634
EXP_SCALE = SCORE_SCALE * LOG2E
GAIN_ROWS = 16
BF16 = jnp.bfloat16
F32 = jnp.float32


def dot(a, b):
    return jnp.dot(a, b, preferred_element_type=F32)


def dot_nt(a, b):
    return lax.dot_general(a, b, (((1,), (1,)), ((), ())), preferred_element_type=F32)


def vmem_specs(count):
    return [pl.BlockSpec(memory_space=pltpu.VMEM)] * count


def transposed(value):
    return value.astype(F32).T.astype(BF16)


class Place:
    def __init__(self, depth, send_sems, recv_sems):
        dp_index, m = lax.axis_index("dp"), lax.axis_index("mp")
        self.depth = depth
        self.z, self.x = dp_index // 2, dp_index % 2
        self.m, self.y, self.c = m, m // 2, m % 2
        self.send_sems, self.recv_sems = send_sems, recv_sems
        self.count = 0

    def peer(self, kind):
        z, x, y, c = self.z, self.x, self.y, self.c
        if kind == "x":
            x = 1 - x
        elif kind == "y":
            y = 1 - y
        elif kind == "c":
            c = 1 - c
        else:
            z = (z + kind) % self.depth
        return 2 * z + x, 2 * y + c

    def kinds(self):
        return ["x", "y", "c"] + list(range(1, self.depth))

    def barrier(self, kinds=None):
        semaphore = pltpu.get_barrier_semaphore()
        kinds = kinds or self.kinds()
        for kind in kinds:
            pl.semaphore_signal(
                semaphore, inc=1, device_id=self.peer(kind), device_id_type=pl.DeviceIdType.MESH
            )
        pl.semaphore_wait(semaphore, len(kinds))

    def copy(self, kind, source, target=None):
        index = self.count
        self.count += 1
        made = pltpu.make_async_remote_copy(
            src_ref=source,
            dst_ref=source if target is None else target,
            send_sem=self.send_sems.at[index],
            recv_sem=self.recv_sems.at[index],
            device_id=self.peer(kind),
            device_id_type=pl.DeviceIdType.MESH,
        )
        made.start()
        return made


class PlaneGather:
    def __init__(self, place, source, buffer, by_x, part=lambda ref: ref):
        self.place, self.source, self.buffer, self.part = place, source, buffer, part
        self.split = place.depth - by_x
        self.sent, self.last = [], []

    def over_z(self, slot=None):
        p = self.place
        slot = self.part(self.buffer.at[p.y, p.x, p.z]) if slot is None else slot
        self.arriving = [p.copy(k, self.source, slot) for k in range(1, p.depth)]
        self.sent += self.arriving

    def stacked(self):
        for made in self.arriving:
            made.wait_recv()

    def over_x(self):
        p = self.place
        self.by_x = p.copy("x", self.part(self.buffer.at[p.y, p.x]))
        self.sent.append(self.by_x)

    def over_y(self):
        p = self.place
        self.by_y = p.copy("y", self.part(self.buffer.at[p.y, p.x]))
        self.sent.append(self.by_y)

    def diagonal_x(self):
        p = self.place
        self.by_y.wait_recv()
        span = pl.ds(self.split, p.depth - self.split)
        self.last.append(p.copy("x", self.part(self.buffer.at[1 - p.y, p.x, span])))

    def diagonal_y(self):
        p = self.place
        self.by_x.wait_recv()
        if self.split:
            span = pl.ds(0, self.split)
            self.last.append(p.copy("y", self.part(self.buffer.at[p.y, 1 - p.x, span])))

    def arrived(self):
        for made in self.last:
            made.wait_recv()

    def finish(self):
        for made in self.sent + self.last:
            made.wait_send()


def rope(value, cosine, sine):
    lane = lax.broadcasted_iota(jnp.int32, value.shape, 1)
    half = HEAD_DIM // 2
    partner = jnp.where(
        lane % HEAD_DIM < half, pltpu.roll(value, 128 - half, 1), pltpu.roll(value, half, 1)
    )
    return value * cosine + partner * sine


def trimmed(rows, pad):
    return rows if rows % 8 == 0 else pad


def natural(block, depth):
    return 2 * (block % depth) + block // depth


def widen(source, depth, rows, pad):
    filler = jnp.zeros((pad - rows, source.shape[1]), F32)
    parts = []
    for b in range(2 * depth):
        first = natural(b, depth) * rows
        parts += [source[first : first + rows, :].astype(F32), filler]
    return jnp.concatenate(parts, axis=0).T


def narrow(target, value, depth, rows, pad):
    flipped = value.T
    for b in range(2 * depth):
        first = natural(b, depth) * rows
        target[first : first + rows, :] = flipped[b * pad : b * pad + rows, :].astype(target.dtype)


def side_by_side(ref, first, size):
    _, depth, _, pad = ref.shape
    span = pl.ds(first, size)
    return jnp.concatenate(
        [ref[b // depth, b % depth, span, :] for b in range(2 * depth)], axis=1
    )


def lane_tables(table):
    return jnp.concatenate([table] * (256 // HEAD_DIM), axis=0).T


def signed(table, back):
    lane = lax.broadcasted_iota(jnp.int32, table.shape, 1) % HEAD_DIM
    first = lane < HEAD_DIM // 2
    return jnp.where(first, table, -table) if back else jnp.where(first, -table, table)


def mean_rows(value, width):
    return jnp.sum(value, axis=-1, keepdims=True) * (1.0 / width)


def mask_tile(start, query_tile, key_tile):
    key = key_tile * TILE + lax.broadcasted_iota(jnp.int32, (TILE, TILE), 0)
    query = query_tile * TILE + lax.broadcasted_iota(jnp.int32, (TILE, TILE), 1)
    return jnp.where((key >= start) & (key <= query), 0.0, MASK_FILL)


def front_kernel(
    depth, rows, width, in_cols,
    attn_in_t, attn_out, gain_one, gain_two, w_gate, w_up, w_down_t, x_t, cosine_t, sine_t, segments,
    attn, lse, middle, normed2, gains, seg, q_out, kv_out, out_w_out, in_w_out, ffn_w, down_w,
    q, kv, out_w, in_w, a_buf, x_in, cosine, sine, normed1, proj, q_t, k3, v_t, acc, peak, total,
    biases, send_sems, recv_sems, local_sems,
):
    tokens = x_in.shape[0]
    tiles = tokens // TILE
    back = 1024 // TILE
    pad = DPAD // (2 * depth)
    lead = in_cols + GAIN_ROWS
    query_cols = HEADS * HEAD_DIM
    out_cols = query_cols // 4
    p = Place(depth, send_sems, recv_sems)
    block = a_buf.at[p.c, p.y, p.x, p.z]
    block[...] = jnp.zeros_like(block)
    block[0:in_cols, 0:rows] = attn_in_t[...]
    block[in_cols : in_cols + 1, 0:rows] = gain_one[...]
    block[in_cols + 1 : in_cols + 2, 0:rows] = gain_two[...]
    block[lead : lead + out_cols, 0:rows] = attn_out[...]
    moved = pl.ds(0, trimmed(rows, pad))
    trim = lambda ref: ref.at[..., moved, :]
    own = [
        pltpu.make_async_copy(
            source, trim(ffn_w.at[w, p.y, p.x, p.z] if w < 2 else down_w.at[p.z]), local_sems.at[w]
        )
        for w, source in enumerate((w_gate, w_up, w_down_t))
    ]
    for made in own:
        made.start()
    p.barrier()
    first_part = lambda ref: ref.at[..., pl.ds(0, lead), :]
    last_part = lambda ref: ref.at[..., pl.ds(lead, out_cols), :]
    buffer = a_buf.at[p.c]
    plane = PlaneGather(p, first_part(block), buffer, depth // 2, first_part)
    output = PlaneGather(p, last_part(block), buffer, depth // 2, last_part)
    gate = PlaneGather(p, w_gate, ffn_w.at[0], depth, trim)
    up = PlaneGather(p, w_up, ffn_w.at[1], depth // 2, trim)
    down = PlaneGather(p, w_down_t, None, 0)
    plane.over_z()
    x_f = widen(x_t, depth, rows, pad)
    x_in[...] = x_f.astype(BF16)
    cosine[...] = lane_tables(cosine_t[...])
    sine[...] = signed(lane_tables(sine_t[...]), False)
    inv_one = lax.rsqrt(mean_rows(x_f * x_f, width) + EPSILON)
    own_seg = segments[:, pl.ds(pl.multiple_of(p.m * tokens, tokens), tokens)]
    start = jnp.zeros_like(own_seg)
    for n in range(3):
        count = jnp.sum((segments[...] == n).astype(jnp.int32), axis=1, keepdims=True)
        start += jnp.where(own_seg > n, count, 0)
    seg[...] = start
    plane.stacked()
    plane.over_x()
    plane.over_y()
    output.over_z()
    gate.over_z()
    plane.diagonal_y()
    plane.diagonal_x()
    for made in own:
        made.wait()
    up.over_z()
    plane.arrived()
    cross = p.copy("c", first_part(a_buf.at[p.c]))
    output.stacked()
    output.over_x()
    output.over_y()
    gate.stacked()
    gate.over_x()
    gate.over_y()
    cross.wait()
    for b in range(2 * depth):
        gains[:, b * pad : (b + 1) * pad] = a_buf[
            0, 0, b // depth, b % depth, pl.ds(in_cols, 2), :
        ].astype(F32)
    normed1[...] = (x_f * inv_one * gains[0:1, :]).astype(BF16)
    for b in range(4):
        in_w[b % 2, b // 2] = side_by_side(a_buf.at[b % 2, b // 2], 0, in_cols)

    kv_first = query_cols // 128

    def project(blocks, groups):
        def tile(start):
            span = pl.ds(start, TILE)
            for b in blocks:
                proj[span, b * in_cols : (b + 1) * in_cols] = dot_nt(
                    normed1[span, :], in_w[b % 2, b // 2]
                )
            for j in groups:
                lanes = slice(128 * j, 128 * (j + 1))
                proj[span, lanes] = rope(proj[span, lanes], cosine[span, :], sine[span, :])

        row_tiles(tokens, tile)

    project((2, 3), range(kv_first, (HEADS + KV_HEADS) * HEAD_DIM // 128))
    for g in range(KV_HEADS):
        k_first, v_first = query_cols + g * HEAD_DIM, query_cols + (KV_HEADS + g) * HEAD_DIM
        kv[p.m, g] = jnp.concatenate(
            [proj[:, k_first : k_first + HEAD_DIM], proj[:, v_first : v_first + HEAD_DIM]], axis=1
        ).astype(BF16)
    kv_c = p.copy("c", kv.at[p.m])
    kv_y = [p.copy("y", kv.at[p.m, g]) for g in range(KV_HEADS)]
    down.over_z(trim(down_w.at[p.z]))
    project((0, 1), range(kv_first))
    q[...] = proj[:, :query_cols].astype(BF16)
    q_t[...] = proj[:, :query_cols].T.astype(BF16)
    saved = [
        pltpu.make_async_copy(source, target, local_sems.at[3 + n])
        for n, (source, target) in enumerate(((in_w, in_w_out), (q, q_out)))
    ]
    for made in saved:
        made.start()
    acc[...] = jnp.zeros_like(acc)
    peak[...] = jnp.full_like(peak, MASK_FILL)
    total[...] = jnp.zeros_like(total)

    def spread(block, g):
        span = pl.ds(pl.multiple_of(block * tokens, tokens), tokens)
        part = kv[block, g]
        v_t[g * HEAD_DIM : (g + 1) * HEAD_DIM, span] = transposed(part)[HEAD_DIM:]
        k3[g, span, :] = part[:, :HEAD_DIM]

    def attend_unit(i, t, g, bias):
        cols = pl.ds(i * TILE, TILE)
        keys = pl.ds(pl.multiple_of(t * TILE, TILE), TILE)
        k_g = k3[g, keys, :]
        v_g = v_t[pl.ds(pl.multiple_of(g * HEAD_DIM, HEAD_DIM), HEAD_DIM), keys]
        heads = [g * GROUP + j for j in range(GROUP)]
        places = [pl.ds(pl.multiple_of(h * HEAD_DIM, HEAD_DIM), HEAD_DIM) for h in heads]
        old = [peak[pl.ds(h, 1), cols] for h in heads]
        sums = [total[pl.ds(h, 1), cols] for h in heads]
        accs = [acc[s, cols] for s in places]
        scores = [dot(k_g, q_t[s, cols]) + bias[...] for s in places]
        new = [jnp.maximum(o, jnp.max(s, axis=0, keepdims=True)) for o, s in zip(old, scores)]
        probs = [jnp.exp2(s * EXP_SCALE - n * EXP_SCALE) for s, n in zip(scores, new)]
        scale = [jnp.exp2((o - n) * EXP_SCALE) for o, n in zip(old, new)]
        outs = [dot(v_g, b.astype(BF16)) for b in probs]
        for j, h in enumerate(heads):
            peak[pl.ds(h, 1), cols] = new[j]
            total[pl.ds(h, 1), cols] = sums[j] * scale[j] + jnp.sum(
                probs[j], axis=0, keepdims=True
            )
            acc[places[j], cols] = accs[j] * scale[j] + outs[j]

    first_tile = p.m * tiles

    def bias_tile(i, t, slot):
        biases[i, slot] = mask_tile(seg[0:1, i * TILE : (i + 1) * TILE], first_tile + i, t)

    for g in range(KV_HEADS):
        spread(p.m, g)
    for i in range(tiles):
        for t in range(i + 1):
            bias_tile(i, first_tile + t, 0)

            def group(g, carry):
                attend_unit(i, first_tile + t, g, biases.at[i, 0])
                return carry

            lax.fori_loop(0, KV_HEADS, group, 0)
        if i == 0:
            up.stacked()
            up.over_x()
            output.diagonal_x()
            output.diagonal_y()

    lows = [jnp.maximum(first_tile + i - back, 0) for i in range(tiles)]
    for i in range(tiles):

        def fill(t, carry):
            bias_tile(i, t, t - lows[i])
            return carry

        lax.fori_loop(lows[i], first_tile, fill, 0)
    kv_cy = []

    def pass_on(g):
        kv_y[g].wait_recv()
        kv_cy.append(p.copy("c", kv.at[(p.m + 2) % 4, g]))

    kv_c.wait_recv()
    pass_on(0)
    gate.diagonal_x()
    gate.diagonal_y()
    for g in range(KV_HEADS):
        if g + 1 < KV_HEADS:
            pass_on(g + 1)
        if g == 1:
            up.over_y()
            up.diagonal_y()
        if g == 2:
            output.arrived()
            out_cross = p.copy("c", last_part(a_buf.at[p.c]))
        kv_cy[g].wait_recv()
        for n in (1, 2):
            spread(jnp.maximum(p.m - n, 0), g)
        for i in range(tiles):

            def step(t, carry):
                attend_unit(i, t, g, biases.at[i, t - lows[i]])
                return carry

            lax.fori_loop(lows[i], first_tile, step, 0)
    saved.append(pltpu.make_async_copy(kv, kv_out, local_sems.at[5]))
    saved[-1].start()
    for h in range(HEADS):
        span = pl.ds(h * HEAD_DIM, HEAD_DIM)
        acc[span, :] = acc[span, :] / total[h : h + 1, :]
    attn[...] = acc[...].T.astype(BF16)
    lse[...] = peak[...] * EXP_SCALE + jnp.log2(jnp.maximum(total[...], 1e-37))
    out_cross.wait()
    for b in range(4):
        out_w[b % 2, b // 2] = side_by_side(a_buf.at[b % 2, b // 2], lead, out_cols)
    saved.append(pltpu.make_async_copy(out_w, out_w_out, local_sems.at[6]))
    saved[-1].start()
    up.diagonal_x()

    def project_out(r, carry):
        span = pl.ds(pl.multiple_of(r * TILE, TILE), TILE)
        mid = x_in[span, :].astype(F32)
        for b in range(4):
            mid += dot(attn[span, b * out_cols : (b + 1) * out_cols], out_w[b % 2, b // 2])
        middle[span, :] = mid
        inv = lax.rsqrt(mean_rows(mid * mid, width) + EPSILON)
        normed2[span, :] = (mid * inv * gains[1:2, :]).astype(BF16)
        return carry

    lax.fori_loop(0, tiles, project_out, 0)
    gate.arrived()
    up.arrived()
    down.stacked()
    for part in (plane, output, gate, up, down):
        part.finish()
    for made in kv_y + kv_cy + [kv_c]:
        made.wait_send()
    for made in saved:
        made.wait()


def front(
    attn_in_t, attn_out, gain_one, gain_two, w_gate, w_up, w_down_t, x_t, cosine_t, sine_t,
    segments, depth, rows,
):
    width, tokens = x_t.shape
    pad = DPAD // (2 * depth)
    in_cols, cols = attn_in_t.shape[0], w_gate.shape[1]
    a_rows = in_cols + GAIN_ROWS + attn_out.shape[0]
    query_cols, kv_cols = HEADS * HEAD_DIM, 2 * KV_HEADS * HEAD_DIM
    whole = 4 * tokens
    copies = 5 * (depth - 1) + 4 * 4 + 3 + 2 * KV_HEADS
    anywhere = pl.BlockSpec(memory_space=pl.ANY)
    kept = [
        (tokens, query_cols),
        (4, KV_HEADS, tokens, 2 * HEAD_DIM),
        (2, 2, query_cols // 4, DPAD),
        (2, 2, in_cols, DPAD),
    ]
    return pl.pallas_call(
        functools.partial(front_kernel, depth, rows, width, in_cols),
        out_shape=[
            jax.ShapeDtypeStruct((tokens, query_cols), BF16),
            jax.ShapeDtypeStruct((HEADS + 1, tokens), F32),
            jax.ShapeDtypeStruct((tokens, DPAD), F32),
            jax.ShapeDtypeStruct((tokens, DPAD), BF16),
            jax.ShapeDtypeStruct((2, DPAD), F32),
            jax.ShapeDtypeStruct((1, tokens), jnp.int32),
            *[jax.ShapeDtypeStruct(shape, BF16) for shape in kept],
            jax.ShapeDtypeStruct((2, 2, 2, depth, pad, cols), BF16),
            jax.ShapeDtypeStruct((depth, pad, cols), BF16),
        ],
        in_specs=vmem_specs(4) + [anywhere] * 3 + vmem_specs(4),
        out_specs=vmem_specs(6) + [anywhere] * 6,
        scratch_shapes=[
            *[pltpu.VMEM(shape, BF16) for shape in kept],
            pltpu.VMEM((2, 2, 2, depth, a_rows, pad), BF16),
            pltpu.VMEM((tokens, DPAD), BF16),
            pltpu.VMEM((tokens, 128), F32),
            pltpu.VMEM((tokens, 128), F32),
            pltpu.VMEM((tokens, DPAD), BF16),
            pltpu.VMEM((tokens, query_cols + kv_cols), F32),
            pltpu.VMEM((query_cols, tokens), BF16),
            pltpu.VMEM((KV_HEADS, whole, HEAD_DIM), BF16),
            pltpu.VMEM((KV_HEADS * HEAD_DIM, whole), BF16),
            pltpu.VMEM((query_cols, tokens), F32),
            pltpu.VMEM((HEADS + 1, tokens), F32),
            pltpu.VMEM((HEADS + 1, tokens), F32),
            pltpu.VMEM((tokens // TILE, 1024 // TILE, TILE, TILE), F32),
            pltpu.SemaphoreType.DMA((copies,)),
            pltpu.SemaphoreType.DMA((copies,)),
            pltpu.SemaphoreType.DMA((7,)),
        ],
        compiler_params=pltpu.CompilerParams(
            vmem_limit_bytes=58 << 20, collective_id=0, has_side_effects=True
        ),
        cost_estimate=pl.CostEstimate(
            flops=20 << 30, bytes_accessed=40 << 20, transcendentals=8 << 20
        ),
        name="front",
    )(
        attn_in_t, attn_out, gain_one, gain_two, w_gate, w_up, w_down_t, x_t, cosine_t, sine_t,
        segments,
    )


class PlaneScatter:
    def __init__(
        self, place, source, recv, part=lambda ref: ref, stage=None, local_sems=None
    ):
        self.place, self.source, self.recv, self.part = place, source, recv, part
        p, half = place, place.depth // 2
        self.half = half
        places = [(p.y, 1 - p.x, 0, half), (1 - p.y, p.x, half, half), (p.y, p.x, 0, p.depth)]
        views = [
            source.at[y, pl.ds(x * p.depth + first, size)] for y, x, first, size in places
        ]
        self.loads = []
        if stage is None:
            self.by_x, self.by_y, self.total = views
        else:
            self.by_x, self.by_y = stage.at[pl.ds(0, half)], stage.at[pl.ds(half, half)]
            self.total = stage.at[pl.ds(p.depth, p.depth)]
            for n, (view, kept) in enumerate(zip(views, (self.by_x, self.by_y, self.total))):
                self.loads.append(pltpu.make_async_copy(view, kept, local_sems.at[n]))

    def slot(self, n):
        return self.recv.at[pl.ds(n * self.half, self.half)]

    def copy(self, kind, source, slot):
        return self.place.copy(kind, self.part(source), self.part(slot))

    def start(self):
        p, half = self.place, self.half
        for load in self.loads:
            load.start()
        far, here, there = (1 - p.x) * p.depth, p.x * p.depth, 1 - p.y
        self.far_y = self.copy("y", self.source.at[there, pl.ds(far, half)], self.slot(0))
        self.far_x = self.copy("x", self.source.at[there, pl.ds(far + half, half)], self.slot(1))
        self.near_y = self.copy("y", self.source.at[there, pl.ds(here, half)], self.slot(2))
        self.near_x = self.copy("x", self.source.at[p.y, pl.ds(far + half, half)], self.slot(3))
        self.sent = [self.far_y, self.far_x, self.near_y, self.near_x]

    def forward(self):
        p = self.place
        for load in self.loads:
            load.wait()
        self.far_y.wait_recv()
        self.by_x[...] = (self.by_x[...].astype(F32) + self.slot(0)[...].astype(F32)).astype(BF16)
        self.last_x = self.copy("x", self.by_x, self.slot(4))
        self.far_x.wait_recv()
        self.by_y[...] = (self.by_y[...].astype(F32) + self.slot(1)[...].astype(F32)).astype(BF16)
        self.last_y = self.copy("y", self.by_y, self.slot(5))
        self.sent += [self.last_x, self.last_y]

    def add(self):
        half = self.half
        for made in (self.near_y, self.near_x, self.last_x, self.last_y):
            made.wait_recv()
        for first, slots in ((0, (2, 4)), (half, (3, 5))):
            span = self.total.at[pl.ds(first, half)]
            terms = [self.slot(n)[...].astype(F32) for n in slots]
            span[...] = (span[...].astype(F32) + terms[0] + terms[1]).astype(BF16)

    def over_z(self):
        p, half = self.place, self.half
        self.add()
        self.arriving = [
            self.copy(
                k, self.total.at[(p.z + k) % p.depth], self.recv.at[6 * half + k - 1]
            )
            for k in range(1, p.depth)
        ]
        self.sent += self.arriving

    def result(self):
        value = self.total[self.place.z].astype(F32)
        for k, made in enumerate(self.arriving):
            made.wait_recv()
            value += self.recv[6 * self.half + k].astype(F32)
        return value

    def finish(self):
        for made in self.sent:
            made.wait_send()


def block_shape(size, pad):
    return (size, pad) if pad % 128 == 0 else (pad, size)


def spread_blocks(target, value, pad):
    if pad % 128 == 0:
        for n in range(DPAD // pad):
            target[n] = value[:, n * pad : (n + 1) * pad].astype(BF16)
    else:
        flipped = value.T.astype(BF16)
        for n in range(DPAD // pad):
            target[n] = flipped[n * pad : (n + 1) * pad]


def one_block(value, rows, pad):
    return (value if pad % 128 == 0 else value.T)[:, :rows]


def scatter_slots(depth):
    return 3 * depth + depth - 1


def scatter_copies(depth):
    return 6 + depth - 1


def store_blocks(ref, start, value):
    pad = ref.shape[1]
    for k in range(TILE // pad):
        ref[start // pad + k] = value[k * pad : (k + 1) * pad]


def row_tiles(count, body):
    def step(r, carry):
        body(pl.multiple_of(r * TILE, TILE))
        return carry

    lax.fori_loop(0, count // TILE, step, 0)


def ffn_kernel(
    depth, rows, normed2, cot_t, middle, ffn_w, down_w, grads, down_sum, hidden_out, grad_n2, cot,
    wide_w, down_buf, down_g, down_r, n_other, c_other, hid, d_gate, d_up, n_t, c_t, ffn_own, parts,
    received, packed, send_sems, recv_sems, local_sems,
):
    tokens = normed2.shape[0]
    cols = ffn_w.shape[-1]
    p = Place(depth, send_sems, recv_sems)
    pad = DPAD // (2 * depth)
    count = trimmed(rows, pad)
    moved = pl.ds(0, count)
    trim = lambda ref: ref.at[..., moved, :]
    loads = [
        pltpu.make_async_copy(
            trim(ffn_w.at[w, y]),
            wide_w.at[w, :, :, moved, pl.ds(y * cols, cols)],
            local_sems.at[2 * w + y],
        )
        for w in range(2)
        for y in range(2)
    ]
    loads.append(
        pltpu.make_async_copy(trim(down_w), trim(down_buf.at[p.y, p.x]), local_sems.at[4])
    )
    for load in loads:
        load.start()
    if count < pad:
        wide_w[:, :, :, count:, :] = jnp.zeros((2, 2, depth, pad - count, 2 * cols), BF16)
        down_buf[:, :, :, count:, :] = jnp.zeros((2, 2, depth, pad - count, cols), BF16)
    p.barrier(["c", "x", "y"])
    n_copy = p.copy("c", normed2, n_other)
    down = PlaneGather(p, None, down_buf, depth // 2, trim)
    loads[4].wait()
    down.over_x()
    down.over_y()
    cot[...] = widen(cot_t, depth, rows, pad).astype(BF16)
    c_copy = p.copy("c", cot, c_other)
    for load in loads[:4]:
        load.wait()

    def sides(s):
        return (n_other, c_other) if s else (normed2, cot)

    for s in range(2):
        if s:
            n_copy.wait_recv()
            c_copy.wait_recv()
        n_from, c_from = sides(s)
        both = slice(s * tokens, (s + 1) * tokens)
        n_t[:, both] = transposed(n_from[...])
        c_t[:, both] = transposed(c_from[...])
        def tile(start):
            span = pl.ds(s * tokens + start, TILE)
            n_rows = n_from[pl.ds(start, TILE), :]
            gate = dot(n_rows, wide_w[0].reshape(DPAD, 2 * cols))
            upper = dot(n_rows, wide_w[1].reshape(DPAD, 2 * cols))
            sigma = jax.nn.sigmoid(gate)
            silu = gate * sigma
            hid[span, :] = (silu * upper).astype(BF16)
            d_gate[span, :] = (upper * sigma * (1.0 + gate * (1.0 - sigma))).astype(BF16)
            d_up[span, :] = silu.astype(BF16)

        row_tiles(tokens, tile)
    down.diagonal_y()
    down.diagonal_x()

    def weight_grad(left, right, target):
        def tile(start):
            side = dot(left[pl.ds(start, TILE), :], right[...]).astype(BF16)
            for y in range(2):
                store_blocks(target.at[y], start, side[:, y * cols : (y + 1) * cols])

        row_tiles(DPAD, tile)

    weight_grad(c_t, hid, down_g)
    down.arrived()
    total = PlaneScatter(p, down_g, down_r, trim)
    total.start()

    for s in (1, 0):
        n_from, c_from = sides(s)
        both = slice(s * tokens, (s + 1) * tokens)
        part = None
        for y in range(2):
            lanes = slice(y * cols, (y + 1) * cols)
            w_down = down_buf[y].reshape(DPAD, cols)
            grad_hid = dot(c_from[...], w_down)
            d_gate[both, lanes] = (grad_hid * d_gate[both, lanes].astype(F32)).astype(BF16)
            d_up[both, lanes] = (grad_hid * d_up[both, lanes].astype(F32)).astype(BF16)
            out = dot_nt(hid[both, lanes], w_down)
            part = out if part is None else part + out
        back = dot_nt(d_gate[both, :], wide_w[0].reshape(DPAD, 2 * cols))
        back += dot_nt(d_up[both, :], wide_w[1].reshape(DPAD, 2 * cols))
        if s:
            parts[0] = part.astype(BF16)
            parts[1] = back.astype(BF16)
            shared = [p.copy("c", parts.at[n], received.at[n]) for n in range(2)]
        else:
            ffn_own[...] = part + middle[...]
            grad_n2[...] = back
    total.forward()
    saved = []
    for w, right in ((0, d_gate), (1, d_up)):
        weight_grad(n_t, right, packed.at[w])
        made = pltpu.make_async_copy(packed.at[w], grads.at[w], local_sems.at[w])
        made.start()
        saved.append(made)
    for made in shared:
        made.wait_recv()

    narrow(hidden_out, ffn_own[...] + received[0].astype(F32), depth, rows, pad)
    grad_n2[...] += received[1].astype(F32)
    total.add()
    down_sum[...] = total.total[...]
    total.finish()
    down.finish()
    for made in shared + [n_copy, c_copy]:
        made.wait_send()
    for made in saved:
        made.wait()


def ffn(normed2, cot_t, middle, ffn_w, down_w, rows):
    width, tokens = cot_t.shape
    depth, pad, cols = down_w.shape
    token_rows = pltpu.VMEM((tokens, DPAD), BF16)
    wide = pltpu.VMEM((2 * tokens, 2 * cols), BF16)
    flipped = pltpu.VMEM((DPAD, 2 * tokens), BF16)
    pair = pltpu.VMEM((2, tokens, DPAD), BF16)
    copies = 4 + 4 + 6
    return pl.pallas_call(
        functools.partial(ffn_kernel, depth, rows),
        out_shape=[
            jax.ShapeDtypeStruct((2, 2, 2 * depth, pad, cols), BF16),
            jax.ShapeDtypeStruct((depth, pad, cols), BF16),
            jax.ShapeDtypeStruct((width, tokens), BF16),
            jax.ShapeDtypeStruct((tokens, DPAD), F32),
            jax.ShapeDtypeStruct((tokens, DPAD), BF16),
        ],
        in_specs=vmem_specs(3) + [pl.BlockSpec(memory_space=pl.ANY)] * 2,
        out_specs=[pl.BlockSpec(memory_space=pl.ANY)] + vmem_specs(4),
        scratch_shapes=[
            pltpu.VMEM((2, 2, depth, pad, 2 * cols), BF16),
            pltpu.VMEM((2, 2, depth, pad, cols), BF16),
            pltpu.VMEM((2, 2 * depth, pad, cols), BF16),
            pltpu.VMEM((3 * depth, pad, cols), BF16),
            token_rows, token_rows, wide, wide, wide, flipped, flipped,
            pltpu.VMEM((tokens, DPAD), F32), pair, pair,
            pltpu.VMEM((2, 2, 2 * depth, pad, cols), BF16),
            pltpu.SemaphoreType.DMA((copies,)),
            pltpu.SemaphoreType.DMA((copies,)),
            pltpu.SemaphoreType.DMA((5,)),
        ],
        compiler_params=pltpu.CompilerParams(
            vmem_limit_bytes=61 << 20, collective_id=1, has_side_effects=True
        ),
        cost_estimate=pl.CostEstimate(
            flops=24 << 30, bytes_accessed=30 << 20, transcendentals=2 << 20
        ),
        name="ffn",
    )(normed2, cot_t, middle, ffn_w, down_w)


def mid_kernel(
    depth, width,
    ffn_g, down_sum, grad_n2, middle, cot, gains, out_w, q, kv, attn, lse, seg,
    dq_t, dkv_sum, grad_middle, gain_grad, out_grad, gate_grad, up_grad, down_grad,
    mid_b, out_g, out_c, out_r, ffn_r, down_r, stage, grad_attn, q_t, g_t, q3, g3, k3, v3, k_t,
    delta, dkv, acc_kv, bias, kv_c, kv_y, send_sems, recv_sems, local_sems,
):
    tokens = q.shape[0]
    tiles = tokens // TILE
    back = 1024 // TILE
    rows = gate_grad.shape[0]
    pad = DPAD // (2 * depth)
    out_cols = HEADS * HEAD_DIM // 4
    p = Place(depth, send_sems, recv_sems)
    trim = lambda ref: ref.at[..., pl.ds(0, trimmed(rows, pad)), :]
    p.barrier()
    ffn_sums = [
        PlaneScatter(
            p, ffn_g.at[w], ffn_r.at[w], trim, stage.at[w], local_sems.at[pl.ds(3 * w, 3)]
        )
        for w in range(2)
    ]
    for w in range(2):
        ffn_sums[w].start()
    down_in = [
        p.copy(k, trim(down_sum.at[(p.z + k) % depth]), trim(down_r.at[k - 1]))
        for k in range(1, depth)
    ]

    gain = gains[1:2, :]
    gain_grad[...] = jnp.zeros_like(gain_grad)

    def norm_tile(start):
        span = pl.ds(start, TILE)
        mid, up = middle[span, :], grad_n2[span, :]
        inv = lax.rsqrt(mean_rows(mid * mid, width) + EPSILON)
        scaled = up * gain
        mean = mean_rows(scaled * mid, width)
        grad = cot[span, :].astype(F32) + inv * (scaled - mid * (inv * inv * mean))
        grad_middle[span, :] = grad
        gain_grad[...] += jnp.sum(up * mid * inv, axis=0, keepdims=True)
        mid_b[span, :] = grad.astype(BF16)
        for b in range(4):
            side = dot_nt(mid_b[span, :], out_w[b % 2, b // 2])
            grad_attn[span, b * out_cols : (b + 1) * out_cols] = side.astype(BF16)

    row_tiles(tokens, norm_tile)
    attn_t = attn[...].astype(F32).T
    for b in range(4):
        left = attn_t[b * out_cols : (b + 1) * out_cols, :].astype(BF16)
        spread_blocks(out_g.at[b % 2, b // 2], dot(left, mid_b[...]), pad)
    out_cross = p.copy("c", out_g.at[1 - p.c], out_c)

    g_t[...] = transposed(grad_attn[...])
    for h in range(HEADS):
        span = slice(h * HEAD_DIM, (h + 1) * HEAD_DIM)
        delta[h : h + 1, :] = jnp.sum(
            g_t[span, :].astype(F32) * attn_t[span, :], axis=0, keepdims=True
        )
        q3[h] = q[:, span]
        g3[h] = grad_attn[:, span]
    q_t[...] = transposed(q[...])
    for n in range(3):
        block = jnp.maximum(p.m - n, 0)
        span = pl.ds(pl.multiple_of(block * tokens, tokens), tokens)
        for g in range(KV_HEADS):
            part = kv[block, g]
            k_t[g * HEAD_DIM : (g + 1) * HEAD_DIM, span] = transposed(part)[:HEAD_DIM]
            k3[g, span, :] = part[:, :HEAD_DIM]
            v3[g, span, :] = part[:, HEAD_DIM:]
    dq_t[...] = jnp.zeros_like(dq_t)
    dkv[...] = jnp.zeros_like(dkv)

    def key_tile(t, queries):
        keys = pl.ds(pl.multiple_of(t * TILE, TILE), TILE)
        for i in queries:
            bias[i] = mask_tile(seg[0:1, i * TILE : (i + 1) * TILE], p.m * tiles + i, t)

        def group(g, carry):
            k_g, v_g = k3[g, keys, :], v3[g, keys, :]
            kt_g = k_t[pl.ds(pl.multiple_of(g * HEAD_DIM, HEAD_DIM), HEAD_DIM), keys]
            units = [(i, g * GROUP + j) for i in queries for j in range(GROUP)]
            places = [
                (pl.ds(pl.multiple_of(h * HEAD_DIM, HEAD_DIM), HEAD_DIM), pl.ds(i * TILE, TILE))
                for i, h in units
            ]
            dk, dv = None, None
            for (i, h), (span, cols) in zip(units, places):
                scores = dot(k_g, q_t[span, cols]) * EXP_SCALE + bias[i]
                probs = jnp.exp2(scores - lse[pl.ds(h, 1), cols])
                dprobs = dot(v_g, g_t[span, cols])
                dscores = (probs * (dprobs - delta[pl.ds(h, 1), cols])).astype(BF16)
                add_v = dot(probs.astype(BF16), g3[h, cols, :])
                add_k = dot(dscores, q3[h, cols, :])
                dq_t[span, cols] += dot(kt_g, dscores)
                dk = add_k if dk is None else dk + add_k
                dv = add_v if dv is None else dv + add_v
            acc_kv[g] = dk * SCORE_SCALE
            acc_kv[KV_HEADS + g] = dv
            return carry

        lax.fori_loop(0, KV_HEADS, group, 0)
        for n in range(2 * KV_HEADS):
            dkv[keys, n * HEAD_DIM : (n + 1) * HEAD_DIM] = acc_kv[n].astype(BF16)

    def key_span(low, high, queries):
        def step(t, carry):
            key_tile(t, queries)
            return carry

        lax.fori_loop(low, high, step, 0)

    def part_of(index):
        return dkv.at[pl.ds(pl.multiple_of(index * tokens, tokens), tokens)]

    first = p.m * tiles
    key_span(jnp.maximum(first - back, 0), jnp.maximum(first + 1 - back, 0), (0,))
    ffn_sums[0].forward()
    key_span(jnp.maximum(first + 1 - back, 0), jnp.maximum(first - 2, 0), (0, 1))
    ffn_sums[1].forward()
    key_span(jnp.maximum(first - 2, 0), jnp.maximum(first - 1, 0), (0, 1))
    ffn_sums[0].over_z()
    key_span(jnp.maximum(first - 1, 0), first, (0, 1))
    beside = p.m + 1 - 2 * p.c
    cross = [
        p.copy("c", part_of(index), kv_c.at[n])
        for n, index in enumerate((beside, (beside + 2) % 4))
    ]
    out_cross.wait_recv()
    own = out_g.at[p.c]
    own[...] = (own[...].astype(F32) + out_c[...].astype(F32)).astype(BF16)
    cross[1].wait_recv()
    away = part_of((p.m + 2) % 4)
    away[...] = (away[...].astype(F32) + kv_c[1].astype(F32)).astype(BF16)
    across = p.copy("y", away, kv_y)
    out_sum = PlaneScatter(p, own, out_r)
    out_sum.start()
    ffn_sums[1].over_z()
    key_tile(first + 1, (1,))
    key_span(first, first + 1, (0, 1))
    out_sum.forward()
    for w in range(2):
        (gate_grad, up_grad)[w][...] = ffn_sums[w].result()[:rows]
    value = down_sum[p.z].astype(F32)
    for k, made in enumerate(down_in):
        made.wait_recv()
        value += down_r[k].astype(F32)
    down_grad[...] = value[:rows]
    cross[0].wait_recv()
    out_sum.over_z()
    across.wait_recv()
    dkv_sum[...] = part_of(p.m)[...].astype(F32) + kv_c[0].astype(F32) + kv_y[...].astype(F32)
    out_grad[...] = one_block(out_sum.result(), rows, pad)
    for part in ffn_sums + [out_sum]:
        part.finish()
    for made in cross + [across, out_cross] + down_in:
        made.wait_send()


def middle_back(ffn_g, down_sum, grad_n2, middle, cot, gains, out_w, q, kv, attn, lse, seg,
                depth, rows, width):
    tokens, query_cols = q.shape
    pad = DPAD // (2 * depth)
    cols = ffn_g.shape[-1]
    kv_cols = KV_HEADS * kv.shape[-1]
    out_cols = query_cols // 4
    whole = 4 * tokens
    slots = scatter_slots(depth)
    copies = 3 * scatter_copies(depth) + 4 + depth - 1
    heads_q = pltpu.VMEM((HEADS, tokens, HEAD_DIM), BF16)
    heads_kv = pltpu.VMEM((KV_HEADS, whole, HEAD_DIM), BF16)
    flipped = pltpu.VMEM((query_cols, tokens), BF16)
    return pl.pallas_call(
        functools.partial(mid_kernel, depth, width),
        out_shape=[
            jax.ShapeDtypeStruct((query_cols, tokens), F32),
            jax.ShapeDtypeStruct((tokens, kv_cols), F32),
            jax.ShapeDtypeStruct((tokens, DPAD), F32),
            jax.ShapeDtypeStruct((1, DPAD), F32),
            jax.ShapeDtypeStruct((out_cols, rows), F32),
            *[jax.ShapeDtypeStruct((rows, cols), F32)] * 3,
        ],
        in_specs=[pl.BlockSpec(memory_space=pl.ANY)] + vmem_specs(11),
        out_specs=vmem_specs(8),
        scratch_shapes=[
            pltpu.VMEM((tokens, DPAD), BF16),
            pltpu.VMEM((2, 2, 2 * depth, *block_shape(out_cols, pad)), BF16),
            pltpu.VMEM((2, 2 * depth, *block_shape(out_cols, pad)), BF16),
            pltpu.VMEM((slots, *block_shape(out_cols, pad)), BF16),
            pltpu.VMEM((2, slots, pad, cols), BF16),
            pltpu.VMEM((depth - 1, pad, cols), BF16),
            pltpu.VMEM((2, 2 * depth, pad, cols), BF16),
            pltpu.VMEM((tokens, query_cols), BF16),
            flipped, flipped, heads_q, heads_q, heads_kv, heads_kv,
            pltpu.VMEM((KV_HEADS * HEAD_DIM, whole), BF16),
            pltpu.VMEM((HEADS + 1, tokens), F32),
            pltpu.VMEM((whole, kv_cols), BF16),
            pltpu.VMEM((2 * KV_HEADS, TILE, HEAD_DIM), F32),
            pltpu.VMEM((tokens // TILE, TILE, TILE), F32),
            pltpu.VMEM((2, tokens, kv_cols), BF16),
            pltpu.VMEM((tokens, kv_cols), BF16),
            pltpu.SemaphoreType.DMA((copies,)),
            pltpu.SemaphoreType.DMA((copies,)),
            pltpu.SemaphoreType.DMA((6,)),
        ],
        compiler_params=pltpu.CompilerParams(
            vmem_limit_bytes=61 << 20, collective_id=2, has_side_effects=True
        ),
        cost_estimate=pl.CostEstimate(
            flops=40 << 30, bytes_accessed=50 << 20, transcendentals=8 << 20
        ),
        name="middle_back",
    )(ffn_g, down_sum, grad_n2, middle, cot, gains, out_w, q, kv, attn, lse, seg)


def tail_kernel(
    depth, rows, width,
    dq_t, dkv, cosine_t, sine_t, x_t, grad_middle, gains, in_w, gain2,
    grad_hidden, in_grad, gain1_sum, gain2_sum,
    proj, proj_b, in_g, in_c, in_r, grad_x, gain_own, gain_r, send_sems, recv_sems,
):
    query_cols, tokens = dq_t.shape
    in_cols = in_w.shape[2]
    pad = DPAD // (2 * depth)
    turned = (HEADS + KV_HEADS) * HEAD_DIM
    p = Place(depth, send_sems, recv_sems)
    p.barrier()
    x_f = widen(x_t, depth, rows, pad)
    gain = gains[0:1, :]
    inv = lax.rsqrt(mean_rows(x_f * x_f, width) + EPSILON)
    normed1 = (x_f * inv * gain).astype(BF16)
    cosine = lane_tables(cosine_t[...])
    sine = signed(lane_tables(sine_t[...]), True)
    proj[:, :query_cols] = dq_t[...].T * SCORE_SCALE
    proj[:, query_cols:] = dkv[...]
    for j in range(turned // 128):
        lanes = slice(128 * j, 128 * (j + 1))
        proj[:, lanes] = rope(proj[:, lanes], cosine, sine)
    for b in range(4):
        proj_b[b] = proj[:, b * in_cols : (b + 1) * in_cols].astype(BF16)
    for other in (1, 0):
        c = (1 - p.c) if other else p.c
        for y in range(2):
            left = transposed(proj_b[2 * y + c])
            spread_blocks(in_g.at[c, y], dot(left, normed1), pad)
        if other:
            in_cross = p.copy("c", in_g.at[c], in_c)
    in_cross.wait_recv()
    own = in_g.at[p.c]
    own[...] = (own[...].astype(F32) + in_c[...].astype(F32)).astype(BF16)
    in_sum = PlaneScatter(p, own, in_r)
    in_sum.start()
    up = None
    for b in range(4):
        term = dot(proj_b[b], in_w[b % 2, b // 2])
        up = term if up is None else up + term
    scaled = up * gain
    mean = mean_rows(scaled * x_f, width)
    grad_x[...] = grad_middle[...] + inv * (scaled - x_f * (inv * inv * mean))
    gain_own[...] = jnp.zeros_like(gain_own)
    gain_own[0:1, :] = jnp.sum(up * x_f * inv, axis=0, keepdims=True)
    gain_own[1:2, :] = gain2[...]
    in_sum.forward()
    sent = []
    for n, kind in enumerate(("c", "y", "x")):
        made = p.copy(kind, gain_own.at[pl.ds(8 * n, 8)], gain_r.at[pl.ds(8 * n, 8)])
        sent.append(made)
        if n == 0:
            narrow(grad_hidden, grad_x[...], depth, rows, pad)
        made.wait_recv()
        if n == 1:
            in_sum.over_z()
        gain_own[8 * (n + 1) : 8 * (n + 2), :] = (
            gain_own[8 * n : 8 * (n + 1), :] + gain_r[8 * n : 8 * (n + 1), :]
        )
    last = gain_own.at[pl.ds(24, 8)]
    arriving = [p.copy(k, last, gain_r.at[pl.ds(24 + 8 * k, 8)]) for k in range(1, depth)]
    total = last[...]
    for k, made in enumerate(arriving):
        made.wait_recv()
        total += gain_r[32 + 8 * k : 40 + 8 * k, :]
    mine = jnp.zeros((8, pad), F32)
    for n in range(2 * depth):
        mine = jnp.where(n == p.x * depth + p.z, total[:, n * pad : (n + 1) * pad], mine)
    gain1_sum[...] = mine[0:1, :rows]
    gain2_sum[...] = mine[1:2, :rows]
    in_grad[...] = one_block(in_sum.result(), rows, pad)
    in_sum.finish()
    for made in sent + arriving + [in_cross]:
        made.wait_send()


def tail(dq_t, dkv, cosine_t, sine_t, x_t, grad_middle, gains, in_w, gain2, depth, rows, width):
    tokens = dq_t.shape[1]
    pad = DPAD // (2 * depth)
    in_cols = in_w.shape[2]
    total = dq_t.shape[0] + dkv.shape[1]
    slots = scatter_slots(depth)
    copies = scatter_copies(depth) + 1 + 3 + depth - 1
    return pl.pallas_call(
        functools.partial(tail_kernel, depth, rows, width),
        out_shape=[
            jax.ShapeDtypeStruct((width, tokens), F32),
            jax.ShapeDtypeStruct((in_cols, rows), F32),
            *[jax.ShapeDtypeStruct((1, rows), F32)] * 2,
        ],
        in_specs=vmem_specs(9),
        out_specs=vmem_specs(4),
        scratch_shapes=[
            pltpu.VMEM((tokens, total), F32),
            pltpu.VMEM((4, tokens, in_cols), BF16),
            pltpu.VMEM((2, 2, 2 * depth, *block_shape(in_cols, pad)), BF16),
            pltpu.VMEM((2, 2 * depth, *block_shape(in_cols, pad)), BF16),
            pltpu.VMEM((slots, *block_shape(in_cols, pad)), BF16),
            pltpu.VMEM((tokens, DPAD), F32),
            pltpu.VMEM((32, DPAD), F32),
            pltpu.VMEM((24 + 8 * depth, DPAD), F32),
            pltpu.SemaphoreType.DMA((copies,)),
            pltpu.SemaphoreType.DMA((copies,)),
        ],
        compiler_params=pltpu.CompilerParams(
            vmem_limit_bytes=61 << 20, collective_id=3, has_side_effects=True
        ),
        cost_estimate=pl.CostEstimate(
            flops=8 << 30, bytes_accessed=30 << 20, transcendentals=0
        ),
        name="tail",
    )(dq_t, dkv, cosine_t, sine_t, x_t, grad_middle, gains, in_w, gain2)


def rotary_tables(position_ids):
    half_dim = HEAD_DIM // 2
    frequency = jnp.exp(
        jnp.arange(half_dim, dtype=F32) * (-2.0 * math.log(10000.0) / HEAD_DIM)
    )
    angles = frequency[:, None] * position_ids.astype(F32)[None, :]
    return jnp.cos(angles), jnp.sin(angles)


def per_device(
    hidden_in, cotangent, segments, positions, attn_in, attn_out, w_gate, w_up, w_down,
    norm1_gain, norm2_gain,
):
    tokens, width = hidden_in.shape[1:]
    dp_size = lax.axis_size("dp")
    depth = dp_size // 2
    rows = width // dp_size
    pad = DPAD // dp_size

    ffn_blocks = [w_gate, w_up, w_down.T]
    if trimmed(rows, pad) == pad:
        ffn_blocks = [jnp.pad(w, ((0, pad - rows), (0, 0))) for w in ffn_blocks]
    x_t, cot_t = hidden_in[0].T, cotangent[0].T
    cosine_t, sine_t = rotary_tables(positions[0])
    attn, lse, middle, normed2, gains, seg, q, kv, out_w, in_w, ffn_w, down_w = front(
        attn_in.T, attn_out, norm1_gain[None], norm2_gain[None], *ffn_blocks,
        x_t, cosine_t, sine_t, segments, depth, rows,
    )
    ffn_g, down_sum, hidden_out, grad_n2, cot = ffn(normed2, cot_t, middle, ffn_w, down_w, rows)
    dq_t, dkv, grad_middle, gain2, g_out, g_gate, g_up, g_down = middle_back(
        ffn_g, down_sum, grad_n2, middle, cot, gains, out_w, q, kv, attn, lse, seg,
        depth, rows, width,
    )
    grad_hidden, g_in, *gain_sums = tail(
        dq_t, dkv, cosine_t, sine_t, x_t, grad_middle, gains, in_w, gain2, depth, rows, width
    )
    return (
        hidden_out.T[None],
        grad_hidden.T[None],
        g_in.T,
        g_out,
        g_gate,
        g_up,
        g_down.T,
        gain_sums[0][0],
        gain_sums[1][0],
    )


def solution(mesh):
    return jax.shard_map(
        per_device,
        mesh=mesh,
        in_specs=(
            P("dp", "mp", None),
            P("dp", "mp", None),
            P("dp", None),
            P("dp", "mp"),
            P("dp", "mp"),
            P("mp", "dp"),
            P("dp", "mp"),
            P("dp", "mp"),
            P("mp", "dp"),
            P("dp"),
            P("dp"),
        ),
        out_specs=(
            P("dp", "mp", None),
            P("dp", "mp", None),
            P("dp", "mp"),
            P("mp", "dp"),
            P("dp", "mp"),
            P("dp", "mp"),
            P("mp", "dp"),
            P("dp"),
            P("dp"),
        ),
        check_vma=False,
    )
```

```python
import functools
import math

import jax
import jax.numpy as jnp
from jax import lax
from jax.experimental import pallas as pl
from jax.experimental.pallas import tpu as pltpu
from jax.sharding import PartitionSpec as P

HEADS = 15
KV_HEADS = 5
GROUP = HEADS // KV_HEADS
HEAD_DIM = 64
DPAD = 1024
TILE = 256
EPSILON = 1e-05
SCORE_SCALE = 0.125
MASK_FILL = -1e30
LOG2E = 1.4426950408889634
EXP_SCALE = SCORE_SCALE * LOG2E
GAIN_ROWS = 16
BF16 = jnp.bfloat16
F32 = jnp.float32


def dot(a, b):
    return jnp.dot(a, b, preferred_element_type=F32)


def dot_nt(a, b):
    return lax.dot_general(a, b, (((1,), (1,)), ((), ())), preferred_element_type=F32)


def vmem_specs(count):
    return [pl.BlockSpec(memory_space=pltpu.VMEM)] * count


def transposed(value):
    return value.astype(F32).T.astype(BF16)


class Place:
    def __init__(self, depth, send_sems, recv_sems):
        dp_index, m = lax.axis_index("dp"), lax.axis_index("mp")
        self.depth = depth
        self.z, self.x = dp_index // 2, dp_index % 2
        self.m, self.y, self.c = m, m // 2, m % 2
        self.send_sems, self.recv_sems = send_sems, recv_sems
        self.count = 0

    def peer(self, kind):
        z, x, y, c = self.z, self.x, self.y, self.c
        if kind == "x":
            x = 1 - x
        elif kind == "y":
            y = 1 - y
        elif kind == "c":
            c = 1 - c
        else:
            z = (z + kind) % self.depth
        return 2 * z + x, 2 * y + c

    def kinds(self):
        return ["x", "y", "c"] + list(range(1, self.depth))

    def barrier(self, kinds=None):
        semaphore = pltpu.get_barrier_semaphore()
        kinds = kinds or self.kinds()
        for kind in kinds:
            pl.semaphore_signal(
                semaphore, inc=1, device_id=self.peer(kind), device_id_type=pl.DeviceIdType.MESH
            )
        pl.semaphore_wait(semaphore, len(kinds))

    def copy(self, kind, source, target=None):
        index = self.count
        self.count += 1
        made = pltpu.make_async_remote_copy(
            src_ref=source,
            dst_ref=source if target is None else target,
            send_sem=self.send_sems.at[index],
            recv_sem=self.recv_sems.at[index],
            device_id=self.peer(kind),
            device_id_type=pl.DeviceIdType.MESH,
        )
        made.start()
        return made


class PlaneGather:
    def __init__(self, place, source, buffer, by_x, part=lambda ref: ref):
        self.place, self.source, self.buffer, self.part = place, source, buffer, part
        self.split = place.depth - by_x
        self.sent, self.last = [], []

    def over_z(self, slot=None):
        p = self.place
        slot = self.part(self.buffer.at[p.y, p.x, p.z]) if slot is None else slot
        self.arriving = [p.copy(k, self.source, slot) for k in range(1, p.depth)]
        self.sent += self.arriving

    def stacked(self):
        for made in self.arriving:
            made.wait_recv()

    def over_x(self):
        p = self.place
        self.by_x = p.copy("x", self.part(self.buffer.at[p.y, p.x]))
        self.sent.append(self.by_x)

    def over_y(self):
        p = self.place
        self.by_y = p.copy("y", self.part(self.buffer.at[p.y, p.x]))
        self.sent.append(self.by_y)

    def diagonal_x(self):
        p = self.place
        self.by_y.wait_recv()
        span = pl.ds(self.split, p.depth - self.split)
        self.last.append(p.copy("x", self.part(self.buffer.at[1 - p.y, p.x, span])))

    def diagonal_y(self):
        p = self.place
        self.by_x.wait_recv()
        if self.split:
            span = pl.ds(0, self.split)
            self.last.append(p.copy("y", self.part(self.buffer.at[p.y, 1 - p.x, span])))

    def arrived(self):
        for made in self.last:
            made.wait_recv()

    def finish(self):
        for made in self.sent + self.last:
            made.wait_send()


def rope(value, cosine, sine):
    lane = lax.broadcasted_iota(jnp.int32, value.shape, 1)
    half = HEAD_DIM // 2
    partner = jnp.where(
        lane % HEAD_DIM < half, pltpu.roll(value, 128 - half, 1), pltpu.roll(value, half, 1)
    )
    return value * cosine + partner * sine


def trimmed(rows, pad):
    return rows if rows % 8 == 0 else pad


def natural(block, depth):
    return 2 * (block % depth) + block // depth


def widen(source, depth, rows, pad):
    filler = jnp.zeros((pad - rows, source.shape[1]), F32)
    parts = []
    for b in range(2 * depth):
        first = natural(b, depth) * rows
        parts += [source[first : first + rows, :].astype(F32), filler]
    return jnp.concatenate(parts, axis=0).T


def narrow(target, value, depth, rows, pad):
    flipped = value.T
    for b in range(2 * depth):
        first = natural(b, depth) * rows
        target[first : first + rows, :] = flipped[b * pad : b * pad + rows, :].astype(target.dtype)


def side_by_side(ref, first, size):
    _, depth, _, pad = ref.shape
    span = pl.ds(first, size)
    return jnp.concatenate(
        [ref[b // depth, b % depth, span, :] for b in range(2 * depth)], axis=1
    )


def lane_tables(table):
    return jnp.concatenate([table] * (256 // HEAD_DIM), axis=0).T


def signed(table, back):
    lane = lax.broadcasted_iota(jnp.int32, table.shape, 1) % HEAD_DIM
    first = lane < HEAD_DIM // 2
    return jnp.where(first, table, -table) if back else jnp.where(first, -table, table)


def mean_rows(value, width):
    return jnp.sum(value, axis=-1, keepdims=True) * (1.0 / width)


def mask_tile(start, query_tile, key_tile):
    key = key_tile * TILE + lax.broadcasted_iota(jnp.int32, (TILE, TILE), 0)
    query = query_tile * TILE + lax.broadcasted_iota(jnp.int32, (TILE, TILE), 1)
    return jnp.where((key >= start) & (key <= query), 0.0, MASK_FILL)


def front_kernel(
    depth, rows, width, in_cols,
    attn_in_t, attn_out, gain_one, gain_two, w_gate, w_up, w_down_t, x_t, cosine_t, sine_t, segments,
    attn, lse, middle, normed2, gains, seg, q_out, kv_out, out_w_out, in_w_out, ffn_w, down_w,
    q, kv, out_w, in_w, a_buf, x_in, cosine, sine, normed1, proj, q_t, k3, v_t, acc, peak, total,
    biases, send_sems, recv_sems, local_sems,
):
    tokens = x_in.shape[0]
    tiles = tokens // TILE
    back = 1024 // TILE
    pad = DPAD // (2 * depth)
    lead = in_cols + GAIN_ROWS
    query_cols = HEADS * HEAD_DIM
    out_cols = query_cols // 4
    p = Place(depth, send_sems, recv_sems)
    block = a_buf.at[p.c, p.y, p.x, p.z]
    block[...] = jnp.zeros_like(block)
    block[0:in_cols, 0:rows] = attn_in_t[...]
    block[in_cols : in_cols + 1, 0:rows] = gain_one[...]
    block[in_cols + 1 : in_cols + 2, 0:rows] = gain_two[...]
    block[lead : lead + out_cols, 0:rows] = attn_out[...]
    moved = pl.ds(0, trimmed(rows, pad))
    trim = lambda ref: ref.at[..., moved, :]
    own = [
        pltpu.make_async_copy(
            source, trim(ffn_w.at[w, p.y, p.x, p.z] if w < 2 else down_w.at[p.z]), local_sems.at[w]
        )
        for w, source in enumerate((w_gate, w_up, w_down_t))
    ]
    for made in own:
        made.start()
    p.barrier()
    first_part = lambda ref: ref.at[..., pl.ds(0, lead), :]
    last_part = lambda ref: ref.at[..., pl.ds(lead, out_cols), :]
    buffer = a_buf.at[p.c]
    plane = PlaneGather(p, first_part(block), buffer, depth // 2, first_part)
    output = PlaneGather(p, last_part(block), buffer, depth // 2, last_part)
    gate = PlaneGather(p, w_gate, ffn_w.at[0], depth, trim)
    up = PlaneGather(p, w_up, ffn_w.at[1], depth // 2, trim)
    down = PlaneGather(p, w_down_t, None, 0)
    plane.over_z()
    x_f = widen(x_t, depth, rows, pad)
    x_in[...] = x_f.astype(BF16)
    cosine[...] = lane_tables(cosine_t[...])
    sine[...] = signed(lane_tables(sine_t[...]), False)
    inv_one = lax.rsqrt(mean_rows(x_f * x_f, width) + EPSILON)
    own_seg = segments[:, pl.ds(pl.multiple_of(p.m * tokens, tokens), tokens)]
    start = jnp.zeros_like(own_seg)
    for n in range(3):
        count = jnp.sum((segments[...] == n).astype(jnp.int32), axis=1, keepdims=True)
        start += jnp.where(own_seg > n, count, 0)
    seg[...] = start
    plane.stacked()
    plane.over_x()
    plane.over_y()
    output.over_z()
    gate.over_z()
    plane.diagonal_y()
    plane.diagonal_x()
    for made in own:
        made.wait()
    up.over_z()
    plane.arrived()
    cross = p.copy("c", first_part(a_buf.at[p.c]))
    output.stacked()
    output.over_x()
    output.over_y()
    gate.stacked()
    gate.over_x()
    gate.over_y()
    cross.wait()
    for b in range(2 * depth):
        gains[:, b * pad : (b + 1) * pad] = a_buf[
            0, 0, b // depth, b % depth, pl.ds(in_cols, 2), :
        ].astype(F32)
    normed1[...] = (x_f * inv_one * gains[0:1, :]).astype(BF16)
    for b in range(4):
        in_w[b % 2, b // 2] = side_by_side(a_buf.at[b % 2, b // 2], 0, in_cols)

    kv_first = query_cols // 128

    def project(blocks, groups):
        def tile(start):
            span = pl.ds(start, TILE)
            for b in blocks:
                proj[span, b * in_cols : (b + 1) * in_cols] = dot_nt(
                    normed1[span, :], in_w[b % 2, b // 2]
                )
            for j in groups:
                lanes = slice(128 * j, 128 * (j + 1))
                proj[span, lanes] = rope(proj[span, lanes], cosine[span, :], sine[span, :])

        row_tiles(tokens, tile)

    project((2, 3), range(kv_first, (HEADS + KV_HEADS) * HEAD_DIM // 128))
    for g in range(KV_HEADS):
        k_first, v_first = query_cols + g * HEAD_DIM, query_cols + (KV_HEADS + g) * HEAD_DIM
        kv[p.m, g] = jnp.concatenate(
            [proj[:, k_first : k_first + HEAD_DIM], proj[:, v_first : v_first + HEAD_DIM]], axis=1
        ).astype(BF16)
    kv_c = p.copy("c", kv.at[p.m])
    kv_y = [p.copy("y", kv.at[p.m, g]) for g in range(KV_HEADS)]
    down.over_z(trim(down_w.at[p.z]))
    project((0, 1), range(kv_first))
    q[...] = proj[:, :query_cols].astype(BF16)
    q_t[...] = proj[:, :query_cols].T.astype(BF16)
    saved = [
        pltpu.make_async_copy(source, target, local_sems.at[3 + n])
        for n, (source, target) in enumerate(((in_w, in_w_out), (q, q_out)))
    ]
    for made in saved:
        made.start()
    acc[...] = jnp.zeros_like(acc)
    peak[...] = jnp.full_like(peak, MASK_FILL)
    total[...] = jnp.zeros_like(total)

    def spread(block, g):
        span = pl.ds(pl.multiple_of(block * tokens, tokens), tokens)
        part = kv[block, g]
        v_t[g * HEAD_DIM : (g + 1) * HEAD_DIM, span] = transposed(part)[HEAD_DIM:]
        k3[g, span, :] = part[:, :HEAD_DIM]

    def attend_unit(i, t, g, bias):
        cols = pl.ds(i * TILE, TILE)
        keys = pl.ds(pl.multiple_of(t * TILE, TILE), TILE)
        k_g = k3[g, keys, :]
        v_g = v_t[pl.ds(pl.multiple_of(g * HEAD_DIM, HEAD_DIM), HEAD_DIM), keys]
        heads = [g * GROUP + j for j in range(GROUP)]
        places = [pl.ds(pl.multiple_of(h * HEAD_DIM, HEAD_DIM), HEAD_DIM) for h in heads]
        old = [peak[pl.ds(h, 1), cols] for h in heads]
        sums = [total[pl.ds(h, 1), cols] for h in heads]
        accs = [acc[s, cols] for s in places]
        scores = [dot(k_g, q_t[s, cols]) + bias[...] for s in places]
        new = [jnp.maximum(o, jnp.max(s, axis=0, keepdims=True)) for o, s in zip(old, scores)]
        probs = [jnp.exp2(s * EXP_SCALE - n * EXP_SCALE) for s, n in zip(scores, new)]
        scale = [jnp.exp2((o - n) * EXP_SCALE) for o, n in zip(old, new)]
        outs = [dot(v_g, b.astype(BF16)) for b in probs]
        for j, h in enumerate(heads):
            peak[pl.ds(h, 1), cols] = new[j]
            total[pl.ds(h, 1), cols] = sums[j] * scale[j] + jnp.sum(
                probs[j], axis=0, keepdims=True
            )
            acc[places[j], cols] = accs[j] * scale[j] + outs[j]

    first_tile = p.m * tiles

    def bias_tile(i, t, slot):
        biases[i, slot] = mask_tile(seg[0:1, i * TILE : (i + 1) * TILE], first_tile + i, t)

    for g in range(KV_HEADS):
        spread(p.m, g)
    for i in range(tiles):
        for t in range(i + 1):
            bias_tile(i, first_tile + t, 0)

            def group(g, carry):
                attend_unit(i, first_tile + t, g, biases.at[i, 0])
                return carry

            lax.fori_loop(0, KV_HEADS, group, 0)
        if i == 0:
            up.stacked()
            up.over_x()
            output.diagonal_x()
            output.diagonal_y()

    lows = [jnp.maximum(first_tile + i - back, 0) for i in range(tiles)]
    for i in range(tiles):

        def fill(t, carry):
            bias_tile(i, t, t - lows[i])
            return carry

        lax.fori_loop(lows[i], first_tile, fill, 0)
    kv_cy = []

    def pass_on(g):
        kv_y[g].wait_recv()
        kv_cy.append(p.copy("c", kv.at[(p.m + 2) % 4, g]))

    kv_c.wait_recv()
    pass_on(0)
    gate.diagonal_x()
    gate.diagonal_y()
    for g in range(KV_HEADS):
        if g + 1 < KV_HEADS:
            pass_on(g + 1)
        if g == 1:
            up.over_y()
            up.diagonal_y()
        if g == 2:
            output.arrived()
            out_cross = p.copy("c", last_part(a_buf.at[p.c]))
        kv_cy[g].wait_recv()
        for n in (1, 2):
            spread(jnp.maximum(p.m - n, 0), g)
        for i in range(tiles):

            def step(t, carry):
                attend_unit(i, t, g, biases.at[i, t - lows[i]])
                return carry

            lax.fori_loop(lows[i], first_tile, step, 0)
    saved.append(pltpu.make_async_copy(kv, kv_out, local_sems.at[5]))
    saved[-1].start()
    for h in range(HEADS):
        span = pl.ds(h * HEAD_DIM, HEAD_DIM)
        acc[span, :] = acc[span, :] / total[h : h + 1, :]
    attn[...] = acc[...].T.astype(BF16)
    lse[...] = peak[...] * EXP_SCALE + jnp.log2(jnp.maximum(total[...], 1e-37))
    out_cross.wait()
    for b in range(4):
        out_w[b % 2, b // 2] = side_by_side(a_buf.at[b % 2, b // 2], lead, out_cols)
    saved.append(pltpu.make_async_copy(out_w, out_w_out, local_sems.at[6]))
    saved[-1].start()
    up.diagonal_x()

    def project_out(r, carry):
        span = pl.ds(pl.multiple_of(r * TILE, TILE), TILE)
        mid = x_in[span, :].astype(F32)
        for b in range(4):
            mid += dot(attn[span, b * out_cols : (b + 1) * out_cols], out_w[b % 2, b // 2])
        middle[span, :] = mid
        inv = lax.rsqrt(mean_rows(mid * mid, width) + EPSILON)
        normed2[span, :] = (mid * inv * gains[1:2, :]).astype(BF16)
        return carry

    lax.fori_loop(0, tiles, project_out, 0)
    gate.arrived()
    up.arrived()
    down.stacked()
    for part in (plane, output, gate, up, down):
        part.finish()
    for made in kv_y + kv_cy + [kv_c]:
        made.wait_send()
    for made in saved:
        made.wait()


def front(
    attn_in_t, attn_out, gain_one, gain_two, w_gate, w_up, w_down_t, x_t, cosine_t, sine_t,
    segments, depth, rows,
):
    width, tokens = x_t.shape
    pad = DPAD // (2 * depth)
    in_cols, cols = attn_in_t.shape[0], w_gate.shape[1]
    a_rows = in_cols + GAIN_ROWS + attn_out.shape[0]
    query_cols, kv_cols = HEADS * HEAD_DIM, 2 * KV_HEADS * HEAD_DIM
    whole = 4 * tokens
    copies = 5 * (depth - 1) + 4 * 4 + 3 + 2 * KV_HEADS
    anywhere = pl.BlockSpec(memory_space=pl.ANY)
    kept = [
        (tokens, query_cols),
        (4, KV_HEADS, tokens, 2 * HEAD_DIM),
        (2, 2, query_cols // 4, DPAD),
        (2, 2, in_cols, DPAD),
    ]
    return pl.pallas_call(
        functools.partial(front_kernel, depth, rows, width, in_cols),
        out_shape=[
            jax.ShapeDtypeStruct((tokens, query_cols), BF16),
            jax.ShapeDtypeStruct((HEADS + 1, tokens), F32),
            jax.ShapeDtypeStruct((tokens, DPAD), F32),
            jax.ShapeDtypeStruct((tokens, DPAD), BF16),
            jax.ShapeDtypeStruct((2, DPAD), F32),
            jax.ShapeDtypeStruct((1, tokens), jnp.int32),
            *[jax.ShapeDtypeStruct(shape, BF16) for shape in kept],
            jax.ShapeDtypeStruct((2, 2, 2, depth, pad, cols), BF16),
            jax.ShapeDtypeStruct((depth, pad, cols), BF16),
        ],
        in_specs=vmem_specs(4) + [anywhere] * 3 + vmem_specs(4),
        out_specs=vmem_specs(6) + [anywhere] * 6,
        scratch_shapes=[
            *[pltpu.VMEM(shape, BF16) for shape in kept],
            pltpu.VMEM((2, 2, 2, depth, a_rows, pad), BF16),
            pltpu.VMEM((tokens, DPAD), BF16),
            pltpu.VMEM((tokens, 128), F32),
            pltpu.VMEM((tokens, 128), F32),
            pltpu.VMEM((tokens, DPAD), BF16),
            pltpu.VMEM((tokens, query_cols + kv_cols), F32),
            pltpu.VMEM((query_cols, tokens), BF16),
            pltpu.VMEM((KV_HEADS, whole, HEAD_DIM), BF16),
            pltpu.VMEM((KV_HEADS * HEAD_DIM, whole), BF16),
            pltpu.VMEM((query_cols, tokens), F32),
            pltpu.VMEM((HEADS + 1, tokens), F32),
            pltpu.VMEM((HEADS + 1, tokens), F32),
            pltpu.VMEM((tokens // TILE, 1024 // TILE, TILE, TILE), F32),
            pltpu.SemaphoreType.DMA((copies,)),
            pltpu.SemaphoreType.DMA((copies,)),
            pltpu.SemaphoreType.DMA((7,)),
        ],
        compiler_params=pltpu.CompilerParams(
            vmem_limit_bytes=58 << 20, collective_id=0, has_side_effects=True
        ),
        cost_estimate=pl.CostEstimate(
            flops=20 << 30, bytes_accessed=40 << 20, transcendentals=8 << 20
        ),
        name="front",
    )(
        attn_in_t, attn_out, gain_one, gain_two, w_gate, w_up, w_down_t, x_t, cosine_t, sine_t,
        segments,
    )


class PlaneScatter:
    def __init__(
        self, place, source, recv, part=lambda ref: ref, stage=None, local_sems=None
    ):
        self.place, self.source, self.recv, self.part = place, source, recv, part
        p, half = place, place.depth // 2
        self.half = half
        places = [(p.y, 1 - p.x, 0, half), (1 - p.y, p.x, half, half), (p.y, p.x, 0, p.depth)]
        views = [
            source.at[y, pl.ds(x * p.depth + first, size)] for y, x, first, size in places
        ]
        self.loads = []
        if stage is None:
            self.by_x, self.by_y, self.total = views
        else:
            self.by_x, self.by_y = stage.at[pl.ds(0, half)], stage.at[pl.ds(half, half)]
            self.total = stage.at[pl.ds(p.depth, p.depth)]
            for n, (view, kept) in enumerate(zip(views, (self.by_x, self.by_y, self.total))):
                self.loads.append(pltpu.make_async_copy(view, kept, local_sems.at[n]))

    def slot(self, n):
        return self.recv.at[pl.ds(n * self.half, self.half)]

    def copy(self, kind, source, slot):
        return self.place.copy(kind, self.part(source), self.part(slot))

    def start(self):
        p, half = self.place, self.half
        for load in self.loads:
            load.start()
        far, here, there = (1 - p.x) * p.depth, p.x * p.depth, 1 - p.y
        self.far_y = self.copy("y", self.source.at[there, pl.ds(far, half)], self.slot(0))
        self.far_x = self.copy("x", self.source.at[there, pl.ds(far + half, half)], self.slot(1))
        self.near_y = self.copy("y", self.source.at[there, pl.ds(here, half)], self.slot(2))
        self.near_x = self.copy("x", self.source.at[p.y, pl.ds(far + half, half)], self.slot(3))
        self.sent = [self.far_y, self.far_x, self.near_y, self.near_x]

    def forward(self):
        p = self.place
        for load in self.loads:
            load.wait()
        self.far_y.wait_recv()
        self.by_x[...] = (self.by_x[...].astype(F32) + self.slot(0)[...].astype(F32)).astype(BF16)
        self.last_x = self.copy("x", self.by_x, self.slot(4))
        self.far_x.wait_recv()
        self.by_y[...] = (self.by_y[...].astype(F32) + self.slot(1)[...].astype(F32)).astype(BF16)
        self.last_y = self.copy("y", self.by_y, self.slot(5))
        self.sent += [self.last_x, self.last_y]

    def add(self):
        half = self.half
        for made in (self.near_y, self.near_x, self.last_x, self.last_y):
            made.wait_recv()
        for first, slots in ((0, (2, 4)), (half, (3, 5))):
            span = self.total.at[pl.ds(first, half)]
            terms = [self.slot(n)[...].astype(F32) for n in slots]
            span[...] = (span[...].astype(F32) + terms[0] + terms[1]).astype(BF16)

    def over_z(self):
        p, half = self.place, self.half
        self.add()
        self.arriving = [
            self.copy(
                k, self.total.at[(p.z + k) % p.depth], self.recv.at[6 * half + k - 1]
            )
            for k in range(1, p.depth)
        ]
        self.sent += self.arriving

    def result(self):
        value = self.total[self.place.z].astype(F32)
        for k, made in enumerate(self.arriving):
            made.wait_recv()
            value += self.recv[6 * self.half + k].astype(F32)
        return value

    def finish(self):
        for made in self.sent:
            made.wait_send()


def block_shape(size, pad):
    return (size, pad) if pad % 128 == 0 else (pad, size)


def spread_blocks(target, value, pad):
    if pad % 128 == 0:
        for n in range(DPAD // pad):
            target[n] = value[:, n * pad : (n + 1) * pad].astype(BF16)
    else:
        flipped = value.T.astype(BF16)
        for n in range(DPAD // pad):
            target[n] = flipped[n * pad : (n + 1) * pad]


def one_block(value, rows, pad):
    return (value if pad % 128 == 0 else value.T)[:, :rows]


def scatter_slots(depth):
    return 3 * depth + depth - 1


def scatter_copies(depth):
    return 6 + depth - 1


def store_blocks(ref, start, value):
    pad = ref.shape[1]
    for k in range(TILE // pad):
        ref[start // pad + k] = value[k * pad : (k + 1) * pad]


def row_tiles(count, body):
    def step(r, carry):
        body(pl.multiple_of(r * TILE, TILE))
        return carry

    lax.fori_loop(0, count // TILE, step, 0)


def ffn_kernel(
    depth, rows, normed2, cot_t, middle, ffn_w, down_w, grads, down_sum, hidden_out, grad_n2, cot,
    wide_w, down_buf, down_g, down_r, n_other, c_other, hid, d_gate, d_up, n_t, c_t, ffn_own, parts,
    received, packed, send_sems, recv_sems, local_sems,
):
    tokens = normed2.shape[0]
    cols = ffn_w.shape[-1]
    p = Place(depth, send_sems, recv_sems)
    pad = DPAD // (2 * depth)
    count = trimmed(rows, pad)
    moved = pl.ds(0, count)
    trim = lambda ref: ref.at[..., moved, :]
    loads = [
        pltpu.make_async_copy(
            trim(ffn_w.at[w, y]),
            wide_w.at[w, :, :, moved, pl.ds(y * cols, cols)],
            local_sems.at[2 * w + y],
        )
        for w in range(2)
        for y in range(2)
    ]
    loads.append(
        pltpu.make_async_copy(trim(down_w), trim(down_buf.at[p.y, p.x]), local_sems.at[4])
    )
    for load in loads:
        load.start()
    if count < pad:
        wide_w[:, :, :, count:, :] = jnp.zeros((2, 2, depth, pad - count, 2 * cols), BF16)
        down_buf[:, :, :, count:, :] = jnp.zeros((2, 2, depth, pad - count, cols), BF16)
    p.barrier(["c", "x", "y"])
    n_copy = p.copy("c", normed2, n_other)
    down = PlaneGather(p, None, down_buf, depth // 2, trim)
    loads[4].wait()
    down.over_x()
    down.over_y()
    cot[...] = widen(cot_t, depth, rows, pad).astype(BF16)
    c_copy = p.copy("c", cot, c_other)
    for load in loads[:4]:
        load.wait()

    def sides(s):
        return (n_other, c_other) if s else (normed2, cot)

    for s in range(2):
        if s:
            n_copy.wait_recv()
            c_copy.wait_recv()
        n_from, c_from = sides(s)
        both = slice(s * tokens, (s + 1) * tokens)
        n_t[:, both] = transposed(n_from[...])
        c_t[:, both] = transposed(c_from[...])
        def tile(start):
            span = pl.ds(s * tokens + start, TILE)
            n_rows = n_from[pl.ds(start, TILE), :]
            gate = dot(n_rows, wide_w[0].reshape(DPAD, 2 * cols))
            upper = dot(n_rows, wide_w[1].reshape(DPAD, 2 * cols))
            sigma = jax.nn.sigmoid(gate)
            silu = gate * sigma
            hid[span, :] = (silu * upper).astype(BF16)
            d_gate[span, :] = (upper * sigma * (1.0 + gate * (1.0 - sigma))).astype(BF16)
            d_up[span, :] = silu.astype(BF16)

        row_tiles(tokens, tile)
    down.diagonal_y()
    down.diagonal_x()

    def weight_grad(left, right, target):
        def tile(start):
            side = dot(left[pl.ds(start, TILE), :], right[...]).astype(BF16)
            for y in range(2):
                store_blocks(target.at[y], start, side[:, y * cols : (y + 1) * cols])

        row_tiles(DPAD, tile)

    weight_grad(c_t, hid, down_g)
    down.arrived()
    total = PlaneScatter(p, down_g, down_r, trim)
    total.start()

    for s in (1, 0):
        n_from, c_from = sides(s)
        both = slice(s * tokens, (s + 1) * tokens)
        part = None
        for y in range(2):
            lanes = slice(y * cols, (y + 1) * cols)
            w_down = down_buf[y].reshape(DPAD, cols)
            grad_hid = dot(c_from[...], w_down)
            d_gate[both, lanes] = (grad_hid * d_gate[both, lanes].astype(F32)).astype(BF16)
            d_up[both, lanes] = (grad_hid * d_up[both, lanes].astype(F32)).astype(BF16)
            out = dot_nt(hid[both, lanes], w_down)
            part = out if part is None else part + out
        back = dot_nt(d_gate[both, :], wide_w[0].reshape(DPAD, 2 * cols))
        back += dot_nt(d_up[both, :], wide_w[1].reshape(DPAD, 2 * cols))
        if s:
            parts[0] = part.astype(BF16)
            parts[1] = back.astype(BF16)
            shared = [p.copy("c", parts.at[n], received.at[n]) for n in range(2)]
        else:
            ffn_own[...] = part + middle[...]
            grad_n2[...] = back
    total.forward()
    saved = []
    for w, right in ((0, d_gate), (1, d_up)):
        weight_grad(n_t, right, packed.at[w])
        made = pltpu.make_async_copy(packed.at[w], grads.at[w], local_sems.at[w])
        made.start()
        saved.append(made)
    for made in shared:
        made.wait_recv()

    narrow(hidden_out, ffn_own[...] + received[0].astype(F32), depth, rows, pad)
    grad_n2[...] += received[1].astype(F32)
    total.add()
    down_sum[...] = total.total[...]
    total.finish()
    down.finish()
    for made in shared + [n_copy, c_copy]:
        made.wait_send()
    for made in saved:
        made.wait()


def ffn(normed2, cot_t, middle, ffn_w, down_w, rows):
    width, tokens = cot_t.shape
    depth, pad, cols = down_w.shape
    token_rows = pltpu.VMEM((tokens, DPAD), BF16)
    wide = pltpu.VMEM((2 * tokens, 2 * cols), BF16)
    flipped = pltpu.VMEM((DPAD, 2 * tokens), BF16)
    pair = pltpu.VMEM((2, tokens, DPAD), BF16)
    copies = 4 + 4 + 6
    return pl.pallas_call(
        functools.partial(ffn_kernel, depth, rows),
        out_shape=[
            jax.ShapeDtypeStruct((2, 2, 2 * depth, pad, cols), BF16),
            jax.ShapeDtypeStruct((depth, pad, cols), BF16),
            jax.ShapeDtypeStruct((width, tokens), BF16),
            jax.ShapeDtypeStruct((tokens, DPAD), F32),
            jax.ShapeDtypeStruct((tokens, DPAD), BF16),
        ],
        in_specs=vmem_specs(3) + [pl.BlockSpec(memory_space=pl.ANY)] * 2,
        out_specs=[pl.BlockSpec(memory_space=pl.ANY)] + vmem_specs(4),
        scratch_shapes=[
            pltpu.VMEM((2, 2, depth, pad, 2 * cols), BF16),
            pltpu.VMEM((2, 2, depth, pad, cols), BF16),
            pltpu.VMEM((2, 2 * depth, pad, cols), BF16),
            pltpu.VMEM((3 * depth, pad, cols), BF16),
            token_rows, token_rows, wide, wide, wide, flipped, flipped,
            pltpu.VMEM((tokens, DPAD), F32), pair, pair,
            pltpu.VMEM((2, 2, 2 * depth, pad, cols), BF16),
            pltpu.SemaphoreType.DMA((copies,)),
            pltpu.SemaphoreType.DMA((copies,)),
            pltpu.SemaphoreType.DMA((5,)),
        ],
        compiler_params=pltpu.CompilerParams(
            vmem_limit_bytes=61 << 20, collective_id=1, has_side_effects=True
        ),
        cost_estimate=pl.CostEstimate(
            flops=24 << 30, bytes_accessed=30 << 20, transcendentals=2 << 20
        ),
        name="ffn",
    )(normed2, cot_t, middle, ffn_w, down_w)


def mid_kernel(
    depth, width,
    ffn_g, down_sum, grad_n2, middle, cot, gains, out_w, q, kv, attn, lse, seg,
    dq_t, dkv_sum, grad_middle, gain_grad, out_grad, gate_grad, up_grad, down_grad,
    mid_b, out_g, out_c, out_r, ffn_r, down_r, stage, grad_attn, q_t, g_t, q3, g3, k3, v3, k_t,
    delta, dkv, acc_kv, bias, kv_c, kv_y, send_sems, recv_sems, local_sems,
):
    tokens = q.shape[0]
    tiles = tokens // TILE
    back = 1024 // TILE
    rows = gate_grad.shape[0]
    pad = DPAD // (2 * depth)
    out_cols = HEADS * HEAD_DIM // 4
    p = Place(depth, send_sems, recv_sems)
    trim = lambda ref: ref.at[..., pl.ds(0, trimmed(rows, pad)), :]
    p.barrier()
    ffn_sums = [
        PlaneScatter(
            p, ffn_g.at[w], ffn_r.at[w], trim, stage.at[w], local_sems.at[pl.ds(3 * w, 3)]
        )
        for w in range(2)
    ]
    ffn_sums[0].start()
    down_in = [
        p.copy(k, trim(down_sum.at[(p.z + k) % depth]), trim(down_r.at[k - 1]))
        for k in range(1, depth)
    ]

    gain = gains[1:2, :]
    gain_grad[...] = jnp.zeros_like(gain_grad)

    def norm_tile(start):
        span = pl.ds(start, TILE)
        mid, up = middle[span, :], grad_n2[span, :]
        inv = lax.rsqrt(mean_rows(mid * mid, width) + EPSILON)
        scaled = up * gain
        mean = mean_rows(scaled * mid, width)
        grad = cot[span, :].astype(F32) + inv * (scaled - mid * (inv * inv * mean))
        grad_middle[span, :] = grad
        gain_grad[...] += jnp.sum(up * mid * inv, axis=0, keepdims=True)
        mid_b[span, :] = grad.astype(BF16)
        for b in range(4):
            side = dot_nt(mid_b[span, :], out_w[b % 2, b // 2])
            grad_attn[span, b * out_cols : (b + 1) * out_cols] = side.astype(BF16)

    row_tiles(tokens, norm_tile)
    attn_t = attn[...].astype(F32).T
    for b in range(4):
        left = attn_t[b * out_cols : (b + 1) * out_cols, :].astype(BF16)
        spread_blocks(out_g.at[b % 2, b // 2], dot(left, mid_b[...]), pad)
    out_cross = p.copy("c", out_g.at[1 - p.c], out_c)
    ffn_sums[1].start()

    g_t[...] = transposed(grad_attn[...])
    for h in range(HEADS):
        span = slice(h * HEAD_DIM, (h + 1) * HEAD_DIM)
        delta[h : h + 1, :] = jnp.sum(
            g_t[span, :].astype(F32) * attn_t[span, :], axis=0, keepdims=True
        )
        q3[h] = q[:, span]
        g3[h] = grad_attn[:, span]
    q_t[...] = transposed(q[...])
    for n in range(3):
        block = jnp.maximum(p.m - n, 0)
        span = pl.ds(pl.multiple_of(block * tokens, tokens), tokens)
        for g in range(KV_HEADS):
            part = kv[block, g]
            k_t[g * HEAD_DIM : (g + 1) * HEAD_DIM, span] = transposed(part)[:HEAD_DIM]
            k3[g, span, :] = part[:, :HEAD_DIM]
            v3[g, span, :] = part[:, HEAD_DIM:]
    dq_t[...] = jnp.zeros_like(dq_t)
    dkv[...] = jnp.zeros_like(dkv)
    out_cross.wait_recv()
    own = out_g.at[p.c]
    own[...] = (own[...].astype(F32) + out_c[...].astype(F32)).astype(BF16)
    out_sum = PlaneScatter(p, own, out_r)
    out_sum.start()

    def key_tile(t, queries):
        keys = pl.ds(pl.multiple_of(t * TILE, TILE), TILE)
        for i in queries:
            bias[i] = mask_tile(seg[0:1, i * TILE : (i + 1) * TILE], p.m * tiles + i, t)

        def group(g, carry):
            k_g, v_g = k3[g, keys, :], v3[g, keys, :]
            kt_g = k_t[pl.ds(pl.multiple_of(g * HEAD_DIM, HEAD_DIM), HEAD_DIM), keys]
            units = [(i, g * GROUP + j) for i in queries for j in range(GROUP)]
            places = [
                (pl.ds(pl.multiple_of(h * HEAD_DIM, HEAD_DIM), HEAD_DIM), pl.ds(i * TILE, TILE))
                for i, h in units
            ]
            dk, dv = None, None
            for (i, h), (span, cols) in zip(units, places):
                scores = dot(k_g, q_t[span, cols]) * EXP_SCALE + bias[i]
                probs = jnp.exp2(scores - lse[pl.ds(h, 1), cols])
                dprobs = dot(v_g, g_t[span, cols])
                dscores = (probs * (dprobs - delta[pl.ds(h, 1), cols])).astype(BF16)
                add_v = dot(probs.astype(BF16), g3[h, cols, :])
                add_k = dot(dscores, q3[h, cols, :])
                dq_t[span, cols] += dot(kt_g, dscores)
                dk = add_k if dk is None else dk + add_k
                dv = add_v if dv is None else dv + add_v
            acc_kv[g] = dk * SCORE_SCALE
            acc_kv[KV_HEADS + g] = dv
            return carry

        lax.fori_loop(0, KV_HEADS, group, 0)
        for n in range(2 * KV_HEADS):
            dkv[keys, n * HEAD_DIM : (n + 1) * HEAD_DIM] = acc_kv[n].astype(BF16)

    def key_span(low, high, queries):
        def step(t, carry):
            key_tile(t, queries)
            return carry

        lax.fori_loop(low, high, step, 0)

    def part_of(index):
        return dkv.at[pl.ds(pl.multiple_of(index * tokens, tokens), tokens)]

    first = p.m * tiles
    key_span(jnp.maximum(first - back, 0), jnp.maximum(first + 1 - back, 0), (0,))
    ffn_sums[0].forward()
    key_span(jnp.maximum(first + 1 - back, 0), jnp.maximum(first - 2, 0), (0, 1))
    ffn_sums[1].forward()
    out_sum.forward()
    key_span(jnp.maximum(first - 2, 0), jnp.maximum(first - 1, 0), (0, 1))
    ffn_sums[0].over_z()
    key_span(jnp.maximum(first - 1, 0), first, (0, 1))
    beside = p.m + 1 - 2 * p.c
    cross = [
        p.copy("c", part_of(index), kv_c.at[n])
        for n, index in enumerate((beside, (beside + 2) % 4))
    ]
    cross[1].wait_recv()
    away = part_of((p.m + 2) % 4)
    away[...] = (away[...].astype(F32) + kv_c[1].astype(F32)).astype(BF16)
    across = p.copy("y", away, kv_y)
    ffn_sums[1].over_z()
    out_sum.over_z()
    key_tile(first + 1, (1,))
    key_span(first, first + 1, (0, 1))
    for w in range(2):
        (gate_grad, up_grad)[w][...] = ffn_sums[w].result()[:rows]
    value = down_sum[p.z].astype(F32)
    for k, made in enumerate(down_in):
        made.wait_recv()
        value += down_r[k].astype(F32)
    down_grad[...] = value[:rows]
    cross[0].wait_recv()
    across.wait_recv()
    dkv_sum[...] = part_of(p.m)[...].astype(F32) + kv_c[0].astype(F32) + kv_y[...].astype(F32)
    out_grad[...] = one_block(out_sum.result(), rows, pad)
    for part in ffn_sums + [out_sum]:
        part.finish()
    for made in cross + [across, out_cross] + down_in:
        made.wait_send()


def middle_back(ffn_g, down_sum, grad_n2, middle, cot, gains, out_w, q, kv, attn, lse, seg,
                depth, rows, width):
    tokens, query_cols = q.shape
    pad = DPAD // (2 * depth)
    cols = ffn_g.shape[-1]
    kv_cols = KV_HEADS * kv.shape[-1]
    out_cols = query_cols // 4
    whole = 4 * tokens
    slots = scatter_slots(depth)
    copies = 3 * scatter_copies(depth) + 4 + depth - 1
    heads_q = pltpu.VMEM((HEADS, tokens, HEAD_DIM), BF16)
    heads_kv = pltpu.VMEM((KV_HEADS, whole, HEAD_DIM), BF16)
    flipped = pltpu.VMEM((query_cols, tokens), BF16)
    return pl.pallas_call(
        functools.partial(mid_kernel, depth, width),
        out_shape=[
            jax.ShapeDtypeStruct((query_cols, tokens), F32),
            jax.ShapeDtypeStruct((tokens, kv_cols), F32),
            jax.ShapeDtypeStruct((tokens, DPAD), F32),
            jax.ShapeDtypeStruct((1, DPAD), F32),
            jax.ShapeDtypeStruct((out_cols, rows), F32),
            *[jax.ShapeDtypeStruct((rows, cols), F32)] * 3,
        ],
        in_specs=[pl.BlockSpec(memory_space=pl.ANY)] + vmem_specs(11),
        out_specs=vmem_specs(8),
        scratch_shapes=[
            pltpu.VMEM((tokens, DPAD), BF16),
            pltpu.VMEM((2, 2, 2 * depth, *block_shape(out_cols, pad)), BF16),
            pltpu.VMEM((2, 2 * depth, *block_shape(out_cols, pad)), BF16),
            pltpu.VMEM((slots, *block_shape(out_cols, pad)), BF16),
            pltpu.VMEM((2, slots, pad, cols), BF16),
            pltpu.VMEM((depth - 1, pad, cols), BF16),
            pltpu.VMEM((2, 2 * depth, pad, cols), BF16),
            pltpu.VMEM((tokens, query_cols), BF16),
            flipped, flipped, heads_q, heads_q, heads_kv, heads_kv,
            pltpu.VMEM((KV_HEADS * HEAD_DIM, whole), BF16),
            pltpu.VMEM((HEADS + 1, tokens), F32),
            pltpu.VMEM((whole, kv_cols), BF16),
            pltpu.VMEM((2 * KV_HEADS, TILE, HEAD_DIM), F32),
            pltpu.VMEM((tokens // TILE, TILE, TILE), F32),
            pltpu.VMEM((2, tokens, kv_cols), BF16),
            pltpu.VMEM((tokens, kv_cols), BF16),
            pltpu.SemaphoreType.DMA((copies,)),
            pltpu.SemaphoreType.DMA((copies,)),
            pltpu.SemaphoreType.DMA((6,)),
        ],
        compiler_params=pltpu.CompilerParams(
            vmem_limit_bytes=61 << 20, collective_id=2, has_side_effects=True
        ),
        cost_estimate=pl.CostEstimate(
            flops=40 << 30, bytes_accessed=50 << 20, transcendentals=8 << 20
        ),
        name="middle_back",
    )(ffn_g, down_sum, grad_n2, middle, cot, gains, out_w, q, kv, attn, lse, seg)


def tail_kernel(
    depth, rows, width,
    dq_t, dkv, cosine_t, sine_t, x_t, grad_middle, gains, in_w, gain2,
    grad_hidden, in_grad, gain1_sum, gain2_sum,
    proj, proj_b, in_g, in_c, in_r, grad_x, gain_own, gain_r, send_sems, recv_sems,
):
    query_cols, tokens = dq_t.shape
    in_cols = in_w.shape[2]
    pad = DPAD // (2 * depth)
    turned = (HEADS + KV_HEADS) * HEAD_DIM
    p = Place(depth, send_sems, recv_sems)
    p.barrier()
    x_f = widen(x_t, depth, rows, pad)
    gain = gains[0:1, :]
    inv = lax.rsqrt(mean_rows(x_f * x_f, width) + EPSILON)
    normed1 = (x_f * inv * gain).astype(BF16)
    cosine = lane_tables(cosine_t[...])
    sine = signed(lane_tables(sine_t[...]), True)
    proj[:, :query_cols] = dq_t[...].T * SCORE_SCALE
    proj[:, query_cols:] = dkv[...]
    for j in range(turned // 128):
        lanes = slice(128 * j, 128 * (j + 1))
        proj[:, lanes] = rope(proj[:, lanes], cosine, sine)
    for b in range(4):
        proj_b[b] = proj[:, b * in_cols : (b + 1) * in_cols].astype(BF16)
    for other in (1, 0):
        c = (1 - p.c) if other else p.c
        for y in range(2):
            left = transposed(proj_b[2 * y + c])
            spread_blocks(in_g.at[c, y], dot(left, normed1), pad)
        if other:
            in_cross = p.copy("c", in_g.at[c], in_c)
    in_cross.wait_recv()
    own = in_g.at[p.c]
    own[...] = (own[...].astype(F32) + in_c[...].astype(F32)).astype(BF16)
    in_sum = PlaneScatter(p, own, in_r)
    in_sum.start()
    up = None
    for b in range(4):
        term = dot(proj_b[b], in_w[b % 2, b // 2])
        up = term if up is None else up + term
    scaled = up * gain
    mean = mean_rows(scaled * x_f, width)
    grad_x[...] = grad_middle[...] + inv * (scaled - x_f * (inv * inv * mean))
    gain_own[...] = jnp.zeros_like(gain_own)
    gain_own[0:1, :] = jnp.sum(up * x_f * inv, axis=0, keepdims=True)
    gain_own[1:2, :] = gain2[...]
    in_sum.forward()
    sent = []
    for n, kind in enumerate(("c", "y", "x")):
        made = p.copy(kind, gain_own.at[pl.ds(8 * n, 8)], gain_r.at[pl.ds(8 * n, 8)])
        sent.append(made)
        if n == 0:
            narrow(grad_hidden, grad_x[...], depth, rows, pad)
        made.wait_recv()
        if n == 1:
            in_sum.over_z()
        gain_own[8 * (n + 1) : 8 * (n + 2), :] = (
            gain_own[8 * n : 8 * (n + 1), :] + gain_r[8 * n : 8 * (n + 1), :]
        )
    last = gain_own.at[pl.ds(24, 8)]
    arriving = [p.copy(k, last, gain_r.at[pl.ds(24 + 8 * k, 8)]) for k in range(1, depth)]
    total = last[...]
    for k, made in enumerate(arriving):
        made.wait_recv()
        total += gain_r[32 + 8 * k : 40 + 8 * k, :]
    mine = jnp.zeros((8, pad), F32)
    for n in range(2 * depth):
        mine = jnp.where(n == p.x * depth + p.z, total[:, n * pad : (n + 1) * pad], mine)
    gain1_sum[...] = mine[0:1, :rows]
    gain2_sum[...] = mine[1:2, :rows]
    in_grad[...] = one_block(in_sum.result(), rows, pad)
    in_sum.finish()
    for made in sent + arriving + [in_cross]:
        made.wait_send()


def tail(dq_t, dkv, cosine_t, sine_t, x_t, grad_middle, gains, in_w, gain2, depth, rows, width):
    tokens = dq_t.shape[1]
    pad = DPAD // (2 * depth)
    in_cols = in_w.shape[2]
    total = dq_t.shape[0] + dkv.shape[1]
    slots = scatter_slots(depth)
    copies = scatter_copies(depth) + 1 + 3 + depth - 1
    return pl.pallas_call(
        functools.partial(tail_kernel, depth, rows, width),
        out_shape=[
            jax.ShapeDtypeStruct((width, tokens), F32),
            jax.ShapeDtypeStruct((in_cols, rows), F32),
            *[jax.ShapeDtypeStruct((1, rows), F32)] * 2,
        ],
        in_specs=vmem_specs(9),
        out_specs=vmem_specs(4),
        scratch_shapes=[
            pltpu.VMEM((tokens, total), F32),
            pltpu.VMEM((4, tokens, in_cols), BF16),
            pltpu.VMEM((2, 2, 2 * depth, *block_shape(in_cols, pad)), BF16),
            pltpu.VMEM((2, 2 * depth, *block_shape(in_cols, pad)), BF16),
            pltpu.VMEM((slots, *block_shape(in_cols, pad)), BF16),
            pltpu.VMEM((tokens, DPAD), F32),
            pltpu.VMEM((32, DPAD), F32),
            pltpu.VMEM((24 + 8 * depth, DPAD), F32),
            pltpu.SemaphoreType.DMA((copies,)),
            pltpu.SemaphoreType.DMA((copies,)),
        ],
        compiler_params=pltpu.CompilerParams(
            vmem_limit_bytes=61 << 20, collective_id=3, has_side_effects=True
        ),
        cost_estimate=pl.CostEstimate(
            flops=8 << 30, bytes_accessed=30 << 20, transcendentals=0
        ),
        name="tail",
    )(dq_t, dkv, cosine_t, sine_t, x_t, grad_middle, gains, in_w, gain2)


def rotary_tables(position_ids):
    half_dim = HEAD_DIM // 2
    frequency = jnp.exp(
        jnp.arange(half_dim, dtype=F32) * (-2.0 * math.log(10000.0) / HEAD_DIM)
    )
    angles = frequency[:, None] * position_ids.astype(F32)[None, :]
    return jnp.cos(angles), jnp.sin(angles)


def per_device(
    hidden_in, cotangent, segments, positions, attn_in, attn_out, w_gate, w_up, w_down,
    norm1_gain, norm2_gain,
):
    tokens, width = hidden_in.shape[1:]
    dp_size = lax.axis_size("dp")
    depth = dp_size // 2
    rows = width // dp_size
    pad = DPAD // dp_size

    ffn_blocks = [w_gate, w_up, w_down.T]
    if trimmed(rows, pad) == pad:
        ffn_blocks = [jnp.pad(w, ((0, pad - rows), (0, 0))) for w in ffn_blocks]
    x_t, cot_t = hidden_in[0].T, cotangent[0].T
    cosine_t, sine_t = rotary_tables(positions[0])
    attn, lse, middle, normed2, gains, seg, q, kv, out_w, in_w, ffn_w, down_w = front(
        attn_in.T, attn_out, norm1_gain[None], norm2_gain[None], *ffn_blocks,
        x_t, cosine_t, sine_t, segments, depth, rows,
    )
    ffn_g, down_sum, hidden_out, grad_n2, cot = ffn(normed2, cot_t, middle, ffn_w, down_w, rows)
    dq_t, dkv, grad_middle, gain2, g_out, g_gate, g_up, g_down = middle_back(
        ffn_g, down_sum, grad_n2, middle, cot, gains, out_w, q, kv, attn, lse, seg,
        depth, rows, width,
    )
    grad_hidden, g_in, *gain_sums = tail(
        dq_t, dkv, cosine_t, sine_t, x_t, grad_middle, gains, in_w, gain2, depth, rows, width
    )
    return (
        hidden_out.T[None],
        grad_hidden.T[None],
        g_in.T,
        g_out,
        g_gate,
        g_up,
        g_down.T,
        gain_sums[0][0],
        gain_sums[1][0],
    )


def solution(mesh):
    return jax.shard_map(
        per_device,
        mesh=mesh,
        in_specs=(
            P("dp", "mp", None),
            P("dp", "mp", None),
            P("dp", None),
            P("dp", "mp"),
            P("dp", "mp"),
            P("mp", "dp"),
            P("dp", "mp"),
            P("dp", "mp"),
            P("mp", "dp"),
            P("dp"),
            P("dp"),
        ),
        out_specs=(
            P("dp", "mp", None),
            P("dp", "mp", None),
            P("dp", "mp"),
            P("mp", "dp"),
            P("dp", "mp"),
            P("dp", "mp"),
            P("mp", "dp"),
            P("dp"),
            P("dp"),
        ),
        check_vma=False,
    )
```

```python
import functools
import math

import jax
import jax.numpy as jnp
from jax import lax
from jax.experimental import pallas as pl
from jax.experimental.pallas import tpu as pltpu
from jax.sharding import PartitionSpec as P

HEADS = 15
KV_HEADS = 5
GROUP = HEADS // KV_HEADS
HEAD_DIM = 64
DPAD = 1024
TILE = 256
EPSILON = 1e-05
SCORE_SCALE = 0.125
MASK_FILL = -1e30
LOG2E = 1.4426950408889634
EXP_SCALE = SCORE_SCALE * LOG2E
GAIN_ROWS = 16
SEGMENTS = 4
AUGMENTED = HEAD_DIM + 16
WIDE = GROUP * TILE
BF16 = jnp.bfloat16
F32 = jnp.float32


def dot(a, b):
    return jnp.dot(a, b, preferred_element_type=F32)


def dot_nt(a, b):
    return lax.dot_general(a, b, (((1,), (1,)), ((), ())), preferred_element_type=F32)


def vmem_specs(count):
    return [pl.BlockSpec(memory_space=pltpu.VMEM)] * count


def transposed(value):
    return value.astype(F32).T.astype(BF16)


class Place:
    def __init__(self, depth, send_sems, recv_sems):
        dp_index, m = lax.axis_index("dp"), lax.axis_index("mp")
        self.depth = depth
        self.z, self.x = dp_index // 2, dp_index % 2
        self.m, self.y, self.c = m, m // 2, m % 2
        self.send_sems, self.recv_sems = send_sems, recv_sems
        self.count = 0

    def peer(self, kind):
        z, x, y, c = self.z, self.x, self.y, self.c
        if kind == "x":
            x = 1 - x
        elif kind == "y":
            y = 1 - y
        elif kind == "c":
            c = 1 - c
        else:
            z = (z + kind) % self.depth
        return 2 * z + x, 2 * y + c

    def kinds(self):
        return ["x", "y", "c"] + list(range(1, self.depth))

    def barrier(self, kinds=None):
        semaphore = pltpu.get_barrier_semaphore()
        kinds = kinds or self.kinds()
        for kind in kinds:
            pl.semaphore_signal(
                semaphore, inc=1, device_id=self.peer(kind), device_id_type=pl.DeviceIdType.MESH
            )
        pl.semaphore_wait(semaphore, len(kinds))

    def copy(self, kind, source, target=None):
        index = self.count
        self.count += 1
        made = pltpu.make_async_remote_copy(
            src_ref=source,
            dst_ref=source if target is None else target,
            send_sem=self.send_sems.at[index],
            recv_sem=self.recv_sems.at[index],
            device_id=self.peer(kind),
            device_id_type=pl.DeviceIdType.MESH,
        )
        made.start()
        return made


class PlaneGather:
    def __init__(self, place, source, buffer, by_x, part=lambda ref: ref):
        self.place, self.source, self.buffer, self.part = place, source, buffer, part
        self.split = place.depth - by_x
        self.sent, self.last = [], []

    def over_z(self, slot=None):
        p = self.place
        slot = self.part(self.buffer.at[p.y, p.x, p.z]) if slot is None else slot
        self.arriving = [p.copy(k, self.source, slot) for k in range(1, p.depth)]
        self.sent += self.arriving

    def stacked(self):
        for made in self.arriving:
            made.wait_recv()

    def over_x(self):
        p = self.place
        self.by_x = p.copy("x", self.part(self.buffer.at[p.y, p.x]))
        self.sent.append(self.by_x)

    def over_y(self):
        p = self.place
        self.by_y = p.copy("y", self.part(self.buffer.at[p.y, p.x]))
        self.sent.append(self.by_y)

    def diagonal_x(self):
        p = self.place
        self.by_y.wait_recv()
        span = pl.ds(self.split, p.depth - self.split)
        self.last.append(p.copy("x", self.part(self.buffer.at[1 - p.y, p.x, span])))

    def diagonal_y(self):
        p = self.place
        self.by_x.wait_recv()
        if self.split:
            span = pl.ds(0, self.split)
            self.last.append(p.copy("y", self.part(self.buffer.at[p.y, 1 - p.x, span])))

    def arrived(self):
        for made in self.last:
            made.wait_recv()

    def finish(self):
        for made in self.sent + self.last:
            made.wait_send()


def rope(value, cosine, sine):
    lane = lax.broadcasted_iota(jnp.int32, value.shape, 1)
    half = HEAD_DIM // 2
    partner = jnp.where(
        lane % HEAD_DIM < half, pltpu.roll(value, 128 - half, 1), pltpu.roll(value, half, 1)
    )
    return value * cosine + partner * sine


def trimmed(rows, pad):
    return rows if rows % 8 == 0 else pad


def natural(block, depth):
    return 2 * (block % depth) + block // depth


def widen(source, depth, rows, pad):
    filler = jnp.zeros((pad - rows, source.shape[1]), F32)
    parts = []
    for b in range(2 * depth):
        first = natural(b, depth) * rows
        parts += [source[first : first + rows, :].astype(F32), filler]
    return jnp.concatenate(parts, axis=0).T


def narrow(target, value, depth, rows, pad):
    flipped = value.T
    for b in range(2 * depth):
        first = natural(b, depth) * rows
        target[first : first + rows, :] = flipped[b * pad : b * pad + rows, :].astype(target.dtype)


def side_by_side(ref, first, size):
    _, depth, _, pad = ref.shape
    span = pl.ds(first, size)
    return jnp.concatenate(
        [ref[b // depth, b % depth, span, :] for b in range(2 * depth)], axis=1
    )


def lane_tables(table):
    return jnp.concatenate([table] * (256 // HEAD_DIM), axis=0).T


def signed(table, back):
    lane = lax.broadcasted_iota(jnp.int32, table.shape, 1) % HEAD_DIM
    first = lane < HEAD_DIM // 2
    return jnp.where(first, table, -table) if back else jnp.where(first, -table, table)


def mean_rows(value, width):
    return jnp.sum(value, axis=-1, keepdims=True) * (1.0 / width)


def diagonal_bias():
    key = lax.broadcasted_iota(jnp.int32, (TILE, WIDE), 0)
    query = lax.broadcasted_iota(jnp.int32, (TILE, WIDE), 1) % TILE
    return jnp.where(key <= query, 0.0, MASK_FILL)


def features(first, segment_rows):
    spare = 16 - len(first) - SEGMENTS
    zeros = jnp.zeros((spare, first[0].shape[1]), F32)
    return jnp.concatenate(list(first) + segment_rows + [zeros], axis=0)


def key_features(segment):
    other = [jnp.where(segment != n, MASK_FILL, 0.0) for n in range(SEGMENTS)]
    return features([jnp.ones(segment.shape, F32)] * 3, other).T.astype(BF16)


def query_features(segment, first):
    same = [jnp.where(segment == n, 1.0, 0.0) for n in range(SEGMENTS)]
    return features(first, same).astype(BF16)


def three_parts(value):
    parts = []
    for _ in range(3):
        parts.append(value.astype(BF16).astype(F32))
        value = value - parts[-1]
    return parts


def head_lanes(i, j):
    return slice(i * WIDE + j * TILE, i * WIDE + (j + 1) * TILE)


def front_kernel(
    depth, rows, width, in_cols,
    attn_in_t, attn_out, gain_one, gain_two, w_gate, w_up, w_down_t, x_t, cosine_t, sine_t, segments,
    attn, lse, middle, normed2, gains, q_out, kv_out, out_w_out, in_w_out, ffn_w, down_w,
    q, kv, out_w, in_w, a_buf, x_in, cosine, sine, normed1, proj, q_aug, k3, v_t, acc, peak, flat,
    diagonal, send_sems, recv_sems, local_sems,
):
    tokens = x_in.shape[0]
    tiles = tokens // TILE
    back = 1024 // TILE
    pad = DPAD // (2 * depth)
    lead = in_cols + GAIN_ROWS
    query_cols = HEADS * HEAD_DIM
    out_cols = query_cols // 4
    p = Place(depth, send_sems, recv_sems)
    block = a_buf.at[p.c, p.y, p.x, p.z]
    block[...] = jnp.zeros_like(block)
    block[0:in_cols, 0:rows] = attn_in_t[...]
    block[in_cols : in_cols + 1, 0:rows] = gain_one[...]
    block[in_cols + 1 : in_cols + 2, 0:rows] = gain_two[...]
    block[lead : lead + out_cols, 0:rows] = attn_out[...]
    moved = pl.ds(0, trimmed(rows, pad))
    trim = lambda ref: ref.at[..., moved, :]
    own = [
        pltpu.make_async_copy(
            source, trim(ffn_w.at[w, p.y, p.x, p.z] if w < 2 else down_w.at[p.z]), local_sems.at[w]
        )
        for w, source in enumerate((w_gate, w_up, w_down_t))
    ]
    for made in own:
        made.start()
    p.barrier()
    first_part = lambda ref: ref.at[..., pl.ds(0, lead), :]
    last_part = lambda ref: ref.at[..., pl.ds(lead, out_cols), :]
    buffer = a_buf.at[p.c]
    plane = PlaneGather(p, first_part(block), buffer, depth // 2, first_part)
    output = PlaneGather(p, last_part(block), buffer, depth // 2, last_part)
    gate = PlaneGather(p, w_gate, ffn_w.at[0], depth, trim)
    up = PlaneGather(p, w_up, ffn_w.at[1], depth // 2, trim)
    down = PlaneGather(p, w_down_t, None, 0)
    plane.over_z()
    x_f = widen(x_t, depth, rows, pad)
    x_in[...] = x_f.astype(BF16)
    cosine[...] = lane_tables(cosine_t[...])
    sine[...] = signed(lane_tables(sine_t[...]), False)
    inv_one = lax.rsqrt(mean_rows(x_f * x_f, width) + EPSILON)
    def block_span(block):
        return pl.ds(pl.multiple_of(block * tokens, tokens), tokens)

    plane.stacked()
    plane.over_x()
    plane.over_y()
    output.over_z()
    gate.over_z()
    own_seg = segments[:, block_span(p.m)]
    nothing = jnp.zeros(own_seg.shape, F32)
    own_features = query_features(own_seg, [nothing] * 3)
    for g in range(KV_HEADS):
        for i in range(tiles):
            for j in range(GROUP):
                q_aug[g, HEAD_DIM:, head_lanes(i, j)] = own_features[:, i * TILE : (i + 1) * TILE]
    ones = lax.broadcasted_iota(jnp.int32, (16, 4 * tokens), 0) == 0
    for g in range(KV_HEADS):
        v_t[g, HEAD_DIM:, :] = jnp.where(ones, 1.0, 0.0).astype(BF16)
    diagonal[...] = diagonal_bias()
    acc[...] = jnp.zeros_like(acc)
    peak[...] = jnp.full_like(peak, MASK_FILL)
    plane.diagonal_y()
    plane.diagonal_x()
    for made in own:
        made.wait()
    up.over_z()
    plane.arrived()
    cross = p.copy("c", first_part(a_buf.at[p.c]))
    output.stacked()
    output.over_x()
    output.over_y()
    for n in range(3):
        span = block_span(jnp.maximum(p.m - n, 0))
        added = key_features(segments[:, span])
        for g in range(KV_HEADS):
            k3[g, span, HEAD_DIM:] = added
    gate.stacked()
    gate.over_x()
    gate.over_y()
    cross.wait()
    for b in range(2 * depth):
        gains[:, b * pad : (b + 1) * pad] = a_buf[
            0, 0, b // depth, b % depth, pl.ds(in_cols, 2), :
        ].astype(F32)
    normed1[...] = (x_f * inv_one * gains[0:1, :]).astype(BF16)
    for b in range(4):
        in_w[b % 2, b // 2] = side_by_side(a_buf.at[b % 2, b // 2], 0, in_cols)

    kv_first = query_cols // 128

    def project(blocks, groups):
        def tile(start):
            span = pl.ds(start, TILE)
            for b in blocks:
                proj[span, b * in_cols : (b + 1) * in_cols] = dot_nt(
                    normed1[span, :], in_w[b % 2, b // 2]
                )
            for j in groups:
                lanes = slice(128 * j, 128 * (j + 1))
                proj[span, lanes] = rope(proj[span, lanes], cosine[span, :], sine[span, :])

        row_tiles(tokens, tile)

    project((2, 3), range(kv_first, (HEADS + KV_HEADS) * HEAD_DIM // 128))
    for g in range(KV_HEADS):
        k_first, v_first = query_cols + g * HEAD_DIM, query_cols + (KV_HEADS + g) * HEAD_DIM
        kv[p.m, g] = jnp.concatenate(
            [proj[:, k_first : k_first + HEAD_DIM], proj[:, v_first : v_first + HEAD_DIM]], axis=1
        ).astype(BF16)
    kv_c = p.copy("c", kv.at[p.m])
    kv_y = [p.copy("y", kv.at[p.m, g]) for g in range(KV_HEADS)]
    down.over_z(trim(down_w.at[p.z]))
    project((0, 1), range(kv_first))
    q[...] = proj[:, :query_cols].astype(BF16)
    q_flat = (proj[:, :query_cols].astype(BF16).astype(F32) * SCORE_SCALE).T.astype(BF16)
    for h in range(HEADS):
        for i in range(tiles):
            part = q_flat[h * HEAD_DIM : (h + 1) * HEAD_DIM, i * TILE : (i + 1) * TILE]
            q_aug[h // GROUP, :HEAD_DIM, head_lanes(i, h % GROUP)] = part
    saved = [
        pltpu.make_async_copy(source, target, local_sems.at[3 + n])
        for n, (source, target) in enumerate(((in_w, in_w_out), (q, q_out)))
    ]
    for made in saved:
        made.start()
    def spread(block, g):
        span = block_span(block)
        part = kv[block, g]
        v_t[g, :HEAD_DIM, span] = transposed(part)[HEAD_DIM:]
        k3[g, span, :HEAD_DIM] = part[:, :HEAD_DIM]

    def attend_units(queries, t, g, on_diagonal=()):
        keys = pl.ds(pl.multiple_of(t * TILE, TILE), TILE)
        places = [pl.ds(i * WIDE, WIDE) for i in queries]
        k_g, v_g = k3[g, keys, :], v_t[g, :, keys]
        old = [peak[pl.ds(g, 1), lanes] for lanes in places]
        scores = [dot(k_g, q_aug[g, :, lanes]) for lanes in places]
        scores = [s + diagonal[...] if i in on_diagonal else s for i, s in zip(queries, scores)]
        new = [jnp.maximum(o, jnp.max(s, axis=0, keepdims=True)) for o, s in zip(old, scores)]
        probs = [jnp.exp2(s * LOG2E - n * LOG2E).astype(BF16) for s, n in zip(scores, new)]
        scale = [jnp.exp2((o - n) * LOG2E) for o, n in zip(old, new)]
        outs = [dot(v_g, b) for b in probs]
        for lanes, n, factor, out in zip(places, new, scale, outs):
            peak[pl.ds(g, 1), lanes] = n
            acc[g, :, lanes] = acc[g, :, lanes] * factor + out

    first_tile = p.m * tiles
    for g in range(KV_HEADS):
        spread(p.m, g)
    for queries, t in (((1,), 1), ((0, 1), 0)):

        def group(g, carry):
            attend_units(queries, first_tile + t, g, (t,))
            return carry

        lax.fori_loop(0, KV_HEADS, group, 0)
        if t:
            up.stacked()
            up.over_x()
            output.diagonal_x()
            output.diagonal_y()

    lows = [jnp.maximum(first_tile + i - back, 0) for i in range(tiles)]
    kv_cy = []

    def pass_on(g):
        kv_y[g].wait_recv()
        kv_cy.append(p.copy("c", kv.at[(p.m + 2) % 4, g]))

    kv_c.wait_recv()
    pass_on(0)
    gate.diagonal_x()
    gate.diagonal_y()
    for g in range(KV_HEADS):
        if g + 1 < KV_HEADS:
            pass_on(g + 1)
        if g == 1:
            up.over_y()
            up.diagonal_y()
        if g == 2:
            output.arrived()
            out_cross = p.copy("c", last_part(a_buf.at[p.c]))
        kv_cy[g].wait_recv()
        for n in (1, 2):
            spread(jnp.maximum(p.m - n, 0), g)
        for low, high, queries in ((lows[0], lows[1], (0,)), (lows[1], first_tile, (0, 1))):

            def step(t, carry):
                attend_units(queries, t, g)
                return carry

            lax.fori_loop(low, high, step, 0)
    saved.append(pltpu.make_async_copy(kv, kv_out, local_sems.at[5]))
    saved[-1].start()
    for h in range(HEADS):
        for i in range(tiles):
            part = acc[h // GROUP, :, head_lanes(i, h % GROUP)]
            flat[h * HEAD_DIM : (h + 1) * HEAD_DIM, i * TILE : (i + 1) * TILE] = (
                part[:HEAD_DIM] / part[HEAD_DIM : HEAD_DIM + 1]
            )
    attn[...] = flat[...].T.astype(BF16)
    lse[...] = jnp.zeros_like(lse)
    for g in range(KV_HEADS):
        lse[g : g + 1, :] = peak[g : g + 1, :] + jnp.log(acc[g, HEAD_DIM : HEAD_DIM + 1, :])
    out_cross.wait()
    for b in range(4):
        out_w[b % 2, b // 2] = side_by_side(a_buf.at[b % 2, b // 2], lead, out_cols)
    saved.append(pltpu.make_async_copy(out_w, out_w_out, local_sems.at[6]))
    saved[-1].start()
    up.diagonal_x()

    def project_out(r, carry):
        span = pl.ds(pl.multiple_of(r * TILE, TILE), TILE)
        mid = x_in[span, :].astype(F32)
        for b in range(4):
            mid += dot(attn[span, b * out_cols : (b + 1) * out_cols], out_w[b % 2, b // 2])
        middle[span, :] = mid
        inv = lax.rsqrt(mean_rows(mid * mid, width) + EPSILON)
        normed2[span, :] = (mid * inv * gains[1:2, :]).astype(BF16)
        return carry

    lax.fori_loop(0, tiles, project_out, 0)
    gate.arrived()
    up.arrived()
    down.stacked()
    for part in (plane, output, gate, up, down):
        part.finish()
    for made in kv_y + kv_cy + [kv_c]:
        made.wait_send()
    for made in saved:
        made.wait()


def front(
    attn_in_t, attn_out, gain_one, gain_two, w_gate, w_up, w_down_t, x_t, cosine_t, sine_t,
    segments, depth, rows,
):
    width, tokens = x_t.shape
    pad = DPAD // (2 * depth)
    in_cols, cols = attn_in_t.shape[0], w_gate.shape[1]
    a_rows = in_cols + GAIN_ROWS + attn_out.shape[0]
    query_cols, kv_cols = HEADS * HEAD_DIM, 2 * KV_HEADS * HEAD_DIM
    whole = 4 * tokens
    copies = 5 * (depth - 1) + 4 * 4 + 3 + 2 * KV_HEADS
    anywhere = pl.BlockSpec(memory_space=pl.ANY)
    kept = [
        (tokens, query_cols),
        (4, KV_HEADS, tokens, 2 * HEAD_DIM),
        (2, 2, query_cols // 4, DPAD),
        (2, 2, in_cols, DPAD),
    ]
    return pl.pallas_call(
        functools.partial(front_kernel, depth, rows, width, in_cols),
        out_shape=[
            jax.ShapeDtypeStruct((tokens, query_cols), BF16),
            jax.ShapeDtypeStruct((8, GROUP * tokens), F32),
            jax.ShapeDtypeStruct((tokens, DPAD), F32),
            jax.ShapeDtypeStruct((tokens, DPAD), BF16),
            jax.ShapeDtypeStruct((2, DPAD), F32),
            *[jax.ShapeDtypeStruct(shape, BF16) for shape in kept],
            jax.ShapeDtypeStruct((2, 2, 2, depth, pad, cols), BF16),
            jax.ShapeDtypeStruct((depth, pad, cols), BF16),
        ],
        in_specs=vmem_specs(4) + [anywhere] * 3 + vmem_specs(4),
        out_specs=vmem_specs(5) + [anywhere] * 6,
        scratch_shapes=[
            *[pltpu.VMEM(shape, BF16) for shape in kept],
            pltpu.VMEM((2, 2, 2, depth, a_rows, pad), BF16),
            pltpu.VMEM((tokens, DPAD), BF16),
            pltpu.VMEM((tokens, 128), F32),
            pltpu.VMEM((tokens, 128), F32),
            pltpu.VMEM((tokens, DPAD), BF16),
            pltpu.VMEM((tokens, query_cols + kv_cols), F32),
            pltpu.VMEM((KV_HEADS, AUGMENTED, GROUP * tokens), BF16),
            pltpu.VMEM((KV_HEADS, whole, AUGMENTED), BF16),
            pltpu.VMEM((KV_HEADS, AUGMENTED, whole), BF16),
            pltpu.VMEM((KV_HEADS, AUGMENTED, GROUP * tokens), F32),
            pltpu.VMEM((8, GROUP * tokens), F32),
            pltpu.VMEM((query_cols, tokens), F32),
            pltpu.VMEM((TILE, WIDE), F32),
            pltpu.SemaphoreType.DMA((copies,)),
            pltpu.SemaphoreType.DMA((copies,)),
            pltpu.SemaphoreType.DMA((7,)),
        ],
        compiler_params=pltpu.CompilerParams(
            vmem_limit_bytes=58 << 20, collective_id=0, has_side_effects=True
        ),
        cost_estimate=pl.CostEstimate(
            flops=20 << 30, bytes_accessed=40 << 20, transcendentals=8 << 20
        ),
        name="front",
    )(
        attn_in_t, attn_out, gain_one, gain_two, w_gate, w_up, w_down_t, x_t, cosine_t, sine_t,
        segments,
    )


class ZSum:
    def __init__(self, place, blocks, recv, part=lambda ref: ref):
        self.place, self.blocks, self.recv = place, blocks, recv
        self.sent = [
            place.copy(k, part(blocks.at[(place.z + k) % place.depth]), part(recv.at[k - 1]))
            for k in range(1, place.depth)
        ]

    def result(self):
        value = self.blocks[self.place.z].astype(F32)
        for k, made in enumerate(self.sent):
            made.wait_recv()
            value += self.recv[k].astype(F32)
        return value

    def finish(self):
        for made in self.sent:
            made.wait_send()


class PlaneScatter:
    def __init__(
        self, place, source, recv, split, part=lambda ref: ref, stage=None, local_sems=None
    ):
        self.place, self.source, self.recv, self.part = place, source, recv, part
        p, depth = place, place.depth
        self.split, self.rest = split, depth - split
        places = [(p.y, 1 - p.x, 0, split), (1 - p.y, p.x, split, self.rest), (p.y, p.x, 0, depth)]
        self.loads, self.kept, first = [], [], 0
        for n, (y, x, start, size) in enumerate(places):
            if not size:
                self.kept.append(None)
                continue
            view = source.at[y, pl.ds(x * depth + start, size)]
            if stage is not None:
                kept = stage.at[pl.ds(first, size)]
                self.loads.append(pltpu.make_async_copy(view, kept, local_sems.at[n]))
                view = kept
            first += size
            self.kept.append(view)
        self.total = self.kept[2]

    def copy(self, kind, source, first, size):
        slot = self.recv.at[pl.ds(first, size)]
        return self.place.copy(kind, self.part(source), self.part(slot))

    def start_far(self):
        p, split, rest, depth = self.place, self.split, self.rest, self.place.depth
        for load in self.loads:
            load.start()
        far, there = (1 - p.x) * depth, 1 - p.y
        self.far, self.near = [], []
        if split:
            view = self.source.at[there, pl.ds(far, split)]
            self.far.append(self.copy("y", view, 0, split))
        view = self.source.at[there, pl.ds(far + split, rest)]
        self.far.append(self.copy("x", view, split, rest))
        self.sent = list(self.far)

    def start_near(self):
        p, split, rest, depth = self.place, self.split, self.rest, self.place.depth
        far, here, there = (1 - p.x) * depth, p.x * depth, 1 - p.y
        made = []
        if split:
            view = self.source.at[there, pl.ds(here, split)]
            made.append(self.copy("y", view, depth, split))
        view = self.source.at[p.y, pl.ds(far + split, rest)]
        made.append(self.copy("x", view, depth + split, rest))
        self.near += made
        self.sent += made

    def start(self):
        self.start_far()
        self.start_near()

    def forward(self):
        split, rest, depth = self.split, self.rest, self.place.depth
        for load in self.loads:
            load.wait()
        jobs = [(self.kept[1], "y", split, rest)]
        if split:
            jobs.insert(0, (self.kept[0], "x", 0, split))
        for made, (view, kind, first, size) in zip(self.far, jobs):
            made.wait_recv()
            came = self.recv[first : first + size].astype(F32)
            view[...] = (view[...].astype(F32) + came).astype(BF16)
            self.near.append(self.copy(kind, view, 2 * depth + first, size))
            self.sent.append(self.near[-1])

    def add(self):
        depth = self.place.depth
        for made in self.near:
            made.wait_recv()
        terms = [self.recv[n * depth : (n + 1) * depth].astype(F32) for n in (1, 2)]
        self.total[...] = (self.total[...].astype(F32) + terms[0] + terms[1]).astype(BF16)

    def over_z(self):
        self.add()
        depth = self.place.depth
        slots = self.recv.at[pl.ds(3 * depth, depth - 1)]
        self.along_z = ZSum(self.place, self.total, slots, self.part)
        self.sent += self.along_z.sent

    def result(self):
        return self.along_z.result()

    def finish(self):
        for made in self.sent:
            made.wait_send()


def block_shape(size, pad):
    return (size, pad) if pad % 128 == 0 else (pad, size)


def spread_blocks(target, value, pad):
    if pad % 128 == 0:
        for n in range(DPAD // pad):
            target[n] = value[:, n * pad : (n + 1) * pad].astype(BF16)
    else:
        flipped = value.T.astype(BF16)
        for n in range(DPAD // pad):
            target[n] = flipped[n * pad : (n + 1) * pad]


def one_block(value, rows, pad):
    return (value if pad % 128 == 0 else value.T)[:, :rows]


def scatter_slots(depth):
    return 3 * depth + depth - 1


def scatter_copies(depth):
    return 6 + depth - 1


def store_blocks(ref, start, value):
    pad = ref.shape[1]
    for k in range(TILE // pad):
        ref[start // pad + k] = value[k * pad : (k + 1) * pad]


def row_tiles(count, body):
    def step(r, carry):
        body(pl.multiple_of(r * TILE, TILE))
        return carry

    lax.fori_loop(0, count // TILE, step, 0)


def ffn_kernel(
    depth, rows, normed2, cot_t, middle, ffn_w, down_w, grads, down_sum, hidden_out, grad_n2, cot,
    wide_w, down_buf, down_g, down_r, n_other, c_other, hid, d_gate, d_up, n_t, c_t, ffn_own, parts,
    received, packed, send_sems, recv_sems, local_sems,
):
    tokens = normed2.shape[0]
    cols = ffn_w.shape[-1]
    p = Place(depth, send_sems, recv_sems)
    pad = DPAD // (2 * depth)
    count = trimmed(rows, pad)
    moved = pl.ds(0, count)
    trim = lambda ref: ref.at[..., moved, :]
    loads = [
        pltpu.make_async_copy(
            trim(ffn_w.at[w, y]),
            wide_w.at[w, :, :, moved, pl.ds(y * cols, cols)],
            local_sems.at[2 * w + y],
        )
        for w in range(2)
        for y in range(2)
    ]
    loads.append(
        pltpu.make_async_copy(trim(down_w), trim(down_buf.at[p.y, p.x]), local_sems.at[4])
    )
    for load in loads:
        load.start()
    if count < pad:
        wide_w[:, :, :, count:, :] = jnp.zeros((2, 2, depth, pad - count, 2 * cols), BF16)
        down_buf[:, :, :, count:, :] = jnp.zeros((2, 2, depth, pad - count, cols), BF16)
    p.barrier(["c", "x", "y"])
    n_copy = p.copy("c", normed2, n_other)
    down = PlaneGather(p, None, down_buf, depth // 2, trim)
    loads[4].wait()
    down.over_x()
    down.over_y()
    cot[...] = widen(cot_t, depth, rows, pad).astype(BF16)
    c_copy = p.copy("c", cot, c_other)
    for load in loads[:4]:
        load.wait()

    def sides(s):
        return (n_other, c_other) if s else (normed2, cot)

    for s in range(2):
        if s:
            n_copy.wait_recv()
            c_copy.wait_recv()
        n_from, c_from = sides(s)
        both = slice(s * tokens, (s + 1) * tokens)
        n_t[:, both] = transposed(n_from[...])
        c_t[:, both] = transposed(c_from[...])
        def tile(start):
            span = pl.ds(s * tokens + start, TILE)
            n_rows = n_from[pl.ds(start, TILE), :]
            gate = dot(n_rows, wide_w[0].reshape(DPAD, 2 * cols))
            upper = dot(n_rows, wide_w[1].reshape(DPAD, 2 * cols))
            sigma = jax.nn.sigmoid(gate)
            silu = gate * sigma
            hid[span, :] = (silu * upper).astype(BF16)
            d_gate[span, :] = (upper * sigma * (1.0 + gate * (1.0 - sigma))).astype(BF16)
            d_up[span, :] = silu.astype(BF16)

        row_tiles(tokens, tile)
    down.diagonal_y()
    down.diagonal_x()

    def weight_grad(left, right, target):
        def tile(start):
            side = dot(left[pl.ds(start, TILE), :], right[...]).astype(BF16)
            for y in range(2):
                store_blocks(target.at[y], start, side[:, y * cols : (y + 1) * cols])

        row_tiles(DPAD, tile)

    weight_grad(c_t, hid, down_g)
    total = PlaneScatter(p, down_g, down_r, depth // 2, trim)
    total.start()
    down.arrived()

    for s in (1, 0):
        n_from, c_from = sides(s)
        both = slice(s * tokens, (s + 1) * tokens)
        part = None
        for y in range(2):
            lanes = slice(y * cols, (y + 1) * cols)
            w_down = down_buf[y].reshape(DPAD, cols)
            grad_hid = dot(c_from[...], w_down)
            d_gate[both, lanes] = (grad_hid * d_gate[both, lanes].astype(F32)).astype(BF16)
            d_up[both, lanes] = (grad_hid * d_up[both, lanes].astype(F32)).astype(BF16)
            out = dot_nt(hid[both, lanes], w_down)
            part = out if part is None else part + out
        back = dot_nt(d_gate[both, :], wide_w[0].reshape(DPAD, 2 * cols))
        back += dot_nt(d_up[both, :], wide_w[1].reshape(DPAD, 2 * cols))
        if s:
            parts[0] = part.astype(BF16)
            parts[1] = back.astype(BF16)
            shared = [p.copy("c", parts.at[n], received.at[n]) for n in range(2)]
        else:
            ffn_own[...] = part + middle[...]
            grad_n2[...] = back
    total.forward()
    saved = []
    for w, right in ((0, d_gate), (1, d_up)):
        weight_grad(n_t, right, packed.at[w])
        made = pltpu.make_async_copy(packed.at[w], grads.at[w], local_sems.at[w])
        made.start()
        saved.append(made)
    for made in shared:
        made.wait_recv()

    narrow(hidden_out, ffn_own[...] + received[0].astype(F32), depth, rows, pad)
    grad_n2[...] += received[1].astype(F32)
    total.add()
    down_sum[...] = total.total[...]
    total.finish()
    down.finish()
    for made in shared + [n_copy, c_copy]:
        made.wait_send()
    for made in saved:
        made.wait()


def ffn(normed2, cot_t, middle, ffn_w, down_w, rows):
    width, tokens = cot_t.shape
    depth, pad, cols = down_w.shape
    token_rows = pltpu.VMEM((tokens, DPAD), BF16)
    wide = pltpu.VMEM((2 * tokens, 2 * cols), BF16)
    flipped = pltpu.VMEM((DPAD, 2 * tokens), BF16)
    pair = pltpu.VMEM((2, tokens, DPAD), BF16)
    copies = 4 + 4 + 6
    return pl.pallas_call(
        functools.partial(ffn_kernel, depth, rows),
        out_shape=[
            jax.ShapeDtypeStruct((2, 2, 2 * depth, pad, cols), BF16),
            jax.ShapeDtypeStruct((depth, pad, cols), BF16),
            jax.ShapeDtypeStruct((width, tokens), BF16),
            jax.ShapeDtypeStruct((tokens, DPAD), F32),
            jax.ShapeDtypeStruct((tokens, DPAD), BF16),
        ],
        in_specs=vmem_specs(3) + [pl.BlockSpec(memory_space=pl.ANY)] * 2,
        out_specs=[pl.BlockSpec(memory_space=pl.ANY)] + vmem_specs(4),
        scratch_shapes=[
            pltpu.VMEM((2, 2, depth, pad, 2 * cols), BF16),
            pltpu.VMEM((2, 2, depth, pad, cols), BF16),
            pltpu.VMEM((2, 2 * depth, pad, cols), BF16),
            pltpu.VMEM((3 * depth, pad, cols), BF16),
            token_rows, token_rows, wide, wide, wide, flipped, flipped,
            pltpu.VMEM((tokens, DPAD), F32), pair, pair,
            pltpu.VMEM((2, 2, 2 * depth, pad, cols), BF16),
            pltpu.SemaphoreType.DMA((copies,)),
            pltpu.SemaphoreType.DMA((copies,)),
            pltpu.SemaphoreType.DMA((5,)),
        ],
        compiler_params=pltpu.CompilerParams(
            vmem_limit_bytes=61 << 20, collective_id=1, has_side_effects=True
        ),
        cost_estimate=pl.CostEstimate(
            flops=24 << 30, bytes_accessed=30 << 20, transcendentals=2 << 20
        ),
        name="ffn",
    )(normed2, cot_t, middle, ffn_w, down_w)


def mid_kernel(
    depth, width,
    ffn_g, down_sum, grad_n2, middle, cot, gains, out_w, q, kv, attn, lse, segments,
    dq_t, dkv_sum, grad_middle, gain_grad, out_grad, down_grad, gate_sum, up_sum,
    mid_b, out_g, out_c, out_r, ffn_r, down_r, stage, grad_attn, q_aug, g_aug, q3, g3, k3, v3, k_t,
    dkv, acc_kv, diagonal, kv_c, kv_y, send_sems, recv_sems, local_sems,
):
    tokens = q.shape[0]
    tiles = tokens // TILE
    back = 1024 // TILE
    rows = down_grad.shape[0]
    pad = DPAD // (2 * depth)
    out_cols = HEADS * HEAD_DIM // 4
    p = Place(depth, send_sems, recv_sems)
    trim = lambda ref: ref.at[..., pl.ds(0, trimmed(rows, pad)), :]
    p.barrier()
    ffn_sums = [
        PlaneScatter(
            p, ffn_g.at[w], ffn_r.at[w], (0, depth // 2)[w], trim, stage.at[w],
            local_sems.at[pl.ds(3 * w, 3)],
        )
        for w in range(2)
    ]
    ffn_sums[0].start_far()
    ffn_sums[1].start()
    down_total = ZSum(p, down_sum, down_r, trim)

    gain = gains[1:2, :]
    gain_grad[...] = jnp.zeros_like(gain_grad)

    def norm_tile(start):
        span = pl.ds(start, TILE)
        mid, up = middle[span, :], grad_n2[span, :]
        inv = lax.rsqrt(mean_rows(mid * mid, width) + EPSILON)
        scaled = up * gain
        mean = mean_rows(scaled * mid, width)
        grad = cot[span, :].astype(F32) + inv * (scaled - mid * (inv * inv * mean))
        grad_middle[span, :] = grad
        gain_grad[...] += jnp.sum(up * mid * inv, axis=0, keepdims=True)
        mid_b[span, :] = grad.astype(BF16)
        for b in range(4):
            side = dot_nt(mid_b[span, :], out_w[b % 2, b // 2])
            grad_attn[span, b * out_cols : (b + 1) * out_cols] = side.astype(BF16)

    row_tiles(tokens, norm_tile)
    attn_t = attn[...].astype(F32).T
    for b in range(4):
        left = attn_t[b * out_cols : (b + 1) * out_cols, :].astype(BF16)
        spread_blocks(out_g.at[b % 2, b // 2], dot(left, mid_b[...]), pad)
    out_cross = p.copy("c", out_g.at[1 - p.c], out_c)

    def block_span(block):
        return pl.ds(pl.multiple_of(block * tokens, tokens), tokens)

    own_seg = segments[:, block_span(p.m)]
    nothing = jnp.zeros((1, TILE), F32)
    q_flat = (q[...].astype(F32) * SCORE_SCALE).T.astype(BF16)
    g_flat = grad_attn[...].astype(F32).T
    for h in range(HEADS):
        g, j = h // GROUP, h % GROUP
        span = slice(h * HEAD_DIM, (h + 1) * HEAD_DIM)
        for i in range(tiles):
            cols, lanes = slice(i * TILE, (i + 1) * TILE), head_lanes(i, j)
            sides = g_flat[span, cols]
            delta = jnp.sum(sides * attn_t[span, cols], axis=0, keepdims=True)
            q_aug[g, :HEAD_DIM, lanes] = q_flat[span, cols]
            q_aug[g, HEAD_DIM:, lanes] = query_features(
                own_seg[:, cols], three_parts(-lse[g : g + 1, lanes])
            )
            g_aug[g, :HEAD_DIM, lanes] = sides.astype(BF16)
            g_aug[g, HEAD_DIM:, lanes] = features(
                three_parts(-delta), [nothing] * SEGMENTS
            ).astype(BF16)
            q3[g, lanes, :] = q[cols, span]
            g3[g, lanes, :] = grad_attn[cols, span]
    for n in range(3):
        block = jnp.maximum(p.m - n, 0)
        span = block_span(block)
        added = key_features(segments[:, span])
        for g in range(KV_HEADS):
            part = kv[block, g]
            k_t[g * HEAD_DIM : (g + 1) * HEAD_DIM, span] = transposed(part)[:HEAD_DIM]
            k3[g, span, :HEAD_DIM] = part[:, :HEAD_DIM]
            v3[g, span, :HEAD_DIM] = part[:, HEAD_DIM:]
            k3[g, span, HEAD_DIM:] = added
            v3[g, span, HEAD_DIM:] = added
    diagonal[...] = diagonal_bias()
    dq_t[...] = jnp.zeros_like(dq_t)
    dkv[...] = jnp.zeros_like(dkv)
    out_cross.wait_recv()
    own = out_g.at[p.c]
    own[...] = (own[...].astype(F32) + out_c[...].astype(F32)).astype(BF16)
    out_sum = PlaneScatter(p, own, out_r, depth // 2)
    out_sum.start()
    ffn_sums[0].forward()

    def key_tile(t, queries, on_diagonal=()):
        keys = pl.ds(pl.multiple_of(t * TILE, TILE), TILE)

        def group(g, carry):
            k_g, v_g = k3[g, keys, :], v3[g, keys, :]
            kt_g = k_t[pl.ds(pl.multiple_of(g * HEAD_DIM, HEAD_DIM), HEAD_DIM), keys]
            dk, dv = None, None
            for i in queries:
                lanes = pl.ds(i * WIDE, WIDE)
                scores = dot(k_g, q_aug[g, :, lanes])
                if i in on_diagonal:
                    scores += diagonal[...]
                probs = jnp.exp2(scores * LOG2E)
                dscores = (probs * dot(v_g, g_aug[g, :, lanes])).astype(BF16)
                add_v = dot(probs.astype(BF16), g3[g, lanes, :])
                add_k = dot(dscores, q3[g, lanes, :])
                dq_t[g, :, lanes] += dot(kt_g, dscores)
                dk = add_k if dk is None else dk + add_k
                dv = add_v if dv is None else dv + add_v
            acc_kv[g] = dk * SCORE_SCALE
            acc_kv[KV_HEADS + g] = dv
            return carry

        lax.fori_loop(0, KV_HEADS, group, 0)
        for n in range(2 * KV_HEADS):
            dkv[keys, n * HEAD_DIM : (n + 1) * HEAD_DIM] = acc_kv[n].astype(BF16)

    def key_span(low, high, queries):
        def step(t, carry):
            key_tile(t, queries)
            return carry

        lax.fori_loop(low, high, step, 0)

    def part_of(index):
        return dkv.at[pl.ds(pl.multiple_of(index * tokens, tokens), tokens)]

    first = p.m * tiles
    key_span(jnp.maximum(first - back, 0), jnp.maximum(first + 1 - back, 0), (0,))
    key_span(jnp.maximum(first + 1 - back, 0), jnp.maximum(first - 2, 0), (0, 1))
    ffn_sums[1].forward()
    out_sum.forward()
    ffn_sums[0].start_near()
    key_span(jnp.maximum(first - 2, 0), jnp.maximum(first - 1, 0), (0, 1))
    key_span(jnp.maximum(first - 1, 0), first, (0, 1))
    beside = p.m + 1 - 2 * p.c
    cross = [
        p.copy("c", part_of(index), kv_c.at[n])
        for n, index in enumerate((beside, (beside + 2) % 4))
    ]
    cross[1].wait_recv()
    away = part_of((p.m + 2) % 4)
    away[...] = (away[...].astype(F32) + kv_c[1].astype(F32)).astype(BF16)
    across = p.copy("y", away, kv_y)
    out_sum.over_z()
    key_tile(first + 1, (1,), (1,))
    key_tile(first, (0, 1), (0,))
    down_grad[...] = down_total.result()[:rows]
    for w in range(2):
        ffn_sums[w].add()
        (gate_sum, up_sum)[w][...] = ffn_sums[w].total[...]
    cross[0].wait_recv()
    across.wait_recv()
    dkv_sum[...] = part_of(p.m)[...].astype(F32) + kv_c[0].astype(F32) + kv_y[...].astype(F32)
    out_grad[...] = one_block(out_sum.result(), rows, pad)
    for part in ffn_sums + [out_sum, down_total]:
        part.finish()
    for made in cross + [across, out_cross]:
        made.wait_send()


def middle_back(ffn_g, down_sum, grad_n2, middle, cot, gains, out_w, q, kv, attn, lse, segments,
                depth, rows, width):
    tokens, query_cols = q.shape
    pad = DPAD // (2 * depth)
    cols = ffn_g.shape[-1]
    kv_cols = KV_HEADS * kv.shape[-1]
    out_cols = query_cols // 4
    whole = 4 * tokens
    slots = scatter_slots(depth)
    copies = 3 * scatter_copies(depth) + 4 + depth - 1
    heads_q = pltpu.VMEM((KV_HEADS, GROUP * tokens, HEAD_DIM), BF16)
    heads_kv = pltpu.VMEM((KV_HEADS, whole, AUGMENTED), BF16)
    flipped = pltpu.VMEM((KV_HEADS, AUGMENTED, GROUP * tokens), BF16)
    return pl.pallas_call(
        functools.partial(mid_kernel, depth, width),
        out_shape=[
            jax.ShapeDtypeStruct((KV_HEADS, HEAD_DIM, GROUP * tokens), F32),
            jax.ShapeDtypeStruct((tokens, kv_cols), F32),
            jax.ShapeDtypeStruct((tokens, DPAD), F32),
            jax.ShapeDtypeStruct((1, DPAD), F32),
            jax.ShapeDtypeStruct((out_cols, rows), F32),
            jax.ShapeDtypeStruct((rows, cols), F32),
            *[jax.ShapeDtypeStruct((depth, pad, cols), BF16)] * 2,
        ],
        in_specs=[pl.BlockSpec(memory_space=pl.ANY)] + vmem_specs(11),
        out_specs=vmem_specs(8),
        scratch_shapes=[
            pltpu.VMEM((tokens, DPAD), BF16),
            pltpu.VMEM((2, 2, 2 * depth, *block_shape(out_cols, pad)), BF16),
            pltpu.VMEM((2, 2 * depth, *block_shape(out_cols, pad)), BF16),
            pltpu.VMEM((slots, *block_shape(out_cols, pad)), BF16),
            pltpu.VMEM((2, 3 * depth, pad, cols), BF16),
            pltpu.VMEM((depth - 1, pad, cols), BF16),
            pltpu.VMEM((2, 2 * depth, pad, cols), BF16),
            pltpu.VMEM((tokens, query_cols), BF16),
            flipped, flipped, heads_q, heads_q, heads_kv, heads_kv,
            pltpu.VMEM((KV_HEADS * HEAD_DIM, whole), BF16),
            pltpu.VMEM((whole, kv_cols), BF16),
            pltpu.VMEM((2 * KV_HEADS, TILE, HEAD_DIM), F32),
            pltpu.VMEM((TILE, WIDE), F32),
            pltpu.VMEM((2, tokens, kv_cols), BF16),
            pltpu.VMEM((tokens, kv_cols), BF16),
            pltpu.SemaphoreType.DMA((copies,)),
            pltpu.SemaphoreType.DMA((copies,)),
            pltpu.SemaphoreType.DMA((6,)),
        ],
        compiler_params=pltpu.CompilerParams(
            vmem_limit_bytes=61 << 20, collective_id=2, has_side_effects=True
        ),
        cost_estimate=pl.CostEstimate(
            flops=40 << 30, bytes_accessed=50 << 20, transcendentals=8 << 20
        ),
        name="middle_back",
    )(ffn_g, down_sum, grad_n2, middle, cot, gains, out_w, q, kv, attn, lse, segments)


def tail_kernel(
    depth, rows, width,
    dq_t, dkv, cosine_t, sine_t, x_t, grad_middle, gains, in_w, gain2, gate_sum, up_sum,
    grad_hidden, in_grad, gain1_sum, gain2_sum, gate_grad, up_grad,
    ffn_r, proj, proj_b, in_g, in_c, in_r, grad_x, gain_own, gain_r, send_sems, recv_sems,
):
    tokens = x_t.shape[1]
    query_cols = HEADS * HEAD_DIM
    in_cols = in_w.shape[2]
    pad = DPAD // (2 * depth)
    turned = (HEADS + KV_HEADS) * HEAD_DIM
    p = Place(depth, send_sems, recv_sems)
    p.barrier()
    trim = lambda ref: ref.at[..., pl.ds(0, trimmed(rows, pad)), :]
    ffn_sums = [ZSum(p, total, ffn_r.at[w], trim) for w, total in enumerate((gate_sum, up_sum))]
    x_f = widen(x_t, depth, rows, pad)
    gain = gains[0:1, :]
    inv = lax.rsqrt(mean_rows(x_f * x_f, width) + EPSILON)
    normed1 = (x_f * inv * gain).astype(BF16)
    cosine = lane_tables(cosine_t[...])
    sine = signed(lane_tables(sine_t[...]), True)
    parts = [
        jnp.concatenate(
            [dq_t[h // GROUP, :, head_lanes(i, h % GROUP)] for i in range(tokens // TILE)], axis=1
        )
        for h in range(HEADS)
    ]
    proj[:, :query_cols] = jnp.concatenate(parts, axis=0).T * SCORE_SCALE
    proj[:, query_cols:] = dkv[...]
    for j in range(turned // 128):
        lanes = slice(128 * j, 128 * (j + 1))
        proj[:, lanes] = rope(proj[:, lanes], cosine, sine)
    for b in range(4):
        proj_b[b] = proj[:, b * in_cols : (b + 1) * in_cols].astype(BF16)
    for other in (1, 0):
        c = (1 - p.c) if other else p.c
        for y in range(2):
            left = transposed(proj_b[2 * y + c])
            spread_blocks(in_g.at[c, y], dot(left, normed1), pad)
        if other:
            in_cross = p.copy("c", in_g.at[c], in_c)
    in_cross.wait_recv()
    own = in_g.at[p.c]
    own[...] = (own[...].astype(F32) + in_c[...].astype(F32)).astype(BF16)
    in_sum = PlaneScatter(p, own, in_r, depth // 2)
    in_sum.start()
    up = None
    for b in range(4):
        term = dot(proj_b[b], in_w[b % 2, b // 2])
        up = term if up is None else up + term
    scaled = up * gain
    mean = mean_rows(scaled * x_f, width)
    grad_x[...] = grad_middle[...] + inv * (scaled - x_f * (inv * inv * mean))
    gain_own[...] = jnp.zeros_like(gain_own)
    gain_own[0:1, :] = jnp.sum(up * x_f * inv, axis=0, keepdims=True)
    gain_own[1:2, :] = gain2[...]
    in_sum.forward()
    sent = []
    for n, kind in enumerate(("c", "y", "x")):
        made = p.copy(kind, gain_own.at[pl.ds(8 * n, 8)], gain_r.at[pl.ds(8 * n, 8)])
        sent.append(made)
        if n == 0:
            narrow(grad_hidden, grad_x[...], depth, rows, pad)
        made.wait_recv()
        if n == 1:
            in_sum.over_z()
        gain_own[8 * (n + 1) : 8 * (n + 2), :] = (
            gain_own[8 * n : 8 * (n + 1), :] + gain_r[8 * n : 8 * (n + 1), :]
        )
    last = gain_own.at[pl.ds(24, 8)]
    arriving = [p.copy(k, last, gain_r.at[pl.ds(24 + 8 * k, 8)]) for k in range(1, depth)]
    total = last[...]
    for k, made in enumerate(arriving):
        made.wait_recv()
        total += gain_r[32 + 8 * k : 40 + 8 * k, :]
    mine = jnp.zeros((8, pad), F32)
    for n in range(2 * depth):
        mine = jnp.where(n == p.x * depth + p.z, total[:, n * pad : (n + 1) * pad], mine)
    gain1_sum[...] = mine[0:1, :rows]
    gain2_sum[...] = mine[1:2, :rows]
    for w, target in enumerate((gate_grad, up_grad)):
        target[...] = ffn_sums[w].result()[:rows]
        ffn_sums[w].finish()
    in_grad[...] = one_block(in_sum.result(), rows, pad)
    in_sum.finish()
    for made in sent + arriving + [in_cross]:
        made.wait_send()


def tail(
    dq_t, dkv, cosine_t, sine_t, x_t, grad_middle, gains, in_w, gain2, gate_sum, up_sum,
    depth, rows, width,
):
    tokens = x_t.shape[1]
    pad = DPAD // (2 * depth)
    in_cols = in_w.shape[2]
    total = HEADS * HEAD_DIM + dkv.shape[1]
    slots = scatter_slots(depth)
    copies = scatter_copies(depth) + 1 + 3 + 3 * (depth - 1)
    cols = gate_sum.shape[2]
    return pl.pallas_call(
        functools.partial(tail_kernel, depth, rows, width),
        out_shape=[
            jax.ShapeDtypeStruct((width, tokens), F32),
            jax.ShapeDtypeStruct((in_cols, rows), F32),
            *[jax.ShapeDtypeStruct((1, rows), F32)] * 2,
            *[jax.ShapeDtypeStruct((rows, cols), F32)] * 2,
        ],
        in_specs=vmem_specs(11),
        out_specs=vmem_specs(6),
        scratch_shapes=[
            pltpu.VMEM((2, depth - 1, pad, cols), BF16),
            pltpu.VMEM((tokens, total), F32),
            pltpu.VMEM((4, tokens, in_cols), BF16),
            pltpu.VMEM((2, 2, 2 * depth, *block_shape(in_cols, pad)), BF16),
            pltpu.VMEM((2, 2 * depth, *block_shape(in_cols, pad)), BF16),
            pltpu.VMEM((slots, *block_shape(in_cols, pad)), BF16),
            pltpu.VMEM((tokens, DPAD), F32),
            pltpu.VMEM((32, DPAD), F32),
            pltpu.VMEM((24 + 8 * depth, DPAD), F32),
            pltpu.SemaphoreType.DMA((copies,)),
            pltpu.SemaphoreType.DMA((copies,)),
        ],
        compiler_params=pltpu.CompilerParams(
            vmem_limit_bytes=61 << 20, collective_id=3, has_side_effects=True
        ),
        cost_estimate=pl.CostEstimate(
            flops=8 << 30, bytes_accessed=30 << 20, transcendentals=0
        ),
        name="tail",
    )(dq_t, dkv, cosine_t, sine_t, x_t, grad_middle, gains, in_w, gain2, gate_sum, up_sum)


def rotary_tables(position_ids):
    half_dim = HEAD_DIM // 2
    frequency = jnp.exp(
        jnp.arange(half_dim, dtype=F32) * (-2.0 * math.log(10000.0) / HEAD_DIM)
    )
    angles = frequency[:, None] * position_ids.astype(F32)[None, :]
    return jnp.cos(angles), jnp.sin(angles)


def per_device(
    hidden_in, cotangent, segments, positions, attn_in, attn_out, w_gate, w_up, w_down,
    norm1_gain, norm2_gain,
):
    tokens, width = hidden_in.shape[1:]
    dp_size = lax.axis_size("dp")
    depth = dp_size // 2
    rows = width // dp_size
    pad = DPAD // dp_size

    ffn_blocks = [w_gate, w_up, w_down.T]
    if trimmed(rows, pad) == pad:
        ffn_blocks = [jnp.pad(w, ((0, pad - rows), (0, 0))) for w in ffn_blocks]
    x_t, cot_t = hidden_in[0].T, cotangent[0].T
    cosine_t, sine_t = rotary_tables(positions[0])
    attn, lse, middle, normed2, gains, q, kv, out_w, in_w, ffn_w, down_w = front(
        attn_in.T, attn_out, norm1_gain[None], norm2_gain[None], *ffn_blocks,
        x_t, cosine_t, sine_t, segments, depth, rows,
    )
    ffn_g, down_sum, hidden_out, grad_n2, cot = ffn(normed2, cot_t, middle, ffn_w, down_w, rows)
    dq_t, dkv, grad_middle, gain2, g_out, g_down, gate_sum, up_sum = middle_back(
        ffn_g, down_sum, grad_n2, middle, cot, gains, out_w, q, kv, attn, lse, segments,
        depth, rows, width,
    )
    grad_hidden, g_in, g_gain1, g_gain2, g_gate, g_up = tail(
        dq_t, dkv, cosine_t, sine_t, x_t, grad_middle, gains, in_w, gain2, gate_sum, up_sum,
        depth, rows, width,
    )
    return (
        hidden_out.T[None],
        grad_hidden.T[None],
        g_in.T,
        g_out,
        g_gate,
        g_up,
        g_down.T,
        g_gain1[0],
        g_gain2[0],
    )


def solution(mesh):
    return jax.shard_map(
        per_device,
        mesh=mesh,
        in_specs=(
            P("dp", "mp", None),
            P("dp", "mp", None),
            P("dp", None),
            P("dp", "mp"),
            P("dp", "mp"),
            P("mp", "dp"),
            P("dp", "mp"),
            P("dp", "mp"),
            P("mp", "dp"),
            P("dp"),
            P("dp"),
        ),
        out_specs=(
            P("dp", "mp", None),
            P("dp", "mp", None),
            P("dp", "mp"),
            P("mp", "dp"),
            P("dp", "mp"),
            P("dp", "mp"),
            P("mp", "dp"),
            P("dp"),
            P("dp"),
        ),
        check_vma=False,
    )
```

```python
import functools
import math

import jax
import jax.numpy as jnp
from jax import lax
from jax.experimental import pallas as pl
from jax.experimental.pallas import tpu as pltpu
from jax.sharding import PartitionSpec as P

HEADS = 15
KV_HEADS = 5
GROUP = HEADS // KV_HEADS
HEAD_DIM = 64
DPAD = 1024
TILE = 256
EPSILON = 1e-05
SCORE_SCALE = 0.125
MASK_FILL = -1e30
LOG2E = 1.4426950408889634
EXP_SCALE = SCORE_SCALE * LOG2E
GAIN_ROWS = 16
SEGMENTS = 4
AUGMENTED = HEAD_DIM + 16
WIDE = GROUP * TILE
BF16 = jnp.bfloat16
F32 = jnp.float32


def dot(a, b):
    return jnp.dot(a, b, preferred_element_type=F32)


def dot_nt(a, b):
    return lax.dot_general(a, b, (((1,), (1,)), ((), ())), preferred_element_type=F32)


def vmem_specs(count):
    return [pl.BlockSpec(memory_space=pltpu.VMEM)] * count


def transposed(value):
    return value.astype(F32).T.astype(BF16)


class Place:
    def __init__(self, depth, send_sems, recv_sems):
        dp_index, m = lax.axis_index("dp"), lax.axis_index("mp")
        self.depth = depth
        self.z, self.x = dp_index // 2, dp_index % 2
        self.m, self.y, self.c = m, m // 2, m % 2
        self.send_sems, self.recv_sems = send_sems, recv_sems
        self.count = 0

    def peer(self, kind):
        z, x, y, c = self.z, self.x, self.y, self.c
        if kind == "x":
            x = 1 - x
        elif kind == "y":
            y = 1 - y
        elif kind == "c":
            c = 1 - c
        else:
            z = (z + kind) % self.depth
        return 2 * z + x, 2 * y + c

    def kinds(self):
        return ["x", "y", "c"] + list(range(1, self.depth))

    def barrier(self, kinds=None):
        semaphore = pltpu.get_barrier_semaphore()
        kinds = kinds or self.kinds()
        for kind in kinds:
            pl.semaphore_signal(
                semaphore, inc=1, device_id=self.peer(kind), device_id_type=pl.DeviceIdType.MESH
            )
        pl.semaphore_wait(semaphore, len(kinds))

    def copy(self, kind, source, target=None):
        index = self.count
        self.count += 1
        made = pltpu.make_async_remote_copy(
            src_ref=source,
            dst_ref=source if target is None else target,
            send_sem=self.send_sems.at[index],
            recv_sem=self.recv_sems.at[index],
            device_id=self.peer(kind),
            device_id_type=pl.DeviceIdType.MESH,
        )
        made.start()
        return made


class PlaneGather:
    def __init__(self, place, source, buffer, by_x, part=lambda ref: ref):
        self.place, self.source, self.buffer, self.part = place, source, buffer, part
        self.split = place.depth - by_x
        self.sent, self.last = [], []

    def over_z(self, slot=None):
        p = self.place
        slot = self.part(self.buffer.at[p.y, p.x, p.z]) if slot is None else slot
        self.arriving = [p.copy(k, self.source, slot) for k in range(1, p.depth)]
        self.sent += self.arriving

    def stacked(self):
        for made in self.arriving:
            made.wait_recv()

    def over_x(self):
        p = self.place
        self.by_x = p.copy("x", self.part(self.buffer.at[p.y, p.x]))
        self.sent.append(self.by_x)

    def over_y(self):
        p = self.place
        self.by_y = p.copy("y", self.part(self.buffer.at[p.y, p.x]))
        self.sent.append(self.by_y)

    def diagonal_x(self):
        p = self.place
        self.by_y.wait_recv()
        span = pl.ds(self.split, p.depth - self.split)
        self.last.append(p.copy("x", self.part(self.buffer.at[1 - p.y, p.x, span])))

    def diagonal_y(self):
        p = self.place
        self.by_x.wait_recv()
        if self.split:
            span = pl.ds(0, self.split)
            self.last.append(p.copy("y", self.part(self.buffer.at[p.y, 1 - p.x, span])))

    def arrived(self):
        for made in self.last:
            made.wait_recv()

    def finish(self):
        for made in self.sent + self.last:
            made.wait_send()


def rope(value, cosine, sine):
    lane = lax.broadcasted_iota(jnp.int32, value.shape, 1)
    half = HEAD_DIM // 2
    partner = jnp.where(
        lane % HEAD_DIM < half, pltpu.roll(value, 128 - half, 1), pltpu.roll(value, half, 1)
    )
    return value * cosine + partner * sine


def trimmed(rows, pad):
    return rows if rows % 8 == 0 else pad


def natural(block, depth):
    return 2 * (block % depth) + block // depth


def widen(source, depth, rows, pad):
    filler = jnp.zeros((pad - rows, source.shape[1]), F32)
    parts = []
    for b in range(2 * depth):
        first = natural(b, depth) * rows
        parts += [source[first : first + rows, :].astype(F32), filler]
    return jnp.concatenate(parts, axis=0).T


def narrow(target, value, depth, rows, pad):
    flipped = value.T
    for b in range(2 * depth):
        first = natural(b, depth) * rows
        target[first : first + rows, :] = flipped[b * pad : b * pad + rows, :].astype(target.dtype)


def side_by_side(ref, first, size):
    _, depth, _, pad = ref.shape
    span = pl.ds(first, size)
    return jnp.concatenate(
        [ref[b // depth, b % depth, span, :] for b in range(2 * depth)], axis=1
    )


def lane_tables(table):
    return jnp.concatenate([table] * (256 // HEAD_DIM), axis=0).T


def signed(table, back):
    lane = lax.broadcasted_iota(jnp.int32, table.shape, 1) % HEAD_DIM
    first = lane < HEAD_DIM // 2
    return jnp.where(first, table, -table) if back else jnp.where(first, -table, table)


def mean_rows(value, width):
    return jnp.sum(value, axis=-1, keepdims=True) * (1.0 / width)


def diagonal_bias():
    key = lax.broadcasted_iota(jnp.int32, (TILE, WIDE), 0)
    query = lax.broadcasted_iota(jnp.int32, (TILE, WIDE), 1) % TILE
    return jnp.where(key <= query, 0.0, MASK_FILL)


def features(first, segment_rows):
    spare = 16 - len(first) - SEGMENTS
    zeros = jnp.zeros((spare, first[0].shape[1]), F32)
    return jnp.concatenate(list(first) + segment_rows + [zeros], axis=0)


def key_features(segment):
    other = [jnp.where(segment != n, MASK_FILL, 0.0) for n in range(SEGMENTS)]
    return features([jnp.ones(segment.shape, F32)] * 3, other).T.astype(BF16)


def query_features(segment, first):
    same = [jnp.where(segment == n, 1.0, 0.0) for n in range(SEGMENTS)]
    return features(first, same).astype(BF16)


def three_parts(value):
    parts = []
    for _ in range(3):
        parts.append(value.astype(BF16).astype(F32))
        value = value - parts[-1]
    return parts


def head_lanes(i, j):
    return slice(i * WIDE + j * TILE, i * WIDE + (j + 1) * TILE)


def front_kernel(
    depth, rows, width, in_cols,
    attn_in_t, attn_out, gain_one, gain_two, w_gate, w_up, w_down_t, x_t, cosine_t, sine_t, segments,
    attn, lse, middle, normed2, gains, q_out, kv_out, out_w_out, in_w_out, ffn_w, down_w,
    q, kv, out_w, in_w, a_buf, x_in, cosine, sine, normed1, proj, q_aug, k3, v_t, acc, peak, flat,
    diagonal, send_sems, recv_sems, local_sems,
):
    tokens = x_in.shape[0]
    tiles = tokens // TILE
    back = 1024 // TILE
    pad = DPAD // (2 * depth)
    lead = in_cols + GAIN_ROWS
    query_cols = HEADS * HEAD_DIM
    out_cols = query_cols // 4
    p = Place(depth, send_sems, recv_sems)
    block = a_buf.at[p.c, p.y, p.x, p.z]
    block[...] = jnp.zeros_like(block)
    block[0:in_cols, 0:rows] = attn_in_t[...]
    block[in_cols : in_cols + 1, 0:rows] = gain_one[...]
    block[in_cols + 1 : in_cols + 2, 0:rows] = gain_two[...]
    block[lead : lead + out_cols, 0:rows] = attn_out[...]
    moved = pl.ds(0, trimmed(rows, pad))
    trim = lambda ref: ref.at[..., moved, :]
    own = [
        pltpu.make_async_copy(
            source, trim(ffn_w.at[w, p.y, p.x, p.z] if w < 2 else down_w.at[p.z]), local_sems.at[w]
        )
        for w, source in enumerate((w_gate, w_up, w_down_t))
    ]
    for made in own:
        made.start()
    p.barrier()
    first_part = lambda ref: ref.at[..., pl.ds(0, lead), :]
    last_part = lambda ref: ref.at[..., pl.ds(lead, out_cols), :]
    buffer = a_buf.at[p.c]
    plane = PlaneGather(p, first_part(block), buffer, depth // 2, first_part)
    output = PlaneGather(p, last_part(block), buffer, depth // 2, last_part)
    gate = PlaneGather(p, w_gate, ffn_w.at[0], depth, trim)
    up = PlaneGather(p, w_up, ffn_w.at[1], depth // 2, trim)
    down = PlaneGather(p, w_down_t, None, 0)
    plane.over_z()
    x_f = widen(x_t, depth, rows, pad)
    x_in[...] = x_f.astype(BF16)
    cosine[...] = lane_tables(cosine_t[...])
    sine[...] = signed(lane_tables(sine_t[...]), False)
    inv_one = lax.rsqrt(mean_rows(x_f * x_f, width) + EPSILON)
    def block_span(block):
        return pl.ds(pl.multiple_of(block * tokens, tokens), tokens)

    plane.stacked()
    plane.over_x()
    plane.over_y()
    output.over_z()
    gate.over_z()
    own_seg = segments[:, block_span(p.m)]
    nothing = jnp.zeros(own_seg.shape, F32)
    own_features = query_features(own_seg, [nothing] * 3)
    for g in range(KV_HEADS):
        for i in range(tiles):
            for j in range(GROUP):
                q_aug[g, HEAD_DIM:, head_lanes(i, j)] = own_features[:, i * TILE : (i + 1) * TILE]
    ones = lax.broadcasted_iota(jnp.int32, (16, 4 * tokens), 0) == 0
    for g in range(KV_HEADS):
        v_t[g, HEAD_DIM:, :] = jnp.where(ones, 1.0, 0.0).astype(BF16)
    diagonal[...] = diagonal_bias()
    acc[...] = jnp.zeros_like(acc)
    peak[...] = jnp.full_like(peak, MASK_FILL)
    plane.diagonal_y()
    plane.diagonal_x()
    for made in own:
        made.wait()
    up.over_z()
    plane.arrived()
    cross = p.copy("c", first_part(a_buf.at[p.c]))
    output.stacked()
    output.over_x()
    output.over_y()
    for n in range(3):
        span = block_span(jnp.maximum(p.m - n, 0))
        added = key_features(segments[:, span])
        for g in range(KV_HEADS):
            k3[g, span, HEAD_DIM:] = added
    gate.stacked()
    gate.over_x()
    gate.over_y()
    cross.wait()
    for b in range(2 * depth):
        gains[:, b * pad : (b + 1) * pad] = a_buf[
            0, 0, b // depth, b % depth, pl.ds(in_cols, 2), :
        ].astype(F32)
    normed1[...] = (x_f * inv_one * gains[0:1, :]).astype(BF16)
    for b in range(4):
        in_w[b % 2, b // 2] = side_by_side(a_buf.at[b % 2, b // 2], 0, in_cols)

    kv_first = query_cols // 128

    def project(blocks, groups):
        def tile(start):
            span = pl.ds(start, TILE)
            for b in blocks:
                proj[span, b * in_cols : (b + 1) * in_cols] = dot_nt(
                    normed1[span, :], in_w[b % 2, b // 2]
                )
            for j in groups:
                lanes = slice(128 * j, 128 * (j + 1))
                proj[span, lanes] = rope(proj[span, lanes], cosine[span, :], sine[span, :])

        row_tiles(tokens, tile)

    project((2, 3), range(kv_first, (HEADS + KV_HEADS) * HEAD_DIM // 128))
    for g in range(KV_HEADS):
        k_first, v_first = query_cols + g * HEAD_DIM, query_cols + (KV_HEADS + g) * HEAD_DIM
        kv[p.m, g] = jnp.concatenate(
            [proj[:, k_first : k_first + HEAD_DIM], proj[:, v_first : v_first + HEAD_DIM]], axis=1
        ).astype(BF16)
    kv_c = p.copy("c", kv.at[p.m])
    kv_y = [p.copy("y", kv.at[p.m, g]) for g in range(KV_HEADS)]
    down.over_z(trim(down_w.at[p.z]))
    project((0, 1), range(kv_first))
    q[...] = proj[:, :query_cols].astype(BF16)
    q_flat = (proj[:, :query_cols].astype(BF16).astype(F32) * SCORE_SCALE).T.astype(BF16)
    for h in range(HEADS):
        for i in range(tiles):
            part = q_flat[h * HEAD_DIM : (h + 1) * HEAD_DIM, i * TILE : (i + 1) * TILE]
            q_aug[h // GROUP, :HEAD_DIM, head_lanes(i, h % GROUP)] = part
    saved = [
        pltpu.make_async_copy(source, target, local_sems.at[3 + n])
        for n, (source, target) in enumerate(((in_w, in_w_out), (q, q_out)))
    ]
    for made in saved:
        made.start()
    def spread(block, g):
        span = block_span(block)
        part = kv[block, g]
        v_t[g, :HEAD_DIM, span] = transposed(part)[HEAD_DIM:]
        k3[g, span, :HEAD_DIM] = part[:, :HEAD_DIM]

    def attend_units(queries, t, g, on_diagonal=()):
        keys = pl.ds(pl.multiple_of(t * TILE, TILE), TILE)
        places = [pl.ds(i * WIDE, WIDE) for i in queries]
        k_g, v_g = k3[g, keys, :], v_t[g, :, keys]
        old = [peak[pl.ds(g, 1), lanes] for lanes in places]
        scores = [dot(k_g, q_aug[g, :, lanes]) for lanes in places]
        scores = [s + diagonal[...] if i in on_diagonal else s for i, s in zip(queries, scores)]
        new = [jnp.maximum(o, jnp.max(s, axis=0, keepdims=True)) for o, s in zip(old, scores)]
        probs = [jnp.exp2(s * LOG2E - n * LOG2E).astype(BF16) for s, n in zip(scores, new)]
        scale = [jnp.exp2((o - n) * LOG2E) for o, n in zip(old, new)]
        outs = [dot(v_g, b) for b in probs]
        for lanes, n, factor, out in zip(places, new, scale, outs):
            peak[pl.ds(g, 1), lanes] = n
            acc[g, :, lanes] = acc[g, :, lanes] * factor + out

    first_tile = p.m * tiles
    for g in range(KV_HEADS):
        spread(p.m, g)
    for queries, t in (((1,), 1), ((0, 1), 0)):

        def group(g, carry):
            attend_units(queries, first_tile + t, g, (t,))
            return carry

        lax.fori_loop(0, KV_HEADS, group, 0)
        if t:
            up.stacked()
            up.over_x()
            output.diagonal_x()
            output.diagonal_y()

    lows = [jnp.maximum(first_tile + i - back, 0) for i in range(tiles)]
    kv_cy = []

    def pass_on(g):
        kv_y[g].wait_recv()
        kv_cy.append(p.copy("c", kv.at[(p.m + 2) % 4, g]))

    kv_c.wait_recv()
    pass_on(0)
    gate.diagonal_x()
    gate.diagonal_y()
    for g in range(KV_HEADS):
        if g + 1 < KV_HEADS:
            pass_on(g + 1)
        if g == 1:
            up.over_y()
            up.diagonal_y()
        if g == 2:
            output.arrived()
            out_cross = p.copy("c", last_part(a_buf.at[p.c]))
        kv_cy[g].wait_recv()
        for n in (1, 2):
            spread(jnp.maximum(p.m - n, 0), g)
        for low, high, queries in ((lows[0], lows[1], (0,)), (lows[1], first_tile, (0, 1))):

            def step(t, carry):
                attend_units(queries, t, g)
                return carry

            lax.fori_loop(low, high, step, 0)
    saved.append(pltpu.make_async_copy(kv, kv_out, local_sems.at[5]))
    saved[-1].start()
    for h in range(HEADS):
        for i in range(tiles):
            part = acc[h // GROUP, :, head_lanes(i, h % GROUP)]
            flat[h * HEAD_DIM : (h + 1) * HEAD_DIM, i * TILE : (i + 1) * TILE] = (
                part[:HEAD_DIM] / part[HEAD_DIM : HEAD_DIM + 1]
            )
    attn[...] = flat[...].T.astype(BF16)
    lse[...] = jnp.zeros_like(lse)
    for g in range(KV_HEADS):
        lse[g : g + 1, :] = peak[g : g + 1, :] + jnp.log(acc[g, HEAD_DIM : HEAD_DIM + 1, :])
    out_cross.wait()
    for b in range(4):
        out_w[b % 2, b // 2] = side_by_side(a_buf.at[b % 2, b // 2], lead, out_cols)
    saved.append(pltpu.make_async_copy(out_w, out_w_out, local_sems.at[6]))
    saved[-1].start()
    up.diagonal_x()

    def project_out(r, carry):
        span = pl.ds(pl.multiple_of(r * TILE, TILE), TILE)
        mid = x_in[span, :].astype(F32)
        for b in range(4):
            mid += dot(attn[span, b * out_cols : (b + 1) * out_cols], out_w[b % 2, b // 2])
        middle[span, :] = mid
        inv = lax.rsqrt(mean_rows(mid * mid, width) + EPSILON)
        normed2[span, :] = (mid * inv * gains[1:2, :]).astype(BF16)
        return carry

    lax.fori_loop(0, tiles, project_out, 0)
    gate.arrived()
    up.arrived()
    down.stacked()
    for part in (plane, output, gate, up, down):
        part.finish()
    for made in kv_y + kv_cy + [kv_c]:
        made.wait_send()
    for made in saved:
        made.wait()


def front(
    attn_in_t, attn_out, gain_one, gain_two, w_gate, w_up, w_down_t, x_t, cosine_t, sine_t,
    segments, depth, rows,
):
    width, tokens = x_t.shape
    pad = DPAD // (2 * depth)
    in_cols, cols = attn_in_t.shape[0], w_gate.shape[1]
    a_rows = in_cols + GAIN_ROWS + attn_out.shape[0]
    query_cols, kv_cols = HEADS * HEAD_DIM, 2 * KV_HEADS * HEAD_DIM
    whole = 4 * tokens
    copies = 5 * (depth - 1) + 4 * 4 + 3 + 2 * KV_HEADS
    anywhere = pl.BlockSpec(memory_space=pl.ANY)
    kept = [
        (tokens, query_cols),
        (4, KV_HEADS, tokens, 2 * HEAD_DIM),
        (2, 2, query_cols // 4, DPAD),
        (2, 2, in_cols, DPAD),
    ]
    return pl.pallas_call(
        functools.partial(front_kernel, depth, rows, width, in_cols),
        out_shape=[
            jax.ShapeDtypeStruct((tokens, query_cols), BF16),
            jax.ShapeDtypeStruct((8, GROUP * tokens), F32),
            jax.ShapeDtypeStruct((tokens, DPAD), F32),
            jax.ShapeDtypeStruct((tokens, DPAD), BF16),
            jax.ShapeDtypeStruct((2, DPAD), F32),
            *[jax.ShapeDtypeStruct(shape, BF16) for shape in kept],
            jax.ShapeDtypeStruct((2, 2, 2, depth, pad, cols), BF16),
            jax.ShapeDtypeStruct((depth, pad, cols), BF16),
        ],
        in_specs=vmem_specs(4) + [anywhere] * 3 + vmem_specs(4),
        out_specs=vmem_specs(5) + [anywhere] * 6,
        scratch_shapes=[
            *[pltpu.VMEM(shape, BF16) for shape in kept],
            pltpu.VMEM((2, 2, 2, depth, a_rows, pad), BF16),
            pltpu.VMEM((tokens, DPAD), BF16),
            pltpu.VMEM((tokens, 128), F32),
            pltpu.VMEM((tokens, 128), F32),
            pltpu.VMEM((tokens, DPAD), BF16),
            pltpu.VMEM((tokens, query_cols + kv_cols), F32),
            pltpu.VMEM((KV_HEADS, AUGMENTED, GROUP * tokens), BF16),
            pltpu.VMEM((KV_HEADS, whole, AUGMENTED), BF16),
            pltpu.VMEM((KV_HEADS, AUGMENTED, whole), BF16),
            pltpu.VMEM((KV_HEADS, AUGMENTED, GROUP * tokens), F32),
            pltpu.VMEM((8, GROUP * tokens), F32),
            pltpu.VMEM((query_cols, tokens), F32),
            pltpu.VMEM((TILE, WIDE), F32),
            pltpu.SemaphoreType.DMA((copies,)),
            pltpu.SemaphoreType.DMA((copies,)),
            pltpu.SemaphoreType.DMA((7,)),
        ],
        compiler_params=pltpu.CompilerParams(
            vmem_limit_bytes=58 << 20, collective_id=0, has_side_effects=True
        ),
        cost_estimate=pl.CostEstimate(
            flops=20 << 30, bytes_accessed=40 << 20, transcendentals=8 << 20
        ),
        name="front",
    )(
        attn_in_t, attn_out, gain_one, gain_two, w_gate, w_up, w_down_t, x_t, cosine_t, sine_t,
        segments,
    )


class ZSum:
    def __init__(self, place, blocks, recv, part=lambda ref: ref):
        self.place, self.blocks, self.recv, self.part = place, blocks, recv, part
        self.sent = [
            place.copy(k, part(blocks.at[(place.z + k) % place.depth]), part(recv.at[k - 1]))
            for k in range(1, place.depth)
        ]

    def result(self):
        value = self.part(self.blocks.at[self.place.z])[...].astype(F32)
        for k, made in enumerate(self.sent):
            made.wait_recv()
            value += self.part(self.recv.at[k])[...].astype(F32)
        return value

    def finish(self):
        for made in self.sent:
            made.wait_send()


class PlaneScatter:
    def __init__(
        self, place, source, recv, split, part=lambda ref: ref, stage=None, local_sems=None
    ):
        self.place, self.source, self.recv, self.part = place, source, recv, part
        p, depth = place, place.depth
        self.split, self.rest = split, depth - split
        places = [(p.y, 1 - p.x, 0, split), (1 - p.y, p.x, split, self.rest), (p.y, p.x, 0, depth)]
        self.loads, self.kept, first = [], [], 0
        for n, (y, x, start, size) in enumerate(places):
            if not size:
                self.kept.append(None)
                continue
            view = source.at[y, pl.ds(x * depth + start, size)]
            if stage is not None:
                kept = stage.at[pl.ds(first, size)]
                self.loads.append(pltpu.make_async_copy(view, kept, local_sems.at[n]))
                view = kept
            first += size
            self.kept.append(view)
        self.total = self.kept[2]

    def copy(self, kind, source, first, size):
        slot = self.recv.at[pl.ds(first, size)]
        return self.place.copy(kind, self.part(source), self.part(slot))

    def start_far(self):
        p, split, rest, depth = self.place, self.split, self.rest, self.place.depth
        for load in self.loads:
            load.start()
        far, there = (1 - p.x) * depth, 1 - p.y
        self.far, self.near = [], []
        if split:
            view = self.source.at[there, pl.ds(far, split)]
            self.far.append(self.copy("y", view, 0, split))
        view = self.source.at[there, pl.ds(far + split, rest)]
        self.far.append(self.copy("x", view, split, rest))
        self.sent = list(self.far)

    def start_near(self):
        p, split, rest, depth = self.place, self.split, self.rest, self.place.depth
        far, here, there = (1 - p.x) * depth, p.x * depth, 1 - p.y
        made = []
        if split:
            view = self.source.at[there, pl.ds(here, split)]
            made.append(self.copy("y", view, depth, split))
        view = self.source.at[p.y, pl.ds(far + split, rest)]
        made.append(self.copy("x", view, depth + split, rest))
        self.near += made
        self.sent += made

    def start(self):
        self.start_far()
        self.start_near()

    def forward(self):
        split, rest, depth = self.split, self.rest, self.place.depth
        for load in self.loads:
            load.wait()
        jobs = [(self.kept[1], "y", split, rest)]
        if split:
            jobs.insert(0, (self.kept[0], "x", 0, split))
        for made, (view, kind, first, size) in zip(self.far, jobs):
            made.wait_recv()
            came = self.part(self.recv.at[pl.ds(first, size)])[...].astype(F32)
            kept = self.part(view)
            kept[...] = (kept[...].astype(F32) + came).astype(BF16)
            self.near.append(self.copy(kind, view, 2 * depth + first, size))
            self.sent.append(self.near[-1])

    def add(self):
        depth = self.place.depth
        for made in self.near:
            made.wait_recv()
        terms = [
            self.part(self.recv.at[pl.ds(n * depth, depth)])[...].astype(F32) for n in (1, 2)
        ]
        kept = self.part(self.total)
        kept[...] = (kept[...].astype(F32) + terms[0] + terms[1]).astype(BF16)

    def over_z(self):
        self.add()
        depth = self.place.depth
        slots = self.recv.at[pl.ds(3 * depth, depth - 1)]
        self.along_z = ZSum(self.place, self.total, slots, self.part)
        self.sent += self.along_z.sent

    def result(self):
        return self.along_z.result()

    def finish(self):
        for made in self.sent:
            made.wait_send()


def block_shape(size, pad):
    return (size, pad) if pad % 128 == 0 else (pad, size)


def spread_blocks(target, value, pad):
    if pad % 128 == 0:
        for n in range(DPAD // pad):
            target[n] = value[:, n * pad : (n + 1) * pad].astype(BF16)
    else:
        flipped = value.T.astype(BF16)
        for n in range(DPAD // pad):
            target[n] = flipped[n * pad : (n + 1) * pad]


def halves(count):
    middle = (count // 2 + 15) // 16 * 16
    return pl.ds(0, middle), pl.ds(middle, count - middle)


def one_block(value, rows, pad):
    return (value if pad % 128 == 0 else value.T)[:, :rows]


def scatter_slots(depth):
    return 3 * depth + depth - 1


def scatter_copies(depth):
    return 6 + depth - 1


def store_blocks(ref, start, value):
    pad = ref.shape[1]
    for k in range(TILE // pad):
        ref[start // pad + k] = value[k * pad : (k + 1) * pad]


def row_tiles(count, body):
    def step(r, carry):
        body(pl.multiple_of(r * TILE, TILE))
        return carry

    lax.fori_loop(0, count // TILE, step, 0)


def ffn_kernel(
    depth, rows, normed2, cot_t, middle, ffn_w, down_w, grads, down_sum, hidden_out, grad_n2, cot,
    wide_w, down_buf, down_g, down_r, n_other, c_other, hid, d_gate, d_up, n_t, c_t, ffn_own, parts,
    received, packed, send_sems, recv_sems, local_sems,
):
    tokens = normed2.shape[0]
    cols = ffn_w.shape[-1]
    p = Place(depth, send_sems, recv_sems)
    pad = DPAD // (2 * depth)
    count = trimmed(rows, pad)
    moved = pl.ds(0, count)
    trim = lambda ref: ref.at[..., moved, :]
    loads = [
        pltpu.make_async_copy(
            trim(ffn_w.at[w, y]),
            wide_w.at[w, :, :, moved, pl.ds(y * cols, cols)],
            local_sems.at[2 * w + y],
        )
        for w in range(2)
        for y in range(2)
    ]
    loads.append(
        pltpu.make_async_copy(trim(down_w), trim(down_buf.at[p.y, p.x]), local_sems.at[4])
    )
    for load in loads:
        load.start()
    if count < pad:
        wide_w[:, :, :, count:, :] = jnp.zeros((2, 2, depth, pad - count, 2 * cols), BF16)
        down_buf[:, :, :, count:, :] = jnp.zeros((2, 2, depth, pad - count, cols), BF16)
    p.barrier(["c", "x", "y"])
    n_copy = p.copy("c", normed2, n_other)
    down = PlaneGather(p, None, down_buf, depth // 2, trim)
    loads[4].wait()
    down.over_x()
    down.over_y()
    cot[...] = widen(cot_t, depth, rows, pad).astype(BF16)
    c_copy = p.copy("c", cot, c_other)
    for load in loads[:4]:
        load.wait()

    def sides(s):
        return (n_other, c_other) if s else (normed2, cot)

    for s in range(2):
        if s:
            n_copy.wait_recv()
            c_copy.wait_recv()
        n_from, c_from = sides(s)
        both = slice(s * tokens, (s + 1) * tokens)
        n_t[:, both] = transposed(n_from[...])
        c_t[:, both] = transposed(c_from[...])
        def tile(start):
            span = pl.ds(s * tokens + start, TILE)
            n_rows = n_from[pl.ds(start, TILE), :]
            gate = dot(n_rows, wide_w[0].reshape(DPAD, 2 * cols))
            upper = dot(n_rows, wide_w[1].reshape(DPAD, 2 * cols))
            sigma = jax.nn.sigmoid(gate)
            silu = gate * sigma
            hid[span, :] = (silu * upper).astype(BF16)
            d_gate[span, :] = (upper * sigma * (1.0 + gate * (1.0 - sigma))).astype(BF16)
            d_up[span, :] = silu.astype(BF16)

        row_tiles(tokens, tile)
    down.diagonal_y()
    down.diagonal_x()

    def weight_grad(left, right, target):
        def tile(start):
            side = dot(left[pl.ds(start, TILE), :], right[...]).astype(BF16)
            for y in range(2):
                store_blocks(target.at[y], start, side[:, y * cols : (y + 1) * cols])

        row_tiles(DPAD, tile)

    weight_grad(c_t, hid, down_g)
    total = PlaneScatter(p, down_g, down_r, depth // 2, trim)
    total.start()
    down.arrived()

    for s in (1, 0):
        n_from, c_from = sides(s)
        both = slice(s * tokens, (s + 1) * tokens)
        part = None
        for y in range(2):
            lanes = slice(y * cols, (y + 1) * cols)
            w_down = down_buf[y].reshape(DPAD, cols)
            grad_hid = dot(c_from[...], w_down)
            d_gate[both, lanes] = (grad_hid * d_gate[both, lanes].astype(F32)).astype(BF16)
            d_up[both, lanes] = (grad_hid * d_up[both, lanes].astype(F32)).astype(BF16)
            out = dot_nt(hid[both, lanes], w_down)
            part = out if part is None else part + out
        back = dot_nt(d_gate[both, :], wide_w[0].reshape(DPAD, 2 * cols))
        back += dot_nt(d_up[both, :], wide_w[1].reshape(DPAD, 2 * cols))
        if s:
            parts[0] = part.astype(BF16)
            parts[1] = back.astype(BF16)
            shared = [p.copy("c", parts.at[n], received.at[n]) for n in range(2)]
        else:
            ffn_own[...] = part + middle[...]
            grad_n2[...] = back
    total.forward()
    saved = []
    for w, right in ((0, d_gate), (1, d_up)):
        weight_grad(n_t, right, packed.at[w])
        made = pltpu.make_async_copy(packed.at[w], grads.at[w], local_sems.at[w])
        made.start()
        saved.append(made)
    for made in shared:
        made.wait_recv()

    narrow(hidden_out, ffn_own[...] + received[0].astype(F32), depth, rows, pad)
    grad_n2[...] += received[1].astype(F32)
    total.add()
    down_sum[...] = total.total[...]
    total.finish()
    down.finish()
    for made in shared + [n_copy, c_copy]:
        made.wait_send()
    for made in saved:
        made.wait()


def ffn(normed2, cot_t, middle, ffn_w, down_w, rows):
    width, tokens = cot_t.shape
    depth, pad, cols = down_w.shape
    token_rows = pltpu.VMEM((tokens, DPAD), BF16)
    wide = pltpu.VMEM((2 * tokens, 2 * cols), BF16)
    flipped = pltpu.VMEM((DPAD, 2 * tokens), BF16)
    pair = pltpu.VMEM((2, tokens, DPAD), BF16)
    copies = 4 + 4 + 6
    return pl.pallas_call(
        functools.partial(ffn_kernel, depth, rows),
        out_shape=[
            jax.ShapeDtypeStruct((2, 2, 2 * depth, pad, cols), BF16),
            jax.ShapeDtypeStruct((depth, pad, cols), BF16),
            jax.ShapeDtypeStruct((width, tokens), BF16),
            jax.ShapeDtypeStruct((tokens, DPAD), F32),
            jax.ShapeDtypeStruct((tokens, DPAD), BF16),
        ],
        in_specs=vmem_specs(3) + [pl.BlockSpec(memory_space=pl.ANY)] * 2,
        out_specs=[pl.BlockSpec(memory_space=pl.ANY)] + vmem_specs(4),
        scratch_shapes=[
            pltpu.VMEM((2, 2, depth, pad, 2 * cols), BF16),
            pltpu.VMEM((2, 2, depth, pad, cols), BF16),
            pltpu.VMEM((2, 2 * depth, pad, cols), BF16),
            pltpu.VMEM((3 * depth, pad, cols), BF16),
            token_rows, token_rows, wide, wide, wide, flipped, flipped,
            pltpu.VMEM((tokens, DPAD), F32), pair, pair,
            pltpu.VMEM((2, 2, 2 * depth, pad, cols), BF16),
            pltpu.SemaphoreType.DMA((copies,)),
            pltpu.SemaphoreType.DMA((copies,)),
            pltpu.SemaphoreType.DMA((5,)),
        ],
        compiler_params=pltpu.CompilerParams(
            vmem_limit_bytes=61 << 20, collective_id=1, has_side_effects=True
        ),
        cost_estimate=pl.CostEstimate(
            flops=24 << 30, bytes_accessed=30 << 20, transcendentals=2 << 20
        ),
        name="ffn",
    )(normed2, cot_t, middle, ffn_w, down_w)


def mid_kernel(
    depth, width,
    ffn_g, down_sum, grad_n2, middle, cot, gains, out_w, q, kv, attn, lse, segments,
    dq_t, dkv_sum, grad_middle, gain_grad, out_grad, down_grad, gate_grad, up_sum,
    mid_b, out_g, out_c, out_r, ffn_r, down_r, stage, grad_attn, q_aug, g_aug, q3, g3, k3, v3, k_t,
    dkv, acc_kv, diagonal, kv_c, kv_y, send_sems, recv_sems, local_sems,
):
    tokens = q.shape[0]
    tiles = tokens // TILE
    back = 1024 // TILE
    rows = down_grad.shape[0]
    pad = DPAD // (2 * depth)
    out_cols = HEADS * HEAD_DIM // 4
    p = Place(depth, send_sems, recv_sems)
    trim = lambda ref: ref.at[..., pl.ds(0, trimmed(rows, pad)), :]
    p.barrier()
    ffn_sums = [
        PlaneScatter(
            p, ffn_g.at[w], ffn_r.at[w], (0, depth // 2)[w], trim, stage.at[w],
            local_sems.at[pl.ds(3 * w, 3)],
        )
        for w in range(2)
    ]
    ffn_sums[0].start_far()
    ffn_sums[1].start_far()
    ffn_sums[0].start_near()
    down_total = ZSum(p, down_sum, down_r, trim)

    gain = gains[1:2, :]
    gain_grad[...] = jnp.zeros_like(gain_grad)

    def norm_tile(start):
        span = pl.ds(start, TILE)
        mid, up = middle[span, :], grad_n2[span, :]
        inv = lax.rsqrt(mean_rows(mid * mid, width) + EPSILON)
        scaled = up * gain
        mean = mean_rows(scaled * mid, width)
        grad = cot[span, :].astype(F32) + inv * (scaled - mid * (inv * inv * mean))
        grad_middle[span, :] = grad
        gain_grad[...] += jnp.sum(up * mid * inv, axis=0, keepdims=True)
        mid_b[span, :] = grad.astype(BF16)
        for b in range(4):
            side = dot_nt(mid_b[span, :], out_w[b % 2, b // 2])
            grad_attn[span, b * out_cols : (b + 1) * out_cols] = side.astype(BF16)

    row_tiles(tokens, norm_tile)
    attn_t = attn[...].astype(F32).T
    for b in range(4):
        left = attn_t[b * out_cols : (b + 1) * out_cols, :].astype(BF16)
        spread_blocks(out_g.at[b % 2, b // 2], dot(left, mid_b[...]), pad)
    out_cross = p.copy("c", out_g.at[1 - p.c], out_c)

    def block_span(block):
        return pl.ds(pl.multiple_of(block * tokens, tokens), tokens)

    own_seg = segments[:, block_span(p.m)]
    nothing = jnp.zeros((1, TILE), F32)
    q_flat = (q[...].astype(F32) * SCORE_SCALE).T.astype(BF16)
    g_flat = grad_attn[...].astype(F32).T
    for h in range(HEADS):
        g, j = h // GROUP, h % GROUP
        span = slice(h * HEAD_DIM, (h + 1) * HEAD_DIM)
        for i in range(tiles):
            cols, lanes = slice(i * TILE, (i + 1) * TILE), head_lanes(i, j)
            sides = g_flat[span, cols]
            delta = jnp.sum(sides * attn_t[span, cols], axis=0, keepdims=True)
            q_aug[g, :HEAD_DIM, lanes] = q_flat[span, cols]
            q_aug[g, HEAD_DIM:, lanes] = query_features(
                own_seg[:, cols], three_parts(-lse[g : g + 1, lanes])
            )
            g_aug[g, :HEAD_DIM, lanes] = sides.astype(BF16)
            g_aug[g, HEAD_DIM:, lanes] = features(
                three_parts(-delta), [nothing] * SEGMENTS
            ).astype(BF16)
            q3[g, lanes, :] = q[cols, span]
            g3[g, lanes, :] = grad_attn[cols, span]
    for n in range(3):
        block = jnp.maximum(p.m - n, 0)
        span = block_span(block)
        added = key_features(segments[:, span])
        for g in range(KV_HEADS):
            part = kv[block, g]
            k_t[g * HEAD_DIM : (g + 1) * HEAD_DIM, span] = transposed(part)[:HEAD_DIM]
            k3[g, span, :HEAD_DIM] = part[:, :HEAD_DIM]
            v3[g, span, :HEAD_DIM] = part[:, HEAD_DIM:]
            k3[g, span, HEAD_DIM:] = added
            v3[g, span, HEAD_DIM:] = added
    diagonal[...] = diagonal_bias()
    dq_t[...] = jnp.zeros_like(dq_t)
    dkv[...] = jnp.zeros_like(dkv)
    out_cross.wait_recv()
    own = out_g.at[p.c]
    own[...] = (own[...].astype(F32) + out_c[...].astype(F32)).astype(BF16)
    out_sum = PlaneScatter(p, own, out_r, depth // 2)
    out_sum.start()
    ffn_sums[0].forward()
    ffn_sums[1].start_near()

    def key_tile(t, queries, on_diagonal=()):
        keys = pl.ds(pl.multiple_of(t * TILE, TILE), TILE)

        def group(g, carry):
            k_g, v_g = k3[g, keys, :], v3[g, keys, :]
            kt_g = k_t[pl.ds(pl.multiple_of(g * HEAD_DIM, HEAD_DIM), HEAD_DIM), keys]
            dk, dv = None, None
            for i in queries:
                lanes = pl.ds(i * WIDE, WIDE)
                scores = dot(k_g, q_aug[g, :, lanes])
                if i in on_diagonal:
                    scores += diagonal[...]
                probs = jnp.exp2(scores * LOG2E)
                dscores = (probs * dot(v_g, g_aug[g, :, lanes])).astype(BF16)
                add_v = dot(probs.astype(BF16), g3[g, lanes, :])
                add_k = dot(dscores, q3[g, lanes, :])
                dq_t[g, :, lanes] += dot(kt_g, dscores)
                dk = add_k if dk is None else dk + add_k
                dv = add_v if dv is None else dv + add_v
            acc_kv[g] = dk * SCORE_SCALE
            acc_kv[KV_HEADS + g] = dv
            return carry

        lax.fori_loop(0, KV_HEADS, group, 0)
        for n in range(2 * KV_HEADS):
            dkv[keys, n * HEAD_DIM : (n + 1) * HEAD_DIM] = acc_kv[n].astype(BF16)

    def key_span(low, high, queries):
        def step(t, carry):
            key_tile(t, queries)
            return carry

        lax.fori_loop(low, high, step, 0)

    def part_of(index):
        return dkv.at[pl.ds(pl.multiple_of(index * tokens, tokens), tokens)]

    first = p.m * tiles
    key_span(jnp.maximum(first - back, 0), jnp.maximum(first + 1 - back, 0), (0,))
    key_span(jnp.maximum(first + 1 - back, 0), jnp.maximum(first - 2, 0), (0, 1))
    ffn_sums[1].forward()
    key_span(jnp.maximum(first - 2, 0), jnp.maximum(first - 1, 0), (0, 1))
    key_span(jnp.maximum(first - 1, 0), first, (0, 1))
    beside = p.m + 1 - 2 * p.c
    cross = [
        p.copy("c", part_of(index), kv_c.at[n])
        for n, index in enumerate((beside, (beside + 2) % 4))
    ]
    out_sum.forward()
    cross[1].wait_recv()
    away = part_of((p.m + 2) % 4)
    away[...] = (away[...].astype(F32) + kv_c[1].astype(F32)).astype(BF16)
    across = p.copy("y", away, kv_y)
    ffn_sums[0].over_z()
    key_tile(first + 1, (1,), (1,))
    key_tile(first, (0, 1), (0,))
    out_sum.over_z()
    down_grad[...] = down_total.result()[:rows]
    gate_grad[...] = ffn_sums[0].result()[:rows]
    ffn_sums[1].add()
    up_sum[...] = ffn_sums[1].total[...]
    cross[0].wait_recv()
    across.wait_recv()
    dkv_sum[...] = part_of(p.m)[...].astype(F32) + kv_c[0].astype(F32) + kv_y[...].astype(F32)
    out_grad[...] = one_block(out_sum.result(), rows, pad)
    for part in ffn_sums + [out_sum, down_total]:
        part.finish()
    for made in cross + [across, out_cross]:
        made.wait_send()


def middle_back(ffn_g, down_sum, grad_n2, middle, cot, gains, out_w, q, kv, attn, lse, segments,
                depth, rows, width):
    tokens, query_cols = q.shape
    pad = DPAD // (2 * depth)
    cols = ffn_g.shape[-1]
    kv_cols = KV_HEADS * kv.shape[-1]
    out_cols = query_cols // 4
    whole = 4 * tokens
    slots = scatter_slots(depth)
    copies = 3 * scatter_copies(depth) + 4 + depth - 1
    heads_q = pltpu.VMEM((KV_HEADS, GROUP * tokens, HEAD_DIM), BF16)
    heads_kv = pltpu.VMEM((KV_HEADS, whole, AUGMENTED), BF16)
    flipped = pltpu.VMEM((KV_HEADS, AUGMENTED, GROUP * tokens), BF16)
    return pl.pallas_call(
        functools.partial(mid_kernel, depth, width),
        out_shape=[
            jax.ShapeDtypeStruct((KV_HEADS, HEAD_DIM, GROUP * tokens), F32),
            jax.ShapeDtypeStruct((tokens, kv_cols), F32),
            jax.ShapeDtypeStruct((tokens, DPAD), F32),
            jax.ShapeDtypeStruct((1, DPAD), F32),
            jax.ShapeDtypeStruct((out_cols, rows), F32),
            *[jax.ShapeDtypeStruct((rows, cols), F32)] * 2,
            jax.ShapeDtypeStruct((depth, pad, cols), BF16),
        ],
        in_specs=[pl.BlockSpec(memory_space=pl.ANY)] + vmem_specs(11),
        out_specs=vmem_specs(8),
        scratch_shapes=[
            pltpu.VMEM((tokens, DPAD), BF16),
            pltpu.VMEM((2, 2, 2 * depth, *block_shape(out_cols, pad)), BF16),
            pltpu.VMEM((2, 2 * depth, *block_shape(out_cols, pad)), BF16),
            pltpu.VMEM((slots, *block_shape(out_cols, pad)), BF16),
            pltpu.VMEM((2, slots, pad, cols), BF16),
            pltpu.VMEM((depth - 1, pad, cols), BF16),
            pltpu.VMEM((2, 2 * depth, pad, cols), BF16),
            pltpu.VMEM((tokens, query_cols), BF16),
            flipped, flipped, heads_q, heads_q, heads_kv, heads_kv,
            pltpu.VMEM((KV_HEADS * HEAD_DIM, whole), BF16),
            pltpu.VMEM((whole, kv_cols), BF16),
            pltpu.VMEM((2 * KV_HEADS, TILE, HEAD_DIM), F32),
            pltpu.VMEM((TILE, WIDE), F32),
            pltpu.VMEM((2, tokens, kv_cols), BF16),
            pltpu.VMEM((tokens, kv_cols), BF16),
            pltpu.SemaphoreType.DMA((copies,)),
            pltpu.SemaphoreType.DMA((copies,)),
            pltpu.SemaphoreType.DMA((6,)),
        ],
        compiler_params=pltpu.CompilerParams(
            vmem_limit_bytes=61 << 20, collective_id=2, has_side_effects=True
        ),
        cost_estimate=pl.CostEstimate(
            flops=40 << 30, bytes_accessed=50 << 20, transcendentals=8 << 20
        ),
        name="middle_back",
    )(ffn_g, down_sum, grad_n2, middle, cot, gains, out_w, q, kv, attn, lse, segments)


def tail_kernel(
    depth, rows, width,
    dq_t, dkv, cosine_t, sine_t, x_t, grad_middle, gains, in_w, gain2, up_sum,
    grad_hidden, in_grad, gain1_sum, gain2_sum, up_grad,
    ffn_r, proj, proj_b, in_g, in_c, in_r, grad_x, gain_own, gain_r, send_sems, recv_sems,
):
    tokens = x_t.shape[1]
    query_cols = HEADS * HEAD_DIM
    in_cols = in_w.shape[2]
    pad = DPAD // (2 * depth)
    turned = (HEADS + KV_HEADS) * HEAD_DIM
    p = Place(depth, send_sems, recv_sems)
    p.barrier()
    trim = lambda ref: ref.at[..., pl.ds(0, trimmed(rows, pad)), :]
    up_total = ZSum(p, up_sum, ffn_r, trim)
    x_f = widen(x_t, depth, rows, pad)
    gain = gains[0:1, :]
    inv = lax.rsqrt(mean_rows(x_f * x_f, width) + EPSILON)
    normed1 = (x_f * inv * gain).astype(BF16)
    cosine = lane_tables(cosine_t[...])
    sine = signed(lane_tables(sine_t[...]), True)
    turned_parts = [
        jnp.concatenate(
            [dq_t[h // GROUP, :, head_lanes(i, h % GROUP)] for i in range(tokens // TILE)], axis=1
        )
        for h in range(HEADS)
    ]
    proj[:, :query_cols] = jnp.concatenate(turned_parts, axis=0).T * SCORE_SCALE
    proj[:, query_cols:] = dkv[...]
    for j in range(turned // 128):
        lanes = slice(128 * j, 128 * (j + 1))
        proj[:, lanes] = rope(proj[:, lanes], cosine, sine)
    for b in range(4):
        proj_b[b] = proj[:, b * in_cols : (b + 1) * in_cols].astype(BF16)
    cuts = halves(in_g.shape[-2])
    parts = [lambda ref, cut=cut: ref.at[..., cut, :] for cut in cuts]
    for other in (1, 0):
        c = (1 - p.c) if other else p.c
        for y in range(2):
            left = transposed(proj_b[2 * y + c])
            spread_blocks(in_g.at[c, y], dot(left, normed1), pad)
        if other:
            crosses = [p.copy("c", part(in_g.at[c]), part(in_c)) for part in parts]
    own = in_g.at[p.c]
    in_sums = []
    for part, cross in zip(parts, crosses):
        cross.wait_recv()
        kept = part(own)
        kept[...] = (kept[...].astype(F32) + part(in_c)[...].astype(F32)).astype(BF16)
        in_sums.append(PlaneScatter(p, own, in_r, depth // 2, part))
        in_sums[-1].start_far()
    in_sums[0].forward()
    in_sums[0].start_near()
    up = None
    for b in range(4):
        term = dot(proj_b[b], in_w[b % 2, b // 2])
        up = term if up is None else up + term
    scaled = up * gain
    mean = mean_rows(scaled * x_f, width)
    grad_x[...] = grad_middle[...] + inv * (scaled - x_f * (inv * inv * mean))
    gain_own[...] = jnp.zeros_like(gain_own)
    gain_own[0:1, :] = jnp.sum(up * x_f * inv, axis=0, keepdims=True)
    gain_own[1:2, :] = gain2[...]
    in_sums[1].forward()
    in_sums[1].start_near()
    sent = []
    for n, kind in enumerate(("c", "y", "x")):
        made = p.copy(kind, gain_own.at[pl.ds(8 * n, 8)], gain_r.at[pl.ds(8 * n, 8)])
        sent.append(made)
        if n == 0:
            narrow(grad_hidden, grad_x[...], depth, rows, pad)
        made.wait_recv()
        if n == 0:
            in_sums[0].over_z()
        gain_own[8 * (n + 1) : 8 * (n + 2), :] = (
            gain_own[8 * n : 8 * (n + 1), :] + gain_r[8 * n : 8 * (n + 1), :]
        )
    in_sums[1].over_z()
    last = gain_own.at[pl.ds(24, 8)]
    arriving = [p.copy(k, last, gain_r.at[pl.ds(24 + 8 * k, 8)]) for k in range(1, depth)]
    total = last[...]
    for k, made in enumerate(arriving):
        made.wait_recv()
        total += gain_r[32 + 8 * k : 40 + 8 * k, :]
    mine = jnp.zeros((8, pad), F32)
    for n in range(2 * depth):
        mine = jnp.where(n == p.x * depth + p.z, total[:, n * pad : (n + 1) * pad], mine)
    gain1_sum[...] = mine[0:1, :rows]
    gain2_sum[...] = mine[1:2, :rows]
    up_grad[...] = up_total.result()[:rows]
    up_total.finish()
    value = jnp.concatenate([in_sum.result() for in_sum in in_sums], axis=0)
    in_grad[...] = one_block(value, rows, pad)
    for in_sum in in_sums:
        in_sum.finish()
    for made in sent + arriving + crosses:
        made.wait_send()


def tail(
    dq_t, dkv, cosine_t, sine_t, x_t, grad_middle, gains, in_w, gain2, up_sum,
    depth, rows, width,
):
    tokens = x_t.shape[1]
    pad = DPAD // (2 * depth)
    in_cols = in_w.shape[2]
    total = HEADS * HEAD_DIM + dkv.shape[1]
    slots = scatter_slots(depth)
    copies = 2 * scatter_copies(depth) + 2 + 3 + 2 * (depth - 1)
    cols = up_sum.shape[2]
    return pl.pallas_call(
        functools.partial(tail_kernel, depth, rows, width),
        out_shape=[
            jax.ShapeDtypeStruct((width, tokens), F32),
            jax.ShapeDtypeStruct((in_cols, rows), F32),
            *[jax.ShapeDtypeStruct((1, rows), F32)] * 2,
            jax.ShapeDtypeStruct((rows, cols), F32),
        ],
        in_specs=vmem_specs(10),
        out_specs=vmem_specs(5),
        scratch_shapes=[
            pltpu.VMEM((depth - 1, pad, cols), BF16),
            pltpu.VMEM((tokens, total), F32),
            pltpu.VMEM((4, tokens, in_cols), BF16),
            pltpu.VMEM((2, 2, 2 * depth, *block_shape(in_cols, pad)), BF16),
            pltpu.VMEM((2, 2 * depth, *block_shape(in_cols, pad)), BF16),
            pltpu.VMEM((slots, *block_shape(in_cols, pad)), BF16),
            pltpu.VMEM((tokens, DPAD), F32),
            pltpu.VMEM((32, DPAD), F32),
            pltpu.VMEM((24 + 8 * depth, DPAD), F32),
            pltpu.SemaphoreType.DMA((copies,)),
            pltpu.SemaphoreType.DMA((copies,)),
        ],
        compiler_params=pltpu.CompilerParams(
            vmem_limit_bytes=61 << 20, collective_id=3, has_side_effects=True
        ),
        cost_estimate=pl.CostEstimate(
            flops=8 << 30, bytes_accessed=30 << 20, transcendentals=0
        ),
        name="tail",
    )(dq_t, dkv, cosine_t, sine_t, x_t, grad_middle, gains, in_w, gain2, up_sum)


def rotary_tables(position_ids):
    half_dim = HEAD_DIM // 2
    frequency = jnp.exp(
        jnp.arange(half_dim, dtype=F32) * (-2.0 * math.log(10000.0) / HEAD_DIM)
    )
    angles = frequency[:, None] * position_ids.astype(F32)[None, :]
    return jnp.cos(angles), jnp.sin(angles)


def per_device(
    hidden_in, cotangent, segments, positions, attn_in, attn_out, w_gate, w_up, w_down,
    norm1_gain, norm2_gain,
):
    tokens, width = hidden_in.shape[1:]
    dp_size = lax.axis_size("dp")
    depth = dp_size // 2
    rows = width // dp_size
    pad = DPAD // dp_size

    ffn_blocks = [w_gate, w_up, w_down.T]
    if trimmed(rows, pad) == pad:
        ffn_blocks = [jnp.pad(w, ((0, pad - rows), (0, 0))) for w in ffn_blocks]
    x_t, cot_t = hidden_in[0].T, cotangent[0].T
    cosine_t, sine_t = rotary_tables(positions[0])
    attn, lse, middle, normed2, gains, q, kv, out_w, in_w, ffn_w, down_w = front(
        attn_in.T, attn_out, norm1_gain[None], norm2_gain[None], *ffn_blocks,
        x_t, cosine_t, sine_t, segments, depth, rows,
    )
    ffn_g, down_sum, hidden_out, grad_n2, cot = ffn(normed2, cot_t, middle, ffn_w, down_w, rows)
    dq_t, dkv, grad_middle, gain2, g_out, g_down, g_gate, up_sum = middle_back(
        ffn_g, down_sum, grad_n2, middle, cot, gains, out_w, q, kv, attn, lse, segments,
        depth, rows, width,
    )
    grad_hidden, g_in, g_gain1, g_gain2, g_up = tail(
        dq_t, dkv, cosine_t, sine_t, x_t, grad_middle, gains, in_w, gain2, up_sum,
        depth, rows, width,
    )
    return (
        hidden_out.T[None],
        grad_hidden.T[None],
        g_in.T,
        g_out,
        g_gate,
        g_up,
        g_down.T,
        g_gain1[0],
        g_gain2[0],
    )


def solution(mesh):
    return jax.shard_map(
        per_device,
        mesh=mesh,
        in_specs=(
            P("dp", "mp", None),
            P("dp", "mp", None),
            P("dp", None),
            P("dp", "mp"),
            P("dp", "mp"),
            P("mp", "dp"),
            P("dp", "mp"),
            P("dp", "mp"),
            P("mp", "dp"),
            P("dp"),
            P("dp"),
        ),
        out_specs=(
            P("dp", "mp", None),
            P("dp", "mp", None),
            P("dp", "mp"),
            P("mp", "dp"),
            P("dp", "mp"),
            P("dp", "mp"),
            P("mp", "dp"),
            P("dp"),
            P("dp"),
        ),
        check_vma=False,
    )
```

```python
import functools
import math

import jax
import jax.numpy as jnp
from jax import lax
from jax.experimental import pallas as pl
from jax.experimental.pallas import tpu as pltpu
from jax.sharding import PartitionSpec as P

HEADS = 15
KV_HEADS = 5
GROUP = HEADS // KV_HEADS
HEAD_DIM = 64
DPAD = 1024
TILE = 256
EPSILON = 1e-05
SCORE_SCALE = 0.125
MASK_FILL = -1e30
LOG2E = 1.4426950408889634
EXP_SCALE = SCORE_SCALE * LOG2E
GAIN_ROWS = 16
EARLY = 256
SEGMENTS = 4
AUGMENTED = HEAD_DIM + 16
WIDE = GROUP * TILE
BF16 = jnp.bfloat16
F32 = jnp.float32


def dot(a, b):
    return jnp.dot(a, b, preferred_element_type=F32)


def dot_nt(a, b):
    return lax.dot_general(a, b, (((1,), (1,)), ((), ())), preferred_element_type=F32)


def vmem_specs(count):
    return [pl.BlockSpec(memory_space=pltpu.VMEM)] * count


def transposed(value):
    return value.astype(F32).T.astype(BF16)


class Place:
    def __init__(self, depth, send_sems, recv_sems):
        dp_index, m = lax.axis_index("dp"), lax.axis_index("mp")
        self.depth = depth
        self.z, self.x = dp_index // 2, dp_index % 2
        self.m, self.y, self.c = m, m // 2, m % 2
        self.send_sems, self.recv_sems = send_sems, recv_sems
        self.count = 0

    def peer(self, kind):
        z, x, y, c = self.z, self.x, self.y, self.c
        if kind == "x":
            x = 1 - x
        elif kind == "y":
            y = 1 - y
        elif kind == "c":
            c = 1 - c
        else:
            z = (z + kind) % self.depth
        return 2 * z + x, 2 * y + c

    def kinds(self):
        return ["x", "y", "c"] + list(range(1, self.depth))

    def barrier(self, kinds=None):
        semaphore = pltpu.get_barrier_semaphore()
        kinds = kinds or self.kinds()
        for kind in kinds:
            pl.semaphore_signal(
                semaphore, inc=1, device_id=self.peer(kind), device_id_type=pl.DeviceIdType.MESH
            )
        pl.semaphore_wait(semaphore, len(kinds))

    def copy(self, kind, source, target=None):
        index = self.count
        self.count += 1
        made = pltpu.make_async_remote_copy(
            src_ref=source,
            dst_ref=source if target is None else target,
            send_sem=self.send_sems.at[index],
            recv_sem=self.recv_sems.at[index],
            device_id=self.peer(kind),
            device_id_type=pl.DeviceIdType.MESH,
        )
        made.start()
        return made


class PlaneGather:
    def __init__(self, place, source, buffer, by_x, part=lambda ref: ref):
        self.place, self.source, self.buffer, self.part = place, source, buffer, part
        self.split = place.depth - by_x
        self.sent, self.last = [], []

    def over_z(self, slot=None):
        p = self.place
        slot = self.part(self.buffer.at[p.y, p.x, p.z]) if slot is None else slot
        self.arriving = [p.copy(k, self.source, slot) for k in range(1, p.depth)]
        self.sent += self.arriving

    def stacked(self):
        for made in self.arriving:
            made.wait_recv()

    def over_x(self):
        p = self.place
        self.by_x = p.copy("x", self.part(self.buffer.at[p.y, p.x]))
        self.sent.append(self.by_x)

    def over_y(self):
        p = self.place
        self.by_y = p.copy("y", self.part(self.buffer.at[p.y, p.x]))
        self.sent.append(self.by_y)

    def diagonal_x(self):
        p = self.place
        self.by_y.wait_recv()
        span = pl.ds(self.split, p.depth - self.split)
        self.last.append(p.copy("x", self.part(self.buffer.at[1 - p.y, p.x, span])))

    def diagonal_y(self):
        p = self.place
        self.by_x.wait_recv()
        if self.split:
            span = pl.ds(0, self.split)
            self.last.append(p.copy("y", self.part(self.buffer.at[p.y, 1 - p.x, span])))

    def arrived(self):
        for made in self.last:
            made.wait_recv()

    def finish(self):
        for made in self.sent + self.last:
            made.wait_send()


def rope(value, cosine, sine):
    lane = lax.broadcasted_iota(jnp.int32, value.shape, 1)
    half = HEAD_DIM // 2
    partner = jnp.where(
        lane % HEAD_DIM < half, pltpu.roll(value, 128 - half, 1), pltpu.roll(value, half, 1)
    )
    return value * cosine + partner * sine


def trimmed(rows, pad):
    return rows if rows % 8 == 0 else pad


def natural(block, depth):
    return 2 * (block % depth) + block // depth


def widen(source, depth, rows, pad):
    filler = jnp.zeros((pad - rows, source.shape[1]), F32)
    parts = []
    for b in range(2 * depth):
        first = natural(b, depth) * rows
        parts += [source[first : first + rows, :].astype(F32), filler]
    return jnp.concatenate(parts, axis=0).T


def narrow(target, value, depth, rows, pad):
    flipped = value.T
    for b in range(2 * depth):
        first = natural(b, depth) * rows
        target[first : first + rows, :] = flipped[b * pad : b * pad + rows, :].astype(target.dtype)


def side_by_side(ref, first, size):
    _, depth, _, pad = ref.shape
    span = pl.ds(first, size)
    return jnp.concatenate(
        [ref[b // depth, b % depth, span, :] for b in range(2 * depth)], axis=1
    )


def lane_tables(table):
    return jnp.concatenate([table] * (256 // HEAD_DIM), axis=0).T


def signed(table, back):
    lane = lax.broadcasted_iota(jnp.int32, table.shape, 1) % HEAD_DIM
    first = lane < HEAD_DIM // 2
    return jnp.where(first, table, -table) if back else jnp.where(first, -table, table)


def mean_rows(value, width):
    return jnp.sum(value, axis=-1, keepdims=True) * (1.0 / width)


def diagonal_bias():
    key = lax.broadcasted_iota(jnp.int32, (TILE, WIDE), 0)
    query = lax.broadcasted_iota(jnp.int32, (TILE, WIDE), 1) % TILE
    return jnp.where(key <= query, 0.0, MASK_FILL)


def features(first, segment_rows):
    spare = 16 - len(first) - SEGMENTS
    zeros = jnp.zeros((spare, first[0].shape[1]), F32)
    return jnp.concatenate(list(first) + segment_rows + [zeros], axis=0)


def key_features(segment):
    other = [jnp.where(segment != n, MASK_FILL, 0.0) for n in range(SEGMENTS)]
    return features([jnp.ones(segment.shape, F32)] * 3, other).T.astype(BF16)


def query_features(segment, first):
    same = [jnp.where(segment == n, 1.0, 0.0) for n in range(SEGMENTS)]
    return features(first, same).astype(BF16)


def three_parts(value):
    parts = []
    for _ in range(3):
        parts.append(value.astype(BF16).astype(F32))
        value = value - parts[-1]
    return parts


def head_lanes(i, j):
    return slice(i * WIDE + j * TILE, i * WIDE + (j + 1) * TILE)


def front_kernel(
    depth, rows, width, in_cols,
    attn_in_t, attn_out, gain_one, gain_two, w_gate, w_up, w_down_t, x_t, cosine_t, sine_t, segments,
    attn, lse, middle, normed2, gains, q_out, kv_out, out_w_out, in_w_out, ffn_w, down_w,
    q, kv, out_w, in_w, a_buf, x_in, cosine, sine, normed1, proj, q_aug, k3, v_t, acc, peak, flat,
    diagonal, send_sems, recv_sems, local_sems,
):
    tokens = x_in.shape[0]
    tiles = tokens // TILE
    back = 1024 // TILE
    pad = DPAD // (2 * depth)
    lead = in_cols + GAIN_ROWS
    query_cols = HEADS * HEAD_DIM
    out_cols = query_cols // 4
    p = Place(depth, send_sems, recv_sems)
    block = a_buf.at[p.c, p.y, p.x, p.z]
    block[...] = jnp.zeros_like(block)
    block[0:in_cols, 0:rows] = attn_in_t[...]
    block[in_cols : in_cols + 1, 0:rows] = gain_one[...]
    block[in_cols + 1 : in_cols + 2, 0:rows] = gain_two[...]
    block[lead : lead + out_cols, 0:rows] = attn_out[...]
    moved = pl.ds(0, trimmed(rows, pad))
    trim = lambda ref: ref.at[..., moved, :]
    own = [
        pltpu.make_async_copy(
            source, trim(ffn_w.at[w, p.y, p.x, p.z] if w < 2 else down_w.at[p.z]), local_sems.at[w]
        )
        for w, source in enumerate((w_gate, w_up, w_down_t))
    ]
    for made in own:
        made.start()
    p.barrier()
    first_part = lambda ref: ref.at[..., pl.ds(0, lead), :]
    last_part = lambda ref: ref.at[..., pl.ds(lead, out_cols), :]
    buffer = a_buf.at[p.c]
    plane = PlaneGather(p, first_part(block), buffer, depth // 2, first_part)
    output = PlaneGather(p, last_part(block), buffer, depth // 2, last_part)
    gate = PlaneGather(p, w_gate, ffn_w.at[0], depth, trim)
    early = lambda ref: ref.at[..., moved, pl.ds(0, EARLY)]
    rest = pl.ds(EARLY, w_up.shape[1] - EARLY)
    late = lambda ref: ref.at[..., moved, rest]
    up = PlaneGather(p, w_up.at[:, rest], ffn_w.at[1], depth // 2, late)
    down = PlaneGather(p, w_down_t, None, 0)
    plane.over_z()
    early_own = early(ffn_w.at[1, p.y, p.x, p.z])
    early_xy = [p.copy(kind, w_up.at[:, pl.ds(0, EARLY)], early_own) for kind in ("x", "y")]
    x_f = widen(x_t, depth, rows, pad)
    x_in[...] = x_f.astype(BF16)
    cosine[...] = lane_tables(cosine_t[...])
    sine[...] = signed(lane_tables(sine_t[...]), False)
    inv_one = lax.rsqrt(mean_rows(x_f * x_f, width) + EPSILON)
    def block_span(block):
        return pl.ds(pl.multiple_of(block * tokens, tokens), tokens)

    early_xy[1].wait_recv()
    early_far = p.copy("x", early(ffn_w.at[1, 1 - p.y, p.x, p.z]))
    plane.stacked()
    plane.over_x()
    plane.over_y()
    output.over_z()
    gate.over_z()
    own_seg = segments[:, block_span(p.m)]
    nothing = jnp.zeros(own_seg.shape, F32)
    own_features = query_features(own_seg, [nothing] * 3)
    for g in range(KV_HEADS):
        for i in range(tiles):
            for j in range(GROUP):
                q_aug[g, HEAD_DIM:, head_lanes(i, j)] = own_features[:, i * TILE : (i + 1) * TILE]
    ones = lax.broadcasted_iota(jnp.int32, (16, 4 * tokens), 0) == 0
    for g in range(KV_HEADS):
        v_t[g, HEAD_DIM:, :] = jnp.where(ones, 1.0, 0.0).astype(BF16)
    diagonal[...] = diagonal_bias()
    acc[...] = jnp.zeros_like(acc)
    peak[...] = jnp.full_like(peak, MASK_FILL)
    plane.diagonal_y()
    plane.diagonal_x()
    for made in own:
        made.wait()
    up.over_z()
    early_xy[0].wait_recv()
    early_far.wait_recv()
    column = early(ffn_w.at[1, :, :, p.z])
    early_z = [p.copy(k, column) for k in range(1, depth)]
    plane.arrived()
    cross = p.copy("c", first_part(a_buf.at[p.c]))
    output.stacked()
    output.over_x()
    output.over_y()
    for n in range(3):
        span = block_span(jnp.maximum(p.m - n, 0))
        added = key_features(segments[:, span])
        for g in range(KV_HEADS):
            k3[g, span, HEAD_DIM:] = added
    gate.stacked()
    gate.over_x()
    gate.over_y()
    cross.wait()
    for b in range(2 * depth):
        gains[:, b * pad : (b + 1) * pad] = a_buf[
            0, 0, b // depth, b % depth, pl.ds(in_cols, 2), :
        ].astype(F32)
    normed1[...] = (x_f * inv_one * gains[0:1, :]).astype(BF16)
    for b in range(4):
        in_w[b % 2, b // 2] = side_by_side(a_buf.at[b % 2, b // 2], 0, in_cols)

    kv_first = query_cols // 128

    def project(blocks, groups):
        def tile(start):
            span = pl.ds(start, TILE)
            for b in blocks:
                proj[span, b * in_cols : (b + 1) * in_cols] = dot_nt(
                    normed1[span, :], in_w[b % 2, b // 2]
                )
            for j in groups:
                lanes = slice(128 * j, 128 * (j + 1))
                proj[span, lanes] = rope(proj[span, lanes], cosine[span, :], sine[span, :])

        row_tiles(tokens, tile)

    project((2, 3), range(kv_first, (HEADS + KV_HEADS) * HEAD_DIM // 128))
    for g in range(KV_HEADS):
        k_first, v_first = query_cols + g * HEAD_DIM, query_cols + (KV_HEADS + g) * HEAD_DIM
        kv[p.m, g] = jnp.concatenate(
            [proj[:, k_first : k_first + HEAD_DIM], proj[:, v_first : v_first + HEAD_DIM]], axis=1
        ).astype(BF16)
    kv_c = p.copy("c", kv.at[p.m])
    kv_y = [p.copy("y", kv.at[p.m, g]) for g in range(KV_HEADS)]
    down.over_z(trim(down_w.at[p.z]))
    project((0, 1), range(kv_first))
    q[...] = proj[:, :query_cols].astype(BF16)
    q_flat = (proj[:, :query_cols].astype(BF16).astype(F32) * SCORE_SCALE).T.astype(BF16)
    for h in range(HEADS):
        for i in range(tiles):
            part = q_flat[h * HEAD_DIM : (h + 1) * HEAD_DIM, i * TILE : (i + 1) * TILE]
            q_aug[h // GROUP, :HEAD_DIM, head_lanes(i, h % GROUP)] = part
    saved = [
        pltpu.make_async_copy(source, target, local_sems.at[3 + n])
        for n, (source, target) in enumerate(((in_w, in_w_out), (q, q_out)))
    ]
    for made in saved:
        made.start()
    def spread(block, g):
        span = block_span(block)
        part = kv[block, g]
        v_t[g, :HEAD_DIM, span] = transposed(part)[HEAD_DIM:]
        k3[g, span, :HEAD_DIM] = part[:, :HEAD_DIM]

    def attend_units(queries, t, g, on_diagonal=()):
        keys = pl.ds(pl.multiple_of(t * TILE, TILE), TILE)
        places = [pl.ds(i * WIDE, WIDE) for i in queries]
        k_g, v_g = k3[g, keys, :], v_t[g, :, keys]
        old = [peak[pl.ds(g, 1), lanes] for lanes in places]
        scores = [dot(k_g, q_aug[g, :, lanes]) for lanes in places]
        scores = [s + diagonal[...] if i in on_diagonal else s for i, s in zip(queries, scores)]
        new = [jnp.maximum(o, jnp.max(s, axis=0, keepdims=True)) for o, s in zip(old, scores)]
        probs = [jnp.exp2(s * LOG2E - n * LOG2E).astype(BF16) for s, n in zip(scores, new)]
        scale = [jnp.exp2((o - n) * LOG2E) for o, n in zip(old, new)]
        outs = [dot(v_g, b) for b in probs]
        for lanes, n, factor, out in zip(places, new, scale, outs):
            peak[pl.ds(g, 1), lanes] = n
            acc[g, :, lanes] = acc[g, :, lanes] * factor + out

    first_tile = p.m * tiles
    for g in range(KV_HEADS):
        spread(p.m, g)
    for queries, t in (((1,), 1), ((0, 1), 0)):

        def group(g, carry):
            attend_units(queries, first_tile + t, g, (t,))
            return carry

        lax.fori_loop(0, KV_HEADS, group, 0)
        if t:
            up.stacked()
            up.over_x()
            output.diagonal_x()
            output.diagonal_y()

    lows = [jnp.maximum(first_tile + i - back, 0) for i in range(tiles)]
    kv_cy = []

    def pass_on(g):
        kv_y[g].wait_recv()
        kv_cy.append(p.copy("c", kv.at[(p.m + 2) % 4, g]))

    kv_c.wait_recv()
    pass_on(0)
    gate.diagonal_x()
    gate.diagonal_y()
    for g in range(KV_HEADS):
        if g + 1 < KV_HEADS:
            pass_on(g + 1)
        if g == 1:
            up.over_y()
            up.diagonal_y()
        if g == 2:
            output.arrived()
            out_cross = p.copy("c", last_part(a_buf.at[p.c]))
        kv_cy[g].wait_recv()
        for n in (1, 2):
            spread(jnp.maximum(p.m - n, 0), g)
        for low, high, queries in ((lows[0], lows[1], (0,)), (lows[1], first_tile, (0, 1))):

            def step(t, carry):
                attend_units(queries, t, g)
                return carry

            lax.fori_loop(low, high, step, 0)
    saved.append(pltpu.make_async_copy(kv, kv_out, local_sems.at[5]))
    saved[-1].start()
    for h in range(HEADS):
        for i in range(tiles):
            part = acc[h // GROUP, :, head_lanes(i, h % GROUP)]
            flat[h * HEAD_DIM : (h + 1) * HEAD_DIM, i * TILE : (i + 1) * TILE] = (
                part[:HEAD_DIM] / part[HEAD_DIM : HEAD_DIM + 1]
            )
    attn[...] = flat[...].T.astype(BF16)
    lse[...] = jnp.zeros_like(lse)
    for g in range(KV_HEADS):
        lse[g : g + 1, :] = peak[g : g + 1, :] + jnp.log(acc[g, HEAD_DIM : HEAD_DIM + 1, :])
    out_cross.wait()
    for b in range(4):
        out_w[b % 2, b // 2] = side_by_side(a_buf.at[b % 2, b // 2], lead, out_cols)
    saved.append(pltpu.make_async_copy(out_w, out_w_out, local_sems.at[6]))
    saved[-1].start()
    up.diagonal_x()

    def project_out(r, carry):
        span = pl.ds(pl.multiple_of(r * TILE, TILE), TILE)
        mid = x_in[span, :].astype(F32)
        for b in range(4):
            mid += dot(attn[span, b * out_cols : (b + 1) * out_cols], out_w[b % 2, b // 2])
        middle[span, :] = mid
        inv = lax.rsqrt(mean_rows(mid * mid, width) + EPSILON)
        normed2[span, :] = (mid * inv * gains[1:2, :]).astype(BF16)
        return carry

    lax.fori_loop(0, tiles, project_out, 0)
    gate.arrived()
    up.arrived()
    for made in early_z:
        made.wait_recv()
    down.stacked()
    for part in (plane, output, gate, up, down):
        part.finish()
    for made in kv_y + kv_cy + early_xy + early_z + [kv_c, early_far]:
        made.wait_send()
    for made in saved:
        made.wait()


def front(
    attn_in_t, attn_out, gain_one, gain_two, w_gate, w_up, w_down_t, x_t, cosine_t, sine_t,
    segments, depth, rows,
):
    width, tokens = x_t.shape
    pad = DPAD // (2 * depth)
    in_cols, cols = attn_in_t.shape[0], w_gate.shape[1]
    a_rows = in_cols + GAIN_ROWS + attn_out.shape[0]
    query_cols, kv_cols = HEADS * HEAD_DIM, 2 * KV_HEADS * HEAD_DIM
    whole = 4 * tokens
    copies = 6 * (depth - 1) + 4 * 4 + 6 + 2 * KV_HEADS
    anywhere = pl.BlockSpec(memory_space=pl.ANY)
    kept = [
        (tokens, query_cols),
        (4, KV_HEADS, tokens, 2 * HEAD_DIM),
        (2, 2, query_cols // 4, DPAD),
        (2, 2, in_cols, DPAD),
    ]
    return pl.pallas_call(
        functools.partial(front_kernel, depth, rows, width, in_cols),
        out_shape=[
            jax.ShapeDtypeStruct((tokens, query_cols), BF16),
            jax.ShapeDtypeStruct((8, GROUP * tokens), F32),
            jax.ShapeDtypeStruct((tokens, DPAD), F32),
            jax.ShapeDtypeStruct((tokens, DPAD), BF16),
            jax.ShapeDtypeStruct((2, DPAD), F32),
            *[jax.ShapeDtypeStruct(shape, BF16) for shape in kept],
            jax.ShapeDtypeStruct((2, 2, 2, depth, pad, cols), BF16),
            jax.ShapeDtypeStruct((depth, pad, cols), BF16),
        ],
        in_specs=vmem_specs(4) + [anywhere] * 3 + vmem_specs(4),
        out_specs=vmem_specs(5) + [anywhere] * 6,
        scratch_shapes=[
            *[pltpu.VMEM(shape, BF16) for shape in kept],
            pltpu.VMEM((2, 2, 2, depth, a_rows, pad), BF16),
            pltpu.VMEM((tokens, DPAD), BF16),
            pltpu.VMEM((tokens, 128), F32),
            pltpu.VMEM((tokens, 128), F32),
            pltpu.VMEM((tokens, DPAD), BF16),
            pltpu.VMEM((tokens, query_cols + kv_cols), F32),
            pltpu.VMEM((KV_HEADS, AUGMENTED, GROUP * tokens), BF16),
            pltpu.VMEM((KV_HEADS, whole, AUGMENTED), BF16),
            pltpu.VMEM((KV_HEADS, AUGMENTED, whole), BF16),
            pltpu.VMEM((KV_HEADS, AUGMENTED, GROUP * tokens), F32),
            pltpu.VMEM((8, GROUP * tokens), F32),
            pltpu.VMEM((query_cols, tokens), F32),
            pltpu.VMEM((TILE, WIDE), F32),
            pltpu.SemaphoreType.DMA((copies,)),
            pltpu.SemaphoreType.DMA((copies,)),
            pltpu.SemaphoreType.DMA((7,)),
        ],
        compiler_params=pltpu.CompilerParams(
            vmem_limit_bytes=58 << 20, collective_id=0, has_side_effects=True
        ),
        cost_estimate=pl.CostEstimate(
            flops=20 << 30, bytes_accessed=40 << 20, transcendentals=8 << 20
        ),
        name="front",
    )(
        attn_in_t, attn_out, gain_one, gain_two, w_gate, w_up, w_down_t, x_t, cosine_t, sine_t,
        segments,
    )


class ZSum:
    def __init__(self, place, blocks, recv, part=lambda ref: ref):
        self.place, self.blocks, self.recv, self.part = place, blocks, recv, part
        self.sent = [
            place.copy(k, part(blocks.at[(place.z + k) % place.depth]), part(recv.at[k - 1]))
            for k in range(1, place.depth)
        ]

    def result(self):
        value = self.part(self.blocks.at[self.place.z])[...].astype(F32)
        for k, made in enumerate(self.sent):
            made.wait_recv()
            value += self.part(self.recv.at[k])[...].astype(F32)
        return value

    def finish(self):
        for made in self.sent:
            made.wait_send()


class PlaneScatter:
    def __init__(
        self, place, source, recv, split, part=lambda ref: ref, stage=None, local_sems=None
    ):
        self.place, self.source, self.recv, self.part = place, source, recv, part
        p, depth = place, place.depth
        self.split, self.rest = split, depth - split
        places = [(p.y, 1 - p.x, 0, split), (1 - p.y, p.x, split, self.rest), (p.y, p.x, 0, depth)]
        self.loads, self.kept, first = [], [], 0
        for n, (y, x, start, size) in enumerate(places):
            if not size:
                self.kept.append(None)
                continue
            view = source.at[y, pl.ds(x * depth + start, size)]
            if stage is not None:
                kept = stage.at[pl.ds(first, size)]
                self.loads.append(pltpu.make_async_copy(view, kept, local_sems.at[n]))
                view = kept
            first += size
            self.kept.append(view)
        self.total = self.kept[2]

    def copy(self, kind, source, first, size):
        slot = self.recv.at[pl.ds(first, size)]
        return self.place.copy(kind, self.part(source), self.part(slot))

    def start_far(self):
        p, split, rest, depth = self.place, self.split, self.rest, self.place.depth
        for load in self.loads:
            load.start()
        far, there = (1 - p.x) * depth, 1 - p.y
        self.far, self.near = [], []
        if split:
            view = self.source.at[there, pl.ds(far, split)]
            self.far.append(self.copy("y", view, 0, split))
        view = self.source.at[there, pl.ds(far + split, rest)]
        self.far.append(self.copy("x", view, split, rest))
        self.sent = list(self.far)

    def start_near(self):
        p, split, rest, depth = self.place, self.split, self.rest, self.place.depth
        far, here, there = (1 - p.x) * depth, p.x * depth, 1 - p.y
        made = []
        if split:
            view = self.source.at[there, pl.ds(here, split)]
            made.append(self.copy("y", view, depth, split))
        view = self.source.at[p.y, pl.ds(far + split, rest)]
        made.append(self.copy("x", view, depth + split, rest))
        self.near += made
        self.sent += made

    def start(self):
        self.start_far()
        self.start_near()

    def forward(self):
        split, rest, depth = self.split, self.rest, self.place.depth
        for load in self.loads:
            load.wait()
        jobs = [(self.kept[1], "y", split, rest)]
        if split:
            jobs.insert(0, (self.kept[0], "x", 0, split))
        for made, (view, kind, first, size) in zip(self.far, jobs):
            made.wait_recv()
            came = self.part(self.recv.at[pl.ds(first, size)])[...].astype(F32)
            kept = self.part(view)
            kept[...] = (kept[...].astype(F32) + came).astype(BF16)
            self.near.append(self.copy(kind, view, 2 * depth + first, size))
            self.sent.append(self.near[-1])

    def add(self):
        depth = self.place.depth
        for made in self.near:
            made.wait_recv()
        terms = [
            self.part(self.recv.at[pl.ds(n * depth, depth)])[...].astype(F32) for n in (1, 2)
        ]
        kept = self.part(self.total)
        kept[...] = (kept[...].astype(F32) + terms[0] + terms[1]).astype(BF16)

    def over_z(self):
        self.add()
        depth = self.place.depth
        slots = self.recv.at[pl.ds(3 * depth, depth - 1)]
        self.along_z = ZSum(self.place, self.total, slots, self.part)
        self.sent += self.along_z.sent

    def result(self):
        return self.along_z.result()

    def finish(self):
        for made in self.sent:
            made.wait_send()


def block_shape(size, pad):
    return (size, pad) if pad % 128 == 0 else (pad, size)


def spread_blocks(target, value, pad):
    if pad % 128 == 0:
        for n in range(DPAD // pad):
            target[n] = value[:, n * pad : (n + 1) * pad].astype(BF16)
    else:
        flipped = value.T.astype(BF16)
        for n in range(DPAD // pad):
            target[n] = flipped[n * pad : (n + 1) * pad]


def halves(count):
    middle = (count // 2 + 15) // 16 * 16
    return pl.ds(0, middle), pl.ds(middle, count - middle)


def one_block(value, rows, pad):
    return (value if pad % 128 == 0 else value.T)[:, :rows]


def scatter_slots(depth):
    return 3 * depth + depth - 1


def scatter_copies(depth):
    return 6 + depth - 1


def store_blocks(ref, start, value):
    pad = ref.shape[1]
    for k in range(TILE // pad):
        ref[start // pad + k] = value[k * pad : (k + 1) * pad]


def row_tiles(count, body):
    def step(r, carry):
        body(pl.multiple_of(r * TILE, TILE))
        return carry

    lax.fori_loop(0, count // TILE, step, 0)


def ffn_kernel(
    depth, rows, normed2, cot_t, middle, ffn_w, down_w, grads, down_sum, hidden_out, grad_n2, cot,
    wide_w, down_buf, down_g, down_r, n_other, c_other, hid, d_gate, d_up, n_t, c_t, ffn_own, parts,
    received, packed, send_sems, recv_sems, local_sems,
):
    tokens = normed2.shape[0]
    cols = ffn_w.shape[-1]
    p = Place(depth, send_sems, recv_sems)
    pad = DPAD // (2 * depth)
    count = trimmed(rows, pad)
    moved = pl.ds(0, count)
    trim = lambda ref: ref.at[..., moved, :]
    loads = [
        pltpu.make_async_copy(
            trim(ffn_w.at[w, y]),
            wide_w.at[w, :, :, moved, pl.ds(y * cols, cols)],
            local_sems.at[2 * w + y],
        )
        for w in range(2)
        for y in range(2)
    ]
    loads.append(
        pltpu.make_async_copy(trim(down_w), trim(down_buf.at[p.y, p.x]), local_sems.at[4])
    )
    for load in loads:
        load.start()
    if count < pad:
        wide_w[:, :, :, count:, :] = jnp.zeros((2, 2, depth, pad - count, 2 * cols), BF16)
        down_buf[:, :, :, count:, :] = jnp.zeros((2, 2, depth, pad - count, cols), BF16)
    p.barrier(["c", "x", "y"])
    n_copy = p.copy("c", normed2, n_other)
    down = PlaneGather(p, None, down_buf, depth // 2, trim)
    loads[4].wait()
    down.over_x()
    down.over_y()
    cot[...] = widen(cot_t, depth, rows, pad).astype(BF16)
    c_copy = p.copy("c", cot, c_other)
    for load in loads[:4]:
        load.wait()

    def sides(s):
        return (n_other, c_other) if s else (normed2, cot)

    for s in range(2):
        if s:
            n_copy.wait_recv()
            c_copy.wait_recv()
        n_from, c_from = sides(s)
        both = slice(s * tokens, (s + 1) * tokens)
        n_t[:, both] = transposed(n_from[...])
        c_t[:, both] = transposed(c_from[...])
        def tile(start):
            span = pl.ds(s * tokens + start, TILE)
            n_rows = n_from[pl.ds(start, TILE), :]
            gate = dot(n_rows, wide_w[0].reshape(DPAD, 2 * cols))
            upper = dot(n_rows, wide_w[1].reshape(DPAD, 2 * cols))
            sigma = jax.nn.sigmoid(gate)
            silu = gate * sigma
            hid[span, :] = (silu * upper).astype(BF16)
            d_gate[span, :] = (upper * sigma * (1.0 + gate * (1.0 - sigma))).astype(BF16)
            d_up[span, :] = silu.astype(BF16)

        row_tiles(tokens, tile)
    down.diagonal_y()
    down.diagonal_x()

    def weight_grad(left, right, target):
        def tile(start):
            side = dot(left[pl.ds(start, TILE), :], right[...]).astype(BF16)
            for y in range(2):
                store_blocks(target.at[y], start, side[:, y * cols : (y + 1) * cols])

        row_tiles(DPAD, tile)

    weight_grad(c_t, hid, down_g)
    total = PlaneScatter(p, down_g, down_r, depth // 2, trim)
    total.start()
    down.arrived()

    for s in (1, 0):
        n_from, c_from = sides(s)

        def tile(start):
            span, both = pl.ds(start, TILE), pl.ds(s * tokens + start, TILE)
            part = None
            for y in range(2):
                lanes = slice(y * cols, (y + 1) * cols)
                w_down = down_buf[y].reshape(DPAD, cols)
                grad_hid = dot(c_from[span, :], w_down)
                d_gate[both, lanes] = (grad_hid * d_gate[both, lanes].astype(F32)).astype(BF16)
                d_up[both, lanes] = (grad_hid * d_up[both, lanes].astype(F32)).astype(BF16)
                out = dot_nt(hid[both, lanes], w_down)
                part = out if part is None else part + out
            back = dot_nt(d_gate[both, :], wide_w[0].reshape(DPAD, 2 * cols))
            back += dot_nt(d_up[both, :], wide_w[1].reshape(DPAD, 2 * cols))
            if s:
                parts[0, span, :] = part.astype(BF16)
                parts[1, span, :] = back.astype(BF16)
            else:
                ffn_own[span, :] = part + middle[span, :]
                grad_n2[span, :] = back

        row_tiles(tokens, tile)
        if s:
            shared = [p.copy("c", parts.at[n], received.at[n]) for n in range(2)]
    total.forward()
    saved = []
    for w, right in ((0, d_gate), (1, d_up)):
        weight_grad(n_t, right, packed.at[w])
        made = pltpu.make_async_copy(packed.at[w], grads.at[w], local_sems.at[w])
        made.start()
        saved.append(made)
    for made in shared:
        made.wait_recv()

    narrow(hidden_out, ffn_own[...] + received[0].astype(F32), depth, rows, pad)
    grad_n2[...] += received[1].astype(F32)
    total.add()
    down_sum[...] = total.total[...]
    total.finish()
    down.finish()
    for made in shared + [n_copy, c_copy]:
        made.wait_send()
    for made in saved:
        made.wait()


def ffn(normed2, cot_t, middle, ffn_w, down_w, rows):
    width, tokens = cot_t.shape
    depth, pad, cols = down_w.shape
    token_rows = pltpu.VMEM((tokens, DPAD), BF16)
    wide = pltpu.VMEM((2 * tokens, 2 * cols), BF16)
    flipped = pltpu.VMEM((DPAD, 2 * tokens), BF16)
    pair = pltpu.VMEM((2, tokens, DPAD), BF16)
    copies = 4 + 4 + 6
    return pl.pallas_call(
        functools.partial(ffn_kernel, depth, rows),
        out_shape=[
            jax.ShapeDtypeStruct((2, 2, 2 * depth, pad, cols), BF16),
            jax.ShapeDtypeStruct((depth, pad, cols), BF16),
            jax.ShapeDtypeStruct((width, tokens), BF16),
            jax.ShapeDtypeStruct((tokens, DPAD), F32),
            jax.ShapeDtypeStruct((tokens, DPAD), BF16),
        ],
        in_specs=vmem_specs(3) + [pl.BlockSpec(memory_space=pl.ANY)] * 2,
        out_specs=[pl.BlockSpec(memory_space=pl.ANY)] + vmem_specs(4),
        scratch_shapes=[
            pltpu.VMEM((2, 2, depth, pad, 2 * cols), BF16),
            pltpu.VMEM((2, 2, depth, pad, cols), BF16),
            pltpu.VMEM((2, 2 * depth, pad, cols), BF16),
            pltpu.VMEM((3 * depth, pad, cols), BF16),
            token_rows, token_rows, wide, wide, wide, flipped, flipped,
            pltpu.VMEM((tokens, DPAD), F32), pair, pair,
            pltpu.VMEM((2, 2, 2 * depth, pad, cols), BF16),
            pltpu.SemaphoreType.DMA((copies,)),
            pltpu.SemaphoreType.DMA((copies,)),
            pltpu.SemaphoreType.DMA((5,)),
        ],
        compiler_params=pltpu.CompilerParams(
            vmem_limit_bytes=61 << 20, collective_id=1, has_side_effects=True
        ),
        cost_estimate=pl.CostEstimate(
            flops=24 << 30, bytes_accessed=30 << 20, transcendentals=2 << 20
        ),
        name="ffn",
    )(normed2, cot_t, middle, ffn_w, down_w)


def mid_kernel(
    depth, width,
    ffn_g, down_sum, grad_n2, middle, cot, gains, out_w, q, kv, attn, lse, segments,
    dq_t, dkv_sum, grad_middle, gain_grad, out_grad, down_grad, gate_grad, up_sum,
    mid_b, out_g, out_c, out_r, ffn_r, down_r, stage, grad_attn, q_aug, g_aug, q3, g3, k3, v3, k_t,
    dkv, acc_kv, diagonal, kv_c, kv_y, send_sems, recv_sems, local_sems,
):
    tokens = q.shape[0]
    tiles = tokens // TILE
    back = 1024 // TILE
    rows = down_grad.shape[0]
    pad = DPAD // (2 * depth)
    out_cols = HEADS * HEAD_DIM // 4
    p = Place(depth, send_sems, recv_sems)
    trim = lambda ref: ref.at[..., pl.ds(0, trimmed(rows, pad)), :]
    p.barrier()
    ffn_sums = [
        PlaneScatter(
            p, ffn_g.at[w], ffn_r.at[w], (0, depth // 2)[w], trim, stage.at[w],
            local_sems.at[pl.ds(3 * w, 3)],
        )
        for w in range(2)
    ]
    ffn_sums[0].start_far()
    ffn_sums[1].start_far()
    ffn_sums[0].start_near()
    down_total = ZSum(p, down_sum, down_r, trim)

    gain = gains[1:2, :]
    gain_grad[...] = jnp.zeros_like(gain_grad)

    def norm_tile(start):
        span = pl.ds(start, TILE)
        mid, up = middle[span, :], grad_n2[span, :]
        inv = lax.rsqrt(mean_rows(mid * mid, width) + EPSILON)
        scaled = up * gain
        mean = mean_rows(scaled * mid, width)
        grad = cot[span, :].astype(F32) + inv * (scaled - mid * (inv * inv * mean))
        grad_middle[span, :] = grad
        gain_grad[...] += jnp.sum(up * mid * inv, axis=0, keepdims=True)
        mid_b[span, :] = grad.astype(BF16)
        for b in range(4):
            side = dot_nt(mid_b[span, :], out_w[b % 2, b // 2])
            grad_attn[span, b * out_cols : (b + 1) * out_cols] = side.astype(BF16)

    row_tiles(tokens, norm_tile)
    attn_t = attn[...].astype(F32).T
    for b in range(4):
        left = attn_t[b * out_cols : (b + 1) * out_cols, :].astype(BF16)
        spread_blocks(out_g.at[b % 2, b // 2], dot(left, mid_b[...]), pad)
    out_cross = p.copy("c", out_g.at[1 - p.c], out_c)

    def block_span(block):
        return pl.ds(pl.multiple_of(block * tokens, tokens), tokens)

    own_seg = segments[:, block_span(p.m)]
    nothing = jnp.zeros((1, TILE), F32)
    q_flat = (q[...].astype(F32) * SCORE_SCALE).T.astype(BF16)
    g_flat = grad_attn[...].astype(F32).T
    for h in range(HEADS):
        g, j = h // GROUP, h % GROUP
        span = slice(h * HEAD_DIM, (h + 1) * HEAD_DIM)
        for i in range(tiles):
            cols, lanes = slice(i * TILE, (i + 1) * TILE), head_lanes(i, j)
            sides = g_flat[span, cols]
            delta = jnp.sum(sides * attn_t[span, cols], axis=0, keepdims=True)
            q_aug[g, :HEAD_DIM, lanes] = q_flat[span, cols]
            q_aug[g, HEAD_DIM:, lanes] = query_features(
                own_seg[:, cols], three_parts(-lse[g : g + 1, lanes])
            )
            g_aug[g, :HEAD_DIM, lanes] = sides.astype(BF16)
            g_aug[g, HEAD_DIM:, lanes] = features(
                three_parts(-delta), [nothing] * SEGMENTS
            ).astype(BF16)
            q3[g, lanes, :] = q[cols, span]
            g3[g, lanes, :] = grad_attn[cols, span]
    for n in range(3):
        block = jnp.maximum(p.m - n, 0)
        span = block_span(block)
        added = key_features(segments[:, span])
        for g in range(KV_HEADS):
            part = kv[block, g]
            k_t[g * HEAD_DIM : (g + 1) * HEAD_DIM, span] = transposed(part)[:HEAD_DIM]
            k3[g, span, :HEAD_DIM] = part[:, :HEAD_DIM]
            v3[g, span, :HEAD_DIM] = part[:, HEAD_DIM:]
            k3[g, span, HEAD_DIM:] = added
            v3[g, span, HEAD_DIM:] = added
    diagonal[...] = diagonal_bias()
    dq_t[...] = jnp.zeros_like(dq_t)
    dkv[...] = jnp.zeros_like(dkv)
    out_cross.wait_recv()
    own = out_g.at[p.c]
    own[...] = (own[...].astype(F32) + out_c[...].astype(F32)).astype(BF16)
    out_sum = PlaneScatter(p, own, out_r, depth // 2)
    out_sum.start()
    ffn_sums[0].forward()
    ffn_sums[1].start_near()

    def key_tile(t, queries, on_diagonal=()):
        keys = pl.ds(pl.multiple_of(t * TILE, TILE), TILE)

        def group(g, carry):
            k_g, v_g = k3[g, keys, :], v3[g, keys, :]
            kt_g = k_t[pl.ds(pl.multiple_of(g * HEAD_DIM, HEAD_DIM), HEAD_DIM), keys]
            dk, dv = None, None
            for i in queries:
                lanes = pl.ds(i * WIDE, WIDE)
                scores = dot(k_g, q_aug[g, :, lanes])
                if i in on_diagonal:
                    scores += diagonal[...]
                probs = jnp.exp2(scores * LOG2E)
                dscores = (probs * dot(v_g, g_aug[g, :, lanes])).astype(BF16)
                add_v = dot(probs.astype(BF16), g3[g, lanes, :])
                add_k = dot(dscores, q3[g, lanes, :])
                dq_t[g, :, lanes] += dot(kt_g, dscores)
                dk = add_k if dk is None else dk + add_k
                dv = add_v if dv is None else dv + add_v
            acc_kv[g] = dk * SCORE_SCALE
            acc_kv[KV_HEADS + g] = dv
            return carry

        lax.fori_loop(0, KV_HEADS, group, 0)
        for n in range(2 * KV_HEADS):
            dkv[keys, n * HEAD_DIM : (n + 1) * HEAD_DIM] = acc_kv[n].astype(BF16)

    def key_span(low, high, queries):
        def step(t, carry):
            key_tile(t, queries)
            return carry

        lax.fori_loop(low, high, step, 0)

    def part_of(index):
        return dkv.at[pl.ds(pl.multiple_of(index * tokens, tokens), tokens)]

    first = p.m * tiles
    key_span(jnp.maximum(first - back, 0), jnp.maximum(first + 1 - back, 0), (0,))
    key_span(jnp.maximum(first + 1 - back, 0), jnp.maximum(first - 2, 0), (0, 1))
    ffn_sums[1].forward()
    key_span(jnp.maximum(first - 2, 0), jnp.maximum(first - 1, 0), (0, 1))
    key_span(jnp.maximum(first - 1, 0), first, (0, 1))
    beside = p.m + 1 - 2 * p.c
    cross = [
        p.copy("c", part_of(index), kv_c.at[n])
        for n, index in enumerate((beside, (beside + 2) % 4))
    ]
    out_sum.forward()
    cross[1].wait_recv()
    away = part_of((p.m + 2) % 4)
    away[...] = (away[...].astype(F32) + kv_c[1].astype(F32)).astype(BF16)
    across = p.copy("y", away, kv_y)
    ffn_sums[0].over_z()
    key_tile(first + 1, (1,), (1,))
    key_tile(first, (0, 1), (0,))
    out_sum.over_z()
    down_grad[...] = down_total.result()[:rows]
    gate_grad[...] = ffn_sums[0].result()[:rows]
    ffn_sums[1].add()
    up_sum[...] = ffn_sums[1].total[...]
    cross[0].wait_recv()
    across.wait_recv()
    dkv_sum[...] = part_of(p.m)[...].astype(F32) + kv_c[0].astype(F32) + kv_y[...].astype(F32)
    out_grad[...] = one_block(out_sum.result(), rows, pad)
    for part in ffn_sums + [out_sum, down_total]:
        part.finish()
    for made in cross + [across, out_cross]:
        made.wait_send()


def middle_back(ffn_g, down_sum, grad_n2, middle, cot, gains, out_w, q, kv, attn, lse, segments,
                depth, rows, width):
    tokens, query_cols = q.shape
    pad = DPAD // (2 * depth)
    cols = ffn_g.shape[-1]
    kv_cols = KV_HEADS * kv.shape[-1]
    out_cols = query_cols // 4
    whole = 4 * tokens
    slots = scatter_slots(depth)
    copies = 3 * scatter_copies(depth) + 4 + depth - 1
    heads_q = pltpu.VMEM((KV_HEADS, GROUP * tokens, HEAD_DIM), BF16)
    heads_kv = pltpu.VMEM((KV_HEADS, whole, AUGMENTED), BF16)
    flipped = pltpu.VMEM((KV_HEADS, AUGMENTED, GROUP * tokens), BF16)
    return pl.pallas_call(
        functools.partial(mid_kernel, depth, width),
        out_shape=[
            jax.ShapeDtypeStruct((KV_HEADS, HEAD_DIM, GROUP * tokens), F32),
            jax.ShapeDtypeStruct((tokens, kv_cols), F32),
            jax.ShapeDtypeStruct((tokens, DPAD), F32),
            jax.ShapeDtypeStruct((1, DPAD), F32),
            jax.ShapeDtypeStruct((out_cols, rows), F32),
            *[jax.ShapeDtypeStruct((rows, cols), F32)] * 2,
            jax.ShapeDtypeStruct((depth, pad, cols), BF16),
        ],
        in_specs=[pl.BlockSpec(memory_space=pl.ANY)] + vmem_specs(11),
        out_specs=vmem_specs(8),
        scratch_shapes=[
            pltpu.VMEM((tokens, DPAD), BF16),
            pltpu.VMEM((2, 2, 2 * depth, *block_shape(out_cols, pad)), BF16),
            pltpu.VMEM((2, 2 * depth, *block_shape(out_cols, pad)), BF16),
            pltpu.VMEM((slots, *block_shape(out_cols, pad)), BF16),
            pltpu.VMEM((2, slots, pad, cols), BF16),
            pltpu.VMEM((depth - 1, pad, cols), BF16),
            pltpu.VMEM((2, 2 * depth, pad, cols), BF16),
            pltpu.VMEM((tokens, query_cols), BF16),
            flipped, flipped, heads_q, heads_q, heads_kv, heads_kv,
            pltpu.VMEM((KV_HEADS * HEAD_DIM, whole), BF16),
            pltpu.VMEM((whole, kv_cols), BF16),
            pltpu.VMEM((2 * KV_HEADS, TILE, HEAD_DIM), F32),
            pltpu.VMEM((TILE, WIDE), F32),
            pltpu.VMEM((2, tokens, kv_cols), BF16),
            pltpu.VMEM((tokens, kv_cols), BF16),
            pltpu.SemaphoreType.DMA((copies,)),
            pltpu.SemaphoreType.DMA((copies,)),
            pltpu.SemaphoreType.DMA((6,)),
        ],
        compiler_params=pltpu.CompilerParams(
            vmem_limit_bytes=61 << 20, collective_id=2, has_side_effects=True
        ),
        cost_estimate=pl.CostEstimate(
            flops=40 << 30, bytes_accessed=50 << 20, transcendentals=8 << 20
        ),
        name="middle_back",
    )(ffn_g, down_sum, grad_n2, middle, cot, gains, out_w, q, kv, attn, lse, segments)


def tail_kernel(
    depth, rows, width,
    dq_t, dkv, cosine_t, sine_t, x_t, grad_middle, gains, in_w, gain2, up_sum,
    grad_hidden, in_grad, gain1_sum, gain2_sum, up_grad,
    ffn_r, proj, proj_b, in_g, in_c, in_r, grad_x, gain_own, gain_r, send_sems, recv_sems,
):
    tokens = x_t.shape[1]
    query_cols = HEADS * HEAD_DIM
    in_cols = in_w.shape[2]
    pad = DPAD // (2 * depth)
    turned = (HEADS + KV_HEADS) * HEAD_DIM
    p = Place(depth, send_sems, recv_sems)
    p.barrier()
    trim = lambda ref: ref.at[..., pl.ds(0, trimmed(rows, pad)), :]
    up_total = ZSum(p, up_sum, ffn_r, trim)
    x_f = widen(x_t, depth, rows, pad)
    gain = gains[0:1, :]
    inv = lax.rsqrt(mean_rows(x_f * x_f, width) + EPSILON)
    normed1 = (x_f * inv * gain).astype(BF16)
    cosine = lane_tables(cosine_t[...])
    sine = signed(lane_tables(sine_t[...]), True)
    turned_parts = [
        jnp.concatenate(
            [dq_t[h // GROUP, :, head_lanes(i, h % GROUP)] for i in range(tokens // TILE)], axis=1
        )
        for h in range(HEADS)
    ]
    proj[:, :query_cols] = jnp.concatenate(turned_parts, axis=0).T * SCORE_SCALE
    proj[:, query_cols:] = dkv[...]
    for j in range(turned // 128):
        lanes = slice(128 * j, 128 * (j + 1))
        proj[:, lanes] = rope(proj[:, lanes], cosine, sine)
    for b in range(4):
        proj_b[b] = proj[:, b * in_cols : (b + 1) * in_cols].astype(BF16)
    cuts = halves(in_g.shape[-2])
    parts = [lambda ref, cut=cut: ref.at[..., cut, :] for cut in cuts]
    for other in (1, 0):
        c = (1 - p.c) if other else p.c
        for y in range(2):
            left = transposed(proj_b[2 * y + c])
            spread_blocks(in_g.at[c, y], dot(left, normed1), pad)
        if other:
            crosses = [p.copy("c", part(in_g.at[c]), part(in_c)) for part in parts]
    own = in_g.at[p.c]
    in_sums = []
    for part, cross in zip(parts, crosses):
        cross.wait_recv()
        kept = part(own)
        kept[...] = (kept[...].astype(F32) + part(in_c)[...].astype(F32)).astype(BF16)
        in_sums.append(PlaneScatter(p, own, in_r, depth // 2, part))
        in_sums[-1].start_far()
    in_sums[0].forward()
    in_sums[0].start_near()
    up = None
    for b in range(4):
        term = dot(proj_b[b], in_w[b % 2, b // 2])
        up = term if up is None else up + term
    scaled = up * gain
    mean = mean_rows(scaled * x_f, width)
    grad_x[...] = grad_middle[...] + inv * (scaled - x_f * (inv * inv * mean))
    gain_own[...] = jnp.zeros_like(gain_own)
    gain_own[0:1, :] = jnp.sum(up * x_f * inv, axis=0, keepdims=True)
    gain_own[1:2, :] = gain2[...]
    in_sums[1].forward()
    in_sums[1].start_near()
    sent = []
    for n, kind in enumerate(("c", "y", "x")):
        made = p.copy(kind, gain_own.at[pl.ds(8 * n, 8)], gain_r.at[pl.ds(8 * n, 8)])
        sent.append(made)
        if n == 0:
            narrow(grad_hidden, grad_x[...], depth, rows, pad)
        made.wait_recv()
        if n == 0:
            in_sums[0].over_z()
        gain_own[8 * (n + 1) : 8 * (n + 2), :] = (
            gain_own[8 * n : 8 * (n + 1), :] + gain_r[8 * n : 8 * (n + 1), :]
        )
    in_sums[1].over_z()
    last = gain_own.at[pl.ds(24, 8)]
    arriving = [p.copy(k, last, gain_r.at[pl.ds(24 + 8 * k, 8)]) for k in range(1, depth)]
    total = last[...]
    for k, made in enumerate(arriving):
        made.wait_recv()
        total += gain_r[32 + 8 * k : 40 + 8 * k, :]
    mine = jnp.zeros((8, pad), F32)
    for n in range(2 * depth):
        mine = jnp.where(n == p.x * depth + p.z, total[:, n * pad : (n + 1) * pad], mine)
    gain1_sum[...] = mine[0:1, :rows]
    gain2_sum[...] = mine[1:2, :rows]
    up_grad[...] = up_total.result()[:rows]
    up_total.finish()
    value = jnp.concatenate([in_sum.result() for in_sum in in_sums], axis=0)
    in_grad[...] = one_block(value, rows, pad)
    for in_sum in in_sums:
        in_sum.finish()
    for made in sent + arriving + crosses:
        made.wait_send()


def tail(
    dq_t, dkv, cosine_t, sine_t, x_t, grad_middle, gains, in_w, gain2, up_sum,
    depth, rows, width,
):
    tokens = x_t.shape[1]
    pad = DPAD // (2 * depth)
    in_cols = in_w.shape[2]
    total = HEADS * HEAD_DIM + dkv.shape[1]
    slots = scatter_slots(depth)
    copies = 2 * scatter_copies(depth) + 2 + 3 + 2 * (depth - 1)
    cols = up_sum.shape[2]
    return pl.pallas_call(
        functools.partial(tail_kernel, depth, rows, width),
        out_shape=[
            jax.ShapeDtypeStruct((width, tokens), F32),
            jax.ShapeDtypeStruct((in_cols, rows), F32),
            *[jax.ShapeDtypeStruct((1, rows), F32)] * 2,
            jax.ShapeDtypeStruct((rows, cols), F32),
        ],
        in_specs=vmem_specs(10),
        out_specs=vmem_specs(5),
        scratch_shapes=[
            pltpu.VMEM((depth - 1, pad, cols), BF16),
            pltpu.VMEM((tokens, total), F32),
            pltpu.VMEM((4, tokens, in_cols), BF16),
            pltpu.VMEM((2, 2, 2 * depth, *block_shape(in_cols, pad)), BF16),
            pltpu.VMEM((2, 2 * depth, *block_shape(in_cols, pad)), BF16),
            pltpu.VMEM((slots, *block_shape(in_cols, pad)), BF16),
            pltpu.VMEM((tokens, DPAD), F32),
            pltpu.VMEM((32, DPAD), F32),
            pltpu.VMEM((24 + 8 * depth, DPAD), F32),
            pltpu.SemaphoreType.DMA((copies,)),
            pltpu.SemaphoreType.DMA((copies,)),
        ],
        compiler_params=pltpu.CompilerParams(
            vmem_limit_bytes=61 << 20, collective_id=3, has_side_effects=True
        ),
        cost_estimate=pl.CostEstimate(
            flops=8 << 30, bytes_accessed=30 << 20, transcendentals=0
        ),
        name="tail",
    )(dq_t, dkv, cosine_t, sine_t, x_t, grad_middle, gains, in_w, gain2, up_sum)


def rotary_tables(position_ids):
    half_dim = HEAD_DIM // 2
    frequency = jnp.exp(
        jnp.arange(half_dim, dtype=F32) * (-2.0 * math.log(10000.0) / HEAD_DIM)
    )
    angles = frequency[:, None] * position_ids.astype(F32)[None, :]
    return jnp.cos(angles), jnp.sin(angles)


def per_device(
    hidden_in, cotangent, segments, positions, attn_in, attn_out, w_gate, w_up, w_down,
    norm1_gain, norm2_gain,
):
    tokens, width = hidden_in.shape[1:]
    dp_size = lax.axis_size("dp")
    depth = dp_size // 2
    rows = width // dp_size
    pad = DPAD // dp_size

    ffn_blocks = [w_gate, w_up, w_down.T]
    if trimmed(rows, pad) == pad:
        ffn_blocks = [jnp.pad(w, ((0, pad - rows), (0, 0))) for w in ffn_blocks]
    x_t, cot_t = hidden_in[0].T, cotangent[0].T
    cosine_t, sine_t = rotary_tables(positions[0])
    attn, lse, middle, normed2, gains, q, kv, out_w, in_w, ffn_w, down_w = front(
        attn_in.T, attn_out, norm1_gain[None], norm2_gain[None], *ffn_blocks,
        x_t, cosine_t, sine_t, segments, depth, rows,
    )
    ffn_g, down_sum, hidden_out, grad_n2, cot = ffn(normed2, cot_t, middle, ffn_w, down_w, rows)
    dq_t, dkv, grad_middle, gain2, g_out, g_down, g_gate, up_sum = middle_back(
        ffn_g, down_sum, grad_n2, middle, cot, gains, out_w, q, kv, attn, lse, segments,
        depth, rows, width,
    )
    grad_hidden, g_in, g_gain1, g_gain2, g_up = tail(
        dq_t, dkv, cosine_t, sine_t, x_t, grad_middle, gains, in_w, gain2, up_sum,
        depth, rows, width,
    )
    return (
        hidden_out.T[None],
        grad_hidden.T[None],
        g_in.T,
        g_out,
        g_gate,
        g_up,
        g_down.T,
        g_gain1[0],
        g_gain2[0],
    )


def solution(mesh):
    return jax.shard_map(
        per_device,
        mesh=mesh,
        in_specs=(
            P("dp", "mp", None),
            P("dp", "mp", None),
            P("dp", None),
            P("dp", "mp"),
            P("dp", "mp"),
            P("mp", "dp"),
            P("dp", "mp"),
            P("dp", "mp"),
            P("mp", "dp"),
            P("dp"),
            P("dp"),
        ),
        out_specs=(
            P("dp", "mp", None),
            P("dp", "mp", None),
            P("dp", "mp"),
            P("mp", "dp"),
            P("dp", "mp"),
            P("dp", "mp"),
            P("mp", "dp"),
            P("dp"),
            P("dp"),
        ),
        check_vma=False,
    )
```

```python
import functools
import math

import jax
import jax.numpy as jnp
from jax import lax
from jax.experimental import pallas as pl
from jax.experimental.pallas import tpu as pltpu
from jax.sharding import PartitionSpec as P

HEADS = 15
KV_HEADS = 5
GROUP = HEADS // KV_HEADS
HEAD_DIM = 64
DPAD = 1024
TILE = 256
EPSILON = 1e-05
SCORE_SCALE = 0.125
MASK_FILL = -1e30
LOG2E = 1.4426950408889634
EXP_SCALE = SCORE_SCALE * LOG2E
GAIN_ROWS = 16
EARLY = 256
SEGMENTS = 4
AUGMENTED = HEAD_DIM + 16
WIDE = GROUP * TILE
BF16 = jnp.bfloat16
F32 = jnp.float32


def dot(a, b):
    return jnp.dot(a, b, preferred_element_type=F32)


def dot_nt(a, b):
    return lax.dot_general(a, b, (((1,), (1,)), ((), ())), preferred_element_type=F32)


def vmem_specs(count):
    return [pl.BlockSpec(memory_space=pltpu.VMEM)] * count


def transposed(value):
    return value.astype(F32).T.astype(BF16)


class Place:
    def __init__(self, depth, send_sems, recv_sems):
        dp_index, m = lax.axis_index("dp"), lax.axis_index("mp")
        self.depth = depth
        self.z, self.x = dp_index // 2, dp_index % 2
        self.m, self.y, self.c = m, m // 2, m % 2
        self.send_sems, self.recv_sems = send_sems, recv_sems
        self.count = 0

    def peer(self, kind):
        z, x, y, c = self.z, self.x, self.y, self.c
        if kind == "x":
            x = 1 - x
        elif kind == "y":
            y = 1 - y
        elif kind == "c":
            c = 1 - c
        else:
            z = (z + kind) % self.depth
        return 2 * z + x, 2 * y + c

    def kinds(self):
        return ["x", "y", "c"] + list(range(1, self.depth))

    def barrier(self, kinds=None):
        semaphore = pltpu.get_barrier_semaphore()
        kinds = kinds or self.kinds()
        for kind in kinds:
            pl.semaphore_signal(
                semaphore, inc=1, device_id=self.peer(kind), device_id_type=pl.DeviceIdType.MESH
            )
        pl.semaphore_wait(semaphore, len(kinds))

    def copy(self, kind, source, target=None):
        index = self.count
        self.count += 1
        made = pltpu.make_async_remote_copy(
            src_ref=source,
            dst_ref=source if target is None else target,
            send_sem=self.send_sems.at[index],
            recv_sem=self.recv_sems.at[index],
            device_id=self.peer(kind),
            device_id_type=pl.DeviceIdType.MESH,
        )
        made.start()
        return made


class PlaneGather:
    def __init__(self, place, source, buffer, by_x, part=lambda ref: ref):
        self.place, self.source, self.buffer, self.part = place, source, buffer, part
        self.split = place.depth - by_x
        self.sent, self.last = [], []

    def over_z(self, slot=None):
        p = self.place
        slot = self.part(self.buffer.at[p.y, p.x, p.z]) if slot is None else slot
        self.arriving = [p.copy(k, self.source, slot) for k in range(1, p.depth)]
        self.sent += self.arriving

    def stacked(self):
        for made in self.arriving:
            made.wait_recv()

    def over_x(self):
        p = self.place
        self.by_x = p.copy("x", self.part(self.buffer.at[p.y, p.x]))
        self.sent.append(self.by_x)

    def over_y(self):
        p = self.place
        self.by_y = p.copy("y", self.part(self.buffer.at[p.y, p.x]))
        self.sent.append(self.by_y)

    def diagonal_x(self):
        p = self.place
        self.by_y.wait_recv()
        span = pl.ds(self.split, p.depth - self.split)
        self.last.append(p.copy("x", self.part(self.buffer.at[1 - p.y, p.x, span])))

    def diagonal_y(self):
        p = self.place
        self.by_x.wait_recv()
        if self.split:
            span = pl.ds(0, self.split)
            self.last.append(p.copy("y", self.part(self.buffer.at[p.y, 1 - p.x, span])))

    def arrived(self):
        for made in self.last:
            made.wait_recv()

    def finish(self):
        for made in self.sent + self.last:
            made.wait_send()


def rope(value, cosine, sine):
    lane = lax.broadcasted_iota(jnp.int32, value.shape, 1)
    half = HEAD_DIM // 2
    partner = jnp.where(
        lane % HEAD_DIM < half, pltpu.roll(value, 128 - half, 1), pltpu.roll(value, half, 1)
    )
    return value * cosine + partner * sine


def trimmed(rows, pad):
    return rows if rows % 8 == 0 else pad


def natural(block, depth):
    return 2 * (block % depth) + block // depth


def widen(source, depth, rows, pad):
    filler = jnp.zeros((pad - rows, source.shape[1]), F32)
    parts = []
    for b in range(2 * depth):
        first = natural(b, depth) * rows
        parts += [source[first : first + rows, :].astype(F32), filler]
    return jnp.concatenate(parts, axis=0).T


def narrow(target, value, depth, rows, pad):
    flipped = value.T
    for b in range(2 * depth):
        first = natural(b, depth) * rows
        target[first : first + rows, :] = flipped[b * pad : b * pad + rows, :].astype(target.dtype)


def side_by_side(ref, first, size):
    _, depth, _, pad = ref.shape
    span = pl.ds(first, size)
    return jnp.concatenate(
        [ref[b // depth, b % depth, span, :] for b in range(2 * depth)], axis=1
    )


def lane_tables(table):
    return jnp.concatenate([table] * (256 // HEAD_DIM), axis=0).T


def signed(table, back):
    lane = lax.broadcasted_iota(jnp.int32, table.shape, 1) % HEAD_DIM
    first = lane < HEAD_DIM // 2
    return jnp.where(first, table, -table) if back else jnp.where(first, -table, table)


def mean_rows(value, width):
    return jnp.sum(value, axis=-1, keepdims=True) * (1.0 / width)


def diagonal_bias():
    key = lax.broadcasted_iota(jnp.int32, (TILE, WIDE), 0)
    query = lax.broadcasted_iota(jnp.int32, (TILE, WIDE), 1) % TILE
    return jnp.where(key <= query, 0.0, MASK_FILL)


def features(first, segment_rows):
    spare = 16 - len(first) - SEGMENTS
    zeros = jnp.zeros((spare, first[0].shape[1]), F32)
    return jnp.concatenate(list(first) + segment_rows + [zeros], axis=0)


def key_features(segment):
    other = [jnp.where(segment != n, MASK_FILL, 0.0) for n in range(SEGMENTS)]
    return features([jnp.ones(segment.shape, F32)] * 3, other).T.astype(BF16)


def query_features(segment, first):
    same = [jnp.where(segment == n, 1.0, 0.0) for n in range(SEGMENTS)]
    return features(first, same).astype(BF16)


def three_parts(value):
    parts = []
    for _ in range(3):
        parts.append(value.astype(BF16).astype(F32))
        value = value - parts[-1]
    return parts


def head_lanes(i, j):
    return slice(i * WIDE + j * TILE, i * WIDE + (j + 1) * TILE)


def front_kernel(
    depth, rows, width, in_cols,
    attn_in_t, attn_out, gain_one, gain_two, w_gate, w_up, w_down_t, x_t, cosine_t, sine_t, segments,
    attn, lse, middle, normed2, gains, q_out, kv_out, out_w_out, in_w_out, ffn_w, down_w,
    q, kv, out_w, in_w, a_buf, x_in, cosine, sine, normed1, proj, q_aug, k3, v_t, acc, peak, flat,
    diagonal, send_sems, recv_sems, local_sems,
):
    tokens = x_in.shape[0]
    tiles = tokens // TILE
    back = 1024 // TILE
    pad = DPAD // (2 * depth)
    lead = in_cols + GAIN_ROWS
    query_cols = HEADS * HEAD_DIM
    out_cols = query_cols // 4
    p = Place(depth, send_sems, recv_sems)
    block = a_buf.at[p.c, p.y, p.x, p.z]
    block[...] = jnp.zeros_like(block)
    block[0:in_cols, 0:rows] = attn_in_t[...]
    block[in_cols : in_cols + 1, 0:rows] = gain_one[...]
    block[in_cols + 1 : in_cols + 2, 0:rows] = gain_two[...]
    block[lead : lead + out_cols, 0:rows] = attn_out[...]
    moved = pl.ds(0, trimmed(rows, pad))
    trim = lambda ref: ref.at[..., moved, :]
    own = [
        pltpu.make_async_copy(
            source, trim(ffn_w.at[w, p.y, p.x, p.z] if w < 2 else down_w.at[p.z]), local_sems.at[w]
        )
        for w, source in enumerate((w_gate, w_up, w_down_t))
    ]
    for made in own:
        made.start()
    p.barrier()
    first_part = lambda ref: ref.at[..., pl.ds(0, lead), :]
    last_part = lambda ref: ref.at[..., pl.ds(lead, out_cols), :]
    buffer = a_buf.at[p.c]
    plane = PlaneGather(p, first_part(block), buffer, depth // 2, first_part)
    output = PlaneGather(p, last_part(block), buffer, depth // 2, last_part)
    gate = PlaneGather(p, w_gate, ffn_w.at[0], depth, trim)
    early = lambda ref: ref.at[..., moved, pl.ds(0, EARLY)]
    rest = pl.ds(EARLY, w_up.shape[1] - EARLY)
    late = lambda ref: ref.at[..., moved, rest]
    up = PlaneGather(p, w_up.at[:, rest], ffn_w.at[1], depth // 2, late)
    down = PlaneGather(p, w_down_t, None, 0)
    plane.over_z()
    early_own = early(ffn_w.at[1, p.y, p.x, p.z])
    early_xy = [p.copy(kind, w_up.at[:, pl.ds(0, EARLY)], early_own) for kind in ("x", "y")]
    x_f = widen(x_t, depth, rows, pad)
    x_in[...] = x_f.astype(BF16)
    cosine[...] = lane_tables(cosine_t[...])
    sine[...] = signed(lane_tables(sine_t[...]), False)
    inv_one = lax.rsqrt(mean_rows(x_f * x_f, width) + EPSILON)
    def block_span(block):
        return pl.ds(pl.multiple_of(block * tokens, tokens), tokens)

    early_xy[1].wait_recv()
    early_far = p.copy("x", early(ffn_w.at[1, 1 - p.y, p.x, p.z]))
    plane.stacked()
    plane.over_x()
    plane.over_y()
    output.over_z()
    gate.over_z()
    own_seg = segments[:, block_span(p.m)]
    nothing = jnp.zeros(own_seg.shape, F32)
    own_features = query_features(own_seg, [nothing] * 3)
    for g in range(KV_HEADS):
        for i in range(tiles):
            for j in range(GROUP):
                q_aug[g, HEAD_DIM:, head_lanes(i, j)] = own_features[:, i * TILE : (i + 1) * TILE]
    ones = lax.broadcasted_iota(jnp.int32, (16, 4 * tokens), 0) == 0
    for g in range(KV_HEADS):
        v_t[g, HEAD_DIM:, :] = jnp.where(ones, 1.0, 0.0).astype(BF16)
    diagonal[...] = diagonal_bias()
    acc[...] = jnp.zeros_like(acc)
    peak[...] = jnp.full_like(peak, MASK_FILL)
    plane.diagonal_y()
    plane.diagonal_x()
    for made in own:
        made.wait()
    up.over_z()
    early_xy[0].wait_recv()
    early_far.wait_recv()
    column = early(ffn_w.at[1, :, :, p.z])
    early_z = [p.copy(k, column) for k in range(1, depth)]
    plane.arrived()
    cross = p.copy("c", first_part(a_buf.at[p.c]))
    output.stacked()
    output.over_x()
    output.over_y()
    for n in range(3):
        span = block_span(jnp.maximum(p.m - n, 0))
        added = key_features(segments[:, span])
        for g in range(KV_HEADS):
            k3[g, span, HEAD_DIM:] = added
    gate.stacked()
    gate.over_x()
    gate.over_y()
    cross.wait()
    for b in range(2 * depth):
        gains[:, b * pad : (b + 1) * pad] = a_buf[
            0, 0, b // depth, b % depth, pl.ds(in_cols, 2), :
        ].astype(F32)
    normed1[...] = (x_f * inv_one * gains[0:1, :]).astype(BF16)
    for b in range(4):
        in_w[b % 2, b // 2] = side_by_side(a_buf.at[b % 2, b // 2], 0, in_cols)

    kv_first = query_cols // 128

    def project(blocks, groups):
        def tile(start):
            span = pl.ds(start, TILE)
            for b in blocks:
                proj[span, b * in_cols : (b + 1) * in_cols] = dot_nt(
                    normed1[span, :], in_w[b % 2, b // 2]
                )
            for j in groups:
                lanes = slice(128 * j, 128 * (j + 1))
                proj[span, lanes] = rope(proj[span, lanes], cosine[span, :], sine[span, :])

        row_tiles(tokens, tile)

    project((2, 3), range(kv_first, (HEADS + KV_HEADS) * HEAD_DIM // 128))
    for g in range(KV_HEADS):
        k_first, v_first = query_cols + g * HEAD_DIM, query_cols + (KV_HEADS + g) * HEAD_DIM
        kv[p.m, g] = jnp.concatenate(
            [proj[:, k_first : k_first + HEAD_DIM], proj[:, v_first : v_first + HEAD_DIM]], axis=1
        ).astype(BF16)
    kv_c = p.copy("c", kv.at[p.m])
    kv_y = [p.copy("y", kv.at[p.m, g]) for g in range(KV_HEADS)]
    down.over_z(trim(down_w.at[p.z]))
    project((0, 1), range(kv_first))
    q[...] = proj[:, :query_cols].astype(BF16)
    q_flat = (proj[:, :query_cols].astype(BF16).astype(F32) * SCORE_SCALE).T.astype(BF16)
    for h in range(HEADS):
        for i in range(tiles):
            part = q_flat[h * HEAD_DIM : (h + 1) * HEAD_DIM, i * TILE : (i + 1) * TILE]
            q_aug[h // GROUP, :HEAD_DIM, head_lanes(i, h % GROUP)] = part
    saved = [
        pltpu.make_async_copy(source, target, local_sems.at[3 + n])
        for n, (source, target) in enumerate(((in_w, in_w_out), (q, q_out)))
    ]
    for made in saved:
        made.start()
    def spread(block, g):
        span = block_span(block)
        part = kv[block, g]
        v_t[g, :HEAD_DIM, span] = transposed(part)[HEAD_DIM:]
        k3[g, span, :HEAD_DIM] = part[:, :HEAD_DIM]

    def attend_units(queries, t, g, on_diagonal=()):
        keys = pl.ds(pl.multiple_of(t * TILE, TILE), TILE)
        places = [pl.ds(i * WIDE, WIDE) for i in queries]
        k_g, v_g = k3[g, keys, :], v_t[g, :, keys]
        old = [peak[pl.ds(g, 1), lanes] for lanes in places]
        scores = [dot(k_g, q_aug[g, :, lanes]) for lanes in places]
        scores = [s + diagonal[...] if i in on_diagonal else s for i, s in zip(queries, scores)]
        new = [jnp.maximum(o, jnp.max(s, axis=0, keepdims=True)) for o, s in zip(old, scores)]
        probs = [jnp.exp2(s * LOG2E - n * LOG2E).astype(BF16) for s, n in zip(scores, new)]
        scale = [jnp.exp2((o - n) * LOG2E) for o, n in zip(old, new)]
        outs = [dot(v_g, b) for b in probs]
        for lanes, n, factor, out in zip(places, new, scale, outs):
            peak[pl.ds(g, 1), lanes] = n
            acc[g, :, lanes] = acc[g, :, lanes] * factor + out

    first_tile = p.m * tiles
    for g in range(KV_HEADS):
        spread(p.m, g)
    for queries, t in (((1,), 1), ((0, 1), 0)):

        def group(g, carry):
            attend_units(queries, first_tile + t, g, (t,))
            return carry

        lax.fori_loop(0, KV_HEADS, group, 0)
        if t:
            up.stacked()
            up.over_x()
            output.diagonal_x()
            output.diagonal_y()

    lows = [jnp.maximum(first_tile + i - back, 0) for i in range(tiles)]
    kv_cy = []

    def pass_on(g):
        kv_y[g].wait_recv()
        kv_cy.append(p.copy("c", kv.at[(p.m + 2) % 4, g]))

    kv_c.wait_recv()
    pass_on(0)
    gate.diagonal_x()
    gate.diagonal_y()
    for g in range(KV_HEADS):
        if g + 1 < KV_HEADS:
            pass_on(g + 1)
        if g == 1:
            up.over_y()
            up.diagonal_y()
        if g == 2:
            output.arrived()
            out_cross = p.copy("c", last_part(a_buf.at[p.c]))
        kv_cy[g].wait_recv()
        for n in (1, 2):
            spread(jnp.maximum(p.m - n, 0), g)
        for low, high, queries in ((lows[0], lows[1], (0,)), (lows[1], first_tile, (0, 1))):

            def step(t, carry):
                attend_units(queries, t, g)
                return carry

            lax.fori_loop(low, high, step, 0)
    saved.append(pltpu.make_async_copy(kv, kv_out, local_sems.at[5]))
    saved[-1].start()
    for h in range(HEADS):
        for i in range(tiles):
            part = acc[h // GROUP, :, head_lanes(i, h % GROUP)]
            flat[h * HEAD_DIM : (h + 1) * HEAD_DIM, i * TILE : (i + 1) * TILE] = (
                part[:HEAD_DIM] / part[HEAD_DIM : HEAD_DIM + 1]
            )
    attn[...] = flat[...].T.astype(BF16)
    lse[...] = jnp.zeros_like(lse)
    for g in range(KV_HEADS):
        lse[g : g + 1, :] = peak[g : g + 1, :] + jnp.log(acc[g, HEAD_DIM : HEAD_DIM + 1, :])
    out_cross.wait()
    for b in range(4):
        out_w[b % 2, b // 2] = side_by_side(a_buf.at[b % 2, b // 2], lead, out_cols)
    saved.append(pltpu.make_async_copy(out_w, out_w_out, local_sems.at[6]))
    saved[-1].start()
    up.diagonal_x()

    def project_out(r, carry):
        span = pl.ds(pl.multiple_of(r * TILE, TILE), TILE)
        mid = x_in[span, :].astype(F32)
        for b in range(4):
            mid += dot(attn[span, b * out_cols : (b + 1) * out_cols], out_w[b % 2, b // 2])
        middle[span, :] = mid
        inv = lax.rsqrt(mean_rows(mid * mid, width) + EPSILON)
        normed2[span, :] = (mid * inv * gains[1:2, :]).astype(BF16)
        return carry

    lax.fori_loop(0, tiles, project_out, 0)
    gate.arrived()
    up.arrived()
    for made in early_z:
        made.wait_recv()
    down.stacked()
    for part in (plane, output, gate, up, down):
        part.finish()
    for made in kv_y + kv_cy + early_xy + early_z + [kv_c, early_far]:
        made.wait_send()
    for made in saved:
        made.wait()


def front(
    attn_in_t, attn_out, gain_one, gain_two, w_gate, w_up, w_down_t, x_t, cosine_t, sine_t,
    segments, depth, rows,
):
    width, tokens = x_t.shape
    pad = DPAD // (2 * depth)
    in_cols, cols = attn_in_t.shape[0], w_gate.shape[1]
    a_rows = in_cols + GAIN_ROWS + attn_out.shape[0]
    query_cols, kv_cols = HEADS * HEAD_DIM, 2 * KV_HEADS * HEAD_DIM
    whole = 4 * tokens
    copies = 6 * (depth - 1) + 4 * 4 + 6 + 2 * KV_HEADS
    anywhere = pl.BlockSpec(memory_space=pl.ANY)
    kept = [
        (tokens, query_cols),
        (4, KV_HEADS, tokens, 2 * HEAD_DIM),
        (2, 2, query_cols // 4, DPAD),
        (2, 2, in_cols, DPAD),
    ]
    return pl.pallas_call(
        functools.partial(front_kernel, depth, rows, width, in_cols),
        out_shape=[
            jax.ShapeDtypeStruct((tokens, query_cols), BF16),
            jax.ShapeDtypeStruct((8, GROUP * tokens), F32),
            jax.ShapeDtypeStruct((tokens, DPAD), F32),
            jax.ShapeDtypeStruct((tokens, DPAD), BF16),
            jax.ShapeDtypeStruct((2, DPAD), F32),
            *[jax.ShapeDtypeStruct(shape, BF16) for shape in kept],
            jax.ShapeDtypeStruct((2, 2, 2, depth, pad, cols), BF16),
            jax.ShapeDtypeStruct((depth, pad, cols), BF16),
        ],
        in_specs=vmem_specs(4) + [anywhere] * 3 + vmem_specs(4),
        out_specs=vmem_specs(5) + [anywhere] * 6,
        scratch_shapes=[
            *[pltpu.VMEM(shape, BF16) for shape in kept],
            pltpu.VMEM((2, 2, 2, depth, a_rows, pad), BF16),
            pltpu.VMEM((tokens, DPAD), BF16),
            pltpu.VMEM((tokens, 128), F32),
            pltpu.VMEM((tokens, 128), F32),
            pltpu.VMEM((tokens, DPAD), BF16),
            pltpu.VMEM((tokens, query_cols + kv_cols), F32),
            pltpu.VMEM((KV_HEADS, AUGMENTED, GROUP * tokens), BF16),
            pltpu.VMEM((KV_HEADS, whole, AUGMENTED), BF16),
            pltpu.VMEM((KV_HEADS, AUGMENTED, whole), BF16),
            pltpu.VMEM((KV_HEADS, AUGMENTED, GROUP * tokens), F32),
            pltpu.VMEM((8, GROUP * tokens), F32),
            pltpu.VMEM((query_cols, tokens), F32),
            pltpu.VMEM((TILE, WIDE), F32),
            pltpu.SemaphoreType.DMA((copies,)),
            pltpu.SemaphoreType.DMA((copies,)),
            pltpu.SemaphoreType.DMA((7,)),
        ],
        compiler_params=pltpu.CompilerParams(
            vmem_limit_bytes=58 << 20, collective_id=0, has_side_effects=True
        ),
        cost_estimate=pl.CostEstimate(
            flops=20 << 30, bytes_accessed=40 << 20, transcendentals=8 << 20
        ),
        name="front",
    )(
        attn_in_t, attn_out, gain_one, gain_two, w_gate, w_up, w_down_t, x_t, cosine_t, sine_t,
        segments,
    )


class ZSum:
    def __init__(self, place, blocks, recv, part=lambda ref: ref):
        self.place, self.blocks, self.recv, self.part = place, blocks, recv, part
        self.sent = [
            place.copy(k, part(blocks.at[(place.z + k) % place.depth]), part(recv.at[k - 1]))
            for k in range(1, place.depth)
        ]

    def result(self):
        value = self.part(self.blocks.at[self.place.z])[...].astype(F32)
        for k, made in enumerate(self.sent):
            made.wait_recv()
            value += self.part(self.recv.at[k])[...].astype(F32)
        return value

    def finish(self):
        for made in self.sent:
            made.wait_send()


class PlaneScatter:
    def __init__(
        self, place, source, recv, split, part=lambda ref: ref, stage=None, local_sems=None
    ):
        self.place, self.source, self.recv, self.part = place, source, recv, part
        p, depth = place, place.depth
        self.split, self.rest = split, depth - split
        places = [(p.y, 1 - p.x, 0, split), (1 - p.y, p.x, split, self.rest), (p.y, p.x, 0, depth)]
        self.loads, self.kept, first = [], [], 0
        for n, (y, x, start, size) in enumerate(places):
            if not size:
                self.kept.append(None)
                continue
            view = source.at[y, pl.ds(x * depth + start, size)]
            if stage is not None:
                kept = stage.at[pl.ds(first, size)]
                self.loads.append(pltpu.make_async_copy(view, kept, local_sems.at[n]))
                view = kept
            first += size
            self.kept.append(view)
        self.total = self.kept[2]

    def copy(self, kind, source, first, size):
        slot = self.recv.at[pl.ds(first, size)]
        return self.place.copy(kind, self.part(source), self.part(slot))

    def start_far(self):
        p, split, rest, depth = self.place, self.split, self.rest, self.place.depth
        for load in self.loads:
            load.start()
        far, there = (1 - p.x) * depth, 1 - p.y
        self.far, self.near = [], []
        if split:
            view = self.source.at[there, pl.ds(far, split)]
            self.far.append(self.copy("y", view, 0, split))
        view = self.source.at[there, pl.ds(far + split, rest)]
        self.far.append(self.copy("x", view, split, rest))
        self.sent = list(self.far)

    def start_near(self):
        p, split, rest, depth = self.place, self.split, self.rest, self.place.depth
        far, here, there = (1 - p.x) * depth, p.x * depth, 1 - p.y
        made = []
        if split:
            view = self.source.at[there, pl.ds(here, split)]
            made.append(self.copy("y", view, depth, split))
        view = self.source.at[p.y, pl.ds(far + split, rest)]
        made.append(self.copy("x", view, depth + split, rest))
        self.near += made
        self.sent += made

    def start(self):
        self.start_far()
        self.start_near()

    def forward(self):
        split, rest, depth = self.split, self.rest, self.place.depth
        for load in self.loads:
            load.wait()
        jobs = [(self.kept[1], "y", split, rest)]
        if split:
            jobs.insert(0, (self.kept[0], "x", 0, split))
        for made, (view, kind, first, size) in zip(self.far, jobs):
            made.wait_recv()
            came = self.part(self.recv.at[pl.ds(first, size)])[...].astype(F32)
            kept = self.part(view)
            kept[...] = (kept[...].astype(F32) + came).astype(BF16)
            self.near.append(self.copy(kind, view, 2 * depth + first, size))
            self.sent.append(self.near[-1])

    def add(self):
        depth = self.place.depth
        for made in self.near:
            made.wait_recv()
        terms = [
            self.part(self.recv.at[pl.ds(n * depth, depth)])[...].astype(F32) for n in (1, 2)
        ]
        kept = self.part(self.total)
        kept[...] = (kept[...].astype(F32) + terms[0] + terms[1]).astype(BF16)

    def over_z(self):
        self.add()
        depth = self.place.depth
        slots = self.recv.at[pl.ds(3 * depth, depth - 1)]
        self.along_z = ZSum(self.place, self.total, slots, self.part)
        self.sent += self.along_z.sent

    def result(self):
        return self.along_z.result()

    def finish(self):
        for made in self.sent:
            made.wait_send()


def block_shape(size, pad):
    return (size, pad) if pad % 128 == 0 else (pad, size)


def spread_blocks(target, value, pad):
    if pad % 128 == 0:
        for n in range(DPAD // pad):
            target[n] = value[:, n * pad : (n + 1) * pad].astype(BF16)
    else:
        flipped = value.T.astype(BF16)
        for n in range(DPAD // pad):
            target[n] = flipped[n * pad : (n + 1) * pad]


def halves(count):
    middle = (count // 2 + 15) // 16 * 16
    return pl.ds(0, middle), pl.ds(middle, count - middle)


def one_block(value, rows, pad):
    return (value if pad % 128 == 0 else value.T)[:, :rows]


def scatter_slots(depth):
    return 3 * depth + depth - 1


def scatter_copies(depth):
    return 6 + depth - 1


def store_blocks(ref, start, value):
    pad = ref.shape[1]
    for k in range(TILE // pad):
        ref[start // pad + k] = value[k * pad : (k + 1) * pad]


def row_tiles(count, body):
    def step(r, carry):
        body(pl.multiple_of(r * TILE, TILE))
        return carry

    lax.fori_loop(0, count // TILE, step, 0)


def ffn_kernel(
    depth, rows, normed2, cot_t, middle, ffn_w, down_w, grads, down_sum, hidden_out, grad_n2, cot,
    wide_w, down_buf, down_g, down_r, n_other, c_other, hid, d_gate, d_up, n_t, c_t, ffn_own, parts,
    received, packed, send_sems, recv_sems, local_sems,
):
    tokens = normed2.shape[0]
    cols = ffn_w.shape[-1]
    p = Place(depth, send_sems, recv_sems)
    pad = DPAD // (2 * depth)
    count = trimmed(rows, pad)
    moved = pl.ds(0, count)
    trim = lambda ref: ref.at[..., moved, :]
    loads = [
        pltpu.make_async_copy(
            trim(ffn_w.at[w, y]),
            wide_w.at[w, :, :, moved, pl.ds(y * cols, cols)],
            local_sems.at[2 * w + y],
        )
        for w in range(2)
        for y in range(2)
    ]
    loads.append(
        pltpu.make_async_copy(trim(down_w), trim(down_buf.at[p.y, p.x]), local_sems.at[4])
    )
    for load in loads:
        load.start()
    if count < pad:
        wide_w[:, :, :, count:, :] = jnp.zeros((2, 2, depth, pad - count, 2 * cols), BF16)
        down_buf[:, :, :, count:, :] = jnp.zeros((2, 2, depth, pad - count, cols), BF16)
    p.barrier(["c", "x", "y"])
    n_copy = p.copy("c", normed2, n_other)
    down = PlaneGather(p, None, down_buf, depth // 2, trim)
    loads[4].wait()
    down.over_x()
    down.over_y()
    cot[...] = widen(cot_t, depth, rows, pad).astype(BF16)
    c_copy = p.copy("c", cot, c_other)
    for load in loads[:4]:
        load.wait()

    def sides(s):
        return (n_other, c_other) if s else (normed2, cot)

    for s in range(2):
        if s:
            n_copy.wait_recv()
            c_copy.wait_recv()
        n_from, c_from = sides(s)
        both = slice(s * tokens, (s + 1) * tokens)
        n_t[:, both] = transposed(n_from[...])
        c_t[:, both] = transposed(c_from[...])
        def tile(start):
            span = pl.ds(s * tokens + start, TILE)
            n_rows = n_from[pl.ds(start, TILE), :]
            gate = dot(n_rows, wide_w[0].reshape(DPAD, 2 * cols))
            upper = dot(n_rows, wide_w[1].reshape(DPAD, 2 * cols))
            sigma = jax.nn.sigmoid(gate)
            silu = gate * sigma
            hid[span, :] = (silu * upper).astype(BF16)
            d_gate[span, :] = (upper * sigma * (1.0 + gate * (1.0 - sigma))).astype(BF16)
            d_up[span, :] = silu.astype(BF16)

        row_tiles(tokens, tile)
    down.diagonal_y()
    down.diagonal_x()

    def weight_grad(left, right, target):
        def tile(start):
            side = dot(left[pl.ds(start, TILE), :], right[...]).astype(BF16)
            for y in range(2):
                store_blocks(target.at[y], start, side[:, y * cols : (y + 1) * cols])

        row_tiles(DPAD, tile)

    weight_grad(c_t, hid, down_g)
    total = PlaneScatter(p, down_g, down_r, depth // 2, trim)
    total.start()
    down.arrived()

    for s in (1, 0):
        n_from, c_from = sides(s)

        def tile(start):
            span, both = pl.ds(start, TILE), pl.ds(s * tokens + start, TILE)
            part = None
            for y in range(2):
                lanes = slice(y * cols, (y + 1) * cols)
                w_down = down_buf[y].reshape(DPAD, cols)
                grad_hid = dot(c_from[span, :], w_down)
                d_gate[both, lanes] = (grad_hid * d_gate[both, lanes].astype(F32)).astype(BF16)
                d_up[both, lanes] = (grad_hid * d_up[both, lanes].astype(F32)).astype(BF16)
                out = dot_nt(hid[both, lanes], w_down)
                part = out if part is None else part + out
            back = dot_nt(d_gate[both, :], wide_w[0].reshape(DPAD, 2 * cols))
            back += dot_nt(d_up[both, :], wide_w[1].reshape(DPAD, 2 * cols))
            if s:
                parts[0, span, :] = part.astype(BF16)
                parts[1, span, :] = back.astype(BF16)
            else:
                ffn_own[span, :] = part + middle[span, :]
                grad_n2[span, :] = back

        row_tiles(tokens, tile)
        if s:
            shared = [p.copy("c", parts.at[n], received.at[n]) for n in range(2)]
            total.forward()
    saved = []
    for w, right in ((0, d_gate), (1, d_up)):
        weight_grad(n_t, right, packed.at[w])
        made = pltpu.make_async_copy(packed.at[w], grads.at[w], local_sems.at[w])
        made.start()
        saved.append(made)
    for made in shared:
        made.wait_recv()

    narrow(hidden_out, ffn_own[...] + received[0].astype(F32), depth, rows, pad)
    grad_n2[...] += received[1].astype(F32)
    total.add()
    down_sum[...] = total.total[...]
    total.finish()
    down.finish()
    for made in shared + [n_copy, c_copy]:
        made.wait_send()
    for made in saved:
        made.wait()


def ffn(normed2, cot_t, middle, ffn_w, down_w, rows):
    width, tokens = cot_t.shape
    depth, pad, cols = down_w.shape
    token_rows = pltpu.VMEM((tokens, DPAD), BF16)
    wide = pltpu.VMEM((2 * tokens, 2 * cols), BF16)
    flipped = pltpu.VMEM((DPAD, 2 * tokens), BF16)
    pair = pltpu.VMEM((2, tokens, DPAD), BF16)
    copies = 4 + 4 + 6
    return pl.pallas_call(
        functools.partial(ffn_kernel, depth, rows),
        out_shape=[
            jax.ShapeDtypeStruct((2, 2, 2 * depth, pad, cols), BF16),
            jax.ShapeDtypeStruct((depth, pad, cols), BF16),
            jax.ShapeDtypeStruct((width, tokens), BF16),
            jax.ShapeDtypeStruct((tokens, DPAD), F32),
            jax.ShapeDtypeStruct((tokens, DPAD), BF16),
        ],
        in_specs=vmem_specs(3) + [pl.BlockSpec(memory_space=pl.ANY)] * 2,
        out_specs=[pl.BlockSpec(memory_space=pl.ANY)] + vmem_specs(4),
        scratch_shapes=[
            pltpu.VMEM((2, 2, depth, pad, 2 * cols), BF16),
            pltpu.VMEM((2, 2, depth, pad, cols), BF16),
            pltpu.VMEM((2, 2 * depth, pad, cols), BF16),
            pltpu.VMEM((3 * depth, pad, cols), BF16),
            token_rows, token_rows, wide, wide, wide, flipped, flipped,
            pltpu.VMEM((tokens, DPAD), F32), pair, pair,
            pltpu.VMEM((2, 2, 2 * depth, pad, cols), BF16),
            pltpu.SemaphoreType.DMA((copies,)),
            pltpu.SemaphoreType.DMA((copies,)),
            pltpu.SemaphoreType.DMA((5,)),
        ],
        compiler_params=pltpu.CompilerParams(
            vmem_limit_bytes=61 << 20, collective_id=1, has_side_effects=True
        ),
        cost_estimate=pl.CostEstimate(
            flops=24 << 30, bytes_accessed=30 << 20, transcendentals=2 << 20
        ),
        name="ffn",
    )(normed2, cot_t, middle, ffn_w, down_w)


def mid_kernel(
    depth, width,
    ffn_g, down_sum, grad_n2, middle, cot, gains, out_w, q, kv, attn, lse, segments,
    dq_t, dkv_sum, grad_middle, gain_grad, out_grad, down_grad, gate_grad, up_sum,
    mid_b, out_g, out_c, out_r, ffn_r, down_r, stage, grad_attn, q_aug, g_aug, q3, g3, k3, v3, k_t,
    dkv, acc_kv, diagonal, kv_c, kv_y, send_sems, recv_sems, local_sems,
):
    tokens = q.shape[0]
    tiles = tokens // TILE
    back = 1024 // TILE
    rows = down_grad.shape[0]
    pad = DPAD // (2 * depth)
    out_cols = HEADS * HEAD_DIM // 4
    p = Place(depth, send_sems, recv_sems)
    trim = lambda ref: ref.at[..., pl.ds(0, trimmed(rows, pad)), :]
    p.barrier()
    ffn_sums = [
        PlaneScatter(
            p, ffn_g.at[w], ffn_r.at[w], (0, depth // 2)[w], trim, stage.at[w],
            local_sems.at[pl.ds(3 * w, 3)],
        )
        for w in range(2)
    ]
    ffn_sums[0].start_far()
    ffn_sums[1].start_far()
    ffn_sums[0].start_near()
    down_total = ZSum(p, down_sum, down_r, trim)

    gain = gains[1:2, :]
    gain_grad[...] = jnp.zeros_like(gain_grad)

    def norm_tile(start):
        span = pl.ds(start, TILE)
        mid, up = middle[span, :], grad_n2[span, :]
        inv = lax.rsqrt(mean_rows(mid * mid, width) + EPSILON)
        scaled = up * gain
        mean = mean_rows(scaled * mid, width)
        grad = cot[span, :].astype(F32) + inv * (scaled - mid * (inv * inv * mean))
        grad_middle[span, :] = grad
        gain_grad[...] += jnp.sum(up * mid * inv, axis=0, keepdims=True)
        mid_b[span, :] = grad.astype(BF16)
        for b in range(4):
            side = dot_nt(mid_b[span, :], out_w[b % 2, b // 2])
            grad_attn[span, b * out_cols : (b + 1) * out_cols] = side.astype(BF16)

    row_tiles(tokens, norm_tile)
    attn_t = attn[...].astype(F32).T
    for b in range(4):
        left = attn_t[b * out_cols : (b + 1) * out_cols, :].astype(BF16)
        spread_blocks(out_g.at[b % 2, b // 2], dot(left, mid_b[...]), pad)
    out_cross = p.copy("c", out_g.at[1 - p.c], out_c)

    def block_span(block):
        return pl.ds(pl.multiple_of(block * tokens, tokens), tokens)

    own_seg = segments[:, block_span(p.m)]
    nothing = jnp.zeros((1, TILE), F32)
    q_flat = (q[...].astype(F32) * SCORE_SCALE).T.astype(BF16)
    g_flat = grad_attn[...].astype(F32).T
    for h in range(HEADS):
        g, j = h // GROUP, h % GROUP
        span = slice(h * HEAD_DIM, (h + 1) * HEAD_DIM)
        for i in range(tiles):
            cols, lanes = slice(i * TILE, (i + 1) * TILE), head_lanes(i, j)
            sides = g_flat[span, cols]
            delta = jnp.sum(sides * attn_t[span, cols], axis=0, keepdims=True)
            q_aug[g, :HEAD_DIM, lanes] = q_flat[span, cols]
            q_aug[g, HEAD_DIM:, lanes] = query_features(
                own_seg[:, cols], three_parts(-lse[g : g + 1, lanes])
            )
            g_aug[g, :HEAD_DIM, lanes] = sides.astype(BF16)
            g_aug[g, HEAD_DIM:, lanes] = features(
                three_parts(-delta), [nothing] * SEGMENTS
            ).astype(BF16)
            q3[g, lanes, :] = q[cols, span]
            g3[g, lanes, :] = grad_attn[cols, span]
    for n in range(3):
        block = jnp.maximum(p.m - n, 0)
        span = block_span(block)
        added = key_features(segments[:, span])
        for g in range(KV_HEADS):
            part = kv[block, g]
            k_t[g * HEAD_DIM : (g + 1) * HEAD_DIM, span] = transposed(part)[:HEAD_DIM]
            k3[g, span, :HEAD_DIM] = part[:, :HEAD_DIM]
            v3[g, span, :HEAD_DIM] = part[:, HEAD_DIM:]
            k3[g, span, HEAD_DIM:] = added
            v3[g, span, HEAD_DIM:] = added
    diagonal[...] = diagonal_bias()
    dq_t[...] = jnp.zeros_like(dq_t)
    dkv[...] = jnp.zeros_like(dkv)
    out_cross.wait_recv()
    own = out_g.at[p.c]
    own[...] = (own[...].astype(F32) + out_c[...].astype(F32)).astype(BF16)
    out_sum = PlaneScatter(p, own, out_r, depth // 2)
    out_sum.start()
    ffn_sums[0].forward()
    ffn_sums[1].start_near()

    def key_tile(t, queries, on_diagonal=()):
        keys = pl.ds(pl.multiple_of(t * TILE, TILE), TILE)

        def group(g, carry):
            k_g, v_g = k3[g, keys, :], v3[g, keys, :]
            kt_g = k_t[pl.ds(pl.multiple_of(g * HEAD_DIM, HEAD_DIM), HEAD_DIM), keys]
            dk, dv = None, None
            for i in queries:
                lanes = pl.ds(i * WIDE, WIDE)
                scores = dot(k_g, q_aug[g, :, lanes])
                if i in on_diagonal:
                    scores += diagonal[...]
                probs = jnp.exp2(scores * LOG2E)
                dscores = (probs * dot(v_g, g_aug[g, :, lanes])).astype(BF16)
                add_v = dot(probs.astype(BF16), g3[g, lanes, :])
                add_k = dot(dscores, q3[g, lanes, :])
                dq_t[g, :, lanes] += dot(kt_g, dscores)
                dk = add_k if dk is None else dk + add_k
                dv = add_v if dv is None else dv + add_v
            acc_kv[g] = dk * SCORE_SCALE
            acc_kv[KV_HEADS + g] = dv
            return carry

        lax.fori_loop(0, KV_HEADS, group, 0)
        for n in range(2 * KV_HEADS):
            dkv[keys, n * HEAD_DIM : (n + 1) * HEAD_DIM] = acc_kv[n].astype(BF16)

    def key_span(low, high, queries):
        def step(t, carry):
            key_tile(t, queries)
            return carry

        lax.fori_loop(low, high, step, 0)

    def part_of(index):
        return dkv.at[pl.ds(pl.multiple_of(index * tokens, tokens), tokens)]

    first = p.m * tiles
    key_span(jnp.maximum(first - back, 0), jnp.maximum(first + 1 - back, 0), (0,))
    key_span(jnp.maximum(first + 1 - back, 0), jnp.maximum(first - 2, 0), (0, 1))
    ffn_sums[1].forward()
    key_span(jnp.maximum(first - 2, 0), jnp.maximum(first - 1, 0), (0, 1))
    key_span(jnp.maximum(first - 1, 0), first, (0, 1))
    beside = p.m + 1 - 2 * p.c
    cross = [
        p.copy("c", part_of(index), kv_c.at[n])
        for n, index in enumerate((beside, (beside + 2) % 4))
    ]
    out_sum.forward()
    cross[1].wait_recv()
    away = part_of((p.m + 2) % 4)
    away[...] = (away[...].astype(F32) + kv_c[1].astype(F32)).astype(BF16)
    across = p.copy("y", away, kv_y)
    ffn_sums[0].over_z()
    key_tile(first + 1, (1,), (1,))
    key_tile(first, (0, 1), (0,))
    out_sum.over_z()
    down_grad[...] = down_total.result()[:rows]
    gate_grad[...] = ffn_sums[0].result()[:rows]
    ffn_sums[1].add()
    up_sum[...] = ffn_sums[1].total[...]
    cross[0].wait_recv()
    across.wait_recv()
    dkv_sum[...] = part_of(p.m)[...].astype(F32) + kv_c[0].astype(F32) + kv_y[...].astype(F32)
    out_grad[...] = one_block(out_sum.result(), rows, pad)
    for part in ffn_sums + [out_sum, down_total]:
        part.finish()
    for made in cross + [across, out_cross]:
        made.wait_send()


def middle_back(ffn_g, down_sum, grad_n2, middle, cot, gains, out_w, q, kv, attn, lse, segments,
                depth, rows, width):
    tokens, query_cols = q.shape
    pad = DPAD // (2 * depth)
    cols = ffn_g.shape[-1]
    kv_cols = KV_HEADS * kv.shape[-1]
    out_cols = query_cols // 4
    whole = 4 * tokens
    slots = scatter_slots(depth)
    copies = 3 * scatter_copies(depth) + 4 + depth - 1
    heads_q = pltpu.VMEM((KV_HEADS, GROUP * tokens, HEAD_DIM), BF16)
    heads_kv = pltpu.VMEM((KV_HEADS, whole, AUGMENTED), BF16)
    flipped = pltpu.VMEM((KV_HEADS, AUGMENTED, GROUP * tokens), BF16)
    return pl.pallas_call(
        functools.partial(mid_kernel, depth, width),
        out_shape=[
            jax.ShapeDtypeStruct((KV_HEADS, HEAD_DIM, GROUP * tokens), F32),
            jax.ShapeDtypeStruct((tokens, kv_cols), F32),
            jax.ShapeDtypeStruct((tokens, DPAD), F32),
            jax.ShapeDtypeStruct((1, DPAD), F32),
            jax.ShapeDtypeStruct((out_cols, rows), F32),
            *[jax.ShapeDtypeStruct((rows, cols), F32)] * 2,
            jax.ShapeDtypeStruct((depth, pad, cols), BF16),
        ],
        in_specs=[pl.BlockSpec(memory_space=pl.ANY)] + vmem_specs(11),
        out_specs=vmem_specs(8),
        scratch_shapes=[
            pltpu.VMEM((tokens, DPAD), BF16),
            pltpu.VMEM((2, 2, 2 * depth, *block_shape(out_cols, pad)), BF16),
            pltpu.VMEM((2, 2 * depth, *block_shape(out_cols, pad)), BF16),
            pltpu.VMEM((slots, *block_shape(out_cols, pad)), BF16),
            pltpu.VMEM((2, slots, pad, cols), BF16),
            pltpu.VMEM((depth - 1, pad, cols), BF16),
            pltpu.VMEM((2, 2 * depth, pad, cols), BF16),
            pltpu.VMEM((tokens, query_cols), BF16),
            flipped, flipped, heads_q, heads_q, heads_kv, heads_kv,
            pltpu.VMEM((KV_HEADS * HEAD_DIM, whole), BF16),
            pltpu.VMEM((whole, kv_cols), BF16),
            pltpu.VMEM((2 * KV_HEADS, TILE, HEAD_DIM), F32),
            pltpu.VMEM((TILE, WIDE), F32),
            pltpu.VMEM((2, tokens, kv_cols), BF16),
            pltpu.VMEM((tokens, kv_cols), BF16),
            pltpu.SemaphoreType.DMA((copies,)),
            pltpu.SemaphoreType.DMA((copies,)),
            pltpu.SemaphoreType.DMA((6,)),
        ],
        compiler_params=pltpu.CompilerParams(
            vmem_limit_bytes=61 << 20, collective_id=2, has_side_effects=True
        ),
        cost_estimate=pl.CostEstimate(
            flops=40 << 30, bytes_accessed=50 << 20, transcendentals=8 << 20
        ),
        name="middle_back",
    )(ffn_g, down_sum, grad_n2, middle, cot, gains, out_w, q, kv, attn, lse, segments)


def tail_kernel(
    depth, rows, width,
    dq_t, dkv, cosine_t, sine_t, x_t, grad_middle, gains, in_w, gain2, up_sum,
    grad_hidden, in_grad, gain1_sum, gain2_sum, up_grad,
    ffn_r, proj, proj_b, in_g, in_c, in_r, grad_x, gain_own, gain_r, send_sems, recv_sems,
):
    tokens = x_t.shape[1]
    query_cols = HEADS * HEAD_DIM
    in_cols = in_w.shape[2]
    pad = DPAD // (2 * depth)
    turned = (HEADS + KV_HEADS) * HEAD_DIM
    p = Place(depth, send_sems, recv_sems)
    p.barrier()
    trim = lambda ref: ref.at[..., pl.ds(0, trimmed(rows, pad)), :]
    up_total = ZSum(p, up_sum, ffn_r, trim)
    x_f = widen(x_t, depth, rows, pad)
    gain = gains[0:1, :]
    inv = lax.rsqrt(mean_rows(x_f * x_f, width) + EPSILON)
    normed1 = (x_f * inv * gain).astype(BF16)
    cosine = lane_tables(cosine_t[...])
    sine = signed(lane_tables(sine_t[...]), True)
    turned_parts = [
        jnp.concatenate(
            [dq_t[h // GROUP, :, head_lanes(i, h % GROUP)] for i in range(tokens // TILE)], axis=1
        )
        for h in range(HEADS)
    ]
    proj[:, :query_cols] = jnp.concatenate(turned_parts, axis=0).T * SCORE_SCALE
    proj[:, query_cols:] = dkv[...]
    for j in range(turned // 128):
        lanes = slice(128 * j, 128 * (j + 1))
        proj[:, lanes] = rope(proj[:, lanes], cosine, sine)
    for b in range(4):
        proj_b[b] = proj[:, b * in_cols : (b + 1) * in_cols].astype(BF16)
    cuts = halves(in_g.shape[-2])
    parts = [lambda ref, cut=cut: ref.at[..., cut, :] for cut in cuts]
    for other in (1, 0):
        c = (1 - p.c) if other else p.c
        for y in range(2):
            left = transposed(proj_b[2 * y + c])
            spread_blocks(in_g.at[c, y], dot(left, normed1), pad)
        if other:
            crosses = [p.copy("c", part(in_g.at[c]), part(in_c)) for part in parts]
    own = in_g.at[p.c]
    in_sums = []
    for part, cross in zip(parts, crosses):
        cross.wait_recv()
        kept = part(own)
        kept[...] = (kept[...].astype(F32) + part(in_c)[...].astype(F32)).astype(BF16)
        in_sums.append(PlaneScatter(p, own, in_r, depth // 2, part))
        in_sums[-1].start_far()
    in_sums[0].forward()
    in_sums[0].start_near()
    up = None
    for b in range(4):
        term = dot(proj_b[b], in_w[b % 2, b // 2])
        up = term if up is None else up + term
    scaled = up * gain
    mean = mean_rows(scaled * x_f, width)
    grad_x[...] = grad_middle[...] + inv * (scaled - x_f * (inv * inv * mean))
    gain_own[...] = jnp.zeros_like(gain_own)
    gain_own[0:1, :] = jnp.sum(up * x_f * inv, axis=0, keepdims=True)
    gain_own[1:2, :] = gain2[...]
    in_sums[1].forward()
    in_sums[1].start_near()
    sent = []
    for n, kind in enumerate(("c", "y", "x")):
        made = p.copy(kind, gain_own.at[pl.ds(8 * n, 8)], gain_r.at[pl.ds(8 * n, 8)])
        sent.append(made)
        if n == 0:
            narrow(grad_hidden, grad_x[...], depth, rows, pad)
        made.wait_recv()
        if n == 0:
            in_sums[0].over_z()
        gain_own[8 * (n + 1) : 8 * (n + 2), :] = (
            gain_own[8 * n : 8 * (n + 1), :] + gain_r[8 * n : 8 * (n + 1), :]
        )
    in_sums[1].over_z()
    last = gain_own.at[pl.ds(24, 8)]
    arriving = [p.copy(k, last, gain_r.at[pl.ds(24 + 8 * k, 8)]) for k in range(1, depth)]
    total = last[...]
    for k, made in enumerate(arriving):
        made.wait_recv()
        total += gain_r[32 + 8 * k : 40 + 8 * k, :]
    mine = jnp.zeros((8, pad), F32)
    for n in range(2 * depth):
        mine = jnp.where(n == p.x * depth + p.z, total[:, n * pad : (n + 1) * pad], mine)
    gain1_sum[...] = mine[0:1, :rows]
    gain2_sum[...] = mine[1:2, :rows]
    up_grad[...] = up_total.result()[:rows]
    up_total.finish()
    value = jnp.concatenate([in_sum.result() for in_sum in in_sums], axis=0)
    in_grad[...] = one_block(value, rows, pad)
    for in_sum in in_sums:
        in_sum.finish()
    for made in sent + arriving + crosses:
        made.wait_send()


def tail(
    dq_t, dkv, cosine_t, sine_t, x_t, grad_middle, gains, in_w, gain2, up_sum,
    depth, rows, width,
):
    tokens = x_t.shape[1]
    pad = DPAD // (2 * depth)
    in_cols = in_w.shape[2]
    total = HEADS * HEAD_DIM + dkv.shape[1]
    slots = scatter_slots(depth)
    copies = 2 * scatter_copies(depth) + 2 + 3 + 2 * (depth - 1)
    cols = up_sum.shape[2]
    return pl.pallas_call(
        functools.partial(tail_kernel, depth, rows, width),
        out_shape=[
            jax.ShapeDtypeStruct((width, tokens), F32),
            jax.ShapeDtypeStruct((in_cols, rows), F32),
            *[jax.ShapeDtypeStruct((1, rows), F32)] * 2,
            jax.ShapeDtypeStruct((rows, cols), F32),
        ],
        in_specs=vmem_specs(10),
        out_specs=vmem_specs(5),
        scratch_shapes=[
            pltpu.VMEM((depth - 1, pad, cols), BF16),
            pltpu.VMEM((tokens, total), F32),
            pltpu.VMEM((4, tokens, in_cols), BF16),
            pltpu.VMEM((2, 2, 2 * depth, *block_shape(in_cols, pad)), BF16),
            pltpu.VMEM((2, 2 * depth, *block_shape(in_cols, pad)), BF16),
            pltpu.VMEM((slots, *block_shape(in_cols, pad)), BF16),
            pltpu.VMEM((tokens, DPAD), F32),
            pltpu.VMEM((32, DPAD), F32),
            pltpu.VMEM((24 + 8 * depth, DPAD), F32),
            pltpu.SemaphoreType.DMA((copies,)),
            pltpu.SemaphoreType.DMA((copies,)),
        ],
        compiler_params=pltpu.CompilerParams(
            vmem_limit_bytes=61 << 20, collective_id=3, has_side_effects=True
        ),
        cost_estimate=pl.CostEstimate(
            flops=8 << 30, bytes_accessed=30 << 20, transcendentals=0
        ),
        name="tail",
    )(dq_t, dkv, cosine_t, sine_t, x_t, grad_middle, gains, in_w, gain2, up_sum)


def rotary_tables(position_ids):
    half_dim = HEAD_DIM // 2
    frequency = jnp.exp(
        jnp.arange(half_dim, dtype=F32) * (-2.0 * math.log(10000.0) / HEAD_DIM)
    )
    angles = frequency[:, None] * position_ids.astype(F32)[None, :]
    return jnp.cos(angles), jnp.sin(angles)


def per_device(
    hidden_in, cotangent, segments, positions, attn_in, attn_out, w_gate, w_up, w_down,
    norm1_gain, norm2_gain,
):
    tokens, width = hidden_in.shape[1:]
    dp_size = lax.axis_size("dp")
    depth = dp_size // 2
    rows = width // dp_size
    pad = DPAD // dp_size

    ffn_blocks = [w_gate, w_up, w_down.T]
    if trimmed(rows, pad) == pad:
        ffn_blocks = [jnp.pad(w, ((0, pad - rows), (0, 0))) for w in ffn_blocks]
    x_t, cot_t = hidden_in[0].T, cotangent[0].T
    cosine_t, sine_t = rotary_tables(positions[0])
    attn, lse, middle, normed2, gains, q, kv, out_w, in_w, ffn_w, down_w = front(
        attn_in.T, attn_out, norm1_gain[None], norm2_gain[None], *ffn_blocks,
        x_t, cosine_t, sine_t, segments, depth, rows,
    )
    ffn_g, down_sum, hidden_out, grad_n2, cot = ffn(normed2, cot_t, middle, ffn_w, down_w, rows)
    dq_t, dkv, grad_middle, gain2, g_out, g_down, g_gate, up_sum = middle_back(
        ffn_g, down_sum, grad_n2, middle, cot, gains, out_w, q, kv, attn, lse, segments,
        depth, rows, width,
    )
    grad_hidden, g_in, g_gain1, g_gain2, g_up = tail(
        dq_t, dkv, cosine_t, sine_t, x_t, grad_middle, gains, in_w, gain2, up_sum,
        depth, rows, width,
    )
    return (
        hidden_out.T[None],
        grad_hidden.T[None],
        g_in.T,
        g_out,
        g_gate,
        g_up,
        g_down.T,
        g_gain1[0],
        g_gain2[0],
    )


def solution(mesh):
    return jax.shard_map(
        per_device,
        mesh=mesh,
        in_specs=(
            P("dp", "mp", None),
            P("dp", "mp", None),
            P("dp", None),
            P("dp", "mp"),
            P("dp", "mp"),
            P("mp", "dp"),
            P("dp", "mp"),
            P("dp", "mp"),
            P("mp", "dp"),
            P("dp"),
            P("dp"),
        ),
        out_specs=(
            P("dp", "mp", None),
            P("dp", "mp", None),
            P("dp", "mp"),
            P("mp", "dp"),
            P("dp", "mp"),
            P("dp", "mp"),
            P("mp", "dp"),
            P("dp"),
            P("dp"),
        ),
        check_vma=False,
    )
```
